32 devices in a mesh: dp: 4 (over y, core), ctx: 4 (over z), tp: 2 (over x).
Axes of the slice: x: 2, y: 2, z: 4, core: 2. Of those that a mesh axis runs over, the one named last changes fastest.
Arguments:
- prompt_in: bfloat16 [8, 1024, 768], P('dp', ('ctx', 'tp')), may hold values from -6 to 6
- cont_in: bfloat16 [8, 8, 128, 768], P('dp', 'ctx', 'tp'), may hold values from -6 to 6
- prompt_embed: bfloat16 [8, 1024, 768], P('dp', ('ctx', 'tp')), may hold values from -6 to 6
- cont_embed: bfloat16 [8, 8, 128, 768], P('dp', 'ctx', 'tp'), may hold values from -6 to 6
- prompt_earlier: bfloat16 [3, 8, 1024, 768], P(None, 'dp', ('ctx', 'tp')), may hold values from -6 to 6
- cont_earlier: bfloat16 [3, 8, 8, 128, 768], P(None, 'dp', 'ctx', 'tp'), may hold values from -6 to 6
- ln1_gain: bfloat16 [768], P('dp'), may hold values from 0.5 to 1.5
- ln1_bias: bfloat16 [768], P('dp'), may hold values from -1.75 to 1.75
- ln2_gain: bfloat16 [768], P('dp'), may hold values from 0.5 to 1.5
- ln2_bias: bfloat16 [768], P('dp'), may hold values from -1.75 to 1.75
- w_qkv: bfloat16 [768, 3, 768], P('dp', None, 'tp'), may hold values from -0.21875 to 0.21875
- w_out: bfloat16 [768, 768], P('tp', 'dp'), may hold values from -3 to 3
- w_up: bfloat16 [768, 3072], P('dp', 'tp'), may hold values from -0.21875 to 0.21875
- w_down: bfloat16 [3072, 768], P('tp', 'dp'), may hold values from -0.109375 to 0.109375
- mix_weights: float32 [5], replicated, may hold values from 0.3 to 1
- prompt_cot: bfloat16 [8, 1024, 768], P('dp', ('ctx', 'tp')), may hold values from -6 to 6
- cont_cot: bfloat16 [8, 8, 128, 768], P('dp', 'ctx', 'tp'), may hold values from -6 to 6
Outputs:
- prompt_out: bfloat16 [8, 1024, 768], P('dp', ('ctx', 'tp'))
- cont_out: bfloat16 [8, 8, 128, 768], P('dp', 'ctx', 'tp')
- prompt_in_grad: bfloat16 [8, 1024, 768], P('dp', ('ctx', 'tp'))
- cont_in_grad: bfloat16 [8, 8, 128, 768], P('dp', 'ctx', 'tp')
- ln1_gain_grad: float32 [768], P('dp')
- ln1_bias_grad: float32 [768], P('dp')
- ln2_gain_grad: float32 [768], P('dp')
- ln2_bias_grad: float32 [768], P('dp')
- w_qkv_grad: float32 [768, 3, 768], P('dp', None, 'tp')
- w_out_grad: float32 [768, 768], P('tp', 'dp')
- w_up_grad: float32 [768, 3072], P('dp', 'tp')
- w_down_grad: float32 [3072, 768], P('tp', 'dp')
- mix_grad: float32 [5], replicated
The draws below stay inside these ranges and needn't reach their ends.
All inputs are finite; a program needn't handle non-finite values.
Results may differ from the reference program's by a relative error of at most 0.02.
Values may be sent and summed in bfloat16 or wider, within the bound.
A program may use at most 256 MiB of HBM per device.

```python
from functools import partial
import jax
import jax.numpy as jnp
from jax import lax

D = 768
H = 12
HD = 64
FF = 3072
HH = 768
PROMPT = 1024
CONT = 8
CL = 128
GROUPS = 8


def steps_of(rng, extent, split, least, largest):
    gain, own = 1.0, jax.random.fold_in(rng, 6)
    for axis_at, blocks in split:
        heights = jnp.exp(jax.random.uniform(jax.random.fold_in(own, axis_at), (blocks,), jnp.float32, least / len(split), largest / len(split)))
        gain = gain * jnp.repeat(heights, extent[axis_at] // blocks).reshape([-1 if axis == axis_at else 1 for axis in range(len(extent))])
    return gain


def normal_values(key, extent, width, reach, pieces=(), kind=jnp.bfloat16):
    loudness = steps_of(key, extent, pieces, -0.22, 0.18) if pieces else 1.0
    entries = jax.random.normal(key, extent, jnp.float32) * width * loudness
    return jnp.minimum(jnp.maximum(entries, -reach), reach).astype(kind)


def setup_inputs(seed: int = 0) -> dict:
    seeds = jax.random.split(jax.random.key(seed), 18)
    return {
        "prompt_in": normal_values(seeds[0], (GROUPS, PROMPT, D), 1.0, 6.0, ((0, 4), (1, 8))),
        "cont_in": normal_values(seeds[1], (GROUPS, CONT, CL, D), 1.0, 6.0, ((0, 4), (1, 4), (2, 2))),
        "prompt_embed": normal_values(seeds[2], (GROUPS, PROMPT, D), 1.0, 6.0, ((0, 4), (1, 8))),
        "cont_embed": normal_values(seeds[3], (GROUPS, CONT, CL, D), 1.0, 6.0, ((0, 4), (1, 4), (2, 2))),
        "prompt_earlier": normal_values(seeds[4], (3, GROUPS, PROMPT, D), 1.0, 6.0, ((1, 4), (2, 8))),
        "cont_earlier": normal_values(seeds[5], (3, GROUPS, CONT, CL, D), 1.0, 6.0, ((1, 4), (2, 4), (3, 2))),
        "ln1_gain": jnp.clip(1.0 + 0.1 * jax.random.normal(seeds[6], (D,), jnp.float32), 0.5, 1.5).astype(jnp.bfloat16),
        "ln1_bias": normal_values(seeds[7], (D,), 0.3, 1.75, ((0, 4),)),
        "ln2_gain": jnp.clip(1.0 + 0.1 * jax.random.normal(seeds[8], (D,), jnp.float32), 0.5, 1.5).astype(jnp.bfloat16),
        "ln2_bias": normal_values(seeds[9], (D,), 0.3, 1.75, ((0, 4),)),
        "w_qkv": normal_values(seeds[10], (D, 3, HH), D ** -0.5, 0.21875, ((0, 4), (2, 2))),
        "w_out": normal_values(seeds[11], (HH, D), 4 ** -0.5, 3.0, ((0, 2), (1, 4))),
        "w_up": normal_values(seeds[12], (D, FF), D ** -0.5, 0.21875, ((0, 4), (1, 2))),
        "w_down": normal_values(seeds[13], (FF, D), FF ** -0.5, 0.109375, ((0, 2), (1, 4))),
        "mix_weights": jnp.clip(jax.random.uniform(seeds[14], (5,), jnp.float32, 0.3, 1.0), 0.3, 1.0),
        "prompt_cot": normal_values(seeds[15], (GROUPS, PROMPT, D), 1.0, 6.0, ((0, 4), (1, 8))),
        "cont_cot": normal_values(seeds[16], (GROUPS, CONT, CL, D), 1.0, 6.0, ((0, 4), (1, 4), (2, 2))),
    }


HIGH = lax.Precision.HIGHEST
eps_norm = 1e-05
neg_fill = -1e+30
theta_base = 10000.0

@jax.custom_vjp
def low(v):
    return lax.optimization_barrier(v.astype(jnp.bfloat16)).astype(jnp.float32)

@jax.custom_vjp
def low_back(v):
    return v

def low_keep(v):
    return (low(v), None)

def low_pass(kept, grad):
    return (grad,)

def back_keep(v):
    return (v, None)

def back_low(kept, grad):
    return (low(grad),)
low.defvjp(low_keep, low_pass)
low_back.defvjp(back_keep, back_low)

def layer_norm(features, norm_gain, norm_bias):
    average = lax.optimization_barrier(jnp.mean(features, axis=-1, keepdims=True))
    centered = features - average
    variance = lax.optimization_barrier(jnp.mean(centered * centered, axis=-1, keepdims=True))
    return centered * lax.rsqrt(variance + eps_norm) * norm_gain + norm_bias

def angle_tables(positions, half_dim):
    frequency = theta_base ** (-(jnp.arange(half_dim).astype(jnp.float32) / half_dim))
    angles = positions.astype(jnp.float32)[:, None] * frequency[None, :]
    return (jnp.cos(angles), jnp.sin(angles))

def rotate(features, cosine, sine_table):
    half_dim = features.shape[-1] // 2
    leading = features[..., :half_dim]
    trailing = features[..., half_dim:]
    cos_rows = cosine[:, None, :]
    sin_rows = sine_table[:, None, :]
    return jnp.concatenate([leading * cos_rows - trailing * sin_rows, trailing * cos_rows + leading * sin_rows], axis=-1)

def attend(queries, key_vecs, values, allowed):
    scores = low_back(jnp.einsum('qhd,khd->hqk', queries, key_vecs, precision=HIGH) * 0.125)
    scores = jnp.where(allowed[None], scores, neg_fill)
    row_max = lax.optimization_barrier(jnp.max(scores, axis=-1, keepdims=True))
    exponent = jnp.exp(scores - row_max)
    weights_low = low(exponent / lax.optimization_barrier(jnp.sum(exponent, axis=-1, keepdims=True)))
    return jnp.einsum('hqk,khd->qhd', weights_low, values, precision=HIGH)

def one_group(params, group_data):
    gain_one, bias_one, gain_two, bias_two, weight_qkv, weight_out, weight_up, weight_down = params
    prompt_rows, cont_rows = group_data
    group_rows = jnp.concatenate([prompt_rows, cont_rows.reshape(CONT * CL, D)], axis=0)
    normed = low(layer_norm(group_rows, gain_one, bias_one))
    mixed_qkv = low_back(jnp.dot(normed, weight_qkv.reshape(D, 3 * HH), precision=HIGH)).reshape(-1, 3, H, HD)
    positions = jnp.concatenate([jnp.arange(PROMPT).astype(jnp.int32), PROMPT + jnp.tile(jnp.arange(CL).astype(jnp.int32), CONT)])
    cosine, sine_table = angle_tables(positions, HD // 2)
    queries = low(rotate(mixed_qkv[:, 0], cosine, sine_table))
    key_vecs = low(rotate(mixed_qkv[:, 1], cosine, sine_table))
    values = low(mixed_qkv[:, 2])
    causal = jnp.arange(PROMPT).astype(jnp.int32)[:, None] >= jnp.arange(PROMPT).astype(jnp.int32)[None, :]
    prompt_att = attend(queries[:PROMPT], key_vecs[:PROMPT], values[:PROMPT], causal)
    own_mask = jnp.arange(CL).astype(jnp.int32)[:, None] >= jnp.arange(CL).astype(jnp.int32)[None, :]
    cont_allowed = jnp.concatenate([jnp.ones((CL, PROMPT), dtype=jnp.bool_), own_mask], axis=1)

    def one_cont(member):
        cont_queries, cont_keys, cont_values = member
        return attend(cont_queries, jnp.concatenate([key_vecs[:PROMPT], cont_keys], axis=0), jnp.concatenate([values[:PROMPT], cont_values], axis=0), cont_allowed)
    cont_att = jax.vmap(one_cont)((queries[PROMPT:].reshape(CONT, CL, H, HD), key_vecs[PROMPT:].reshape(CONT, CL, H, HD), values[PROMPT:].reshape(CONT, CL, H, HD)))
    attended = jnp.concatenate([prompt_att, cont_att.reshape(CONT * CL, H, HD)], axis=0).reshape(-1, HH)
    attended = low_back(low(attended))
    branch = low_back(jnp.dot(attended, weight_out, precision=HIGH))
    resid = group_rows + branch
    normed_two = low(layer_norm(resid, gain_two, bias_two))
    up_proj = low_back(jnp.dot(normed_two, weight_up, precision=HIGH))
    activated = low(jax.nn.gelu(up_proj, approximate=True))
    down_proj = low_back(jnp.dot(activated, weight_down, precision=HIGH))
    output = resid + down_proj
    return (output[:PROMPT], output[PROMPT:].reshape(CONT, CL, D))

def forward(prompt_in, cont_in, prompt_embed, cont_embed, prompt_earlier, cont_earlier, ln1_gain, ln1_bias, ln2_gain, ln2_bias, w_qkv, w_out, w_up, w_down, mix_weights):
    params = (ln1_gain, ln1_bias, ln2_gain, ln2_bias, w_qkv, w_out, w_up, w_down)
    prompt_block, cont_block = lax.map(jax.checkpoint(partial(one_group, params)), (prompt_in, cont_in))
    prompt_mix = mix_weights[0] * prompt_embed + mix_weights[1] * prompt_earlier[0] + mix_weights[2] * prompt_earlier[1] + mix_weights[3] * prompt_earlier[2] + mix_weights[4] * prompt_block
    cont_mix = mix_weights[0] * cont_embed + mix_weights[1] * cont_earlier[0] + mix_weights[2] * cont_earlier[1] + mix_weights[3] * cont_earlier[2] + mix_weights[4] * cont_block
    return (prompt_mix, cont_mix)

def reference(prompt_in, cont_in, prompt_embed, cont_embed, prompt_earlier, cont_earlier, ln1_gain, ln1_bias, ln2_gain, ln2_bias, w_qkv, w_out, w_up, w_down, mix_weights, prompt_cot, cont_cot):
    primals = tuple((member.astype(jnp.float32) for member in (prompt_in, cont_in, prompt_embed, cont_embed, prompt_earlier, cont_earlier, ln1_gain, ln1_bias, ln2_gain, ln2_bias, w_qkv, w_out, w_up, w_down, mix_weights)))
    outputs, backward = jax.vjp(forward, *primals)
    gradients = backward((prompt_cot.astype(jnp.float32), cont_cot.astype(jnp.float32)))
    return (outputs[0].astype(jnp.bfloat16), outputs[1].astype(jnp.bfloat16), gradients[0].astype(jnp.bfloat16), gradients[1].astype(jnp.bfloat16), gradients[6], gradients[7], gradients[8], gradients[9], gradients[10], gradients[11], gradients[12], gradients[13], gradients[14])
```

```python
from functools import partial

import jax
import jax.numpy as jnp
import numpy as np
from jax import lax
from jax.experimental import pallas as pl
from jax.experimental.pallas import tpu as pltpu
from jax.sharding import PartitionSpec as P

HD = 64
CL = 128
EPS = 1e-05
NEG = -1e30
F32 = jnp.float32
BF16 = jnp.bfloat16
VMEM_LIMIT = 62 * 1024 * 1024


def dot(a, b):
    return lax.dot_general(a, b, (((1,), (0,)), ((), ())), preferred_element_type=F32)


def dot_nt(a, b):
    return lax.dot_general(a, b, (((1,), (1,)), ((), ())), preferred_element_type=F32)


def norm_stats(x):
    mean = jnp.mean(x, axis=-1, keepdims=True)
    centered = x - mean
    var = jnp.mean(centered * centered, axis=-1, keepdims=True)
    scale = lax.rsqrt(var + EPS)
    return centered * scale, scale


def norm_back(grad, gain, hat, scale):
    gh = grad * gain
    return scale * (
        gh
        - jnp.mean(gh, axis=-1, keepdims=True)
        - hat * jnp.mean(gh * hat, axis=-1, keepdims=True)
    )


def rotate(x, cos, sin_hi, sin_lo):
    return x * cos + pltpu.roll(x, 32, 1) * sin_hi + pltpu.roll(x, 96, 1) * sin_lo


def rotate_back(x, cos, sin_hi, sin_lo):
    return x * cos - pltpu.roll(x, 32, 1) * sin_hi - pltpu.roll(x, 96, 1) * sin_lo


def lane_pick(shape, low):
    lanes = lax.broadcasted_iota(jnp.int32, shape, 1)
    return lanes < HD if low else lanes >= HD


def sublane_pick(shape, low):
    rows = lax.broadcasted_iota(jnp.int32, shape, 0)
    return rows < HD if low else rows >= HD


def transpose(x):
    return x.astype(F32).T.astype(x.dtype)


class Dims:
    def __init__(self, groups, prompt, pb, nc, ch, d, heads):
        self.G, self.P, self.PB, self.NC, self.CH, self.D = groups, prompt, pb, nc, ch, d
        self.NCH = nc * ch
        self.R = prompt + nc * CL
        self.NX = nc * CL
        self.NR = pb + self.NCH
        self.NP = groups * pb
        self.NT = groups * self.NR
        self.PAIRS = heads // 2
        self.COLS = 2 * self.NR


def fill_masks(dm, maskp, maskx):
    block = lax.axis_index("ctx") * lax.axis_size("tp") + lax.axis_index("tp")
    keys = lax.broadcasted_iota(jnp.int32, maskp.shape, 0)
    cols = lax.broadcasted_iota(jnp.int32, maskp.shape, 1) % dm.PB
    maskp[...] = jnp.where(keys <= cols + block * dm.PB, 0.0, NEG)
    keys = lax.broadcasted_iota(jnp.int32, maskx.shape, 0)
    cols = lax.broadcasted_iota(jnp.int32, maskx.shape, 1) % dm.NCH
    seen = (keys // CL == cols // dm.CH) & (
        keys % CL <= cols % dm.CH + lax.axis_index("tp") * dm.CH
    )
    maskx[...] = jnp.where(seen, 0.0, NEG)


def heads_columns(a, b):
    lo_a, lo_b = sublane_pick(a.shape, True), sublane_pick(b.shape, True)
    zero_a, zero_b = jnp.zeros_like(a), jnp.zeros_like(b)
    return jnp.concatenate(
        [
            jnp.where(lo_a, a, zero_a),
            jnp.where(lo_a, zero_a, a),
            jnp.where(lo_b, b, zero_b),
            jnp.where(lo_b, zero_b, b),
        ],
        axis=1,
    )


def heads_rows(a, b):
    lo_a, lo_b = lane_pick(a.shape, True), lane_pick(b.shape, True)
    zero_a, zero_b = jnp.zeros_like(a), jnp.zeros_like(b)
    return jnp.concatenate(
        [
            jnp.where(lo_a, a, zero_a),
            jnp.where(lo_a, zero_a, a),
            jnp.where(lo_b, b, zero_b),
            jnp.where(lo_b, zero_b, b),
        ],
        axis=0,
    )


def forward_kernel(
    dm,
    xp,
    xc,
    op,
    oc,
    ln,
    cos,
    shi,
    slo,
    w,
    n_out,
    k_out,
    v_out,
    q_out,
    att_out,
    lse_out,
    maskp,
    maskx,
    sbuf,
):
    G, R, PB, NCH, D = dm.G, dm.R, dm.PB, dm.NCH, dm.D
    HC = w.shape[2] // 3
    TP = w.shape[0]
    gain, bias = ln[0:1, :].astype(F32), ln[1:2, :].astype(F32)
    fill_masks(dm, maskp, maskx)

    def normed(x):
        hat, _ = norm_stats(x.astype(F32))
        return (hat * gain + bias).astype(BF16)

    def keys_values(g, x, row, table):
        rows = x.shape[0]
        n = normed(x)
        n_out[g, pl.ds(row, rows), :] = n
        c = cos[pl.ds(table, rows), :]
        hi = shi[pl.ds(table, rows), :]
        lo = slo[pl.ds(table, rows), :]
        for t in range(TP):
            kk = dot(n, w[t, :, HC : 2 * HC])
            for j in range(HC // 128):
                tile = rotate(kk[:, j * 128 : (j + 1) * 128], c, hi, lo)
                k_out[g, pl.ds(row, rows), t * HC + j * 128 : t * HC + (j + 1) * 128] = tile.astype(BF16)
            v_out[g, pl.ds(row, rows), t * HC : (t + 1) * HC] = dot(n, w[t, :, 2 * HC :]).astype(BF16)

    CHUNK = 256
    steps = dm.P // CHUNK

    def prompt_chunk(i, carry):
        g, row = i // steps, pl.multiple_of((i % steps) * CHUNK, CHUNK)
        keys_values(g, xp[g, pl.ds(row, CHUNK), :], row, row)
        return carry

    lax.fori_loop(0, G * steps, prompt_chunk, 0)

    def cont_chunk(i, carry):
        g, c = i // dm.NC, i % dm.NC
        row = pl.multiple_of(dm.P + c * CL, CL)
        keys_values(g, xc[g, c], row, dm.P)
        return carry

    lax.fori_loop(0, G * dm.NC, cont_chunk, 0)

    block = lax.axis_index("ctx") * lax.axis_size("tp") + lax.axis_index("tp")

    def queries(x, row, table):
        rows = x.shape[0]
        n = normed(x)
        c = cos[pl.ds(table, rows), :]
        hi = shi[pl.ds(table, rows), :]
        lo = slo[pl.ds(table, rows), :]
        for t in range(TP):
            qq = dot(n, w[t, :, :HC])
            for j in range(HC // 128):
                tile = rotate(qq[:, j * 128 : (j + 1) * 128], c, hi, lo).astype(BF16)
                q_out[pl.ds(row, rows), t * HC + j * 128 : t * HC + (j + 1) * 128] = (
                    tile.astype(F32) * 0.125
                ).astype(BF16)

    def own_prompt(g, carry):
        queries(op[g], pl.multiple_of(g * PB, PB), pl.multiple_of(block * PB, PB))
        return carry

    lax.fori_loop(0, G, own_prompt, 0)

    def own_cont(i, carry):
        g, c = i // dm.NC, i % dm.NC
        queries(
            oc[g, c],
            pl.multiple_of(dm.NP + i * dm.CH, dm.CH),
            pl.multiple_of(dm.P + lax.axis_index("tp") * dm.CH, dm.CH),
        )
        return carry

    lax.fori_loop(0, G * dm.NC, own_cont, 0)

    TILE = 256
    tiles = dm.P // TILE

    def attend(i, carry):
        g, pair = i // dm.PAIRS, i % dm.PAIRS
        lanes = pl.ds(pl.multiple_of(pair * 128, 128), 128)
        qp = q_out[pl.ds(pl.multiple_of(g * PB, PB), PB), lanes]
        qc = q_out[pl.ds(pl.multiple_of(dm.NP + g * NCH, NCH), NCH), lanes]
        qt = heads_columns(transpose(qp), transpose(qc))
        top = None
        for j in range(tiles):
            s = dot(k_out[g, j * TILE : (j + 1) * TILE, lanes], qt)
            sbuf[j * TILE : (j + 1) * TILE, : 2 * PB] = (
                s[:, : 2 * PB] + maskp[j * TILE : (j + 1) * TILE, :]
            )
            sbuf[j * TILE : (j + 1) * TILE, 2 * PB :] = s[:, 2 * PB :]
            here = jnp.max(sbuf[j * TILE : (j + 1) * TILE, :], axis=0, keepdims=True)
            top = here if top is None else jnp.maximum(top, here)
        sx = dot(k_out[g, dm.P :, lanes], qt[:, 2 * PB :]) + maskx[...]
        topx = jnp.max(sx, axis=0, keepdims=True)
        top = jnp.concatenate([top[:, : 2 * PB], jnp.maximum(top[:, 2 * PB :], topx)], axis=1)
        total, acc = None, None
        for j in range(tiles):
            e = jnp.exp(sbuf[j * TILE : (j + 1) * TILE, :] - top)
            here = jnp.sum(e, axis=0, keepdims=True)
            vt = transpose(v_out[g, j * TILE : (j + 1) * TILE, lanes])
            part = dot(vt, e.astype(BF16))
            total = here if total is None else total + here
            acc = part if acc is None else acc + part
        ex = jnp.exp(sx - top[:, 2 * PB :])
        partx = dot(transpose(v_out[g, dm.P :, lanes]), ex.astype(BF16))
        totalx = jnp.sum(ex, axis=0, keepdims=True)
        total = jnp.concatenate([total[:, : 2 * PB], total[:, 2 * PB :] + totalx], axis=1)
        acc_p = acc[:, : 2 * PB] / total[:, : 2 * PB]
        acc_c = (acc[:, 2 * PB :] + partx) / total[:, 2 * PB :]
        lse_out[i] = top + jnp.log(total)
        outp = jnp.where(sublane_pick((128, PB), True), acc_p[:, :PB], acc_p[:, PB:])
        outc = jnp.where(sublane_pick((128, NCH), True), acc_c[:, :NCH], acc_c[:, NCH:])
        att_out[pl.ds(pl.multiple_of(g * PB, PB), PB), lanes] = outp.T.astype(BF16)
        att_out[pl.ds(pl.multiple_of(dm.NP + g * NCH, NCH), NCH), lanes] = outc.T.astype(BF16)
        return carry

    lax.fori_loop(0, G * dm.PAIRS, attend, 0)


def mlp_kernel(
    dm,
    steps,
    mix,
    att,
    op,
    oc,
    ep,
    ec,
    yp,
    yc,
    tp_,
    tc,
    ln,
    wo,
    wu,
    wd,
    outp,
    outc,
    resg,
    gatt,
    gwo,
    gwu,
    gwd,
    small,
    resid,
    hat,
    scale,
    hn,
    hnt,
    gd,
    gdt,
    blk,
    gh,
):
    D, NP, NT, G, PB = dm.D, dm.NP, dm.NT, dm.G, dm.PB
    TP, HC = wo.shape[0], wo.shape[2]
    t, j = pl.program_id(0), pl.program_id(1)
    gain, bias = ln[2:3, :].astype(F32), ln[3:4, :].astype(F32)

    def own(prompt, cont):
        return jnp.concatenate([prompt.reshape(NP, D), cont.reshape(NT - NP, D)], axis=0)

    @pl.when((t == 0) & (j == 0))
    def _():
        branch = dot_nt(att[:, :HC], wo[0])
        for s in range(1, TP):
            branch += dot_nt(att[:, s * HC : (s + 1) * HC], wo[s])
        r = own(op[...], oc[...]).astype(F32) + branch
        resid[...] = r
        h, sc = norm_stats(r)
        hat[...] = h
        scale[...] = jnp.broadcast_to(sc, scale.shape)
        n = (h * gain + bias).astype(BF16)
        hn[...] = n
        hnt[...] = transpose(n)
        g = (mix[4] * own(tp_[...], tc[...]).astype(F32)).astype(BF16)
        gd[...] = g
        gdt[...] = transpose(g)
        blk[...] = r
        gh[...] = jnp.zeros_like(gh)

    up, dn = wu[0], wd[0]
    u = dot(hn[...], up)
    c0 = 0.7978845608028654
    u2 = u * u
    th = jnp.tanh(c0 * u * (1.0 + 0.044715 * u2))
    half = 0.5 * (1.0 + th)
    act = (u * half).astype(BF16)
    slope = half + 0.5 * u * (1.0 - th * th) * (c0 * (1.0 + 3 * 0.044715 * u2))
    blk[...] += dot_nt(act, dn)
    gwd[0] = dot(gdt[...], act).astype(BF16)
    gu = (dot(gd[...], dn) * slope).astype(BF16)
    gwu[0] = dot(hnt[...], gu).astype(BF16)
    gh[...] += dot_nt(gu, up)

    @pl.when((t == TP - 1) & (j == steps - 1))
    def _():
        cot = own(tp_[...], tc[...]).astype(F32)
        block = blk[...]
        arrays = [own(ep[...], ec[...])] + [own(yp[i], yc[i]) for i in range(3)]
        res = mix[4] * block
        for i in range(4):
            a = arrays[i].astype(F32)
            res += mix[i] * a
            small[2 + i : 3 + i, :] = jnp.sum(cot * a, axis=0, keepdims=True)
        small[6:7, :] = jnp.sum(cot * block, axis=0, keepdims=True)
        small[7:8, :] = jnp.zeros((1, D), F32)
        res = res.astype(BF16)
        outp[...] = res[:NP].reshape(outp.shape)
        outc[...] = res[NP:].reshape(outc.shape)
        g = gh[...]
        h = hat[...]
        small[0:1, :] = jnp.sum(g * h, axis=0, keepdims=True)
        small[1:2, :] = jnp.sum(g, axis=0, keepdims=True)
        gr = mix[4] * cot + norm_back(g, gain, h, scale[:, 0:1])
        resg[...] = gr
        gb = gr.astype(BF16)
        gbt = transpose(gb)
        for s in range(TP):
            gatt[:, s * HC : (s + 1) * HC] = dot(gb, wo[s]).astype(BF16)
            gwo[s] = dot(gbt, att[:, s * HC : (s + 1) * HC]).astype(BF16)


def backward_kernel(
    dm,
    q,
    k,
    v,
    att,
    gatt,
    lse,
    n_all,
    cos,
    shi,
    slo,
    w,
    dx,
    dxq,
    gw,
    maskp,
    maskx,
    dk,
    dv,
    dq,
    nt,
):
    G, R, PB, NCH, D, NX = dm.G, dm.R, dm.PB, dm.NCH, dm.D, dm.NX
    TP, HC = w.shape[0], w.shape[2] // 3
    fill_masks(dm, maskp, maskx)
    block = lax.axis_index("ctx") * lax.axis_size("tp") + lax.axis_index("tp")
    TILE = 256
    tiles = dm.P // TILE

    def attend(i, carry):
        g, pair = i // dm.PAIRS, i % dm.PAIRS
        lanes = pl.ds(pl.multiple_of(pair * 128, 128), 128)
        rp = pl.ds(pl.multiple_of(g * PB, PB), PB)
        rc = pl.ds(pl.multiple_of(dm.NP + g * NCH, NCH), NCH)
        qp, qc = q[rp, lanes], q[rc, lanes]
        gp, gc = gatt[rp, lanes], gatt[rc, lanes]
        ap, ac = att[rp, lanes].astype(F32), att[rc, lanes].astype(F32)
        qt = heads_columns(transpose(qp), transpose(qc))
        gpt, gct = gp.astype(F32).T, gc.astype(F32).T
        gt = heads_columns(gpt.astype(BF16), gct.astype(BF16))
        qs, gs = heads_rows(qp, qc), heads_rows(gp, gc)
        prodp, prodc = gpt * ap.T, gct * ac.T
        delta = jnp.concatenate(
            [
                jnp.sum(prodp[:HD], axis=0, keepdims=True),
                jnp.sum(prodp[HD:], axis=0, keepdims=True),
                jnp.sum(prodc[:HD], axis=0, keepdims=True),
                jnp.sum(prodc[HD:], axis=0, keepdims=True),
            ],
            axis=1,
        )
        stat = lse[i]

        def grads(s, kt, vt, cols):
            p = jnp.exp(s - stat[:, cols:])
            dp = dot(vt, gt[:, cols:])
            ds = (p * (dp - delta[:, cols:])).astype(BF16)
            gv = dot(p.astype(BF16), gs[cols:])
            gk = dot(ds, qs[cols:])
            gq = dot(transpose(kt), ds)
            return gk, gv, gq

        acc = None
        for j in range(tiles):
            rows = slice(j * TILE, (j + 1) * TILE)
            kt = k[g, rows, lanes]
            s = dot(kt, qt)
            s = jnp.concatenate([s[:, : 2 * PB] + maskp[rows, :], s[:, 2 * PB :]], axis=1)
            gk, gv, gq = grads(s, kt, v[g, rows, lanes], 0)
            gk = rotate_back(gk, cos[rows, :], shi[rows, :], slo[rows, :])
            out = pl.ds(pl.multiple_of(g * R + j * TILE, 128), TILE)
            dk[out, lanes] = gk.astype(BF16)
            dv[out, lanes] = gv.astype(BF16)
            acc = gq if acc is None else acc + gq
        kt = k[g, dm.P :, lanes]
        s = dot(kt, qt[:, 2 * PB :]) + maskx[...]
        gk, gv, gq = grads(s, kt, v[g, dm.P :, lanes], 2 * PB)
        for c in range(dm.NC):
            rows = slice(dm.P, dm.P + CL)
            out = pl.ds(pl.multiple_of(g * R + dm.P + c * CL, 128), CL)
            part = rotate_back(gk[c * CL : (c + 1) * CL], cos[rows, :], shi[rows, :], slo[rows, :])
            dk[out, lanes] = part.astype(BF16)
            dv[out, lanes] = gv[c * CL : (c + 1) * CL].astype(BF16)
        accp = acc[:, : 2 * PB] * 0.125
        accc = (acc[:, 2 * PB :] + gq) * 0.125
        outp = jnp.where(sublane_pick((128, PB), True), accp[:, :PB], accp[:, PB:]).T
        outc = jnp.where(sublane_pick((128, NCH), True), accc[:, :NCH], accc[:, NCH:]).T
        tab = pl.ds(pl.multiple_of(block * PB, PB), PB)
        dq[rp, lanes] = rotate_back(outp, cos[tab, :], shi[tab, :], slo[tab, :]).astype(BF16)
        tab = pl.ds(pl.multiple_of(dm.P + lax.axis_index("tp") * dm.CH, dm.CH), dm.CH)
        for c in range(dm.NC):
            part = rotate_back(outc[c * dm.CH : (c + 1) * dm.CH], cos[tab, :], shi[tab, :], slo[tab, :])
            rows = pl.ds(pl.multiple_of(dm.NP + g * NCH + c * dm.CH, dm.CH), dm.CH)
            dq[rows, lanes] = part.astype(BF16)
        return carry

    lax.fori_loop(0, G * dm.PAIRS, attend, 0)

    CHUNK = 256 if R % 256 == 0 else 128

    def project(i, carry):
        rows = pl.ds(pl.multiple_of(i * CHUNK, CHUNK), CHUNK)
        total = None
        for t in range(TP):
            part = dot_nt(dk[rows, t * HC : (t + 1) * HC], w[t, :, HC : 2 * HC])
            total = part if total is None else total + part
            total += dot_nt(dv[rows, t * HC : (t + 1) * HC], w[t, :, 2 * HC :])
        dx[rows, :] = total.astype(BF16)
        nt[:, rows] = transpose(n_all[rows, :])
        return carry

    lax.fori_loop(0, G * R // CHUNK, project, 0)
    total = dot_nt(dq[:, :HC], w[0, :, :HC])
    for t in range(1, TP):
        total += dot_nt(dq[:, t * HC : (t + 1) * HC], w[t, :, :HC])
    dxq[...] = total
    for t in range(TP):
        gw[t, :, HC : 2 * HC] = dot(nt[...], dk[:, t * HC : (t + 1) * HC]).astype(BF16)
        gw[t, :, 2 * HC :] = dot(nt[...], dv[:, t * HC : (t + 1) * HC]).astype(BF16)
        acc = None
        for g in range(G):
            rows = pl.ds(pl.multiple_of(g * R + block * PB, PB), PB)
            part = dot(transpose(n_all[rows, :]), dq[g * PB : (g + 1) * PB, t * HC : (t + 1) * HC])
            acc = part if acc is None else acc + part
            for c in range(dm.NC):
                first = g * R + dm.P + c * CL + lax.axis_index("tp") * dm.CH
                rows = pl.ds(pl.multiple_of(first, dm.CH), dm.CH)
                mine = dm.NP + g * NCH + c * dm.CH
                acc += dot(
                    transpose(n_all[rows, :]),
                    dq[mine : mine + dm.CH, t * HC : (t + 1) * HC],
                )
        gw[t, :, :HC] = acc.astype(BF16)


def whole(shape):
    zeros = (0,) * len(shape)
    return pl.BlockSpec(shape, lambda *_: zeros)


def params(**more):
    return pltpu.CompilerParams(vmem_limit_bytes=VMEM_LIMIT, **more)


def per_device(
    prompt_in,
    cont_in,
    prompt_embed,
    cont_embed,
    prompt_earlier,
    cont_earlier,
    ln1_gain,
    ln1_bias,
    ln2_gain,
    ln2_bias,
    w_qkv,
    w_out,
    w_up,
    w_down,
    mix_weights,
    prompt_cot,
    cont_cot,
):
    G, PB, D = prompt_in.shape
    NC, CH = cont_in.shape[1], cont_in.shape[2]
    TP = lax.axis_size("tp")
    PROMPT = PB * TP * lax.axis_size("ctx")
    HC, FC = w_qkv.shape[2], w_up.shape[1]
    S = w_qkv.shape[0]
    dm = Dims(G, PROMPT, PB, NC, CH, D, HC * TP // HD)
    R, NT, NP = dm.R, dm.NT, dm.NP

    sds = jax.ShapeDtypeStruct
    ln = lax.all_gather(jnp.stack([ln1_gain, ln1_bias, ln2_gain, ln2_bias]), "dp", axis=1, tiled=True)
    xp = lax.all_gather(prompt_in, ("ctx", "tp"), axis=1, tiled=True)
    xc = lax.all_gather(cont_in, "tp", axis=2, tiled=True)
    wq = lax.all_gather(w_qkv.reshape(S, 3 * HC), ("tp", "dp"), axis=0, tiled=True)
    wq = wq.reshape(TP, D, 3 * HC)
    shard = jnp.concatenate([w_out.T, w_up, w_down.T], axis=1)
    wm = lax.all_gather(shard, ("tp", "dp"), axis=0, tiled=True).reshape(TP, D, HC + 2 * FC)
    wo, wu, wd = wm[:, :, :HC], wm[:, :, HC : HC + FC], wm[:, :, HC + FC :]

    positions = jnp.arange(PROMPT + CL, dtype=jnp.int32).astype(F32)
    lane = jnp.arange(128, dtype=jnp.int32)
    freq = 10000.0 ** (-((lane % 32).astype(F32) / 32))
    angles = positions[:, None] * freq[None, :]
    cos, sin = jnp.cos(angles), jnp.sin(angles)
    second = (lane % 64) >= 32
    shi = jnp.where(second[None, :], sin, 0.0)
    slo = jnp.where(second[None, :], 0.0, -sin)

    n_all, k, v, q, att, lse = pl.pallas_call(
        partial(forward_kernel, dm),
        out_shape=(
            sds((G, R, D), BF16),
            sds((G, R, D), BF16),
            sds((G, R, D), BF16),
            sds((NT, D), BF16),
            sds((NT, D), BF16),
            sds((G * dm.PAIRS, 1, dm.COLS), F32),
        ),
        scratch_shapes=[
            pltpu.VMEM((PROMPT, 2 * PB), F32),
            pltpu.VMEM((dm.NX, 2 * dm.NCH), F32),
            pltpu.VMEM((PROMPT, dm.COLS), F32),
        ],
        compiler_params=params(),
        name="forward",
    )(xp, xc, prompt_in, cont_in, ln, cos, shi, slo, wq)

    T = 512 if FC % 512 == 0 else 256
    steps = FC // T
    row_specs = [whole(a.shape) for a in (att, prompt_in, cont_in, prompt_embed, cont_embed, prompt_earlier, cont_earlier, prompt_cot, cont_cot, ln, wo)]
    tile = pl.BlockSpec((1, D, T), lambda t, j: (t, 0, j))
    outp, outc, resg, gatt, gwo, gwu, gwd, small = pl.pallas_call(
        partial(mlp_kernel, dm, steps),
        grid=(TP, steps),
        out_shape=(
            sds(prompt_in.shape, BF16),
            sds(cont_in.shape, BF16),
            sds((NT, D), F32),
            sds((NT, D), BF16),
            sds((TP, D, HC), BF16),
            sds((TP, D, FC), BF16),
            sds((TP, D, FC), BF16),
            sds((8, D), F32),
        ),
        in_specs=[pl.BlockSpec(memory_space=pltpu.SMEM)] + row_specs + [tile, tile],
        out_specs=(
            whole(prompt_in.shape),
            whole(cont_in.shape),
            whole((NT, D)),
            whole((NT, D)),
            whole((TP, D, HC)),
            tile,
            tile,
            whole((8, D)),
        ),
        scratch_shapes=[
            pltpu.VMEM((NT, D), F32),
            pltpu.VMEM((NT, D), F32),
            pltpu.VMEM((NT, 128), F32),
            pltpu.VMEM((NT, D), BF16),
            pltpu.VMEM((D, NT), BF16),
            pltpu.VMEM((NT, D), BF16),
            pltpu.VMEM((D, NT), BF16),
            pltpu.VMEM((NT, D), F32),
            pltpu.VMEM((NT, D), F32),
        ],
        compiler_params=params(),
        name="feed",
    )(
        mix_weights,
        att,
        prompt_in,
        cont_in,
        prompt_embed,
        cont_embed,
        prompt_earlier,
        cont_earlier,
        prompt_cot,
        cont_cot,
        ln,
        wo,
        wu,
        wd,
    )

    dx, dxq, gwq = pl.pallas_call(
        partial(backward_kernel, dm),
        out_shape=(sds((G * R, D), BF16), sds((NT, D), F32), sds((TP, D, 3 * HC), BF16)),
        scratch_shapes=[
            pltpu.VMEM((PROMPT, 2 * PB), F32),
            pltpu.VMEM((dm.NX, 2 * dm.NCH), F32),
            pltpu.VMEM((G * R, D), BF16),
            pltpu.VMEM((G * R, D), BF16),
            pltpu.VMEM((NT, D), BF16),
            pltpu.VMEM((D, G * R), BF16),
        ],
        compiler_params=params(),
        name="backward",
    )(q, k, v, att, gatt, lse, n_all.reshape(G * R, D), cos, shi, slo, wq)

    dx = dx.reshape(G, R, D)
    gp = lax.psum_scatter(dx[:, :PROMPT], ("ctx", "tp"), scatter_dimension=1, tiled=True)
    gc = lax.psum_scatter(dx[:, PROMPT:].reshape(G, NC, CL, D), "tp", scatter_dimension=2, tiled=True)
    gn = jnp.concatenate([gp.reshape(NP, D), gc.reshape(NT - NP, D)], axis=0).astype(F32) + dxq
    x = jnp.concatenate([prompt_in.reshape(NP, D), cont_in.reshape(NT - NP, D)], axis=0).astype(F32)
    hat, scale = norm_stats(x)
    gin = (resg + norm_back(gn, ln[0:1].astype(F32), hat, scale)).astype(BF16)
    small = jnp.concatenate(
        [small[:7], jnp.sum(gn * hat, axis=0)[None], jnp.sum(gn, axis=0)[None]], axis=0
    )
    small = lax.psum(small, ("dp", "ctx", "tp"))

    def reduce(g):
        g = lax.psum_scatter(g.reshape(TP * D, -1), ("tp", "dp"), scatter_dimension=0, tiled=True)
        return lax.psum(g, "ctx").astype(F32)

    gm = reduce(jnp.concatenate([gwo, gwu, gwd], axis=2))
    gq = reduce(gwq)
    start = lax.axis_index("dp") * S
    mine = lax.dynamic_slice_in_dim(small, start, S, axis=1)
    return (
        outp,
        outc,
        gin[:NP].reshape(prompt_in.shape),
        gin[NP:].reshape(cont_in.shape),
        mine[7],
        mine[8],
        mine[0],
        mine[1],
        gq.reshape(S, 3, HC),
        gm[:, :HC].T,
        gm[:, HC : HC + FC],
        gm[:, HC + FC :].T,
        jnp.sum(small[2:7], axis=1),
    )


def solution(mesh):
    tokens = P("dp", ("ctx", "tp"), None)
    conts = P("dp", "ctx", "tp", None)
    weights = (P("dp", None, "tp"), P("tp", "dp"), P("dp", "tp"), P("tp", "dp"))
    in_specs = (
        tokens,
        conts,
        tokens,
        conts,
        P(None, "dp", ("ctx", "tp"), None),
        P(None, "dp", "ctx", "tp", None),
        P("dp"),
        P("dp"),
        P("dp"),
        P("dp"),
        *weights,
        P(),
        tokens,
        conts,
    )
    out_specs = (
        tokens,
        conts,
        tokens,
        conts,
        P("dp"),
        P("dp"),
        P("dp"),
        P("dp"),
        *weights,
        P(),
    )
    return jax.shard_map(
        per_device, mesh=mesh, in_specs=in_specs, out_specs=out_specs, check_vma=False
    )
```

```python
from functools import partial

import jax
import jax.numpy as jnp
import numpy as np
from jax import lax
from jax.experimental import pallas as pl
from jax.experimental.pallas import tpu as pltpu
from jax.sharding import PartitionSpec as P

HD = 64
CL = 128
EPS = 1e-05
NEG = -1e30
F32 = jnp.float32
BF16 = jnp.bfloat16
VMEM_LIMIT = 62 * 1024 * 1024


def dot(a, b):
    return lax.dot_general(a, b, (((1,), (0,)), ((), ())), preferred_element_type=F32)


def dot_nt(a, b):
    return lax.dot_general(a, b, (((1,), (1,)), ((), ())), preferred_element_type=F32)


def norm_stats(x):
    mean = jnp.mean(x, axis=-1, keepdims=True)
    centered = x - mean
    var = jnp.mean(centered * centered, axis=-1, keepdims=True)
    scale = lax.rsqrt(var + EPS)
    return centered * scale, scale


def norm_back(grad, gain, hat, scale):
    gh = grad * gain
    return scale * (
        gh
        - jnp.mean(gh, axis=-1, keepdims=True)
        - hat * jnp.mean(gh * hat, axis=-1, keepdims=True)
    )


def rotate(x, cos, sin_hi, sin_lo):
    return x * cos + pltpu.roll(x, 32, 1) * sin_hi + pltpu.roll(x, 96, 1) * sin_lo


def rotate_back(x, cos, sin_hi, sin_lo):
    return x * cos - pltpu.roll(x, 32, 1) * sin_hi - pltpu.roll(x, 96, 1) * sin_lo


def lane_pick(shape, low):
    lanes = lax.broadcasted_iota(jnp.int32, shape, 1)
    return lanes < HD if low else lanes >= HD


def sublane_pick(shape, low):
    rows = lax.broadcasted_iota(jnp.int32, shape, 0)
    return rows < HD if low else rows >= HD


def transpose(x):
    return x.astype(F32).T.astype(x.dtype)


class Dims:
    def __init__(self, groups, prompt, pb, nc, ch, d, heads):
        self.G, self.P, self.PB, self.NC, self.CH, self.D = groups, prompt, pb, nc, ch, d
        self.NCH = nc * ch
        self.R = prompt + nc * CL
        self.NX = nc * CL
        self.NR = pb + self.NCH
        self.NP = groups * pb
        self.NT = groups * self.NR
        self.PAIRS = heads // 2
        self.COLS = 2 * self.NR


MESH = pl.DeviceIdType.MESH


def half_index():
    return lax.axis_index("dp") % 2


def block_index():
    return lax.axis_index("ctx") * 2 + half_index()


class Peers:
    def __init__(self):
        self.ctxs = lax.axis_size("ctx")
        self.chips = lax.axis_size("dp") // 2
        self.tps = lax.axis_size("tp")
        self.dp = lax.axis_index("dp")
        self.ctx = lax.axis_index("ctx")
        self.tp = lax.axis_index("tp")
        self.core = self.dp % 2
        self.chip = self.dp // 2

    def at(self, dp=None, ctx=None, tp=None):
        return {
            "dp": self.dp if dp is None else dp,
            "ctx": self.ctx if ctx is None else ctx,
            "tp": self.tp if tp is None else tp,
        }

    def across(self):
        return self.at(tp=1 - self.tp)

    def mate(self):
        return self.at(dp=self.chip * 2 + 1 - self.core)

    def chip_after(self, k):
        return lax.rem(self.chip + k, self.chips)

    def chip_before(self, k):
        return lax.rem(self.chip + self.chips - k, self.chips)

    def row(self, k):
        return self.at(dp=self.chip_after(k) * 2 + self.core)

    def ctx_after(self, k):
        return lax.rem(self.ctx + k, self.ctxs)

    def ctx_before(self, k):
        return lax.rem(self.ctx + self.ctxs - k, self.ctxs)

    def plane(self, k):
        return self.at(ctx=self.ctx_after(k))

    def greet(self):
        barrier = pltpu.get_barrier_semaphore()
        peers = [self.across(), self.mate()]
        peers += [self.row(k) for k in range(1, self.chips)]
        peers += [self.plane(k) for k in range(1, self.ctxs)]
        for peer in peers:
            pl.semaphore_signal(barrier, inc=1, device_id=peer, device_id_type=MESH)
        pl.semaphore_wait(barrier, len(peers))


def send(src, dst, send_sem, recv_sem, device):
    copy = pltpu.make_async_remote_copy(
        src_ref=src,
        dst_ref=dst,
        send_sem=send_sem,
        recv_sem=recv_sem,
        device_id=device,
        device_id_type=MESH,
    )
    copy.start()
    return copy


def arrived(ref, sem, peers):
    pltpu.make_async_remote_copy(
        src_ref=ref,
        dst_ref=ref,
        send_sem=sem,
        recv_sem=sem,
        device_id=peers.mate(),
        device_id_type=MESH,
    ).wait_recv()


class WeightGather:
    def __init__(self, peers, shard, full, sends, across, rows, mate):
        self.p, self.shard, self.full = peers, shard, full
        self.sends, self.across, self.rows, self.from_mate = sends, across, rows, mate
        self.copies = []
        self.count = 0
        self.size = shard.shape[0]

    @staticmethod
    def semaphores(chips):
        return [
            pltpu.SemaphoreType.DMA((1 + 2 * (chips - 1) + 2 * chips,)),
            pltpu.SemaphoreType.DMA((1,)),
            pltpu.SemaphoreType.DMA((2, max(chips - 1, 1))),
            pltpu.SemaphoreType.DMA((2, chips)),
        ]

    def piece(self, tp, dp):
        return self.full.at[tp, pl.ds(pl.multiple_of(dp * self.size, 16), self.size), :]

    def go(self, src, dst, recv_sem, device):
        self.copies.append(send(src, dst, self.sends.at[self.count], recv_sem, device))
        self.count += 1

    def start(self):
        p = self.p
        self.go(self.shard, self.piece(p.tp, p.dp), self.across.at[0], p.across())
        for k in range(1, p.chips):
            self.go(self.shard, self.piece(p.tp, p.dp), self.rows.at[0, k - 1], p.row(k))
        self.go(self.shard, self.piece(p.tp, p.dp), self.from_mate.at[0, 0], p.mate())

    def relay_across(self):
        p = self.p
        got = self.piece(1 - p.tp, p.dp)
        arrived(got, self.across.at[0], p)
        for k in range(1, p.chips):
            self.go(got, got, self.rows.at[1, k - 1], p.row(k))
        self.go(got, got, self.from_mate.at[1, 0], p.mate())

    def relay_rows(self, part):
        p = self.p
        tp = p.tp if part == 0 else 1 - p.tp
        for k in range(1, p.chips):
            got = self.piece(tp, p.chip_before(k) * 2 + p.core)
            arrived(got, self.rows.at[part, k - 1], p)
            self.go(got, got, self.from_mate.at[part, k], p.mate())

    def finish(self):
        p = self.p
        for part in range(2):
            tp = p.tp if part == 0 else 1 - p.tp
            for k in range(p.chips):
                dp = p.chip_before(k) * 2 + 1 - p.core
                arrived(self.piece(tp, dp), self.from_mate.at[part, k], p)

    def drain(self):
        for copy in self.copies:
            copy.wait_send()


def fill_masks(dm, maskp, maskx):
    block = block_index()
    keys = lax.broadcasted_iota(jnp.int32, maskp.shape, 0)
    cols = lax.broadcasted_iota(jnp.int32, maskp.shape, 1) % dm.PB
    maskp[...] = jnp.where(keys <= cols + block * dm.PB, 0.0, NEG)
    keys = lax.broadcasted_iota(jnp.int32, maskx.shape, 0)
    cols = lax.broadcasted_iota(jnp.int32, maskx.shape, 1) % dm.NCH
    seen = (keys // CL == cols // dm.CH) & (
        keys % CL <= cols % dm.CH + half_index() * dm.CH
    )
    maskx[...] = jnp.where(seen, 0.0, NEG)


def heads_columns(a, b):
    lo_a, lo_b = sublane_pick(a.shape, True), sublane_pick(b.shape, True)
    zero_a, zero_b = jnp.zeros_like(a), jnp.zeros_like(b)
    return jnp.concatenate(
        [
            jnp.where(lo_a, a, zero_a),
            jnp.where(lo_a, zero_a, a),
            jnp.where(lo_b, b, zero_b),
            jnp.where(lo_b, zero_b, b),
        ],
        axis=1,
    )


def heads_rows(a, b):
    lo_a, lo_b = lane_pick(a.shape, True), lane_pick(b.shape, True)
    zero_a, zero_b = jnp.zeros_like(a), jnp.zeros_like(b)
    return jnp.concatenate(
        [
            jnp.where(lo_a, a, zero_a),
            jnp.where(lo_a, zero_a, a),
            jnp.where(lo_b, b, zero_b),
            jnp.where(lo_b, zero_b, b),
        ],
        axis=0,
    )


def forward_kernel(
    dm,
    op,
    oc,
    cos,
    shi,
    slo,
    wq,
    wm,
    n_out,
    k_out,
    v_out,
    q_out,
    att_out,
    lse_out,
    w_out,
    ln_out,
    wm_out,
    maskp,
    maskx,
    sbuf,
    xp,
    xc,
    w,
    put_sem,
    x_send,
    x_plane,
    x_mate,
    c_send,
    c_mate,
    own_sem,
    *sems,
):
    G, R, PB, NCH, D = dm.G, dm.R, dm.PB, dm.NCH, dm.D
    HC = (w.shape[2] - 128) // 3
    TP = w.shape[0]
    p = Peers()
    block = block_index()
    gq = WeightGather(p, wq, w, *sems[:4])
    gm = WeightGather(p, wm, wm_out, *sems[4:])
    size = wq.shape[0]
    mine = pl.ds(pl.multiple_of(p.dp * size, 16), size)
    local = [
        pltpu.make_async_copy(wq, w.at[p.tp, mine, :], own_sem.at[0]),
        pltpu.make_async_copy(wm, wm_out.at[p.tp, mine, :], own_sem.at[1]),
        pltpu.make_async_copy(op, xp.at[block], own_sem.at[2]),
        pltpu.make_async_copy(oc, xc.at[p.core], own_sem.at[3]),
    ]
    for copy in local:
        copy.start()
    p.greet()
    gq.start()
    sent = []
    for k in range(1, p.ctxs):
        sent.append(send(op, xp.at[block], x_send.at[k - 1], x_plane.at[k - 1], p.plane(k)))
    sent.append(send(op, xp.at[block], x_send.at[p.ctxs - 1], x_mate.at[0], p.mate()))
    sent.append(send(oc, xc.at[p.core], c_send, c_mate, p.mate()))
    fill_masks(dm, maskp, maskx)
    gq.relay_across()
    gq.relay_rows(0)
    gq.relay_rows(1)
    gm.start()
    gq.finish()
    for copy in local:
        copy.wait()
    put = pltpu.make_async_copy(w, w_out, put_sem)
    put.start()
    ln = w[0, :, 3 * HC :].astype(F32).T[:8, :]
    ln_out[...] = ln
    gain, bias = ln[0:1, :], ln[1:2, :]

    def normed(x):
        hat, _ = norm_stats(x.astype(F32))
        return (hat * gain + bias).astype(BF16)

    def queries(x, row, table):
        rows = x.shape[0]
        n = normed(x)
        c = cos[pl.ds(table, rows), :]
        hi = shi[pl.ds(table, rows), :]
        lo = slo[pl.ds(table, rows), :]
        for t in range(TP):
            qq = dot(n, w[t, :, :HC])
            for j in range(HC // 128):
                tile = rotate(qq[:, j * 128 : (j + 1) * 128], c, hi, lo).astype(BF16)
                q_out[pl.ds(row, rows), t * HC + j * 128 : t * HC + (j + 1) * 128] = (
                    tile.astype(F32) * 0.125
                ).astype(BF16)

    def own_prompt(g, carry):
        queries(op[g], pl.multiple_of(g * PB, PB), pl.multiple_of(block * PB, PB))
        return carry

    lax.fori_loop(0, G, own_prompt, 0)

    def own_cont(i, carry):
        g, c = i // dm.NC, i % dm.NC
        queries(
            oc[g, c],
            pl.multiple_of(dm.NP + i * dm.CH, dm.CH),
            pl.multiple_of(dm.P + p.core * dm.CH, dm.CH),
        )
        return carry

    lax.fori_loop(0, G * dm.NC, own_cont, 0)

    def keys_values(g, x, row, table):
        rows = x.shape[0]
        n = normed(x)
        n_out[g, pl.ds(row, rows), :] = n
        c = cos[pl.ds(table, rows), :]
        hi = shi[pl.ds(table, rows), :]
        lo = slo[pl.ds(table, rows), :]
        for t in range(TP):
            kk = dot(n, w[t, :, HC : 2 * HC])
            for j in range(HC // 128):
                tile = rotate(kk[:, j * 128 : (j + 1) * 128], c, hi, lo)
                k_out[g, pl.ds(row, rows), t * HC + j * 128 : t * HC + (j + 1) * 128] = tile.astype(BF16)
            v_out[g, pl.ds(row, rows), t * HC : (t + 1) * HC] = dot(n, w[t, :, 2 * HC : 3 * HC]).astype(BF16)

    def block_chunk(g, b):
        row = pl.multiple_of(b * PB, PB)
        keys_values(g, xp[b, g], row, row)

    arrived(xc.at[1 - p.core], c_mate, p)

    def cont_chunk(i, carry):
        g, c = i // dm.NC, i % dm.NC
        row = pl.multiple_of(dm.P + c * CL, CL)
        x = jnp.concatenate([xc[0, g, c], xc[1, g, c]], axis=0)
        keys_values(g, x, row, dm.P)
        return carry

    lax.fori_loop(0, G * dm.NC, cont_chunk, 0)

    def relay(k):
        b = p.ctx_before(k) * 2 + p.core
        arrived(xp.at[b], x_plane.at[k - 1], p)
        return send(xp.at[b], xp.at[b], x_send.at[p.ctxs + k - 1], x_mate.at[k], p.mate())

    for k in range(1, p.ctxs):
        sent.append(relay(k))
    for k in range(p.ctxs):
        arrived(xp.at[p.ctx_before(k) * 2 + 1 - p.core], x_mate.at[k], p)

    def prompt_chunk(i, carry):
        block_chunk(i // (2 * p.ctxs), i % (2 * p.ctxs))
        return carry

    lax.fori_loop(0, G * 2 * p.ctxs, prompt_chunk, 0)
    gm.relay_across()

    TILE = 256
    tiles = dm.P // TILE

    def attend(i, carry):
        g, pair = i // dm.PAIRS, i % dm.PAIRS
        lanes = pl.ds(pl.multiple_of(pair * 128, 128), 128)
        qp = q_out[pl.ds(pl.multiple_of(g * PB, PB), PB), lanes]
        qc = q_out[pl.ds(pl.multiple_of(dm.NP + g * NCH, NCH), NCH), lanes]
        qt = heads_columns(transpose(qp), transpose(qc))
        top = None
        for j in range(tiles):
            s = dot(k_out[g, j * TILE : (j + 1) * TILE, lanes], qt)
            sbuf[j * TILE : (j + 1) * TILE, : 2 * PB] = (
                s[:, : 2 * PB] + maskp[j * TILE : (j + 1) * TILE, :]
            )
            sbuf[j * TILE : (j + 1) * TILE, 2 * PB :] = s[:, 2 * PB :]
            here = jnp.max(sbuf[j * TILE : (j + 1) * TILE, :], axis=0, keepdims=True)
            top = here if top is None else jnp.maximum(top, here)
        sx = dot(k_out[g, dm.P :, lanes], qt[:, 2 * PB :]) + maskx[...]
        topx = jnp.max(sx, axis=0, keepdims=True)
        top = jnp.concatenate([top[:, : 2 * PB], jnp.maximum(top[:, 2 * PB :], topx)], axis=1)
        total, acc = None, None
        for j in range(tiles):
            e = jnp.exp(sbuf[j * TILE : (j + 1) * TILE, :] - top)
            here = jnp.sum(e, axis=0, keepdims=True)
            vt = transpose(v_out[g, j * TILE : (j + 1) * TILE, lanes])
            part = dot(vt, e.astype(BF16))
            total = here if total is None else total + here
            acc = part if acc is None else acc + part
        ex = jnp.exp(sx - top[:, 2 * PB :])
        partx = dot(transpose(v_out[g, dm.P :, lanes]), ex.astype(BF16))
        totalx = jnp.sum(ex, axis=0, keepdims=True)
        total = jnp.concatenate([total[:, : 2 * PB], total[:, 2 * PB :] + totalx], axis=1)
        acc_p = acc[:, : 2 * PB] / total[:, : 2 * PB]
        acc_c = (acc[:, 2 * PB :] + partx) / total[:, 2 * PB :]
        lse_out[i] = top + jnp.log(total)
        outp = jnp.where(sublane_pick((128, PB), True), acc_p[:, :PB], acc_p[:, PB:])
        outc = jnp.where(sublane_pick((128, NCH), True), acc_c[:, :NCH], acc_c[:, NCH:])
        att_out[pl.ds(pl.multiple_of(g * PB, PB), PB), lanes] = outp.T.astype(BF16)
        att_out[pl.ds(pl.multiple_of(dm.NP + g * NCH, NCH), NCH), lanes] = outc.T.astype(BF16)
        return carry

    lax.fori_loop(0, G * dm.PAIRS, attend, 0)
    gm.relay_rows(0)
    gm.relay_rows(1)
    gm.finish()
    gq.drain()
    gm.drain()
    for copy in sent:
        copy.wait_send()
    put.wait()


def mlp_kernel(
    dm,
    steps,
    mix,
    att,
    op,
    oc,
    tp_,
    tc,
    ln,
    wo,
    wu,
    wd,
    blk_out,
    resg,
    gatt,
    gwo,
    gwu,
    gwd,
    small,
    resid,
    hat,
    scale,
    hn,
    hnt,
    gd,
    gdt,
    blk,
    gh,
):
    D, NP, NT, G, PB = dm.D, dm.NP, dm.NT, dm.G, dm.PB
    TP, HC = wo.shape[0], wo.shape[2]
    t, j = pl.program_id(0), pl.program_id(1)
    gain, bias = ln[2:3, :], ln[3:4, :]

    def own(prompt, cont):
        return jnp.concatenate([prompt.reshape(NP, D), cont.reshape(NT - NP, D)], axis=0)

    @pl.when((t == 0) & (j == 0))
    def _():
        branch = dot_nt(att[:, :HC], wo[0])
        for s in range(1, TP):
            branch += dot_nt(att[:, s * HC : (s + 1) * HC], wo[s])
        r = own(op[...], oc[...]).astype(F32) + branch
        resid[...] = r
        h, sc = norm_stats(r)
        hat[...] = h
        scale[...] = jnp.broadcast_to(sc, scale.shape)
        n = (h * gain + bias).astype(BF16)
        hn[...] = n
        hnt[...] = transpose(n)
        g = (mix[4] * own(tp_[...], tc[...]).astype(F32)).astype(BF16)
        gd[...] = g
        gdt[...] = transpose(g)
        blk[...] = r
        gh[...] = jnp.zeros_like(gh)

    up, dn = wu[0], wd[0]
    u = dot(hn[...], up)
    c0 = 0.7978845608028654
    u2 = u * u
    th = jnp.tanh(c0 * u * (1.0 + 0.044715 * u2))
    half = 0.5 * (1.0 + th)
    act = (u * half).astype(BF16)
    slope = half + 0.5 * u * (1.0 - th * th) * (c0 * (1.0 + 3 * 0.044715 * u2))
    blk[...] += dot_nt(act, dn)
    gwd[0] = dot(gdt[...], act).astype(BF16)
    gu = (dot(gd[...], dn) * slope).astype(BF16)
    gwu[0] = dot(hnt[...], gu).astype(BF16)
    gh[...] += dot_nt(gu, up)

    @pl.when((t == TP - 1) & (j == steps - 1))
    def _():
        cot = own(tp_[...], tc[...]).astype(F32)
        block = blk[...]
        blk_out[...] = block.astype(BF16)
        small[2:3, :] = jnp.sum(cot * block, axis=0, keepdims=True)
        small[3:, :] = jnp.zeros((5, D), F32)
        g = gh[...]
        h = hat[...]
        small[0:1, :] = jnp.sum(g * h, axis=0, keepdims=True)
        small[1:2, :] = jnp.sum(g, axis=0, keepdims=True)
        gr = mix[4] * cot + norm_back(g, gain, h, scale[:, 0:1])
        resg[...] = gr
        gb = gr.astype(BF16)
        gbt = transpose(gb)
        for s in range(TP):
            gatt[:, s * HC : (s + 1) * HC] = dot(gb, wo[s]).astype(BF16)
            gwo[s] = dot(gbt, att[:, s * HC : (s + 1) * HC]).astype(BF16)


def backward_kernel(
    dm,
    q,
    k,
    v,
    att,
    gatt,
    lse,
    n_all,
    cos,
    shi,
    slo,
    w,
    dx,
    dxq,
    gw,
    maskp,
    maskx,
    dk,
    dv,
    dq,
    nt,
):
    G, R, PB, NCH, D, NX = dm.G, dm.R, dm.PB, dm.NCH, dm.D, dm.NX
    TP, HC = w.shape[0], (w.shape[2] - 128) // 3
    fill_masks(dm, maskp, maskx)
    block = block_index()
    TILE = 256
    tiles = dm.P // TILE

    def attend(i, carry):
        g, pair = i // dm.PAIRS, i % dm.PAIRS
        lanes = pl.ds(pl.multiple_of(pair * 128, 128), 128)
        rp = pl.ds(pl.multiple_of(g * PB, PB), PB)
        rc = pl.ds(pl.multiple_of(dm.NP + g * NCH, NCH), NCH)
        qp, qc = q[rp, lanes], q[rc, lanes]
        gp, gc = gatt[rp, lanes], gatt[rc, lanes]
        ap, ac = att[rp, lanes].astype(F32), att[rc, lanes].astype(F32)
        qt = heads_columns(transpose(qp), transpose(qc))
        gpt, gct = gp.astype(F32).T, gc.astype(F32).T
        gt = heads_columns(gpt.astype(BF16), gct.astype(BF16))
        qs, gs = heads_rows(qp, qc), heads_rows(gp, gc)
        prodp, prodc = gpt * ap.T, gct * ac.T
        delta = jnp.concatenate(
            [
                jnp.sum(prodp[:HD], axis=0, keepdims=True),
                jnp.sum(prodp[HD:], axis=0, keepdims=True),
                jnp.sum(prodc[:HD], axis=0, keepdims=True),
                jnp.sum(prodc[HD:], axis=0, keepdims=True),
            ],
            axis=1,
        )
        stat = lse[i]

        def grads(s, kt, vt, cols):
            p = jnp.exp(s - stat[:, cols:])
            dp = dot(vt, gt[:, cols:])
            ds = (p * (dp - delta[:, cols:])).astype(BF16)
            gv = dot(p.astype(BF16), gs[cols:])
            gk = dot(ds, qs[cols:])
            gq = dot(transpose(kt), ds)
            return gk, gv, gq

        acc = None
        for j in range(tiles):
            rows = slice(j * TILE, (j + 1) * TILE)
            kt = k[g, rows, lanes]
            s = dot(kt, qt)
            s = jnp.concatenate([s[:, : 2 * PB] + maskp[rows, :], s[:, 2 * PB :]], axis=1)
            gk, gv, gq = grads(s, kt, v[g, rows, lanes], 0)
            gk = rotate_back(gk, cos[rows, :], shi[rows, :], slo[rows, :])
            out = pl.ds(pl.multiple_of(g * R + j * TILE, 128), TILE)
            dk[out, lanes] = gk.astype(BF16)
            dv[out, lanes] = gv.astype(BF16)
            acc = gq if acc is None else acc + gq
        kt = k[g, dm.P :, lanes]
        s = dot(kt, qt[:, 2 * PB :]) + maskx[...]
        gk, gv, gq = grads(s, kt, v[g, dm.P :, lanes], 2 * PB)
        for c in range(dm.NC):
            rows = slice(dm.P, dm.P + CL)
            out = pl.ds(pl.multiple_of(g * R + dm.P + c * CL, 128), CL)
            part = rotate_back(gk[c * CL : (c + 1) * CL], cos[rows, :], shi[rows, :], slo[rows, :])
            dk[out, lanes] = part.astype(BF16)
            dv[out, lanes] = gv[c * CL : (c + 1) * CL].astype(BF16)
        accp = acc[:, : 2 * PB] * 0.125
        accc = (acc[:, 2 * PB :] + gq) * 0.125
        outp = jnp.where(sublane_pick((128, PB), True), accp[:, :PB], accp[:, PB:]).T
        outc = jnp.where(sublane_pick((128, NCH), True), accc[:, :NCH], accc[:, NCH:]).T
        tab = pl.ds(pl.multiple_of(block * PB, PB), PB)
        dq[rp, lanes] = rotate_back(outp, cos[tab, :], shi[tab, :], slo[tab, :]).astype(BF16)
        tab = pl.ds(pl.multiple_of(dm.P + half_index() * dm.CH, dm.CH), dm.CH)
        for c in range(dm.NC):
            part = rotate_back(outc[c * dm.CH : (c + 1) * dm.CH], cos[tab, :], shi[tab, :], slo[tab, :])
            rows = pl.ds(pl.multiple_of(dm.NP + g * NCH + c * dm.CH, dm.CH), dm.CH)
            dq[rows, lanes] = part.astype(BF16)
        return carry

    lax.fori_loop(0, G * dm.PAIRS, attend, 0)

    CHUNK = 256 if R % 256 == 0 else 128

    def project(i, carry):
        rows = pl.ds(pl.multiple_of(i * CHUNK, CHUNK), CHUNK)
        total = None
        for t in range(TP):
            part = dot_nt(dk[rows, t * HC : (t + 1) * HC], w[t, :, HC : 2 * HC])
            total = part if total is None else total + part
            total += dot_nt(dv[rows, t * HC : (t + 1) * HC], w[t, :, 2 * HC : 3 * HC])
        dx[rows, :] = total.astype(BF16)
        nt[:, rows] = transpose(n_all[rows, :])
        return carry

    lax.fori_loop(0, G * R // CHUNK, project, 0)
    total = dot_nt(dq[:, :HC], w[0, :, :HC])
    for t in range(1, TP):
        total += dot_nt(dq[:, t * HC : (t + 1) * HC], w[t, :, :HC])
    dxq[...] = total
    for t in range(TP):
        gw[t, :, HC : 2 * HC] = dot(nt[...], dk[:, t * HC : (t + 1) * HC]).astype(BF16)
        gw[t, :, 2 * HC :] = dot(nt[...], dv[:, t * HC : (t + 1) * HC]).astype(BF16)
        acc = None
        for g in range(G):
            rows = pl.ds(pl.multiple_of(g * R + block * PB, PB), PB)
            part = dot(transpose(n_all[rows, :]), dq[g * PB : (g + 1) * PB, t * HC : (t + 1) * HC])
            acc = part if acc is None else acc + part
            for c in range(dm.NC):
                first = g * R + dm.P + c * CL + half_index() * dm.CH
                rows = pl.ds(pl.multiple_of(first, dm.CH), dm.CH)
                mine = dm.NP + g * NCH + c * dm.CH
                acc += dot(
                    transpose(n_all[rows, :]),
                    dq[mine : mine + dm.CH, t * HC : (t + 1) * HC],
                )
        gw[t, :, :HC] = acc.astype(BF16)


def whole(shape):
    zeros = (0,) * len(shape)
    return pl.BlockSpec(shape, lambda *_: zeros)


def params(**more):
    return pltpu.CompilerParams(vmem_limit_bytes=VMEM_LIMIT, **more)


def per_device(
    prompt_in,
    cont_in,
    prompt_embed,
    cont_embed,
    prompt_earlier,
    cont_earlier,
    ln1_gain,
    ln1_bias,
    ln2_gain,
    ln2_bias,
    w_qkv,
    w_out,
    w_up,
    w_down,
    mix_weights,
    prompt_cot,
    cont_cot,
):
    G, PB, D = prompt_in.shape
    NC, CH = cont_in.shape[1], cont_in.shape[2]
    TP = lax.axis_size("tp")
    PROMPT = PB * TP * lax.axis_size("ctx")
    HC, FC = w_qkv.shape[2], w_up.shape[1]
    S = w_qkv.shape[0]
    dm = Dims(G, PROMPT, PB, NC, CH, D, HC * TP // HD)
    R, NT, NP = dm.R, dm.NT, dm.NP

    sds = jax.ShapeDtypeStruct
    chips, ctxs = lax.axis_size("dp") // 2, lax.axis_size("ctx")
    swap = [(4 * y + 2 * c + t, 4 * y + 2 * t + c) for y in range(chips) for c in (0, 1) for t in (0, 1)]

    def trade(x):
        return lax.ppermute(x, ("dp", "tp"), swap)

    own_p, own_c = trade(prompt_in), trade(cont_in)
    cot_p, cot_c = trade(prompt_cot), trade(cont_cot)
    norms = jnp.stack([ln1_gain, ln1_bias, ln2_gain, ln2_bias], axis=1)
    norms = jnp.pad(norms, ((0, 0), (0, 124)))
    wq_shard = jnp.concatenate([w_qkv.reshape(S, 3 * HC), norms], axis=1)
    wm_shard = jnp.concatenate([w_out.T, w_up, w_down.T], axis=1)

    positions = jnp.arange(PROMPT + CL, dtype=jnp.int32).astype(F32)
    lane = jnp.arange(128, dtype=jnp.int32)
    freq = 10000.0 ** (-((lane % 32).astype(F32) / 32))
    angles = positions[:, None] * freq[None, :]
    cos, sin = jnp.cos(angles), jnp.sin(angles)
    second = (lane % 64) >= 32
    shi = jnp.where(second[None, :], sin, 0.0)
    slo = jnp.where(second[None, :], 0.0, -sin)

    any_ = pl.BlockSpec(memory_space=pl.ANY)
    vmem = pl.BlockSpec(memory_space=pltpu.VMEM)
    dma = pltpu.SemaphoreType.DMA
    n_all, k, v, q, att, lse, wq, ln, wm = pl.pallas_call(
        partial(forward_kernel, dm),
        out_shape=(
            sds((G, R, D), BF16),
            sds((G, R, D), BF16),
            sds((G, R, D), BF16),
            sds((NT, D), BF16),
            sds((NT, D), BF16),
            sds((G * dm.PAIRS, 1, dm.COLS), F32),
            sds((TP, D, 3 * HC + 128), BF16),
            sds((8, D), F32),
            sds((TP, D, HC + 2 * FC), BF16),
        ),
        in_specs=[vmem] * 6 + [any_],
        out_specs=(vmem,) * 6 + (any_, vmem, any_),
        scratch_shapes=[
            pltpu.VMEM((PROMPT, 2 * PB), F32),
            pltpu.VMEM((dm.NX, 2 * dm.NCH), F32),
            pltpu.VMEM((PROMPT, dm.COLS), F32),
            pltpu.VMEM((2 * ctxs, G, PB, D), BF16),
            pltpu.VMEM((2, G, NC, CH, D), BF16),
            pltpu.VMEM((TP, D, 3 * HC + 128), BF16),
            dma,
            dma((2 * ctxs - 1,)),
            dma((ctxs - 1,)),
            dma((ctxs,)),
            dma,
            dma,
            dma((4,)),
        ]
        + WeightGather.semaphores(chips)
        + WeightGather.semaphores(chips),
        compiler_params=params(collective_id=0, has_side_effects=True),
        name="forward",
    )(own_p, own_c, cos, shi, slo, wq_shard, wm_shard)
    wo, wu, wd = wm[:, :, :HC], wm[:, :, HC : HC + FC], wm[:, :, HC + FC :]

    T = 512 if FC % 512 == 0 else 256
    steps = FC // T
    row_specs = [whole(a.shape) for a in (att, own_p, own_c, cot_p, cot_c, ln, wo)]
    tile = pl.BlockSpec((1, D, T), lambda t, j: (t, 0, j))
    blk, resg, gatt, gwo, gwu, gwd, small = pl.pallas_call(
        partial(mlp_kernel, dm, steps),
        grid=(TP, steps),
        out_shape=(
            sds((NT, D), BF16),
            sds((NT, D), F32),
            sds((NT, D), BF16),
            sds((TP, D, HC), BF16),
            sds((TP, D, FC), BF16),
            sds((TP, D, FC), BF16),
            sds((8, D), F32),
        ),
        in_specs=[pl.BlockSpec(memory_space=pltpu.SMEM)] + row_specs + [tile, tile],
        out_specs=(
            whole((NT, D)),
            whole((NT, D)),
            whole((NT, D)),
            whole((TP, D, HC)),
            tile,
            tile,
            whole((8, D)),
        ),
        scratch_shapes=[
            pltpu.VMEM((NT, D), F32),
            pltpu.VMEM((NT, D), F32),
            pltpu.VMEM((NT, 128), F32),
            pltpu.VMEM((NT, D), BF16),
            pltpu.VMEM((D, NT), BF16),
            pltpu.VMEM((NT, D), BF16),
            pltpu.VMEM((D, NT), BF16),
            pltpu.VMEM((NT, D), F32),
            pltpu.VMEM((NT, D), F32),
        ],
        compiler_params=params(),
        name="feed",
    )(
        mix_weights,
        att,
        own_p,
        own_c,
        cot_p,
        cot_c,
        ln,
        wo,
        wu,
        wd,
    )

    dx, dxq, gwq = pl.pallas_call(
        partial(backward_kernel, dm),
        out_shape=(sds((G * R, D), BF16), sds((NT, D), F32), sds((TP, D, 3 * HC), BF16)),
        in_specs=[vmem] * 11,
        out_specs=(vmem,) * 3,
        scratch_shapes=[
            pltpu.VMEM((PROMPT, 2 * PB), F32),
            pltpu.VMEM((dm.NX, 2 * dm.NCH), F32),
            pltpu.VMEM((G * R, D), BF16),
            pltpu.VMEM((G * R, D), BF16),
            pltpu.VMEM((NT, D), BF16),
            pltpu.VMEM((D, G * R), BF16),
        ],
        compiler_params=params(),
        name="backward",
    )(q, k, v, att, gatt, lse, n_all.reshape(G * R, D), cos, shi, slo, wq)

    dx = dx.reshape(G, R, D)
    ways = [[2 * i, 2 * i + 1] for i in range(chips)]

    def halves(x, axis):
        return lax.psum_scatter(x, "dp", scatter_dimension=axis, axis_index_groups=ways, tiled=True)

    gp = halves(dx[:, :PROMPT].reshape(G, ctxs, 2, PB, D), 2)
    gp = lax.psum_scatter(gp.reshape(G, ctxs * PB, D), "ctx", scatter_dimension=1, tiled=True)
    gc = halves(dx[:, PROMPT:].reshape(G, NC, CL, D), 2)
    gn = jnp.concatenate([gp.reshape(NP, D), gc.reshape(NT - NP, D)], axis=0).astype(F32) + dxq
    x = jnp.concatenate([own_p.reshape(NP, D), own_c.reshape(NT - NP, D)], axis=0).astype(F32)
    hat, scale = norm_stats(x)
    gin = (resg + norm_back(gn, ln[0:1], hat, scale)).astype(BF16)
    gin = trade(gin)
    blk = trade(blk).astype(F32)
    outs, sums = [], 0.0
    for b, e, y, c in (
        (blk[:NP].reshape(prompt_in.shape), prompt_embed, prompt_earlier, prompt_cot),
        (blk[NP:].reshape(cont_in.shape), cont_embed, cont_earlier, cont_cot),
    ):
        terms = [e.astype(F32)] + [y[i].astype(F32) for i in range(3)]
        total = mix_weights[4] * b
        for i in range(4):
            total += mix_weights[i] * terms[i]
        outs.append(total.astype(BF16))
        c = c.astype(F32)
        sums += jnp.stack([jnp.sum((c * a).reshape(-1, D), axis=0) for a in terms])
    small = jnp.concatenate(
        [small[:3], sums, jnp.sum(gn * hat, axis=0)[None], jnp.sum(gn, axis=0)[None]], axis=0
    )
    small = lax.psum(small, ("dp", "ctx", "tp"))

    def reduce(g):
        g = lax.psum_scatter(g.reshape(TP * D, -1), ("tp", "dp"), scatter_dimension=0, tiled=True)
        return lax.psum(g, "ctx").astype(F32)

    gm = reduce(jnp.concatenate([gwo, gwu, gwd], axis=2))
    gq = reduce(gwq)
    start = lax.axis_index("dp") * S
    mine = lax.dynamic_slice_in_dim(small, start, S, axis=1)
    return (
        outs[0],
        outs[1],
        gin[:NP].reshape(prompt_in.shape),
        gin[NP:].reshape(cont_in.shape),
        mine[7],
        mine[8],
        mine[0],
        mine[1],
        gq.reshape(S, 3, HC),
        gm[:, :HC].T,
        gm[:, HC : HC + FC],
        gm[:, HC + FC :].T,
        jnp.sum(jnp.concatenate([small[3:7], small[2:3]]), axis=1),
    )


def solution(mesh):
    tokens = P("dp", ("ctx", "tp"), None)
    conts = P("dp", "ctx", "tp", None)
    weights = (P("dp", None, "tp"), P("tp", "dp"), P("dp", "tp"), P("tp", "dp"))
    in_specs = (
        tokens,
        conts,
        tokens,
        conts,
        P(None, "dp", ("ctx", "tp"), None),
        P(None, "dp", "ctx", "tp", None),
        P("dp"),
        P("dp"),
        P("dp"),
        P("dp"),
        *weights,
        P(),
        tokens,
        conts,
    )
    out_specs = (
        tokens,
        conts,
        tokens,
        conts,
        P("dp"),
        P("dp"),
        P("dp"),
        P("dp"),
        *weights,
        P(),
    )
    return jax.shard_map(
        per_device, mesh=mesh, in_specs=in_specs, out_specs=out_specs, check_vma=False
    )
```

```python
from functools import partial

import jax
import jax.numpy as jnp
import numpy as np
from jax import lax
from jax.experimental import pallas as pl
from jax.experimental.pallas import tpu as pltpu
from jax.sharding import PartitionSpec as P

HD = 64
CL = 128
EPS = 1e-05
NEG = -1e30
F32 = jnp.float32
BF16 = jnp.bfloat16
VMEM_LIMIT = 62 * 1024 * 1024


def dot(a, b):
    return lax.dot_general(a, b, (((1,), (0,)), ((), ())), preferred_element_type=F32)


def dot_nt(a, b):
    return lax.dot_general(a, b, (((1,), (1,)), ((), ())), preferred_element_type=F32)


def norm_stats(x):
    mean = jnp.mean(x, axis=-1, keepdims=True)
    centered = x - mean
    var = jnp.mean(centered * centered, axis=-1, keepdims=True)
    scale = lax.rsqrt(var + EPS)
    return centered * scale, scale


def norm_back(grad, gain, hat, scale):
    gh = grad * gain
    return scale * (
        gh
        - jnp.mean(gh, axis=-1, keepdims=True)
        - hat * jnp.mean(gh * hat, axis=-1, keepdims=True)
    )


def rotate(x, cos, sin_hi, sin_lo):
    return x * cos + pltpu.roll(x, 32, 1) * sin_hi + pltpu.roll(x, 96, 1) * sin_lo


def rotate_back(x, cos, sin_hi, sin_lo):
    return x * cos - pltpu.roll(x, 32, 1) * sin_hi - pltpu.roll(x, 96, 1) * sin_lo


def lane_pick(shape, low):
    lanes = lax.broadcasted_iota(jnp.int32, shape, 1)
    return lanes < HD if low else lanes >= HD


def sublane_pick(shape, low):
    rows = lax.broadcasted_iota(jnp.int32, shape, 0)
    return rows < HD if low else rows >= HD


def transpose(x):
    return x.astype(F32).T.astype(x.dtype)


class Dims:
    def __init__(self, groups, prompt, pb, nc, ch, d, heads):
        self.G, self.P, self.PB, self.NC, self.CH, self.D = groups, prompt, pb, nc, ch, d
        self.NCH = nc * ch
        self.R = prompt + nc * CL
        self.NX = nc * CL
        self.NR = pb + self.NCH
        self.NP = groups * pb
        self.NT = groups * self.NR
        self.PAIRS = heads // 2
        self.COLS = 2 * self.NR


MESH = pl.DeviceIdType.MESH


def half_index():
    return lax.axis_index("dp") % 2


def block_index():
    return lax.axis_index("ctx") * 2 + half_index()


class Peers:
    def __init__(self):
        self.ctxs = lax.axis_size("ctx")
        self.chips = lax.axis_size("dp") // 2
        self.tps = lax.axis_size("tp")
        self.dp = lax.axis_index("dp")
        self.ctx = lax.axis_index("ctx")
        self.tp = lax.axis_index("tp")
        self.core = self.dp % 2
        self.chip = self.dp // 2

    def at(self, dp=None, ctx=None, tp=None):
        return {
            "dp": self.dp if dp is None else dp,
            "ctx": self.ctx if ctx is None else ctx,
            "tp": self.tp if tp is None else tp,
        }

    def across(self):
        return self.at(tp=1 - self.tp)

    def mate(self):
        return self.at(dp=self.chip * 2 + 1 - self.core)

    def chip_after(self, k):
        return lax.rem(self.chip + k, self.chips)

    def chip_before(self, k):
        return lax.rem(self.chip + self.chips - k, self.chips)

    def row(self, k):
        return self.at(dp=self.chip_after(k) * 2 + self.core)

    def ctx_after(self, k):
        return lax.rem(self.ctx + k, self.ctxs)

    def ctx_before(self, k):
        return lax.rem(self.ctx + self.ctxs - k, self.ctxs)

    def plane(self, k):
        return self.at(ctx=self.ctx_after(k))

    def greet(self):
        barrier = pltpu.get_barrier_semaphore()
        peers = [self.across(), self.mate()]
        peers += [self.row(k) for k in range(1, self.chips)]
        peers += [self.plane(k) for k in range(1, self.ctxs)]
        for peer in peers:
            pl.semaphore_signal(barrier, inc=1, device_id=peer, device_id_type=MESH)
        pl.semaphore_wait(barrier, len(peers))


def send(src, dst, send_sem, recv_sem, device):
    copy = pltpu.make_async_remote_copy(
        src_ref=src,
        dst_ref=dst,
        send_sem=send_sem,
        recv_sem=recv_sem,
        device_id=device,
        device_id_type=MESH,
    )
    copy.start()
    return copy


def arrived(ref, sem, peers):
    pltpu.make_async_remote_copy(
        src_ref=ref,
        dst_ref=ref,
        send_sem=sem,
        recv_sem=sem,
        device_id=peers.mate(),
        device_id_type=MESH,
    ).wait_recv()


class WeightGather:
    def __init__(self, peers, shard, full, sends, across, rows, mate):
        self.p, self.shard, self.full = peers, shard, full
        self.sends, self.across, self.rows, self.from_mate = sends, across, rows, mate
        self.copies = []
        self.count = 0
        self.size = shard.shape[0]

    @staticmethod
    def semaphores(chips):
        return [
            pltpu.SemaphoreType.DMA((1 + 2 * (chips - 1) + 2 * chips,)),
            pltpu.SemaphoreType.DMA((1,)),
            pltpu.SemaphoreType.DMA((2, max(chips - 1, 1))),
            pltpu.SemaphoreType.DMA((2, chips)),
        ]

    def piece(self, tp, dp):
        return self.full.at[tp, pl.ds(pl.multiple_of(dp * self.size, 16), self.size), :]

    def go(self, src, dst, recv_sem, device):
        self.copies.append(send(src, dst, self.sends.at[self.count], recv_sem, device))
        self.count += 1

    def start(self):
        p = self.p
        self.go(self.shard, self.piece(p.tp, p.dp), self.across.at[0], p.across())
        for k in range(1, p.chips):
            self.go(self.shard, self.piece(p.tp, p.dp), self.rows.at[0, k - 1], p.row(k))
        self.go(self.shard, self.piece(p.tp, p.dp), self.from_mate.at[0, 0], p.mate())

    def relay_across(self):
        p = self.p
        got = self.piece(1 - p.tp, p.dp)
        arrived(got, self.across.at[0], p)
        for k in range(1, p.chips):
            self.go(got, got, self.rows.at[1, k - 1], p.row(k))
        self.go(got, got, self.from_mate.at[1, 0], p.mate())

    def relay_rows(self, part):
        p = self.p
        tp = p.tp if part == 0 else 1 - p.tp
        for k in range(1, p.chips):
            got = self.piece(tp, p.chip_before(k) * 2 + p.core)
            arrived(got, self.rows.at[part, k - 1], p)
            self.go(got, got, self.from_mate.at[part, k], p.mate())

    def finish(self):
        p = self.p
        for part in range(2):
            tp = p.tp if part == 0 else 1 - p.tp
            for k in range(p.chips):
                dp = p.chip_before(k) * 2 + 1 - p.core
                arrived(self.piece(tp, dp), self.from_mate.at[part, k], p)

    def drain(self):
        for copy in self.copies:
            copy.wait_send()


def fill_masks(dm, maskp, maskx):
    block = block_index()
    keys = lax.broadcasted_iota(jnp.int32, maskp.shape, 0)
    cols = lax.broadcasted_iota(jnp.int32, maskp.shape, 1) % dm.PB
    maskp[...] = jnp.where(keys <= cols + block * dm.PB, 0.0, NEG)
    keys = lax.broadcasted_iota(jnp.int32, maskx.shape, 0)
    cols = lax.broadcasted_iota(jnp.int32, maskx.shape, 1) % dm.NCH
    seen = (keys // CL == cols // dm.CH) & (
        keys % CL <= cols % dm.CH + half_index() * dm.CH
    )
    maskx[...] = jnp.where(seen, 0.0, NEG)


def heads_columns(a, b):
    lo_a, lo_b = sublane_pick(a.shape, True), sublane_pick(b.shape, True)
    zero_a, zero_b = jnp.zeros_like(a), jnp.zeros_like(b)
    return jnp.concatenate(
        [
            jnp.where(lo_a, a, zero_a),
            jnp.where(lo_a, zero_a, a),
            jnp.where(lo_b, b, zero_b),
            jnp.where(lo_b, zero_b, b),
        ],
        axis=1,
    )


def heads_rows(a, b):
    lo_a, lo_b = lane_pick(a.shape, True), lane_pick(b.shape, True)
    zero_a, zero_b = jnp.zeros_like(a), jnp.zeros_like(b)
    return jnp.concatenate(
        [
            jnp.where(lo_a, a, zero_a),
            jnp.where(lo_a, zero_a, a),
            jnp.where(lo_b, b, zero_b),
            jnp.where(lo_b, zero_b, b),
        ],
        axis=0,
    )


def forward_kernel(
    dm,
    op,
    oc,
    cos,
    shi,
    slo,
    wq,
    wm,
    nt_out,
    own_out,
    k_out,
    v_out,
    q_out,
    att_out,
    lse_out,
    w_out,
    ln_out,
    wm_out,
    maskp,
    maskx,
    sbuf,
    all_rows,
    own_rows,
    xp,
    xc,
    w,
    put_sem,
    x_send,
    x_plane,
    x_mate,
    c_send,
    c_mate,
    own_sem,
    *sems,
):
    G, R, PB, NCH, D = dm.G, dm.R, dm.PB, dm.NCH, dm.D
    HC = (w.shape[2] - 128) // 3
    TP = w.shape[0]
    p = Peers()
    block = block_index()
    gq = WeightGather(p, wq, w, *sems[:4])
    gm = WeightGather(p, wm, wm_out, *sems[4:])
    size = wq.shape[0]
    mine = pl.ds(pl.multiple_of(p.dp * size, 16), size)
    local = [
        pltpu.make_async_copy(wq, w.at[p.tp, mine, :], own_sem.at[0]),
        pltpu.make_async_copy(wm, wm_out.at[p.tp, mine, :], own_sem.at[1]),
        pltpu.make_async_copy(op, xp.at[block], own_sem.at[2]),
        pltpu.make_async_copy(oc, xc.at[p.core], own_sem.at[3]),
    ]
    for copy in local:
        copy.start()
    p.greet()
    gq.start()
    sent = []
    for k in range(1, p.ctxs):
        sent.append(send(op, xp.at[block], x_send.at[k - 1], x_plane.at[k - 1], p.plane(k)))
    sent.append(send(op, xp.at[block], x_send.at[p.ctxs - 1], x_mate.at[0], p.mate()))
    sent.append(send(oc, xc.at[p.core], c_send, c_mate, p.mate()))
    fill_masks(dm, maskp, maskx)
    gq.relay_across()
    gq.relay_rows(0)
    gq.relay_rows(1)
    gm.start()
    gq.finish()
    for copy in local:
        copy.wait()
    put = pltpu.make_async_copy(w, w_out, put_sem)
    put.start()
    ln = w[0, :, 3 * HC :].astype(F32).T[:8, :]
    ln_out[...] = ln
    gain, bias = ln[0:1, :], ln[1:2, :]

    def normed(x):
        hat, _ = norm_stats(x.astype(F32))
        return (hat * gain + bias).astype(BF16)

    def queries(x, row, table):
        rows = x.shape[0]
        n = normed(x)
        own_rows[pl.ds(row, rows), :] = n
        c = cos[pl.ds(table, rows), :]
        hi = shi[pl.ds(table, rows), :]
        lo = slo[pl.ds(table, rows), :]
        for t in range(TP):
            qq = dot(n, w[t, :, :HC])
            for j in range(HC // 128):
                tile = rotate(qq[:, j * 128 : (j + 1) * 128], c, hi, lo).astype(BF16)
                q_out[pl.ds(row, rows), t * HC + j * 128 : t * HC + (j + 1) * 128] = (
                    tile.astype(F32) * 0.125
                ).astype(BF16)

    def own_prompt(g, carry):
        queries(op[g], pl.multiple_of(g * PB, PB), pl.multiple_of(block * PB, PB))
        return carry

    lax.fori_loop(0, G, own_prompt, 0)

    def own_cont(i, carry):
        g, c = i // dm.NC, i % dm.NC
        queries(
            oc[g, c],
            pl.multiple_of(dm.NP + i * dm.CH, dm.CH),
            pl.multiple_of(dm.P + p.core * dm.CH, dm.CH),
        )
        return carry

    lax.fori_loop(0, G * dm.NC, own_cont, 0)
    own_out[...] = transpose(own_rows[...])

    def keys_values(g, x, row, table, place):
        rows = x.shape[0]
        n = normed(x)
        all_rows[pl.ds(place, rows), :] = n
        c = cos[pl.ds(table, rows), :]
        hi = shi[pl.ds(table, rows), :]
        lo = slo[pl.ds(table, rows), :]
        for t in range(TP):
            kk = dot(n, w[t, :, HC : 2 * HC])
            for j in range(HC // 128):
                tile = rotate(kk[:, j * 128 : (j + 1) * 128], c, hi, lo)
                k_out[g, pl.ds(row, rows), t * HC + j * 128 : t * HC + (j + 1) * 128] = tile.astype(BF16)
            v_out[g, pl.ds(row, rows), t * HC : (t + 1) * HC] = dot(n, w[t, :, 2 * HC : 3 * HC]).astype(BF16)

    def block_chunk(g, b):
        row = pl.multiple_of(b * PB, PB)
        keys_values(g, xp[b, g], row, row, pl.multiple_of((b * G + g) * PB, PB))

    arrived(xc.at[1 - p.core], c_mate, p)

    def cont_chunk(i, carry):
        g, c = i // dm.NC, i % dm.NC
        row = pl.multiple_of(dm.P + c * CL, CL)
        x = jnp.concatenate([xc[0, g, c], xc[1, g, c]], axis=0)
        keys_values(g, x, row, dm.P, pl.multiple_of(G * dm.P + i * CL, CL))
        return carry

    lax.fori_loop(0, G * dm.NC, cont_chunk, 0)

    def relay(k):
        b = p.ctx_before(k) * 2 + p.core
        arrived(xp.at[b], x_plane.at[k - 1], p)
        return send(xp.at[b], xp.at[b], x_send.at[p.ctxs + k - 1], x_mate.at[k], p.mate())

    for k in range(1, p.ctxs):
        sent.append(relay(k))
    for k in range(p.ctxs):
        arrived(xp.at[p.ctx_before(k) * 2 + 1 - p.core], x_mate.at[k], p)

    def prompt_chunk(i, carry):
        block_chunk(i // (2 * p.ctxs), i % (2 * p.ctxs))
        return carry

    lax.fori_loop(0, G * 2 * p.ctxs, prompt_chunk, 0)
    gm.relay_across()

    def turn(i, carry):
        rows = pl.ds(pl.multiple_of(i * 256, 256), 256)
        nt_out[:, rows] = transpose(all_rows[rows, :])
        return carry

    lax.fori_loop(0, G * R // 256, turn, 0)

    TILE = 256
    tiles = dm.P // TILE

    def attend(i, carry):
        g, pair = i // dm.PAIRS, i % dm.PAIRS
        lanes = pl.ds(pl.multiple_of(pair * 128, 128), 128)
        qp = q_out[pl.ds(pl.multiple_of(g * PB, PB), PB), lanes]
        qc = q_out[pl.ds(pl.multiple_of(dm.NP + g * NCH, NCH), NCH), lanes]
        qt = heads_columns(transpose(qp), transpose(qc))
        top = None
        for j in range(tiles):
            s = dot(k_out[g, j * TILE : (j + 1) * TILE, lanes], qt)
            sbuf[j * TILE : (j + 1) * TILE, : 2 * PB] = (
                s[:, : 2 * PB] + maskp[j * TILE : (j + 1) * TILE, :]
            )
            sbuf[j * TILE : (j + 1) * TILE, 2 * PB :] = s[:, 2 * PB :]
            here = jnp.max(sbuf[j * TILE : (j + 1) * TILE, :], axis=0, keepdims=True)
            top = here if top is None else jnp.maximum(top, here)
        sx = dot(k_out[g, dm.P :, lanes], qt[:, 2 * PB :]) + maskx[...]
        topx = jnp.max(sx, axis=0, keepdims=True)
        top = jnp.concatenate([top[:, : 2 * PB], jnp.maximum(top[:, 2 * PB :], topx)], axis=1)
        total, acc = None, None
        for j in range(tiles):
            e = jnp.exp(sbuf[j * TILE : (j + 1) * TILE, :] - top)
            here = jnp.sum(e, axis=0, keepdims=True)
            vt = transpose(v_out[g, j * TILE : (j + 1) * TILE, lanes])
            part = dot(vt, e.astype(BF16))
            total = here if total is None else total + here
            acc = part if acc is None else acc + part
        ex = jnp.exp(sx - top[:, 2 * PB :])
        partx = dot(transpose(v_out[g, dm.P :, lanes]), ex.astype(BF16))
        totalx = jnp.sum(ex, axis=0, keepdims=True)
        total = jnp.concatenate([total[:, : 2 * PB], total[:, 2 * PB :] + totalx], axis=1)
        acc_p = acc[:, : 2 * PB] / total[:, : 2 * PB]
        acc_c = (acc[:, 2 * PB :] + partx) / total[:, 2 * PB :]
        lse_out[i] = top + jnp.log(total)
        outp = jnp.where(sublane_pick((128, PB), True), acc_p[:, :PB], acc_p[:, PB:])
        outc = jnp.where(sublane_pick((128, NCH), True), acc_c[:, :NCH], acc_c[:, NCH:])
        att_out[pl.ds(pl.multiple_of(g * PB, PB), PB), lanes] = outp.T.astype(BF16)
        att_out[pl.ds(pl.multiple_of(dm.NP + g * NCH, NCH), NCH), lanes] = outc.T.astype(BF16)
        return carry

    lax.fori_loop(0, G * dm.PAIRS, attend, 0)
    gm.relay_rows(0)
    gm.relay_rows(1)
    gm.finish()
    gq.drain()
    gm.drain()
    for copy in sent:
        copy.wait_send()
    put.wait()


def mlp_kernel(
    dm,
    steps,
    mix,
    att,
    op,
    oc,
    tp_,
    tc,
    ln,
    wo,
    wu,
    wd,
    blk_out,
    resg,
    gatt,
    gwo,
    gwu,
    gwd,
    small,
    resid,
    hat,
    scale,
    hn,
    hnt,
    gd,
    gdt,
    blk,
    gh,
):
    D, NP, NT, G, PB = dm.D, dm.NP, dm.NT, dm.G, dm.PB
    TP, HC = wo.shape[0], wo.shape[2]
    t, j = pl.program_id(0), pl.program_id(1)
    gain, bias = ln[2:3, :], ln[3:4, :]

    def own(prompt, cont):
        return jnp.concatenate([prompt.reshape(NP, D), cont.reshape(NT - NP, D)], axis=0)

    @pl.when((t == 0) & (j == 0))
    def _():
        branch = dot_nt(att[:, :HC], wo[0])
        for s in range(1, TP):
            branch += dot_nt(att[:, s * HC : (s + 1) * HC], wo[s])
        r = own(op[...], oc[...]).astype(F32) + branch
        resid[...] = r
        h, sc = norm_stats(r)
        hat[...] = h
        scale[...] = jnp.broadcast_to(sc, scale.shape)
        n = (h * gain + bias).astype(BF16)
        hn[...] = n
        hnt[...] = transpose(n)
        g = (mix[4] * own(tp_[...], tc[...]).astype(F32)).astype(BF16)
        gd[...] = g
        gdt[...] = transpose(g)
        blk[...] = r
        gh[...] = jnp.zeros_like(gh)

    up, dn = wu[0], wd[0]
    u = dot(hn[...], up)
    c0 = 0.7978845608028654
    u2 = u * u
    th = jnp.tanh(c0 * u * (1.0 + 0.044715 * u2))
    half = 0.5 * (1.0 + th)
    act = (u * half).astype(BF16)
    slope = half + 0.5 * u * (1.0 - th * th) * (c0 * (1.0 + 3 * 0.044715 * u2))
    blk[...] += dot_nt(act, dn)
    gwd[0] = dot(gdt[...], act).astype(BF16)
    gu = (dot(gd[...], dn) * slope).astype(BF16)
    gwu[0] = dot(hnt[...], gu).astype(BF16)
    gh[...] += dot_nt(gu, up)

    @pl.when((t == TP - 1) & (j == steps - 1))
    def _():
        cot = own(tp_[...], tc[...]).astype(F32)
        block = blk[...]
        blk_out[...] = block.astype(BF16)
        small[2:3, :] = jnp.sum(cot * block, axis=0, keepdims=True)
        small[3:, :] = jnp.zeros((5, D), F32)
        g = gh[...]
        h = hat[...]
        small[0:1, :] = jnp.sum(g * h, axis=0, keepdims=True)
        small[1:2, :] = jnp.sum(g, axis=0, keepdims=True)
        gr = mix[4] * cot + norm_back(g, gain, h, scale[:, 0:1])
        resg[...] = gr
        gb = gr.astype(BF16)
        gbt = transpose(gb)
        for s in range(TP):
            gatt[:, s * HC : (s + 1) * HC] = dot(gb, wo[s]).astype(BF16)
            gwo[s] = dot(gbt, att[:, s * HC : (s + 1) * HC]).astype(BF16)


class Reduce:
    def __init__(self, p, n, refs):
        self.p, self.n = p, n
        self.mine, self.got, self.row, self.acr, self.zin = refs[:5]
        self.sc, self.rc, self.sy, self.ry, self.sx, self.rx, self.sz, self.rz = refs[5:13]
        self.mid = p.ctxs // 2
        self.left = p.ctx < self.mid
        self.centre = (p.ctx == self.mid - 1) | (p.ctx == self.mid)
        self.outer = (p.ctx > 0) & (p.ctx < p.ctxs - 1)
        step = jnp.where(self.left, 1, -1)
        self.inner_at = p.ctx + step
        self.outer_at = jnp.clip(p.ctx - step, 0, p.ctxs - 1)

    REFS = 13

    @staticmethod
    def scratch(n, chips, size, width, slots=2):
        dma = pltpu.SemaphoreType.DMA
        far = max(chips - 1, 1)
        return [
            pltpu.VMEM((slots, chips, 2, size, width), BF16),
            pltpu.VMEM((2 * n, chips, size, width), BF16),
            pltpu.VMEM((2 * n, far, size, width), BF16),
            pltpu.VMEM((n, size, width), BF16),
            pltpu.VMEM((n, 2, size, width), BF16),
            dma((2 * n,)),
            dma((2 * n,)),
            dma((2 * n, far)),
            dma((2 * n, far)),
            dma((n,)),
            dma((n,)),
            dma((n, 2)),
            dma((n, 2)),
        ]

    def copy(self, src, dst, send_sem, recv_sem, device):
        return pltpu.make_async_remote_copy(
            src_ref=src,
            dst_ref=dst,
            send_sem=send_sem,
            recv_sem=recv_sem,
            device_id=device,
            device_id_type=MESH,
        )

    def by_core(self, i, slot):
        p = self.p
        return self.copy(
            self.mine.at[slot, :, 1 - p.core], self.got.at[i], self.sc.at[i], self.rc.at[i], p.mate()
        )

    def by_row(self, i, k):
        p = self.p
        return self.copy(
            self.got.at[i, p.chip_after(k)],
            self.row.at[i, k - 1],
            self.sy.at[i, k - 1],
            self.ry.at[i, k - 1],
            p.row(k),
        )

    def by_tp(self, j):
        p = self.p
        return self.copy(
            self.got.at[j, p.chip], self.acr.at[j], self.sx.at[j], self.rx.at[j], p.across()
        )

    def inward(self, j):
        slot = jnp.where(self.centre, 1, 0)
        return self.copy(
            self.got.at[self.n + j, self.p.chip],
            self.zin.at[j, slot],
            self.sz.at[j, 0],
            self.rz.at[j, slot],
            self.p.at(ctx=self.inner_at),
        )

    def outward(self, j):
        return self.copy(
            self.got.at[self.n + j, self.p.chip],
            self.zin.at[j, 1],
            self.sz.at[j, 1],
            self.rz.at[j, 1],
            self.p.at(ctx=self.outer_at),
        )

    def add(self, i, y, other):
        self.got[i, y] = (self.got[i, y].astype(F32) + other.astype(F32)).astype(BF16)

    def cores_send(self, i, slot):
        self.by_core(i, slot).start()

    def cores_sent(self, i, slot):
        self.by_core(i, slot).wait_send()

    def cores_sum(self, i, slot):
        p = self.p
        self.by_core(i, slot).wait_recv()
        for y in range(p.chips):
            self.add(i, y, self.mine[slot, y, p.core])
        for k in range(1, p.chips):
            self.by_row(i, k).start()

    def rows_sum(self, i):
        p = self.p
        for k in range(1, p.chips):
            self.by_row(i, k).wait_recv()
            self.add(i, p.chip, self.row[i, k - 1])
        if i < self.n:
            self.by_tp(i).start()

    def tp_sum(self, j):
        self.by_tp(j).wait_recv()
        self.add(self.n + j, self.p.chip, self.acr[j])

        @pl.when(jnp.logical_not(self.outer))
        def _():
            self.inward(j).start()

    def ctx_in(self, j):
        @pl.when(self.outer)
        def _():
            pltpu.make_async_copy(self.zin.at[j, 0], self.zin.at[j, 0], self.rz.at[j, 0]).wait()
            self.add(self.n + j, self.p.chip, self.zin[j, 0])
            self.inward(j).start()

    def ctx_out(self, j):
        p = self.p
        pltpu.make_async_copy(self.zin.at[j, 1], self.zin.at[j, 1], self.rz.at[j, 1]).wait()
        self.inward(j).wait_send()

        @pl.when(self.centre)
        def _():
            self.add(self.n + j, p.chip, self.zin[j, 1])

        @pl.when(jnp.logical_not(self.centre))
        def _():
            self.got[self.n + j, p.chip] = self.zin[j, 1]

        @pl.when(self.outer)
        def _():
            self.outward(j).start()
        return self.got[self.n + j, p.chip]

    def drain(self):
        p = self.p
        for i in range(2 * self.n):
            for k in range(1, p.chips):
                self.by_row(i, k).wait_send()
        for j in range(self.n):
            self.by_tp(j).wait_send()

            @pl.when(self.outer)
            def _():
                self.outward(j).wait_send()


def small_sum(p, sm, near, rows, across, planes, ss, rc, ry, rx, rz):
    copies = []

    def go(src, dst, recv_sem, device):
        copies.append(send(src, dst, ss.at[len(copies)], recv_sem, device))

    go(sm, near, rc, p.mate())
    copies[-1].wait_recv()
    rows[p.chip] = sm[...] + near[...]
    for k in range(1, p.chips):
        go(rows.at[p.chip], rows.at[p.chip], ry.at[k - 1], p.row(k))
    for k in range(1, p.chips):
        arrived(rows.at[p.chip_before(k)], ry.at[k - 1], p)
    total = rows[0]
    for y in range(1, p.chips):
        total += rows[y]
    across[0] = total
    go(across.at[0], across.at[1], rx, p.across())
    copies[-1].wait_recv()
    planes[p.ctx] = across[0] + across[1]
    for k in range(1, p.ctxs):
        go(planes.at[p.ctx], planes.at[p.ctx], rz.at[k - 1], p.plane(k))
    for k in range(1, p.ctxs):
        arrived(planes.at[p.ctx_before(k)], rz.at[k - 1], p)
    total = planes[0]
    for z in range(1, p.ctxs):
        total += planes[z]
    for copy in copies:
        copy.wait_send()
    return total


def backward_kernel(
    dm,
    T,
    q,
    att,
    gatt,
    lse,
    nt,
    own_nt,
    cos,
    shi,
    slo,
    w,
    ln,
    own_p,
    own_c,
    resg,
    small,
    k_hbm,
    v_hbm,
    gwo,
    gwu,
    gwd,
    gin_p,
    gin_c,
    gq_out,
    go_out,
    gu_out,
    gd_out,
    small_out,
    maskp,
    maskx,
    kbuf,
    vbuf,
    dk,
    dv,
    dq,
    dxq,
    dxm,
    dxz,
    dxc,
    dxcm,
    kv_sem,
    load_a,
    load_b,
    m_send,
    m_recv,
    z_send,
    z_recv,
    c_send,
    c_recv,
    sm,
    sm_near,
    sm_rows,
    sm_across,
    sm_planes,
    sm_ss,
    sm_rc,
    sm_ry,
    sm_rx,
    sm_rz,
    *refs,
):
    G, R, PB, NCH, D, NX = dm.G, dm.R, dm.PB, dm.NCH, dm.D, dm.NX
    TP, HC = w.shape[0], (w.shape[2] - 128) // 3
    PT = dm.PAIRS // TP
    p = Peers()
    n_a = gwu.shape[-1] // T
    ra = Reduce(p, n_a, refs[: Reduce.REFS])
    rb = Reduce(p, 1 + PT, refs[Reduce.REFS :])
    block = block_index()
    TILE = 256
    tiles = dm.P // TILE
    chips = p.chips

    def tp_of(i, n):
        return 1 - p.tp if i < n else p.tp

    def load_slab(i):
        t, cols, slot = tp_of(i, n_a), slice((i % n_a) * T, (i % n_a + 1) * T), i % 2
        return [
            pltpu.make_async_copy(gwu.at[t, :, :, :, cols], ra.mine.at[slot, :, :, :, :T], load_a.at[0, slot]),
            pltpu.make_async_copy(gwd.at[t, :, :, :, cols], ra.mine.at[slot, :, :, :, T:], load_a.at[1, slot]),
        ]

    def begin(copies):
        for copy in copies:
            copy.start()

    def ready(copies):
        for copy in copies:
            copy.wait()

    def load_kv(it, slot):
        pair_rel, g = it // G, it % G
        t = jnp.where(pair_rel < PT, 1 - p.tp, p.tp)
        lanes = pl.ds(pl.multiple_of((t * PT + pair_rel % PT) * 128, 128), 128)
        return [
            pltpu.make_async_copy(k_hbm.at[g, :, lanes], kbuf.at[slot], kv_sem.at[0, slot]),
            pltpu.make_async_copy(v_hbm.at[g, :, lanes], vbuf.at[slot], kv_sem.at[1, slot]),
        ]

    begin(load_kv(0, 0))
    begin(load_slab(0))
    begin(load_slab(1))
    wo_load = [
        pltpu.make_async_copy(gwo.at[tp_of(i, 1)], rb.mine.at[i], load_b.at[i]) for i in range(2)
    ]
    begin(wo_load)
    p.greet()
    fill_masks(dm, maskp, maskx)
    for i in range(2):
        ready(load_slab(i))
        ra.cores_send(i, i)
    ready(wo_load)
    NB = 1 + PT
    rb.cores_send(0, 0)
    rb.cores_send(NB, 1)
    ra.cores_sum(0, 0)

    def next_slab(i):
        def run():
            ra.cores_sent(i - 2, i % 2)
            begin(load_slab(i))

        return run

    def send_slab(i):
        def run():
            ready(load_slab(i))
            ra.cores_send(i, i % 2)

        return run

    events = {}

    def on(it, step):
        events.setdefault(it, []).append(step)

    for i in range(1, 2 * n_a):
        on(i, partial(ra.cores_sum, i, i % 2))
        if i + 1 < 2 * n_a:
            on(i - 1, next_slab(i + 1))
            on(i, send_slab(i + 1))
    on(2 * n_a, partial(rb.cores_sum, 0, 0))
    on(2 * n_a, partial(rb.cores_sum, NB, 1))

    def wslab(pair_rel):
        return pair_rel + 1 if pair_rel < PT else NB + 1 + pair_rel - PT

    late = []
    wslot = lambda pair_rel: 2 + pair_rel % 2
    for pr in range(TP * PT - 1):
        on(pr * G + 2 * G - 1, partial(rb.cores_sum, wslab(pr), wslot(pr)))
    on(5, partial(ra.rows_sum, 0))
    on(8, partial(ra.rows_sum, 1))
    on(11, partial(ra.rows_sum, 2))

    def attend(it, carry):
        pair_rel, g = it // G, it % G
        t = jnp.where(pair_rel < PT, 1 - p.tp, p.tp)
        pair = t * PT + pair_rel % PT
        slot = it % 2

        @pl.when(it + 1 < G * dm.PAIRS)
        def _():
            begin(load_kv(it + 1, 1 - slot))

        lanes = pl.ds(pl.multiple_of(pair * 128, 128), 128)
        rp = pl.ds(pl.multiple_of(g * PB, PB), PB)
        rc = pl.ds(pl.multiple_of(dm.NP + g * NCH, NCH), NCH)
        qp, qc = q[rp, lanes], q[rc, lanes]
        gp, gc = gatt[rp, lanes], gatt[rc, lanes]
        ap, ac = att[rp, lanes].astype(F32), att[rc, lanes].astype(F32)
        qt = heads_columns(transpose(qp), transpose(qc))
        gpt, gct = gp.astype(F32).T, gc.astype(F32).T
        gt = heads_columns(gpt.astype(BF16), gct.astype(BF16))
        qs, gs = heads_rows(qp, qc), heads_rows(gp, gc)
        prodp, prodc = gpt * ap.T, gct * ac.T
        delta = jnp.concatenate(
            [
                jnp.sum(prodp[:HD], axis=0, keepdims=True),
                jnp.sum(prodp[HD:], axis=0, keepdims=True),
                jnp.sum(prodc[:HD], axis=0, keepdims=True),
                jnp.sum(prodc[HD:], axis=0, keepdims=True),
            ],
            axis=1,
        )
        stat = lse[g * dm.PAIRS + pair]
        ready(load_kv(it, slot))

        def grads(s, kt, vt, cols):
            pr = jnp.exp(s - stat[:, cols:])
            dp = dot(vt, gt[:, cols:])
            ds = (pr * (dp - delta[:, cols:])).astype(BF16)
            gv = dot(pr.astype(BF16), gs[cols:])
            gk = dot(ds, qs[cols:])
            gq = dot(transpose(kt), ds)
            return gk, gv, gq

        acc = None
        for j in range(tiles):
            rows = slice(j * TILE, (j + 1) * TILE)
            kt = kbuf[slot, rows, :]
            s = dot(kt, qt)
            s = jnp.concatenate([s[:, : 2 * PB] + maskp[rows, :], s[:, 2 * PB :]], axis=1)
            gk, gv, gq = grads(s, kt, vbuf[slot, rows, :], 0)
            gk = rotate_back(gk, cos[rows, :], shi[rows, :], slo[rows, :]).astype(BF16)
            gv = gv.astype(BF16)
            for b in range(TILE // PB):
                out = pl.ds(pl.multiple_of(((j * (TILE // PB) + b) * G + g) * PB, PB), PB)
                dk[out, lanes] = gk[b * PB : (b + 1) * PB]
                dv[out, lanes] = gv[b * PB : (b + 1) * PB]
            acc = gq if acc is None else acc + gq
        kt = kbuf[slot, dm.P :, :]
        s = dot(kt, qt[:, 2 * PB :]) + maskx[...]
        gk, gv, gq = grads(s, kt, vbuf[slot, dm.P :, :], 2 * PB)
        for c in range(dm.NC):
            rows = slice(dm.P, dm.P + CL)
            out = pl.ds(pl.multiple_of(G * dm.P + (g * dm.NC + c) * CL, CL), CL)
            part = rotate_back(gk[c * CL : (c + 1) * CL], cos[rows, :], shi[rows, :], slo[rows, :])
            dk[out, lanes] = part.astype(BF16)
            dv[out, lanes] = gv[c * CL : (c + 1) * CL].astype(BF16)
        accp = acc[:, : 2 * PB] * 0.125
        accc = (acc[:, 2 * PB :] + gq) * 0.125
        outp = jnp.where(sublane_pick((128, PB), True), accp[:, :PB], accp[:, PB:]).T
        outc = jnp.where(sublane_pick((128, NCH), True), accc[:, :NCH], accc[:, NCH:]).T
        tab = pl.ds(pl.multiple_of(block * PB, PB), PB)
        dq[rp, lanes] = rotate_back(outp, cos[tab, :], shi[tab, :], slo[tab, :]).astype(BF16)
        tab = pl.ds(pl.multiple_of(dm.P + p.core * dm.CH, dm.CH), dm.CH)
        for c in range(dm.NC):
            part = rotate_back(outc[c * dm.CH : (c + 1) * dm.CH], cos[tab, :], shi[tab, :], slo[tab, :])
            rows = pl.ds(pl.multiple_of(dm.NP + g * NCH + c * dm.CH, dm.CH), dm.CH)
            dq[rows, lanes] = part.astype(BF16)

        @pl.when(g == G - 1)
        def _():
            put = 2 + pair_rel % 2
            index = jnp.where(pair_rel < PT, pair_rel + 1, NB + 1 + pair_rel - PT)

            @pl.when(pair_rel >= 2)
            def _():
                last = pair_rel - 2
                rb.cores_sent(jnp.where(last < PT, last + 1, NB + 1 + last - PT), put)

            size = D // (2 * chips)
            shape = (chips, 2, size)
            both = jnp.concatenate([dk[:, lanes], dv[:, lanes]], axis=1)
            gkv = dot(nt[...], both).astype(BF16).reshape(shape + (256,))
            rb.mine[put, :, :, :, 128:] = gkv
            gqw = dot(own_nt[...], dq[:, lanes]).astype(BF16).reshape(shape + (128,))
            rb.mine[put, :, :, :, :128] = gqw
            rb.cores_send(index, put)

        for when, steps in events.items():

            @pl.when(it == when)
            def _():
                for step in steps:
                    step()

        return carry

    lax.fori_loop(0, G * dm.PAIRS, attend, 0)
    last = G * dm.PAIRS
    for when in sorted(events):
        if when >= last:
            for step in events[when]:
                step()
    tail = TP * PT - 1

    def project(rows):
        total = None
        for t in range(TP):
            part = dot_nt(dk[rows, t * HC : (t + 1) * HC], w[t, :, HC : 2 * HC])
            total = part if total is None else total + part
            total += dot_nt(dv[rows, t * HC : (t + 1) * HC], w[t, :, 2 * HC : 3 * HC])
        return total

    def block_rows(b):
        return pl.ds(pl.multiple_of(b * G * PB, G * PB), G * PB)

    def to_mate(k):
        b = p.ctx_after(k) * 2 + 1 - p.core
        return ra.copy(dk.at[block_rows(b), :], dxm.at[k], m_send.at[k], m_recv.at[k], p.mate())

    def to_plane(k):
        b = p.ctx_after(k) * 2 + p.core
        return ra.copy(
            dk.at[block_rows(b), :],
            dxz.at[k - 1],
            z_send.at[k - 1],
            z_recv.at[k - 1],
            p.at(ctx=p.ctx_after(k)),
        )

    def planes(i, carry):
        k = lax.rem(i + 1, p.ctxs)
        rows = block_rows(p.ctx_after(k) * 2 + 1 - p.core)
        dk[rows, :] = project(rows).astype(BF16)
        to_mate(k).start()
        rows = block_rows(p.ctx_after(k) * 2 + p.core)
        part = project(rows)
        to_mate(k).wait_recv()
        dk[rows, :] = (part + dxm[k].astype(F32)).astype(BF16)

        @pl.when(k > 0)
        def _():
            to_plane(k).start()

        return carry

    lax.fori_loop(0, p.ctxs, planes, 0)
    rb.cores_sum(wslab(tail), wslot(tail))

    def cont_rows(i, carry):
        rows = pl.ds(pl.multiple_of(G * dm.P + i * CL, CL), CL)
        total = project(rows).astype(BF16)
        out = pl.ds(pl.multiple_of(i * dm.CH, dm.CH), dm.CH)
        dxc[0, out, :] = total[: dm.CH]
        dxc[1, out, :] = total[dm.CH :]
        return carry

    lax.fori_loop(0, G * dm.NC, cont_rows, 0)
    cont_copy = ra.copy(dxc.at[1 - p.core], dxcm, c_send, c_recv, p.mate())
    cont_copy.start()
    total = dot_nt(dq[:, :HC], w[0, :, :HC])
    for t in range(1, TP):
        total += dot_nt(dq[:, t * HC : (t + 1) * HC], w[t, :, :HC])
    dxq[...] = total
    for i in range(n_a, 2 * n_a):
        ra.rows_sum(i)
        ra.tp_sum(i - n_a)
    for j in range(n_a):
        ra.ctx_in(j)
    gain = ln[0:1, :]
    cont_copy.wait_recv()
    gn = dxc[p.core].astype(F32) + dxcm[...].astype(F32) + dxq[dm.NP :, :]
    hat, scale = norm_stats(own_c[...].reshape(dm.NT - dm.NP, D).astype(F32))
    gin_c[...] = (resg[dm.NP :, :] + norm_back(gn, gain, hat, scale)).astype(BF16).reshape(gin_c.shape)
    sums = [jnp.sum(gn * hat, axis=0, keepdims=True), jnp.sum(gn, axis=0, keepdims=True)]
    for i in list(range(NB)) + [NB]:
        rb.rows_sum(i)

    def final_a(j):
        total = ra.ctx_out(j)
        gu_out[:, j * T : (j + 1) * T] = total[:, :T].astype(F32)
        gd_out[j * T : (j + 1) * T, :] = total[:, T:].astype(F32).T

    for j in range(n_a):
        final_a(j)
    gn = dk[block_rows(block), :].astype(F32) + dxq[: dm.NP, :]
    for k in range(1, p.ctxs):
        to_plane(k).wait_recv()
        gn += dxz[k - 1].astype(F32)
    hat, scale = norm_stats(own_p[...].reshape(dm.NP, D).astype(F32))
    gin_p[...] = (resg[: dm.NP, :] + norm_back(gn, gain, hat, scale)).astype(BF16).reshape(gin_p.shape)
    sm[...] = small[...]
    sm[7:8, :] = sums[0] + jnp.sum(gn * hat, axis=0, keepdims=True)
    sm[8:9, :] = sums[1] + jnp.sum(gn, axis=0, keepdims=True)
    for i in range(NB + 1, 2 * NB):
        rb.rows_sum(i)
    for j in range(NB):
        rb.tp_sum(j)
    for j in range(NB):
        rb.ctx_in(j)
    small_out[...] = small_sum(
        p, sm, sm_near, sm_rows, sm_across, sm_planes, sm_ss, sm_rc, sm_ry, sm_rx, sm_rz
    )
    for j in range(NB):
        total = rb.ctx_out(j).astype(F32)
        if j == 0:
            go_out[...] = total.T
        else:
            for c in range(3):
                first = c * HC + (j - 1) * 128
                gq_out[:, first : first + 128] = total[:, c * 128 : (c + 1) * 128]
    for i in range(max(0, 2 * n_a - 2), 2 * n_a):
        ra.cores_sent(i, i % 2)
    rb.cores_sent(0, 0)
    rb.cores_sent(NB, 1)
    for pr in (tail - 1, tail):
        rb.cores_sent(wslab(pr), wslot(pr))
    for k in range(p.ctxs):
        to_mate(k).wait_send()
    for k in range(1, p.ctxs):
        to_plane(k).wait_send()
    cont_copy.wait_send()
    ra.drain()
    rb.drain()


def whole(shape):
    zeros = (0,) * len(shape)
    return pl.BlockSpec(shape, lambda *_: zeros)


def params(**more):
    return pltpu.CompilerParams(vmem_limit_bytes=VMEM_LIMIT, **more)


def per_device(
    prompt_in,
    cont_in,
    prompt_embed,
    cont_embed,
    prompt_earlier,
    cont_earlier,
    ln1_gain,
    ln1_bias,
    ln2_gain,
    ln2_bias,
    w_qkv,
    w_out,
    w_up,
    w_down,
    mix_weights,
    prompt_cot,
    cont_cot,
):
    G, PB, D = prompt_in.shape
    NC, CH = cont_in.shape[1], cont_in.shape[2]
    TP = lax.axis_size("tp")
    PROMPT = PB * TP * lax.axis_size("ctx")
    HC, FC = w_qkv.shape[2], w_up.shape[1]
    S = w_qkv.shape[0]
    dm = Dims(G, PROMPT, PB, NC, CH, D, HC * TP // HD)
    R, NT, NP = dm.R, dm.NT, dm.NP

    sds = jax.ShapeDtypeStruct
    chips, ctxs = lax.axis_size("dp") // 2, lax.axis_size("ctx")
    swap = [(4 * y + 2 * c + t, 4 * y + 2 * t + c) for y in range(chips) for c in (0, 1) for t in (0, 1)]

    def trade(x):
        return lax.ppermute(x, ("dp", "tp"), swap)

    own_p, own_c = trade(prompt_in), trade(cont_in)
    cot_p, cot_c = trade(prompt_cot), trade(cont_cot)
    norms = jnp.stack([ln1_gain, ln1_bias, ln2_gain, ln2_bias], axis=1)
    norms = jnp.pad(norms, ((0, 0), (0, 124)))
    wq_shard = jnp.concatenate([w_qkv.reshape(S, 3 * HC), norms], axis=1)
    wm_shard = jnp.concatenate([w_out.T, w_up, w_down.T], axis=1)

    positions = jnp.arange(PROMPT + CL, dtype=jnp.int32).astype(F32)
    lane = jnp.arange(128, dtype=jnp.int32)
    freq = 10000.0 ** (-((lane % 32).astype(F32) / 32))
    angles = positions[:, None] * freq[None, :]
    cos, sin = jnp.cos(angles), jnp.sin(angles)
    second = (lane % 64) >= 32
    shi = jnp.where(second[None, :], sin, 0.0)
    slo = jnp.where(second[None, :], 0.0, -sin)

    any_ = pl.BlockSpec(memory_space=pl.ANY)
    vmem = pl.BlockSpec(memory_space=pltpu.VMEM)
    dma = pltpu.SemaphoreType.DMA
    nt, own_nt, k, v, q, att, lse, wq, ln, wm = pl.pallas_call(
        partial(forward_kernel, dm),
        out_shape=(
            sds((D, G * R), BF16),
            sds((D, NT), BF16),
            sds((G, R, D), BF16),
            sds((G, R, D), BF16),
            sds((NT, D), BF16),
            sds((NT, D), BF16),
            sds((G * dm.PAIRS, 1, dm.COLS), F32),
            sds((TP, D, 3 * HC + 128), BF16),
            sds((8, D), F32),
            sds((TP, D, HC + 2 * FC), BF16),
        ),
        in_specs=[vmem] * 6 + [any_],
        out_specs=(vmem,) * 7 + (any_, vmem, any_),
        scratch_shapes=[
            pltpu.VMEM((PROMPT, 2 * PB), F32),
            pltpu.VMEM((dm.NX, 2 * dm.NCH), F32),
            pltpu.VMEM((PROMPT, dm.COLS), F32),
            pltpu.VMEM((G * R, D), BF16),
            pltpu.VMEM((NT, D), BF16),
            pltpu.VMEM((2 * ctxs, G, PB, D), BF16),
            pltpu.VMEM((2, G, NC, CH, D), BF16),
            pltpu.VMEM((TP, D, 3 * HC + 128), BF16),
            dma,
            dma((2 * ctxs - 1,)),
            dma((ctxs - 1,)),
            dma((ctxs,)),
            dma,
            dma,
            dma((4,)),
        ]
        + WeightGather.semaphores(chips)
        + WeightGather.semaphores(chips),
        compiler_params=params(collective_id=0, has_side_effects=True),
        name="forward",
    )(own_p, own_c, cos, shi, slo, wq_shard, wm_shard)
    wo, wu, wd = wm[:, :, :HC], wm[:, :, HC : HC + FC], wm[:, :, HC + FC :]

    T = 512 if FC % 512 == 0 else 256
    steps = FC // T
    row_specs = [whole(a.shape) for a in (att, own_p, own_c, cot_p, cot_c, ln, wo)]
    tile = pl.BlockSpec((1, D, T), lambda t, j: (t, 0, j))
    blk, resg, gatt, gwo, gwu, gwd, small = pl.pallas_call(
        partial(mlp_kernel, dm, steps),
        grid=(TP, steps),
        out_shape=(
            sds((NT, D), BF16),
            sds((NT, D), F32),
            sds((NT, D), BF16),
            sds((TP, D, HC), BF16),
            sds((TP, D, FC), BF16),
            sds((TP, D, FC), BF16),
            sds((8, D), F32),
        ),
        in_specs=[pl.BlockSpec(memory_space=pltpu.SMEM)] + row_specs + [tile, tile],
        out_specs=(
            whole((NT, D)),
            whole((NT, D)),
            whole((NT, D)),
            whole((TP, D, HC)),
            tile,
            tile,
            whole((8, D)),
        ),
        scratch_shapes=[
            pltpu.VMEM((NT, D), F32),
            pltpu.VMEM((NT, D), F32),
            pltpu.VMEM((NT, 128), F32),
            pltpu.VMEM((NT, D), BF16),
            pltpu.VMEM((D, NT), BF16),
            pltpu.VMEM((NT, D), BF16),
            pltpu.VMEM((D, NT), BF16),
            pltpu.VMEM((NT, D), F32),
            pltpu.VMEM((NT, D), F32),
        ],
        compiler_params=params(),
        name="feed",
    )(
        mix_weights,
        att,
        own_p,
        own_c,
        cot_p,
        cot_c,
        ln,
        wo,
        wu,
        wd,
    )

    sums = []
    for e, y, c in (
        (prompt_embed, prompt_earlier, prompt_cot),
        (cont_embed, cont_earlier, cont_cot),
    ):
        c = c.astype(F32)
        terms = [e.astype(F32)] + [y[i].astype(F32) for i in range(3)]
        sums.append(jnp.stack([jnp.sum((c * a).reshape(-1, D), axis=0) for a in terms]))
    small = jnp.concatenate([small[:3], sums[0] + sums[1], jnp.zeros((9, D), F32)], axis=0)

    blk = trade(blk).astype(F32)
    n_a = FC // T
    split = (TP, chips, 2, S)
    far = max(chips - 1, 1)
    gin_p, gin_c, gq, go, gu, gd, small = pl.pallas_call(
        partial(backward_kernel, dm, T),
        out_shape=(
            sds(prompt_in.shape, BF16),
            sds(cont_in.shape, BF16),
            sds((S, 3 * HC), F32),
            sds((HC, S), F32),
            sds((S, FC), F32),
            sds((FC, S), F32),
            sds((16, D), F32),
        ),
        in_specs=[vmem] * 15 + [any_] * 5,
        out_specs=(vmem,) * 7,
        scratch_shapes=[
            pltpu.VMEM((PROMPT, 2 * PB), F32),
            pltpu.VMEM((dm.NX, 2 * dm.NCH), F32),
            pltpu.VMEM((2, R, 128), BF16),
            pltpu.VMEM((2, R, 128), BF16),
            pltpu.VMEM((G * R, D), BF16),
            pltpu.VMEM((G * R, D), BF16),
            pltpu.VMEM((NT, D), BF16),
            pltpu.VMEM((NT, D), F32),
            pltpu.VMEM((ctxs, G * PB, D), BF16),
            pltpu.VMEM((ctxs - 1, G * PB, D), BF16),
            pltpu.VMEM((2, NT - NP, D), BF16),
            pltpu.VMEM((NT - NP, D), BF16),
            dma((2, 2)),
            dma((2, 2)),
            dma((2,)),
            dma((ctxs,)),
            dma((ctxs,)),
            dma((ctxs - 1,)),
            dma((ctxs - 1,)),
            dma,
            dma,
            pltpu.VMEM((16, D), F32),
            pltpu.VMEM((16, D), F32),
            pltpu.VMEM((chips, 16, D), F32),
            pltpu.VMEM((2, 16, D), F32),
            pltpu.VMEM((ctxs, 16, D), F32),
            dma((1 + chips + ctxs,)),
            dma,
            dma((far,)),
            dma,
            dma((ctxs - 1,)),
        ]
        + Reduce.scratch(n_a, chips, S, 2 * T)
        + Reduce.scratch(1 + dm.PAIRS // TP, chips, S, HC, slots=4),
        compiler_params=params(collective_id=1, has_side_effects=True),
        name="backward",
    )(
        q,
        att,
        gatt,
        lse,
        nt,
        own_nt,
        cos,
        shi,
        slo,
        wq,
        ln,
        own_p,
        own_c,
        resg,
        small,
        k,
        v,
        gwo.reshape(split + (HC,)),
        gwu.reshape(split + (FC,)),
        gwd.reshape(split + (FC,)),
    )
    gin_p, gin_c = trade(gin_p), trade(gin_c)
    outs = []
    for b, e, y in (
        (blk[:NP].reshape(prompt_in.shape), prompt_embed, prompt_earlier),
        (blk[NP:].reshape(cont_in.shape), cont_embed, cont_earlier),
    ):
        total = mix_weights[0] * e.astype(F32) + mix_weights[4] * b
        for i in range(3):
            total += mix_weights[1 + i] * y[i].astype(F32)
        outs.append(total.astype(BF16))
    start = lax.axis_index("dp") * S
    mine = lax.dynamic_slice_in_dim(small, start, S, axis=1)
    return (
        outs[0],
        outs[1],
        gin_p,
        gin_c,
        mine[7],
        mine[8],
        mine[0],
        mine[1],
        gq.reshape(S, 3, HC),
        go,
        gu,
        gd,
        jnp.sum(jnp.concatenate([small[3:7], small[2:3]]), axis=1),
    )


def solution(mesh):
    tokens = P("dp", ("ctx", "tp"), None)
    conts = P("dp", "ctx", "tp", None)
    weights = (P("dp", None, "tp"), P("tp", "dp"), P("dp", "tp"), P("tp", "dp"))
    in_specs = (
        tokens,
        conts,
        tokens,
        conts,
        P(None, "dp", ("ctx", "tp"), None),
        P(None, "dp", "ctx", "tp", None),
        P("dp"),
        P("dp"),
        P("dp"),
        P("dp"),
        *weights,
        P(),
        tokens,
        conts,
    )
    out_specs = (
        tokens,
        conts,
        tokens,
        conts,
        P("dp"),
        P("dp"),
        P("dp"),
        P("dp"),
        *weights,
        P(),
    )
    return jax.shard_map(
        per_device, mesh=mesh, in_specs=in_specs, out_specs=out_specs, check_vma=False
    )
```

```python
from functools import partial

import jax
import jax.numpy as jnp
import numpy as np
from jax import lax
from jax.experimental import pallas as pl
from jax.experimental.pallas import tpu as pltpu
from jax.sharding import PartitionSpec as P

HD = 64
CL = 128
EPS = 1e-05
NEG = -1e30
F32 = jnp.float32
BF16 = jnp.bfloat16
VMEM_LIMIT = 67043328


def dot(a, b):
    return lax.dot_general(a, b, (((1,), (0,)), ((), ())), preferred_element_type=F32)


def dot_nt(a, b):
    return lax.dot_general(a, b, (((1,), (1,)), ((), ())), preferred_element_type=F32)


def norm_stats(x):
    mean = jnp.mean(x, axis=-1, keepdims=True)
    centered = x - mean
    var = jnp.mean(centered * centered, axis=-1, keepdims=True)
    scale = lax.rsqrt(var + EPS)
    return centered * scale, scale


def norm_back(grad, gain, hat, scale):
    gh = grad * gain
    return scale * (
        gh
        - jnp.mean(gh, axis=-1, keepdims=True)
        - hat * jnp.mean(gh * hat, axis=-1, keepdims=True)
    )


def swap_halves(x):
    second = lax.broadcasted_iota(jnp.int32, x.shape, 1) % HD >= HD // 2
    return jnp.where(second, pltpu.roll(x, 32, 1), pltpu.roll(x, 96, 1))


def rotate(x, cos, sin):
    return x * cos + swap_halves(x) * sin


def rotate_back(x, cos, sin):
    return x * cos - swap_halves(x) * sin


def lane_pick(shape, low):
    lanes = lax.broadcasted_iota(jnp.int32, shape, 1)
    return lanes < HD if low else lanes >= HD


def sublane_pick(shape, low):
    rows = lax.broadcasted_iota(jnp.int32, shape, 0)
    return rows < HD if low else rows >= HD


def transpose(x):
    return x.astype(F32).T.astype(x.dtype)


class Dims:
    def __init__(self, groups, prompt, pb, nc, ch, d, heads):
        self.G, self.P, self.PB, self.NC, self.CH, self.D = groups, prompt, pb, nc, ch, d
        self.NCH = nc * ch
        self.R = prompt + nc * CL
        self.NX = nc * CL
        self.NR = pb + self.NCH
        self.NP = groups * pb
        self.NT = groups * self.NR
        self.PAIRS = heads // 2
        self.COLS = 2 * self.NR


MESH = pl.DeviceIdType.MESH


def half_index():
    return lax.axis_index("dp") % 2


def block_index():
    return lax.axis_index("ctx") * 2 + half_index()


class Peers:
    def __init__(self):
        self.ctxs = lax.axis_size("ctx")
        self.chips = lax.axis_size("dp") // 2
        self.tps = lax.axis_size("tp")
        self.dp = lax.axis_index("dp")
        self.ctx = lax.axis_index("ctx")
        self.tp = lax.axis_index("tp")
        self.core = self.dp % 2
        self.chip = self.dp // 2

    def at(self, dp=None, ctx=None, tp=None):
        return {
            "dp": self.dp if dp is None else dp,
            "ctx": self.ctx if ctx is None else ctx,
            "tp": self.tp if tp is None else tp,
        }

    def across(self):
        return self.at(tp=1 - self.tp)

    def mate(self):
        return self.at(dp=self.chip * 2 + 1 - self.core)

    def chip_after(self, k):
        return lax.rem(self.chip + k, self.chips)

    def chip_before(self, k):
        return lax.rem(self.chip + self.chips - k, self.chips)

    def row(self, k):
        return self.at(dp=self.chip_after(k) * 2 + self.core)

    def ctx_after(self, k):
        return lax.rem(self.ctx + k, self.ctxs)

    def ctx_before(self, k):
        return lax.rem(self.ctx + self.ctxs - k, self.ctxs)

    def plane(self, k):
        return self.at(ctx=self.ctx_after(k))

    def partner(self):
        return self.at(dp=self.chip * 2 + self.tp, tp=self.core)

    def greet(self, trades=False):
        barrier = pltpu.get_barrier_semaphore()
        peers = [self.across(), self.mate()]
        peers += [self.row(k) for k in range(1, self.chips)]
        peers += [self.plane(k) for k in range(1, self.ctxs)]
        for peer in peers:
            pl.semaphore_signal(barrier, inc=1, device_id=peer, device_id_type=MESH)
        count = len(peers)
        if trades:
            away = self.core != self.tp

            @pl.when(away)
            def _():
                pl.semaphore_signal(
                    barrier, inc=1, device_id=self.partner(), device_id_type=MESH
                )

            count += jnp.where(away, 1, 0)
        pl.semaphore_wait(barrier, count)


def send(src, dst, send_sem, recv_sem, device):
    copy = pltpu.make_async_remote_copy(
        src_ref=src,
        dst_ref=dst,
        send_sem=send_sem,
        recv_sem=recv_sem,
        device_id=device,
        device_id_type=MESH,
    )
    copy.start()
    return copy


def arrived(ref, sem, peers):
    pltpu.make_async_remote_copy(
        src_ref=ref,
        dst_ref=ref,
        send_sem=sem,
        recv_sem=sem,
        device_id=peers.mate(),
        device_id_type=MESH,
    ).wait_recv()


class WeightGather:
    def __init__(self, peers, shard, full, sends, across, rows, mate):
        self.p, self.shard, self.full = peers, shard, full
        self.sends, self.across, self.rows, self.from_mate = sends, across, rows, mate
        self.copies = []
        self.count = 0
        self.size = shard.shape[0]

    @staticmethod
    def semaphores(chips):
        return [
            pltpu.SemaphoreType.DMA((1 + 2 * (chips - 1) + 2 * chips,)),
            pltpu.SemaphoreType.DMA((1,)),
            pltpu.SemaphoreType.DMA((2, max(chips - 1, 1))),
            pltpu.SemaphoreType.DMA((2, chips)),
        ]

    def piece(self, tp, dp):
        return self.full.at[tp, pl.ds(pl.multiple_of(dp * self.size, 16), self.size), :]

    def go(self, src, dst, recv_sem, device):
        self.copies.append(send(src, dst, self.sends.at[self.count], recv_sem, device))
        self.count += 1

    def start(self):
        p = self.p
        self.go(self.shard, self.piece(p.tp, p.dp), self.across.at[0], p.across())
        for k in range(1, p.chips):
            self.go(self.shard, self.piece(p.tp, p.dp), self.rows.at[0, k - 1], p.row(k))
        self.go(self.shard, self.piece(p.tp, p.dp), self.from_mate.at[0, 0], p.mate())

    def relay_across(self):
        p = self.p
        got = self.piece(1 - p.tp, p.dp)
        arrived(got, self.across.at[0], p)
        for k in range(1, p.chips):
            self.go(got, got, self.rows.at[1, k - 1], p.row(k))
        self.go(got, got, self.from_mate.at[1, 0], p.mate())

    def relay_rows(self, part):
        p = self.p
        tp = p.tp if part == 0 else 1 - p.tp
        for k in range(1, p.chips):
            got = self.piece(tp, p.chip_before(k) * 2 + p.core)
            arrived(got, self.rows.at[part, k - 1], p)
            self.go(got, got, self.from_mate.at[part, k], p.mate())

    def finish(self):
        p = self.p
        for part in range(2):
            tp = p.tp if part == 0 else 1 - p.tp
            for k in range(p.chips):
                dp = p.chip_before(k) * 2 + 1 - p.core
                arrived(self.piece(tp, dp), self.from_mate.at[part, k], p)

    def drain(self):
        for copy in self.copies:
            copy.wait_send()


def fill_masks(dm, maskp, maskx):
    block = block_index()
    keys = lax.broadcasted_iota(jnp.int32, maskp.shape, 0)
    cols = lax.broadcasted_iota(jnp.int32, maskp.shape, 1) % dm.PB
    maskp[...] = jnp.where(keys <= cols + block * dm.PB, 0.0, NEG)
    keys = lax.broadcasted_iota(jnp.int32, maskx.shape, 0)
    cols = lax.broadcasted_iota(jnp.int32, maskx.shape, 1) % dm.NCH
    seen = (keys // CL == cols // dm.CH) & (
        keys % CL <= cols % dm.CH + half_index() * dm.CH
    )
    maskx[...] = jnp.where(seen, 0.0, NEG)


def heads_columns(a, b):
    lo_a, lo_b = sublane_pick(a.shape, True), sublane_pick(b.shape, True)
    zero_a, zero_b = jnp.zeros_like(a), jnp.zeros_like(b)
    return jnp.concatenate(
        [
            jnp.where(lo_a, a, zero_a),
            jnp.where(lo_a, zero_a, a),
            jnp.where(lo_b, b, zero_b),
            jnp.where(lo_b, zero_b, b),
        ],
        axis=1,
    )


def heads_rows(a, b):
    lo_a, lo_b = lane_pick(a.shape, True), lane_pick(b.shape, True)
    zero_a, zero_b = jnp.zeros_like(a), jnp.zeros_like(b)
    return jnp.concatenate(
        [
            jnp.where(lo_a, a, zero_a),
            jnp.where(lo_a, zero_a, a),
            jnp.where(lo_b, b, zero_b),
            jnp.where(lo_b, zero_b, b),
        ],
        axis=0,
    )


def forward_kernel(
    dm,
    op,
    oc,
    cos,
    sin,
    wq,
    wm,
    nt_out,
    own_out,
    k_out,
    v_out,
    q_out,
    att_out,
    lse_out,
    w_out,
    ln_out,
    wm_out,
    maskp,
    maskx,
    sbuf,
    all_rows,
    own_rows,
    xp,
    xc,
    w,
    put_sem,
    x_send,
    x_plane,
    x_mate,
    c_send,
    c_mate,
    own_sem,
    *sems,
):
    G, R, PB, NCH, D = dm.G, dm.R, dm.PB, dm.NCH, dm.D
    HC = (w.shape[2] - 128) // 3
    TP = w.shape[0]
    p = Peers()
    block = block_index()
    gq = WeightGather(p, wq, w, *sems[:4])
    gm = WeightGather(p, wm, wm_out, *sems[4:])
    size = wq.shape[0]
    mine = pl.ds(pl.multiple_of(p.dp * size, 16), size)
    local = [
        pltpu.make_async_copy(wq, w.at[p.tp, mine, :], own_sem.at[0]),
        pltpu.make_async_copy(wm, wm_out.at[p.tp, mine, :], own_sem.at[1]),
        pltpu.make_async_copy(op, xp.at[block], own_sem.at[2]),
        pltpu.make_async_copy(oc, xc.at[p.core], own_sem.at[3]),
    ]
    for copy in local:
        copy.start()
    p.greet()
    gq.start()
    sent = []
    for k in range(1, p.ctxs):
        sent.append(send(op, xp.at[block], x_send.at[k - 1], x_plane.at[k - 1], p.plane(k)))
    sent.append(send(op, xp.at[block], x_send.at[p.ctxs - 1], x_mate.at[0], p.mate()))
    sent.append(send(oc, xc.at[p.core], c_send, c_mate, p.mate()))
    fill_masks(dm, maskp, maskx)
    gq.relay_across()
    gq.relay_rows(0)
    gq.relay_rows(1)
    gm.start()
    gq.finish()
    for copy in local:
        copy.wait()
    put = pltpu.make_async_copy(w, w_out, put_sem)
    put.start()
    ln = w[0, :, 3 * HC :].astype(F32).T[:8, :]
    ln_out[...] = ln
    gain, bias = ln[0:1, :], ln[1:2, :]

    def normed(x):
        hat, _ = norm_stats(x.astype(F32))
        return (hat * gain + bias).astype(BF16)

    def queries(x, row, table):
        rows = x.shape[0]
        n = normed(x)
        own_rows[pl.ds(row, rows), :] = n
        c = cos[pl.ds(table, rows), :]
        sn = sin[pl.ds(table, rows), :]
        for t in range(TP):
            qq = dot(n, w[t, :, :HC])
            for j in range(HC // 128):
                tile = rotate(qq[:, j * 128 : (j + 1) * 128], c, sn).astype(BF16)
                q_out[pl.ds(row, rows), t * HC + j * 128 : t * HC + (j + 1) * 128] = (
                    tile.astype(F32) * 0.125
                ).astype(BF16)

    def own_prompt(g, carry):
        queries(op[g], pl.multiple_of(g * PB, PB), pl.multiple_of(block * PB, PB))
        return carry

    lax.fori_loop(0, G, own_prompt, 0)

    def own_cont(i, carry):
        g, c = i // dm.NC, i % dm.NC
        queries(
            oc[g, c],
            pl.multiple_of(dm.NP + i * dm.CH, dm.CH),
            pl.multiple_of(dm.P + p.core * dm.CH, dm.CH),
        )
        return carry

    lax.fori_loop(0, G * dm.NC, own_cont, 0)
    own_out[...] = transpose(own_rows[...])

    def keys_values(g, x, row, table, place):
        rows = x.shape[0]
        n = normed(x)
        all_rows[pl.ds(place, rows), :] = n
        c = cos[pl.ds(table, rows), :]
        sn = sin[pl.ds(table, rows), :]
        for t in range(TP):
            kk = dot(n, w[t, :, HC : 2 * HC])
            for j in range(HC // 128):
                tile = rotate(kk[:, j * 128 : (j + 1) * 128], c, sn)
                k_out[g, pl.ds(row, rows), t * HC + j * 128 : t * HC + (j + 1) * 128] = tile.astype(BF16)
            v_out[g, pl.ds(row, rows), t * HC : (t + 1) * HC] = dot(n, w[t, :, 2 * HC : 3 * HC]).astype(BF16)

    def block_chunk(g, b):
        row = pl.multiple_of(b * PB, PB)
        keys_values(g, xp[b, g], row, row, pl.multiple_of((b * G + g) * PB, PB))

    arrived(xc.at[1 - p.core], c_mate, p)

    def cont_chunk(i, carry):
        g, c = i // dm.NC, i % dm.NC
        row = pl.multiple_of(dm.P + c * CL, CL)
        x = jnp.concatenate([xc[0, g, c], xc[1, g, c]], axis=0)
        keys_values(g, x, row, dm.P, pl.multiple_of(G * dm.P + i * CL, CL))
        return carry

    lax.fori_loop(0, G * dm.NC, cont_chunk, 0)

    def relay(k):
        b = p.ctx_before(k) * 2 + p.core
        arrived(xp.at[b], x_plane.at[k - 1], p)
        return send(xp.at[b], xp.at[b], x_send.at[p.ctxs + k - 1], x_mate.at[k], p.mate())

    for k in range(1, p.ctxs):
        sent.append(relay(k))
    for k in range(p.ctxs):
        arrived(xp.at[p.ctx_before(k) * 2 + 1 - p.core], x_mate.at[k], p)

    def prompt_chunk(i, carry):
        block_chunk(i // (2 * p.ctxs), i % (2 * p.ctxs))
        return carry

    lax.fori_loop(0, G * 2 * p.ctxs, prompt_chunk, 0)
    gm.relay_across()

    def turn(i, carry):
        rows = pl.ds(pl.multiple_of(i * 256, 256), 256)
        nt_out[:, rows] = transpose(all_rows[rows, :])
        return carry

    lax.fori_loop(0, G * R // 256, turn, 0)

    TILE = 256
    tiles = dm.P // TILE

    def attend(i, carry):
        g, pair = i // dm.PAIRS, i % dm.PAIRS
        lanes = pl.ds(pl.multiple_of(pair * 128, 128), 128)
        qp = q_out[pl.ds(pl.multiple_of(g * PB, PB), PB), lanes]
        qc = q_out[pl.ds(pl.multiple_of(dm.NP + g * NCH, NCH), NCH), lanes]
        qt = heads_columns(transpose(qp), transpose(qc))
        top = None
        for j in range(tiles):
            s = dot(k_out[g, j * TILE : (j + 1) * TILE, lanes], qt)
            sbuf[j * TILE : (j + 1) * TILE, : 2 * PB] = (
                s[:, : 2 * PB] + maskp[j * TILE : (j + 1) * TILE, :]
            )
            sbuf[j * TILE : (j + 1) * TILE, 2 * PB :] = s[:, 2 * PB :]
            here = jnp.max(sbuf[j * TILE : (j + 1) * TILE, :], axis=0, keepdims=True)
            top = here if top is None else jnp.maximum(top, here)
        sx = dot(k_out[g, dm.P :, lanes], qt[:, 2 * PB :]) + maskx[...]
        topx = jnp.max(sx, axis=0, keepdims=True)
        top = jnp.concatenate([top[:, : 2 * PB], jnp.maximum(top[:, 2 * PB :], topx)], axis=1)
        total, acc = None, None
        for j in range(tiles):
            e = jnp.exp(sbuf[j * TILE : (j + 1) * TILE, :] - top)
            here = jnp.sum(e, axis=0, keepdims=True)
            vt = transpose(v_out[g, j * TILE : (j + 1) * TILE, lanes])
            part = dot(vt, e.astype(BF16))
            total = here if total is None else total + here
            acc = part if acc is None else acc + part
        ex = jnp.exp(sx - top[:, 2 * PB :])
        partx = dot(transpose(v_out[g, dm.P :, lanes]), ex.astype(BF16))
        totalx = jnp.sum(ex, axis=0, keepdims=True)
        total = jnp.concatenate([total[:, : 2 * PB], total[:, 2 * PB :] + totalx], axis=1)
        acc_p = acc[:, : 2 * PB] / total[:, : 2 * PB]
        acc_c = (acc[:, 2 * PB :] + partx) / total[:, 2 * PB :]
        lse_out[i] = top + jnp.log(total)
        outp = jnp.where(sublane_pick((128, PB), True), acc_p[:, :PB], acc_p[:, PB:])
        outc = jnp.where(sublane_pick((128, NCH), True), acc_c[:, :NCH], acc_c[:, NCH:])
        att_out[pl.ds(pl.multiple_of(g * PB, PB), PB), lanes] = outp.T.astype(BF16)
        att_out[pl.ds(pl.multiple_of(dm.NP + g * NCH, NCH), NCH), lanes] = outc.T.astype(BF16)
        return carry

    lax.fori_loop(0, G * dm.PAIRS, attend, 0)
    gm.relay_rows(0)
    gm.relay_rows(1)
    gm.finish()
    gq.drain()
    gm.drain()
    for copy in sent:
        copy.wait_send()
    put.wait()


class Reduce:
    REFS = 13

    def __init__(self, p, cross_first, refs):
        self.p, self.n, self.cross_first = p, len(cross_first), cross_first
        self.mine, self.got, self.row, self.acr, self.zin = refs[:5]
        self.sc, self.rc, self.sy, self.ry, self.sx, self.rx, self.sz, self.rz = refs[5:13]
        mid = p.ctxs // 2
        self.centre = (p.ctx == mid - 1) | (p.ctx == mid)
        self.outer = (p.ctx > 0) & (p.ctx < p.ctxs - 1)
        step = jnp.where(p.ctx < mid, 1, -1)
        self.inner_at = p.ctx + step
        self.outer_at = jnp.clip(p.ctx - step, 0, p.ctxs - 1)

    @staticmethod
    def scratch(cross_first, chips, size, width):
        n = len(cross_first)
        dma = pltpu.SemaphoreType.DMA
        far = max(chips - 1, 1)
        rows = n + sum(1 for c in cross_first if not c)
        return [
            pltpu.VMEM((2, chips, 2, size, width), BF16),
            pltpu.VMEM((2 * n, chips, size, width), BF16),
            pltpu.VMEM((rows, far, size, width), BF16),
            pltpu.VMEM((n, chips, size, width), BF16),
            pltpu.VMEM((n, 2, size, width), BF16),
            dma((2 * n,)),
            dma((2 * n,)),
            dma((2 * n, far)),
            dma((2 * n, far)),
            dma((n,)),
            dma((n,)),
            dma((n, 2)),
            dma((n, 2)),
        ]

    def copy(self, src, dst, send_sem, recv_sem, device):
        return pltpu.make_async_remote_copy(
            src_ref=src,
            dst_ref=dst,
            send_sem=send_sem,
            recv_sem=recv_sem,
            device_id=device,
            device_id_type=MESH,
        )

    def crosses(self, i):
        return self.cross_first[i % self.n]

    def travels(self, i):
        return i >= self.n or not self.crosses(i)

    def by_core(self, i, slot):
        p = self.p
        return self.copy(
            self.mine.at[slot, :, 1 - p.core], self.got.at[i], self.sc.at[i], self.rc.at[i], p.mate()
        )

    def row_slot(self, i):
        return sum(1 for e in range(i) if self.travels(e))

    def by_row(self, i, k):
        p = self.p
        return self.copy(
            self.got.at[i, p.chip_after(k)],
            self.row.at[self.row_slot(i), k - 1],
            self.sy.at[i, k - 1],
            self.ry.at[i, k - 1],
            p.row(k),
        )

    def by_tp(self, j):
        p = self.p
        part = slice(None) if self.crosses(j) else p.chip
        return self.copy(
            self.got.at[j, part], self.acr.at[j, part], self.sx.at[j], self.rx.at[j], p.across()
        )

    def inward(self, j):
        slot = jnp.where(self.centre, 1, 0)
        return self.copy(
            self.got.at[self.n + j, self.p.chip],
            self.zin.at[j, slot],
            self.sz.at[j, 0],
            self.rz.at[j, slot],
            self.p.at(ctx=self.inner_at),
        )

    def outward(self, j):
        return self.copy(
            self.got.at[self.n + j, self.p.chip],
            self.zin.at[j, 1],
            self.sz.at[j, 1],
            self.rz.at[j, 1],
            self.p.at(ctx=self.outer_at),
        )

    def add(self, i, y, other):
        self.got[i, y] = (self.got[i, y].astype(F32) + other.astype(F32)).astype(BF16)

    def cores_send(self, i, slot):
        self.by_core(i, slot).start()

    def cores_sent(self, i, slot):
        self.by_core(i, slot).wait_send()

    def rows_send(self, i):
        for k in range(1, self.p.chips):
            self.by_row(i, k).start()

    def cores_sum(self, i, slot):
        p = self.p
        self.by_core(i, slot).wait_recv()
        for y in range(p.chips):
            self.add(i, y, self.mine[slot, y, p.core])
        if not self.crosses(i):
            self.rows_send(i)
        elif i < self.n:
            self.by_tp(i).start()

    def cross_sum(self, j):
        self.by_tp(j).wait_recv()
        for y in range(self.p.chips):
            self.add(self.n + j, y, self.acr[j, y])
        self.rows_send(self.n + j)

    def rows_sum(self, i):
        p = self.p
        for k in range(1, p.chips):
            self.by_row(i, k).wait_recv()
            self.add(i, p.chip, self.row[self.row_slot(i), k - 1])
        if i < self.n:
            self.by_tp(i).start()
            return
        j = i - self.n
        if not self.crosses(i):
            self.by_tp(j).wait_recv()
            self.add(i, p.chip, self.acr[j, p.chip])

        @pl.when(jnp.logical_not(self.outer))
        def _():
            self.inward(j).start()

    def ctx_in(self, j):
        @pl.when(self.outer)
        def _():
            pltpu.make_async_copy(self.zin.at[j, 0], self.zin.at[j, 0], self.rz.at[j, 0]).wait()
            self.add(self.n + j, self.p.chip, self.zin[j, 0])
            self.inward(j).start()

    def ctx_out(self, j):
        p = self.p
        pltpu.make_async_copy(self.zin.at[j, 1], self.zin.at[j, 1], self.rz.at[j, 1]).wait()
        self.inward(j).wait_send()

        @pl.when(self.centre)
        def _():
            self.add(self.n + j, p.chip, self.zin[j, 1])

        @pl.when(jnp.logical_not(self.centre))
        def _():
            self.got[self.n + j, p.chip] = self.zin[j, 1]

        @pl.when(self.outer)
        def _():
            self.outward(j).start()

    def result(self, j):
        return self.got[self.n + j, self.p.chip].astype(F32)

    def drain(self):
        p = self.p
        for i in range(2 * self.n):
            if self.travels(i):
                for k in range(1, p.chips):
                    self.by_row(i, k).wait_send()
        for j in range(self.n):
            self.by_tp(j).wait_send()

            @pl.when(self.outer)
            def _():
                self.outward(j).wait_send()


def small_sum(p, sm, near, rows, across, planes, ss, rc, ry, rx, rz):
    copies = []

    def go(src, dst, recv_sem, device):
        copies.append(send(src, dst, ss.at[len(copies)], recv_sem, device))

    go(sm, near, rc, p.mate())
    copies[-1].wait_recv()
    rows[p.chip] = sm[...] + near[...]
    for k in range(1, p.chips):
        go(rows.at[p.chip], rows.at[p.chip], ry.at[k - 1], p.row(k))
    for k in range(1, p.chips):
        arrived(rows.at[p.chip_before(k)], ry.at[k - 1], p)
    total = rows[0]
    for y in range(1, p.chips):
        total += rows[y]
    across[0] = total
    go(across.at[0], across.at[1], rx, p.across())
    copies[-1].wait_recv()
    planes[p.ctx] = across[0] + across[1]
    for k in range(1, p.ctxs):
        go(planes.at[p.ctx], planes.at[p.ctx], rz.at[k - 1], p.plane(k))
    for k in range(1, p.ctxs):
        arrived(planes.at[p.ctx_before(k)], rz.at[k - 1], p)
    total = planes[0]
    for z in range(1, p.ctxs):
        total += planes[z]
    for copy in copies:
        copy.wait_send()
    return total


def schedule(ra, rb, on, n_a, NB, PT, TP, G):
    def at_pair(pair_rel):
        return pair_rel + 1 if pair_rel < PT else NB + 1 + pair_rel - PT

    last = 2 * n_a - 1
    late = ("a", 0)
    plan = ra.cross_first
    for j in range(n_a):
        if not plan[j]:
            on(("m", last) if j < n_a - 1 else ("a", 1), partial(ra.rows_sum, j))
    for j in range(n_a):
        if plan[j]:
            on(("m", last), partial(ra.cross_sum, j))
    own_at = {0: 6, 1: 3, 2: 8}
    for j in range(n_a):
        on(("a", own_at.get(j, 8)), partial(ra.rows_sum, n_a + j))
        on(("a", min(own_at.get(j, 8) + 3, 11)), partial(ra.ctx_in, j))
    on(late, partial(rb.cores_sum, 0, 0))
    on(late, partial(rb.cores_sum, NB, 1))
    on(("a", 2), partial(rb.cross_sum, 0))
    on(("a", 5), partial(rb.rows_sum, NB))
    on(("a", 8), partial(rb.ctx_in, 0))
    for pr in range(TP * PT - 1):
        on(("a", G * pr + G), partial(rb.cores_sum, at_pair(pr), pr % 2))
        if pr >= PT:
            on(("a", G * pr + G), partial(rb.cross_sum, pr - PT + 1))
    for j in range(1, NB - 1):
        on(("p", j), partial(rb.rows_sum, NB + j))
    for j in range(n_a):
        on(("p", j), partial(ra.ctx_out, j))
    on(("t", 0), partial(rb.rows_sum, 2 * NB - 1))
    for j in range(1, NB):
        on(("t", 10 + j), partial(rb.ctx_in, j))


def backward_kernel(
    dm,
    T,
    FC,
    plan_a,
    plan_b,
    mix,
    att,
    own_p,
    own_c,
    cot_p,
    cot_c,
    ln,
    q,
    lse,
    cos,
    sin,
    wm,
    k_hbm,
    v_hbm,
    nt_hbm,
    own_nt_hbm,
    wq_hbm,
    home_arrays_p,
    home_arrays_c,
    early_p,
    early_c,
    home_cot_p,
    home_cot_c,
    out_p,
    out_c,
    gin_p,
    gin_c,
    gq_out,
    go_out,
    gu_out,
    gd_out,
    small_out,
    resid,
    blk,
    gh,
    wo,
    ring,
    gatt,
    nt,
    own_nt,
    maskp,
    maskx,
    kbuf,
    vbuf,
    dk,
    dv,
    dq,
    dxm,
    dxz,
    blk_away,
    blk_home,
    gin_home,
    put_sem,
    ring_sem,
    wo_sem,
    kv_sem,
    nt_sem,
    wq_sem,
    home_sem,
    b_send,
    b_recv,
    g_send,
    g_recv,
    m_send,
    m_recv,
    z_send,
    z_recv,
    c_send,
    c_recv,
    sm,
    sm_near,
    sm_rows,
    sm_across,
    sm_planes,
    sm_ss,
    sm_rc,
    sm_ry,
    sm_rx,
    sm_rz,
    *refs,
):
    G, R, PB, NCH, D, NX, NP, NT = dm.G, dm.R, dm.PB, dm.NCH, dm.D, dm.NX, dm.NP, dm.NT
    TP, HC = wo.shape[0], wo.shape[2]
    PT = dm.PAIRS // TP
    p = Peers()
    n_a, NB = len(plan_a), len(plan_b)
    ra = Reduce(p, plan_a, refs[: Reduce.REFS])
    rb = Reduce(p, plan_b, refs[Reduce.REFS :])
    block = block_index()
    TILE = 256
    tiles = dm.P // TILE
    chips = p.chips
    S = D // (2 * chips)

    def begin(copies):
        for copy in copies:
            copy.start()

    def ready(copies):
        for copy in copies:
            copy.wait()

    def load_tile(i, slot):
        t = jnp.where(i < n_a, 1 - p.tp, p.tp)
        first = pl.multiple_of(HC + lax.rem(i, n_a) * T, 128)
        return [
            pltpu.make_async_copy(
                wm.at[t, :, pl.ds(first, T)], ring.at[slot, :, pl.ds(0, T)], ring_sem.at[0, slot]
            ),
            pltpu.make_async_copy(
                wm.at[t, :, pl.ds(first + FC, T)], ring.at[slot, :, pl.ds(T, T)], ring_sem.at[1, slot]
            ),
        ]

    def load_kv(it, slot):
        pair_rel, g = it // G, it % G
        t = jnp.where(pair_rel < PT, 1 - p.tp, p.tp)
        lanes = pl.ds(pl.multiple_of((t * PT + pair_rel % PT) * 128, 128), 128)
        return [
            pltpu.make_async_copy(k_hbm.at[g, :, lanes], kbuf.at[slot], kv_sem.at[0, slot]),
            pltpu.make_async_copy(v_hbm.at[g, :, lanes], vbuf.at[slot], kv_sem.at[1, slot]),
        ]

    wo_load = pltpu.make_async_copy(wm.at[:, :, pl.ds(0, HC)], wo, wo_sem)
    wo_load.start()
    begin(load_tile(0, 0))
    begin(load_kv(0, 0))
    p.greet(trades=True)
    fill_masks(dm, maskp, maskx)
    gain_two, bias_two = ln[2:3, :], ln[3:4, :]

    hn, gd = slice(0, NT), slice(NT, 2 * NT)
    STEP = 128

    def by_rows(step):
        def prompt_part(i, carry):
            rows = pl.ds(pl.multiple_of(i * STEP, STEP), STEP)
            step(own_p[rows, :], cot_p[rows, :], i * STEP)
            return carry

        def cont_part(i, carry):
            rows = pl.ds(pl.multiple_of(i * STEP, STEP), STEP)
            step(own_c[rows, :], cot_c[rows, :], NP + i * STEP)
            return carry

        lax.fori_loop(0, NP // STEP, prompt_part, 0)
        lax.fori_loop(0, (NT - NP) // STEP, cont_part, 0)

    def shifted(first, row):
        return pl.ds(pl.multiple_of(first + row, STEP), STEP)

    wo_load.wait()

    def enter(x, cot, row):
        rows = shifted(0, row)
        r = x.astype(F32)
        for t in range(TP):
            r += dot_nt(att[rows, t * HC : (t + 1) * HC], wo[t])
        resid[rows, :] = r
        blk[rows, :] = r
        h, _ = norm_stats(r)
        n = (h * gain_two + bias_two).astype(BF16)
        dk[rows, :] = n
        nt[:, rows] = transpose(n)
        g = (mix[4] * cot.astype(F32)).astype(BF16)
        dk[shifted(NT, row), :] = g
        nt[:, shifted(NT, row)] = transpose(g)
        gh[rows, :] = jnp.zeros((STEP, D), F32)

    by_rows(enter)

    during = {}

    def on(stage, step):
        during.setdefault(stage, []).append(step)

    def run_when(index, name):
        for (kind, when), steps in during.items():
            if kind == name:

                @pl.when(index == when)
                def _():
                    for step in steps:
                        step()

    for i in range(1, 2 * n_a):
        on(("m", i), partial(ra.cores_sum, i - 1, (i - 1) % 2))
    schedule(ra, rb, on, n_a, NB, PT, TP, G)

    def feed(i, carry):
        slot = lax.rem(i, 2)

        @pl.when(i + 1 < 2 * n_a)
        def _():
            begin(load_tile(i + 1, 1 - slot))

        ready(load_tile(i, slot))
        up, dn = ring[slot, :, :T], ring[slot, :, T : 2 * T]
        c0 = 0.7978845608028654
        HALF = NT // 2
        for e in range(2):
            rows = slice(e * HALF, (e + 1) * HALF)
            u = dot(dk[rows, :], up)
            if e == 0:
                run_when(i, "m")
            u2 = u * u
            th = jnp.tanh(c0 * u * (1.0 + 0.044715 * u2))
            half = 0.5 * (1.0 + th)
            act = (u * half).astype(BF16)
            slope = half + 0.5 * u * (1.0 - th * th) * (c0 * (1.0 + 3 * 0.044715 * u2))
            dv[rows, :T] = act
            blk[rows, :] += dot_nt(act, dn)
            gu = (dot(dk[NT + e * HALF : NT + (e + 1) * HALF, :], dn) * slope).astype(BF16)
            dv[NT + e * HALF : NT + (e + 1) * HALF, :T] = gu
            gh[rows, :] += dot_nt(gu, up)

        @pl.when(i >= 2)
        def _():
            ra.cores_sent(i - 2, slot)

        for y in range(chips):
            mine = slice(y * 2 * S, (y + 1) * 2 * S)
            ra.mine[slot, y, :, :, :T] = dot(nt[mine, hn], dv[gd, :T]).astype(BF16).reshape(2, S, T)
            ra.mine[slot, y, :, :, T:] = dot(nt[mine, gd], dv[hn, :T]).astype(BF16).reshape(2, S, T)
        ra.cores_send(i, slot)
        return carry

    lax.fori_loop(0, 2 * n_a, feed, 0)
    blk_away[:NT, :] = blk[...].astype(BF16)
    away = ra.copy(blk_away.at[pl.ds(0, NT), :], blk_home, b_send, b_recv, p.partner())

    @pl.when(p.core != p.tp)
    def _():
        away.start()

    @pl.when(p.core == p.tp)
    def _():
        blk_home[...] = blk_away[:NT, :]

    sm[...] = jnp.zeros_like(sm)

    def leave(x, cot, row):
        rows = shifted(0, row)
        cot = cot.astype(F32)
        sm[2:3, :] += jnp.sum(cot * blk[rows, :], axis=0, keepdims=True)
        h, scale = norm_stats(resid[rows, :])
        g = gh[rows, :]
        sm[0:1, :] += jnp.sum(g * h, axis=0, keepdims=True)
        sm[1:2, :] += jnp.sum(g, axis=0, keepdims=True)
        gr = mix[4] * cot + norm_back(g, gain_two, h, scale)
        resid[rows, :] = gr
        gb = gr.astype(BF16)
        nt[:, shifted(NT, row)] = transpose(gb)
        for t in range(TP):
            gatt[rows, t * HC : (t + 1) * HC] = dot(gb, wo[t]).astype(BF16)

    by_rows(leave)
    for slot, i in enumerate((0, NB)):
        t = p.tp if slot else 1 - p.tp
        lanes = pl.ds(pl.multiple_of(t * HC, 128), HC)
        for y in range(chips):
            mine = slice(y * 2 * S, (y + 1) * 2 * S)
            rb.mine[slot, y] = dot(nt[mine, gd], att[:, lanes]).astype(BF16).reshape(2, S, HC)
        rb.cores_send(i, slot)
    nt_load = [
        pltpu.make_async_copy(nt_hbm, nt, nt_sem.at[0]),
        pltpu.make_async_copy(own_nt_hbm, own_nt, nt_sem.at[1]),
    ]
    begin(nt_load)
    wq_load = pltpu.make_async_copy(wq_hbm.at[:, :, pl.ds(0, 3 * HC)], ring.at[:, :, pl.ds(0, 3 * HC)], wq_sem)
    wq_load.start()
    ra.cores_sum(2 * n_a - 1, 1)
    during.setdefault(("a", 1), []).insert(0, partial(ready, nt_load))

    def wslab(pair_rel):
        return pair_rel + 1 if pair_rel < PT else NB + 1 + pair_rel - PT

    def attend(it, carry):
        pair_rel, g = it // G, it % G
        t = jnp.where(pair_rel < PT, 1 - p.tp, p.tp)
        pair = t * PT + pair_rel % PT
        slot = it % 2

        @pl.when(it + 1 < G * dm.PAIRS)
        def _():
            begin(load_kv(it + 1, 1 - slot))

        run_when(it, "a")
        lanes = pl.ds(pl.multiple_of(pair * 128, 128), 128)
        rp = pl.ds(pl.multiple_of(g * PB, PB), PB)
        rc = pl.ds(pl.multiple_of(dm.NP + g * NCH, NCH), NCH)
        qp, qc = q[rp, lanes], q[rc, lanes]
        gp, gc = gatt[rp, lanes], gatt[rc, lanes]
        ap, ac = att[rp, lanes].astype(F32), att[rc, lanes].astype(F32)
        qt = heads_columns(transpose(qp), transpose(qc))
        gpt, gct = gp.astype(F32).T, gc.astype(F32).T
        gt = heads_columns(gpt.astype(BF16), gct.astype(BF16))
        qs, gs = heads_rows(qp, qc), heads_rows(gp, gc)
        prodp, prodc = gpt * ap.T, gct * ac.T
        delta = jnp.concatenate(
            [
                jnp.sum(prodp[:HD], axis=0, keepdims=True),
                jnp.sum(prodp[HD:], axis=0, keepdims=True),
                jnp.sum(prodc[:HD], axis=0, keepdims=True),
                jnp.sum(prodc[HD:], axis=0, keepdims=True),
            ],
            axis=1,
        )
        stat = lse[g * dm.PAIRS + pair]
        ready(load_kv(it, slot))

        def grads(s, kt, vt, cols):
            pr = jnp.exp(s - stat[:, cols:])
            dp = dot(vt, gt[:, cols:])
            ds = (pr * (dp - delta[:, cols:])).astype(BF16)
            gv = dot(pr.astype(BF16), gs[cols:])
            gk = dot(ds, qs[cols:])
            gq = dot(transpose(kt), ds)
            return gk, gv, gq

        acc = None
        for j in range(tiles):
            rows = slice(j * TILE, (j + 1) * TILE)
            kt = kbuf[slot, rows, :]
            s = dot(kt, qt)
            s = jnp.concatenate([s[:, : 2 * PB] + maskp[rows, :], s[:, 2 * PB :]], axis=1)
            gk, gv, gq = grads(s, kt, vbuf[slot, rows, :], 0)
            gk = rotate_back(gk, cos[rows, :], sin[rows, :]).astype(BF16)
            gv = gv.astype(BF16)
            for b in range(TILE // PB):
                out = pl.ds(pl.multiple_of(((j * (TILE // PB) + b) * G + g) * PB, PB), PB)
                dk[out, lanes] = gk[b * PB : (b + 1) * PB]
                dv[out, lanes] = gv[b * PB : (b + 1) * PB]
            acc = gq if acc is None else acc + gq
        kt = kbuf[slot, dm.P :, :]
        s = dot(kt, qt[:, 2 * PB :]) + maskx[...]
        gk, gv, gq = grads(s, kt, vbuf[slot, dm.P :, :], 2 * PB)
        for c in range(dm.NC):
            rows = slice(dm.P, dm.P + CL)
            out = pl.ds(pl.multiple_of(G * dm.P + (g * dm.NC + c) * CL, CL), CL)
            part = rotate_back(gk[c * CL : (c + 1) * CL], cos[rows, :], sin[rows, :])
            dk[out, lanes] = part.astype(BF16)
            dv[out, lanes] = gv[c * CL : (c + 1) * CL].astype(BF16)
        accp = acc[:, : 2 * PB] * 0.125
        accc = (acc[:, 2 * PB :] + gq) * 0.125
        outp = jnp.where(sublane_pick((128, PB), True), accp[:, :PB], accp[:, PB:]).T
        outc = jnp.where(sublane_pick((128, NCH), True), accc[:, :NCH], accc[:, NCH:]).T
        tab = pl.ds(pl.multiple_of(block * PB, PB), PB)
        dq[rp, lanes] = rotate_back(outp, cos[tab, :], sin[tab, :]).astype(BF16)
        tab = pl.ds(pl.multiple_of(dm.P + p.core * dm.CH, dm.CH), dm.CH)
        for c in range(dm.NC):
            part = rotate_back(outc[c * dm.CH : (c + 1) * dm.CH], cos[tab, :], sin[tab, :])
            rows = pl.ds(pl.multiple_of(dm.NP + g * NCH + c * dm.CH, dm.CH), dm.CH)
            dq[rows, lanes] = part.astype(BF16)

        @pl.when(g == G - 1)
        def _():
            put = pair_rel % 2
            index = jnp.where(pair_rel < PT, pair_rel + 1, NB + 1 + pair_rel - PT)
            last = pair_rel - 2
            before = jnp.where(last < PT, last + 1, NB + 1 + last - PT)
            before = jnp.where(last < 0, jnp.where(put == 0, 0, NB), before)
            rb.cores_sent(before, put)
            both = jnp.concatenate([dk[:, lanes], dv[:, lanes]], axis=1)
            for y in range(chips):
                mine = slice(y * 2 * S, (y + 1) * 2 * S)
                gkv = dot(nt[mine, :], both).astype(BF16)
                rb.mine[put, y, :, :, 128:] = gkv.reshape(2, S, 256)
                gqw = dot(own_nt[mine, :], dq[:, lanes]).astype(BF16)
                rb.mine[put, y, :, :, :128] = gqw.reshape(2, S, 128)
            rb.cores_send(index, put)

        return carry

    lax.fori_loop(0, G * dm.PAIRS, attend, 0)
    last_pair = TP * PT - 1
    wq_load.wait()
    w = ring

    def project(rows):
        total = None
        for t in range(TP):
            part = dot_nt(dk[rows, t * HC : (t + 1) * HC], w[t, :, HC : 2 * HC])
            total = part if total is None else total + part
            total += dot_nt(dv[rows, t * HC : (t + 1) * HC], w[t, :, 2 * HC : 3 * HC])
        return total

    def block_rows(b):
        return pl.ds(pl.multiple_of(b * G * PB, G * PB), G * PB)

    def to_mate(k):
        b = p.ctx_after(k) * 2 + 1 - p.core
        return ra.copy(dk.at[block_rows(b), :], dxm.at[k], m_send.at[k], m_recv.at[k], p.mate())

    def to_plane(k):
        b = p.ctx_after(k) * 2 + p.core
        return ra.copy(
            dk.at[block_rows(b), :],
            dxz.at[k - 1],
            z_send.at[k - 1],
            z_recv.at[k - 1],
            p.at(ctx=p.ctx_after(k)),
        )

    def planes(i, carry):
        k = lax.rem(i + 1, p.ctxs)
        rows = block_rows(p.ctx_after(k) * 2 + 1 - p.core)
        dk[rows, :] = project(rows).astype(BF16)
        to_mate(k).start()
        rows = block_rows(p.ctx_after(k) * 2 + p.core)
        part = project(rows)
        to_mate(k).wait_recv()
        dk[rows, :] = (part + dxm[k].astype(F32)).astype(BF16)

        @pl.when(k > 0)
        def _():
            to_plane(k).start()

        run_when(i, "p")
        return carry

    lax.fori_loop(0, p.ctxs, planes, 0)

    NCONT = NT - NP

    @pl.when(p.core != p.tp)
    def _():
        away.wait_send()

    def cont_rows(i, carry):
        rows = pl.ds(pl.multiple_of(G * dm.P + i * CL, CL), CL)
        total = project(rows).astype(BF16)
        out = pl.ds(pl.multiple_of(i * dm.CH, dm.CH), dm.CH)
        blk_away[out, :] = total[: dm.CH]
        blk_away[pl.ds(pl.multiple_of(NCONT + i * dm.CH, dm.CH), dm.CH), :] = total[dm.CH :]
        return carry

    lax.fori_loop(0, G * dm.NC, cont_rows, 0)
    halves = lambda core: pl.ds(pl.multiple_of(core * NCONT, 16), NCONT)
    dxcm = nt.at[pl.ds(0, NCONT), pl.ds(0, D)]
    cont_copy = ra.copy(blk_away.at[halves(1 - p.core), :], dxcm, c_send, c_recv, p.mate())
    cont_copy.start()
    rb.cores_sum(wslab(last_pair), last_pair % 2)
    rb.cross_sum(NB - 1)
    homes = []
    for i, (a, c) in enumerate(
        [(home_arrays_p, home_arrays_c)]
        + [(early_p.at[e], early_c.at[e]) for e in range(3)]
        + [(home_cot_p, home_cot_c)]
    ):
        homes.append(pltpu.make_async_copy(a, dv.at[pl.ds(i * NT, NP), :], home_sem.at[0, i]))
        homes.append(pltpu.make_async_copy(c, dv.at[pl.ds(i * NT + NP, NT - NP), :], home_sem.at[1, i]))
    begin(homes)

    def project_q(i, carry):
        rows = shifted(0, i * STEP)
        total = dot_nt(dq[rows, :HC], w[0, :, :HC])
        for t in range(1, TP):
            total += dot_nt(dq[rows, t * HC : (t + 1) * HC], w[t, :, :HC])
        blk[rows, :] = total
        return carry

    lax.fori_loop(0, NT // STEP, project_q, 0)
    gain_one = ln[0:1, :]
    cont_copy.wait_recv()
    def enter_back(gn, x, row):
        rows = shifted(0, row)
        gn += blk[rows, :]
        hat, scale = norm_stats(x.astype(F32))
        gatt[rows, :] = (resid[rows, :] + norm_back(gn, gain_one, hat, scale)).astype(BF16)
        sm[7:8, :] += jnp.sum(gn * hat, axis=0, keepdims=True)
        sm[8:9, :] += jnp.sum(gn, axis=0, keepdims=True)

    def cont_back(i, carry):
        rows = shifted(0, i * STEP)
        mine = blk_away[shifted(p.core * NCONT, i * STEP), :].astype(F32)
        enter_back(mine + dxcm[rows, :].astype(F32), own_c[rows, :], NP + i * STEP)
        return carry

    lax.fori_loop(0, NCONT // STEP, cont_back, 0)

    def gin_away(part):
        rows = pl.ds(0, NP) if part == 0 else pl.ds(NP, NT - NP)
        return ra.copy(gatt.at[rows, :], gin_home.at[rows, :], g_send.at[part], g_recv.at[part], p.partner())

    def give(part):
        rows = slice(0, NP) if part == 0 else slice(NP, NT)

        @pl.when(p.core != p.tp)
        def _():
            gin_away(part).start()

        @pl.when(p.core == p.tp)
        def _():
            gin_home[rows, :] = gatt[rows, :]

    give(1)

    ready(homes)

    @pl.when(p.core != p.tp)
    def _():
        away.wait_recv()

    def blend(i, carry):
        rows = shifted(0, i * STEP)
        res = mix[4] * blk_home[rows, :].astype(F32)
        c = dv[shifted(4 * NT, i * STEP), :].astype(F32)
        for e in range(4):
            a = dv[shifted(e * NT, i * STEP), :].astype(F32)
            res += mix[e] * a
            sm[3 + e : 4 + e, :] += jnp.sum(c * a, axis=0, keepdims=True)
        blk_home[rows, :] = res.astype(BF16)
        return carry

    lax.fori_loop(0, NT // STEP, blend, 0)
    puts = [
        pltpu.make_async_copy(blk_home.at[pl.ds(0, NP), :], out_p, put_sem.at[0]),
        pltpu.make_async_copy(blk_home.at[pl.ds(NP, NT - NP), :], out_c, put_sem.at[1]),
    ]
    begin(puts)
    for kind, when in sorted(key for key in during if key[0] == "t"):
        if when < 10:
            for step in during[kind, when]:
                step()
    for k in range(1, p.ctxs):
        to_plane(k).wait_recv()

    def prompt_back(i, carry):
        rows = shifted(0, i * STEP)
        gn = dk[shifted(block * NP, i * STEP), :].astype(F32)
        for k in range(1, p.ctxs):
            gn += dxz[k - 1, rows, :].astype(F32)
        enter_back(gn, own_p[rows, :], i * STEP)
        return carry

    lax.fori_loop(0, NP // STEP, prompt_back, 0)
    give(0)
    for kind, when in sorted(key for key in during if key[0] == "t"):
        if when >= 10:
            for step in during[kind, when]:
                step()
    small_out[...] = small_sum(
        p, sm, sm_near, sm_rows, sm_across, sm_planes, sm_ss, sm_rc, sm_ry, sm_rx, sm_rz
    )
    gu_puts = []
    for j in range(n_a):
        total = ra.result(j)
        gd_out[j * T : (j + 1) * T, :] = total[:, T:].T
        if len(gu_puts) > 0:
            gu_puts[-1].wait()
        gh[:S, :T] = total[:, :T]
        gu_puts.append(
            pltpu.make_async_copy(
                gh.at[pl.ds(0, S), pl.ds(0, T)], gu_out.at[:, pl.ds(j * T, T)], put_sem.at[2]
            )
        )
        gu_puts[-1].start()
    gu_puts[-1].wait()
    for j in range(NB):
        rb.ctx_out(j)
        total = rb.result(j)
        if j == 0:
            go_out[...] = total.T
        else:
            for c in range(3):
                first = c * HC + (j - 1) * 128
                gq_out[:, first : first + 128] = total[:, c * 128 : (c + 1) * 128]

    @pl.when(p.core != p.tp)
    def _():
        for part in range(2):
            gin_away(part).wait_recv()
            gin_away(part).wait_send()

    more = [
        pltpu.make_async_copy(gin_home.at[pl.ds(0, NP), :], gin_p, put_sem.at[2]),
        pltpu.make_async_copy(gin_home.at[pl.ds(NP, NT - NP), :], gin_c, put_sem.at[3]),
    ]
    begin(more)
    ready(puts + more)
    for i in range(2 * n_a - 2, 2 * n_a):
        ra.cores_sent(i, i % 2)
    for pr in (last_pair - 1, last_pair):
        rb.cores_sent(wslab(pr), pr % 2)
    for k in range(p.ctxs):
        to_mate(k).wait_send()
    for k in range(1, p.ctxs):
        to_plane(k).wait_send()
    cont_copy.wait_send()
    ra.drain()
    rb.drain()


def params(**more):
    return pltpu.CompilerParams(vmem_limit_bytes=VMEM_LIMIT, **more)


def per_device(
    prompt_in,
    cont_in,
    prompt_embed,
    cont_embed,
    prompt_earlier,
    cont_earlier,
    ln1_gain,
    ln1_bias,
    ln2_gain,
    ln2_bias,
    w_qkv,
    w_out,
    w_up,
    w_down,
    mix_weights,
    prompt_cot,
    cont_cot,
):
    G, PB, D = prompt_in.shape
    NC, CH = cont_in.shape[1], cont_in.shape[2]
    TP = lax.axis_size("tp")
    PROMPT = PB * TP * lax.axis_size("ctx")
    HC, FC = w_qkv.shape[2], w_up.shape[1]
    S = w_qkv.shape[0]
    dm = Dims(G, PROMPT, PB, NC, CH, D, HC * TP // HD)
    R, NT, NP = dm.R, dm.NT, dm.NP

    sds = jax.ShapeDtypeStruct
    chips, ctxs = lax.axis_size("dp") // 2, lax.axis_size("ctx")
    swap = [(4 * y + 2 * c + t, 4 * y + 2 * t + c) for y in range(chips) for c in (0, 1) for t in (0, 1)]

    def trade(x):
        return lax.ppermute(x, ("dp", "tp"), swap)

    own_p, own_c = trade(prompt_in), trade(cont_in)
    cot_p, cot_c = trade(prompt_cot), trade(cont_cot)
    norms = jnp.stack([ln1_gain, ln1_bias, ln2_gain, ln2_bias], axis=1)
    norms = jnp.pad(norms, ((0, 0), (0, 124)))
    wq_shard = jnp.concatenate([w_qkv.reshape(S, 3 * HC), norms], axis=1)
    wm_shard = jnp.concatenate([w_out.T, w_up, w_down.T], axis=1)

    positions = jnp.arange(PROMPT + CL, dtype=jnp.int32).astype(F32)
    lane = jnp.arange(128, dtype=jnp.int32)
    freq = 10000.0 ** (-((lane % 32).astype(F32) / 32))
    angles = positions[:, None] * freq[None, :]
    cos, sin = jnp.cos(angles), jnp.sin(angles)
    second = (lane % 64) >= 32
    sin = jnp.where(second[None, :], sin, -sin)

    any_ = pl.BlockSpec(memory_space=pl.ANY)
    vmem = pl.BlockSpec(memory_space=pltpu.VMEM)
    dma = pltpu.SemaphoreType.DMA
    nt, own_nt, k, v, q, att, lse, wq, ln, wm = pl.pallas_call(
        partial(forward_kernel, dm),
        out_shape=(
            sds((D, G * R), BF16),
            sds((D, NT), BF16),
            sds((G, R, D), BF16),
            sds((G, R, D), BF16),
            sds((NT, D), BF16),
            sds((NT, D), BF16),
            sds((G * dm.PAIRS, 1, dm.COLS), F32),
            sds((TP, D, 3 * HC + 128), BF16),
            sds((8, D), F32),
            sds((TP, D, HC + 2 * FC), BF16),
        ),
        in_specs=[vmem] * 5 + [any_],
        out_specs=(vmem,) * 7 + (any_, vmem, any_),
        scratch_shapes=[
            pltpu.VMEM((PROMPT, 2 * PB), F32),
            pltpu.VMEM((dm.NX, 2 * dm.NCH), F32),
            pltpu.VMEM((PROMPT, dm.COLS), F32),
            pltpu.VMEM((G * R, D), BF16),
            pltpu.VMEM((NT, D), BF16),
            pltpu.VMEM((2 * ctxs, G, PB, D), BF16),
            pltpu.VMEM((2, G, NC, CH, D), BF16),
            pltpu.VMEM((TP, D, 3 * HC + 128), BF16),
            dma,
            dma((2 * ctxs - 1,)),
            dma((ctxs - 1,)),
            dma((ctxs,)),
            dma,
            dma,
            dma((4,)),
        ]
        + WeightGather.semaphores(chips)
        + WeightGather.semaphores(chips),
        compiler_params=params(collective_id=0, has_side_effects=True),
        name="forward",
    )(own_p, own_c, cos, sin, wq_shard, wm_shard)
    T = 512 if FC % 512 == 0 else 256
    plan_a = [j == 0 for j in range(FC // T)]
    plan_b = [True] * (1 + dm.PAIRS // TP)
    far = max(chips - 1, 1)
    rows = lambda x: x.reshape(-1, D)
    out_p, out_c, gin_p, gin_c, gq, go, gu, gd, small = pl.pallas_call(
        partial(backward_kernel, dm, T, FC, plan_a, plan_b),
        out_shape=(
            sds((NP, D), BF16),
            sds((NT - NP, D), BF16),
            sds((NP, D), BF16),
            sds((NT - NP, D), BF16),
            sds((S, 3 * HC), F32),
            sds((HC, S), F32),
            sds((S, FC), F32),
            sds((FC, S), F32),
            sds((16, D), F32),
        ),
        in_specs=[pl.BlockSpec(memory_space=pltpu.SMEM)] + [vmem] * 10 + [any_] * 12,
        out_specs=(any_,) * 4 + (vmem, vmem, any_, vmem, vmem),
        scratch_shapes=[
            pltpu.VMEM((NT, D), F32),
            pltpu.VMEM((NT, D), F32),
            pltpu.VMEM((NT, D), F32),
            pltpu.VMEM((TP, D, HC), BF16),
            pltpu.VMEM((2, D, max(2 * T, 3 * HC)), BF16),
            pltpu.VMEM((NT, D), BF16),
            pltpu.VMEM((D, G * R), BF16),
            pltpu.VMEM((D, NT), BF16),
            pltpu.VMEM((PROMPT, 2 * PB), F32),
            pltpu.VMEM((dm.NX, 2 * dm.NCH), F32),
            pltpu.VMEM((2, R, 128), BF16),
            pltpu.VMEM((2, R, 128), BF16),
            pltpu.VMEM((G * R, D), BF16),
            pltpu.VMEM((G * R, D), BF16),
            pltpu.VMEM((NT, D), BF16),
            pltpu.VMEM((ctxs, G * PB, D), BF16),
            pltpu.VMEM((ctxs - 1, G * PB, D), BF16),
            pltpu.VMEM((max(NT, 2 * (NT - NP)), D), BF16),
            pltpu.VMEM((NT, D), BF16),
            pltpu.VMEM((NT, D), BF16),
            dma((4,)),
            dma((2, 2)),
            dma,
            dma((2, 2)),
            dma((2,)),
            dma,
            dma((2, 5)),
            dma,
            dma,
            dma((2,)),
            dma((2,)),
            dma((ctxs,)),
            dma((ctxs,)),
            dma((ctxs - 1,)),
            dma((ctxs - 1,)),
            dma,
            dma,
            pltpu.VMEM((16, D), F32),
            pltpu.VMEM((16, D), F32),
            pltpu.VMEM((chips, 16, D), F32),
            pltpu.VMEM((2, 16, D), F32),
            pltpu.VMEM((ctxs, 16, D), F32),
            dma((1 + chips + ctxs,)),
            dma,
            dma((far,)),
            dma,
            dma((ctxs - 1,)),
        ]
        + Reduce.scratch(plan_a, chips, S, 2 * T)
        + Reduce.scratch(plan_b, chips, S, HC),
        compiler_params=params(collective_id=1, has_side_effects=True),
        name="backward",
    )(
        mix_weights,
        att,
        rows(own_p),
        rows(own_c),
        rows(cot_p),
        rows(cot_c),
        ln,
        q,
        lse,
        cos,
        sin,
        wm,
        k,
        v,
        nt,
        own_nt,
        wq,
        rows(prompt_embed),
        rows(cont_embed),
        prompt_earlier.reshape(3, NP, D),
        cont_earlier.reshape(3, NT - NP, D),
        rows(prompt_cot),
        rows(cont_cot),
    )
    start = lax.axis_index("dp") * S
    mine = lax.dynamic_slice_in_dim(small, start, S, axis=1)
    return (
        out_p.reshape(prompt_in.shape),
        out_c.reshape(cont_in.shape),
        gin_p.reshape(prompt_in.shape),
        gin_c.reshape(cont_in.shape),
        mine[7],
        mine[8],
        mine[0],
        mine[1],
        gq.reshape(S, 3, HC),
        go,
        gu,
        gd,
        jnp.sum(jnp.concatenate([small[3:7], small[2:3]]), axis=1),
    )


def solution(mesh):
    tokens = P("dp", ("ctx", "tp"), None)
    conts = P("dp", "ctx", "tp", None)
    weights = (P("dp", None, "tp"), P("tp", "dp"), P("dp", "tp"), P("tp", "dp"))
    in_specs = (
        tokens,
        conts,
        tokens,
        conts,
        P(None, "dp", ("ctx", "tp"), None),
        P(None, "dp", "ctx", "tp", None),
        P("dp"),
        P("dp"),
        P("dp"),
        P("dp"),
        *weights,
        P(),
        tokens,
        conts,
    )
    out_specs = (
        tokens,
        conts,
        tokens,
        conts,
        P("dp"),
        P("dp"),
        P("dp"),
        P("dp"),
        *weights,
        P(),
    )
    return jax.shard_map(
        per_device, mesh=mesh, in_specs=in_specs, out_specs=out_specs, check_vma=False
    )
```

```python
from functools import partial

import jax
import jax.numpy as jnp
import numpy as np
from jax import lax
from jax.experimental import pallas as pl
from jax.experimental.pallas import tpu as pltpu
from jax.sharding import PartitionSpec as P

HD = 64
CL = 128
EPS = 1e-05
NEG = -1e30
F32 = jnp.float32
BF16 = jnp.bfloat16
VMEM_LIMIT = 67043328


def dot(a, b):
    return lax.dot_general(a, b, (((1,), (0,)), ((), ())), preferred_element_type=F32)


def dot_nt(a, b):
    return lax.dot_general(a, b, (((1,), (1,)), ((), ())), preferred_element_type=F32)


def norm_stats(x):
    mean = jnp.mean(x, axis=-1, keepdims=True)
    centered = x - mean
    var = jnp.mean(centered * centered, axis=-1, keepdims=True)
    scale = lax.rsqrt(var + EPS)
    return centered * scale, scale


def norm_back(grad, gain, hat, scale):
    gh = grad * gain
    return scale * (
        gh
        - jnp.mean(gh, axis=-1, keepdims=True)
        - hat * jnp.mean(gh * hat, axis=-1, keepdims=True)
    )


def swap_halves(x):
    second = lax.broadcasted_iota(jnp.int32, x.shape, 1) % HD >= HD // 2
    return jnp.where(second, pltpu.roll(x, 32, 1), pltpu.roll(x, 96, 1))


def rotate(x, cos, sin):
    return x * cos + swap_halves(x) * sin


def rotate_back(x, cos, sin):
    return x * cos - swap_halves(x) * sin


def lane_pick(shape, low):
    lanes = lax.broadcasted_iota(jnp.int32, shape, 1)
    return lanes < HD if low else lanes >= HD


def sublane_pick(shape, low):
    rows = lax.broadcasted_iota(jnp.int32, shape, 0)
    return rows < HD if low else rows >= HD


def transpose(x):
    return x.astype(F32).T.astype(x.dtype)


class Dims:
    def __init__(self, groups, prompt, pb, nc, ch, d, heads):
        self.G, self.P, self.PB, self.NC, self.CH, self.D = groups, prompt, pb, nc, ch, d
        self.NCH = nc * ch
        self.R = prompt + nc * CL
        self.NX = nc * CL
        self.NR = pb + self.NCH
        self.NP = groups * pb
        self.NT = groups * self.NR
        self.PAIRS = heads // 2
        self.COLS = 2 * self.NR


MESH = pl.DeviceIdType.MESH


def half_index():
    return lax.axis_index("dp") % 2


def block_index():
    return lax.axis_index("ctx") * 2 + half_index()


class Peers:
    def __init__(self):
        self.ctxs = lax.axis_size("ctx")
        self.chips = lax.axis_size("dp") // 2
        self.tps = lax.axis_size("tp")
        self.dp = lax.axis_index("dp")
        self.ctx = lax.axis_index("ctx")
        self.tp = lax.axis_index("tp")
        self.core = self.dp % 2
        self.chip = self.dp // 2

    def at(self, dp=None, ctx=None, tp=None):
        return {
            "dp": self.dp if dp is None else dp,
            "ctx": self.ctx if ctx is None else ctx,
            "tp": self.tp if tp is None else tp,
        }

    def across(self):
        return self.at(tp=1 - self.tp)

    def mate(self):
        return self.at(dp=self.chip * 2 + 1 - self.core)

    def chip_after(self, k):
        return lax.rem(self.chip + k, self.chips)

    def chip_before(self, k):
        return lax.rem(self.chip + self.chips - k, self.chips)

    def row(self, k):
        return self.at(dp=self.chip_after(k) * 2 + self.core)

    def ctx_after(self, k):
        return lax.rem(self.ctx + k, self.ctxs)

    def ctx_before(self, k):
        return lax.rem(self.ctx + self.ctxs - k, self.ctxs)

    def plane(self, k):
        return self.at(ctx=self.ctx_after(k))

    def partner(self):
        return self.at(dp=self.chip * 2 + self.tp, tp=self.core)

    def greet(self, trades=False):
        barrier = pltpu.get_barrier_semaphore()
        peers = [self.across(), self.mate()]
        peers += [self.row(k) for k in range(1, self.chips)]
        peers += [self.plane(k) for k in range(1, self.ctxs)]
        for peer in peers:
            pl.semaphore_signal(barrier, inc=1, device_id=peer, device_id_type=MESH)
        count = len(peers)
        if trades:
            away = self.core != self.tp

            @pl.when(away)
            def _():
                pl.semaphore_signal(
                    barrier, inc=1, device_id=self.partner(), device_id_type=MESH
                )

            count += jnp.where(away, 1, 0)
        pl.semaphore_wait(barrier, count)


def send(src, dst, send_sem, recv_sem, device):
    copy = pltpu.make_async_remote_copy(
        src_ref=src,
        dst_ref=dst,
        send_sem=send_sem,
        recv_sem=recv_sem,
        device_id=device,
        device_id_type=MESH,
    )
    copy.start()
    return copy


def arrived(ref, sem, peers):
    pltpu.make_async_remote_copy(
        src_ref=ref,
        dst_ref=ref,
        send_sem=sem,
        recv_sem=sem,
        device_id=peers.mate(),
        device_id_type=MESH,
    ).wait_recv()


class WeightGather:
    def __init__(self, peers, shard, full, sends, across, rows, mate):
        self.p, self.shard, self.full = peers, shard, full
        self.sends, self.across, self.rows, self.from_mate = sends, across, rows, mate
        self.copies = []
        self.count = 0
        self.size = shard.shape[0]

    @staticmethod
    def semaphores(chips):
        return [
            pltpu.SemaphoreType.DMA((1 + 2 * (chips - 1) + 2 * chips,)),
            pltpu.SemaphoreType.DMA((1,)),
            pltpu.SemaphoreType.DMA((2, max(chips - 1, 1))),
            pltpu.SemaphoreType.DMA((2, chips)),
        ]

    def piece(self, tp, dp):
        return self.full.at[tp, pl.ds(pl.multiple_of(dp * self.size, 16), self.size), :]

    def go(self, src, dst, recv_sem, device):
        self.copies.append(send(src, dst, self.sends.at[self.count], recv_sem, device))
        self.count += 1

    def start(self):
        p = self.p
        self.go(self.shard, self.piece(p.tp, p.dp), self.across.at[0], p.across())
        for k in range(1, p.chips):
            self.go(self.shard, self.piece(p.tp, p.dp), self.rows.at[0, k - 1], p.row(k))
        self.go(self.shard, self.piece(p.tp, p.dp), self.from_mate.at[0, 0], p.mate())

    def relay_across(self):
        p = self.p
        got = self.piece(1 - p.tp, p.dp)
        arrived(got, self.across.at[0], p)
        for k in range(1, p.chips):
            self.go(got, got, self.rows.at[1, k - 1], p.row(k))
        self.go(got, got, self.from_mate.at[1, 0], p.mate())

    def relay_rows(self, part):
        p = self.p
        tp = p.tp if part == 0 else 1 - p.tp
        for k in range(1, p.chips):
            got = self.piece(tp, p.chip_before(k) * 2 + p.core)
            arrived(got, self.rows.at[part, k - 1], p)
            self.go(got, got, self.from_mate.at[part, k], p.mate())

    def finish(self):
        p = self.p
        for part in range(2):
            tp = p.tp if part == 0 else 1 - p.tp
            for k in range(p.chips):
                dp = p.chip_before(k) * 2 + 1 - p.core
                arrived(self.piece(tp, dp), self.from_mate.at[part, k], p)

    def drain(self):
        for copy in self.copies:
            copy.wait_send()


def twice(x):
    return jnp.concatenate([x, x], axis=1)


def fill_masks(dm, maskp, maskx):
    block = block_index()
    keys = lax.broadcasted_iota(jnp.int32, maskp.shape, 0)
    cols = lax.broadcasted_iota(jnp.int32, maskp.shape, 1) % dm.PB
    maskp[...] = jnp.where(keys <= cols + block * dm.PB, 0.0, NEG)
    keys = lax.broadcasted_iota(jnp.int32, maskx.shape, 0)
    cols = lax.broadcasted_iota(jnp.int32, maskx.shape, 1) % dm.NCH
    seen = (keys // CL == cols // dm.CH) & (
        keys % CL <= cols % dm.CH + half_index() * dm.CH
    )
    maskx[...] = jnp.where(seen, 0.0, NEG)


def heads_columns(a, b):
    lo_a, lo_b = sublane_pick(a.shape, True), sublane_pick(b.shape, True)
    zero_a, zero_b = jnp.zeros_like(a), jnp.zeros_like(b)
    return jnp.concatenate(
        [
            jnp.where(lo_a, a, zero_a),
            jnp.where(lo_a, zero_a, a),
            jnp.where(lo_b, b, zero_b),
            jnp.where(lo_b, zero_b, b),
        ],
        axis=1,
    )


def heads_rows(a, b):
    lo_a, lo_b = lane_pick(a.shape, True), lane_pick(b.shape, True)
    zero_a, zero_b = jnp.zeros_like(a), jnp.zeros_like(b)
    return jnp.concatenate(
        [
            jnp.where(lo_a, a, zero_a),
            jnp.where(lo_a, zero_a, a),
            jnp.where(lo_b, b, zero_b),
            jnp.where(lo_b, zero_b, b),
        ],
        axis=0,
    )


def forward_kernel(
    dm,
    op,
    oc,
    cos,
    sin,
    wq,
    wm,
    nt_out,
    own_out,
    k_out,
    v_out,
    q_out,
    att_out,
    lse_out,
    w_out,
    ln_out,
    wm_out,
    maskp,
    maskx,
    sbuf,
    all_rows,
    own_rows,
    xp,
    xc,
    w,
    put_sem,
    x_send,
    x_plane,
    x_mate,
    c_send,
    c_mate,
    own_sem,
    *sems,
):
    G, R, PB, NCH, D = dm.G, dm.R, dm.PB, dm.NCH, dm.D
    HC = (w.shape[2] - 128) // 3
    TP = w.shape[0]
    p = Peers()
    block = block_index()
    gq = WeightGather(p, wq, w, *sems[:4])
    gm = WeightGather(p, wm, wm_out, *sems[4:])
    size = wq.shape[0]
    mine = pl.ds(pl.multiple_of(p.dp * size, 16), size)
    local = [
        pltpu.make_async_copy(wq, w.at[p.tp, mine, :], own_sem.at[0]),
        pltpu.make_async_copy(wm, wm_out.at[p.tp, mine, :], own_sem.at[1]),
        pltpu.make_async_copy(op, xp.at[block], own_sem.at[2]),
        pltpu.make_async_copy(oc, xc.at[p.core], own_sem.at[3]),
    ]
    for copy in local:
        copy.start()
    p.greet()
    gq.start()
    sent = []
    for k in range(1, p.ctxs):
        sent.append(send(op, xp.at[block], x_send.at[k - 1], x_plane.at[k - 1], p.plane(k)))
    sent.append(send(op, xp.at[block], x_send.at[p.ctxs - 1], x_mate.at[0], p.mate()))
    sent.append(send(oc, xc.at[p.core], c_send, c_mate, p.mate()))
    fill_masks(dm, maskp, maskx)
    gq.relay_across()
    gq.relay_rows(0)
    gq.relay_rows(1)
    gm.start()
    gq.finish()
    for copy in local:
        copy.wait()
    put = pltpu.make_async_copy(w, w_out, put_sem)
    put.start()
    ln = w[0, :, 3 * HC :].astype(F32).T[:8, :]
    ln_out[...] = ln
    gain, bias = ln[0:1, :], ln[1:2, :]

    def normed(x):
        hat, _ = norm_stats(x.astype(F32))
        return (hat * gain + bias).astype(BF16)

    def queries(x, row, table):
        rows = x.shape[0]
        n = normed(x)
        own_rows[pl.ds(row, rows), :] = n
        c = cos[pl.ds(table, rows), :]
        sn = sin[pl.ds(table, rows), :]
        for t in range(TP):
            qq = dot(n, w[t, :, :HC])
            for j in range(HC // 128):
                tile = rotate(qq[:, j * 128 : (j + 1) * 128], c, sn).astype(BF16)
                q_out[pl.ds(row, rows), t * HC + j * 128 : t * HC + (j + 1) * 128] = (
                    tile.astype(F32) * 0.125
                ).astype(BF16)

    def own_prompt(g, carry):
        queries(op[g], pl.multiple_of(g * PB, PB), pl.multiple_of(block * PB, PB))
        return carry

    lax.fori_loop(0, G, own_prompt, 0)

    def own_cont(i, carry):
        g, c = i // dm.NC, i % dm.NC
        queries(
            oc[g, c],
            pl.multiple_of(dm.NP + i * dm.CH, dm.CH),
            pl.multiple_of(dm.P + p.core * dm.CH, dm.CH),
        )
        return carry

    lax.fori_loop(0, G * dm.NC, own_cont, 0)
    own_out[...] = transpose(own_rows[...])

    def keys_values(g, x, row, table, place):
        rows = x.shape[0]
        n = normed(x)
        all_rows[pl.ds(place, rows), :] = n
        c = cos[pl.ds(table, rows), :]
        sn = sin[pl.ds(table, rows), :]
        for t in range(TP):
            kk = dot(n, w[t, :, HC : 2 * HC])
            for j in range(HC // 128):
                tile = rotate(kk[:, j * 128 : (j + 1) * 128], c, sn)
                k_out[g, pl.ds(row, rows), t * HC + j * 128 : t * HC + (j + 1) * 128] = tile.astype(BF16)
            v_out[g, pl.ds(row, rows), t * HC : (t + 1) * HC] = dot(n, w[t, :, 2 * HC : 3 * HC]).astype(BF16)

    def block_chunk(g, b):
        row = pl.multiple_of(b * PB, PB)
        keys_values(g, xp[b, g], row, row, pl.multiple_of(g * R + row, PB))

    arrived(xc.at[1 - p.core], c_mate, p)

    def cont_chunk(i, carry):
        g, c = i // dm.NC, i % dm.NC
        row = pl.multiple_of(dm.P + c * CL, CL)
        x = jnp.concatenate([xc[0, g, c], xc[1, g, c]], axis=0)
        keys_values(g, x, row, dm.P, pl.multiple_of(g * R + row, CL))
        return carry

    lax.fori_loop(0, G * dm.NC, cont_chunk, 0)

    def relay(k):
        b = p.ctx_before(k) * 2 + p.core
        arrived(xp.at[b], x_plane.at[k - 1], p)
        return send(xp.at[b], xp.at[b], x_send.at[p.ctxs + k - 1], x_mate.at[k], p.mate())

    for k in range(1, p.ctxs):
        sent.append(relay(k))
    for k in range(p.ctxs):
        arrived(xp.at[p.ctx_before(k) * 2 + 1 - p.core], x_mate.at[k], p)

    def prompt_chunk(i, carry):
        block_chunk(i // (2 * p.ctxs), i % (2 * p.ctxs))
        return carry

    lax.fori_loop(0, G * 2 * p.ctxs, prompt_chunk, 0)
    gm.relay_across()

    def turn(i, carry):
        rows = pl.ds(pl.multiple_of(i * 256, 256), 256)
        nt_out[:, rows] = transpose(all_rows[rows, :])
        return carry

    lax.fori_loop(0, G * R // 256, turn, 0)

    TILE = 256
    tiles = dm.P // TILE

    def attend(i, carry):
        g, pair = i // dm.PAIRS, i % dm.PAIRS
        lanes = pl.ds(pl.multiple_of(pair * 128, 128), 128)
        qp = q_out[pl.ds(pl.multiple_of(g * PB, PB), PB), lanes]
        qc = q_out[pl.ds(pl.multiple_of(dm.NP + g * NCH, NCH), NCH), lanes]
        qt = heads_columns(transpose(qp), transpose(qc))
        top = None
        for j in range(tiles):
            s = dot(k_out[g, j * TILE : (j + 1) * TILE, lanes], qt)
            sbuf[j * TILE : (j + 1) * TILE, : 2 * PB] = (
                s[:, : 2 * PB] + twice(maskp[j * TILE : (j + 1) * TILE, :])
            )
            sbuf[j * TILE : (j + 1) * TILE, 2 * PB :] = s[:, 2 * PB :]
            here = jnp.max(sbuf[j * TILE : (j + 1) * TILE, :], axis=0, keepdims=True)
            top = here if top is None else jnp.maximum(top, here)
        sx = dot(k_out[g, dm.P :, lanes], qt[:, 2 * PB :]) + maskx[...]
        topx = jnp.max(sx, axis=0, keepdims=True)
        top = jnp.concatenate([top[:, : 2 * PB], jnp.maximum(top[:, 2 * PB :], topx)], axis=1)
        total, acc = None, None
        for j in range(tiles):
            e = jnp.exp(sbuf[j * TILE : (j + 1) * TILE, :] - top)
            here = jnp.sum(e, axis=0, keepdims=True)
            vt = transpose(v_out[g, j * TILE : (j + 1) * TILE, lanes])
            part = dot(vt, e.astype(BF16))
            total = here if total is None else total + here
            acc = part if acc is None else acc + part
        ex = jnp.exp(sx - top[:, 2 * PB :])
        partx = dot(transpose(v_out[g, dm.P :, lanes]), ex.astype(BF16))
        totalx = jnp.sum(ex, axis=0, keepdims=True)
        total = jnp.concatenate([total[:, : 2 * PB], total[:, 2 * PB :] + totalx], axis=1)
        acc_p = acc[:, : 2 * PB] / total[:, : 2 * PB]
        acc_c = (acc[:, 2 * PB :] + partx) / total[:, 2 * PB :]
        lse_out[i] = top + jnp.log(total)
        outp = jnp.where(sublane_pick((128, PB), True), acc_p[:, :PB], acc_p[:, PB:])
        outc = jnp.where(sublane_pick((128, NCH), True), acc_c[:, :NCH], acc_c[:, NCH:])
        att_out[pl.ds(pl.multiple_of(g * PB, PB), PB), lanes] = outp.T.astype(BF16)
        att_out[pl.ds(pl.multiple_of(dm.NP + g * NCH, NCH), NCH), lanes] = outc.T.astype(BF16)
        return carry

    lax.fori_loop(0, G * dm.PAIRS, attend, 0)
    gm.relay_rows(0)
    gm.relay_rows(1)
    gm.finish()
    gq.drain()
    gm.drain()
    for copy in sent:
        copy.wait_send()
    put.wait()


class Reduce:
    REFS = 13

    def __init__(self, p, cross_first, refs):
        self.p, self.n, self.cross_first = p, len(cross_first), cross_first
        self.mine, self.got, self.row, self.acr, self.zin = refs[:5]
        self.sc, self.rc, self.sy, self.ry, self.sx, self.rx, self.sz, self.rz = refs[5:13]
        mid = p.ctxs // 2
        self.centre = (p.ctx == mid - 1) | (p.ctx == mid)
        self.outer = (p.ctx > 0) & (p.ctx < p.ctxs - 1)
        step = jnp.where(p.ctx < mid, 1, -1)
        self.inner_at = p.ctx + step
        self.outer_at = jnp.clip(p.ctx - step, 0, p.ctxs - 1)

    @staticmethod
    def scratch(cross_first, chips, size, width):
        n = len(cross_first)
        dma = pltpu.SemaphoreType.DMA
        far = max(chips - 1, 1)
        rows = n + sum(1 for c in cross_first if not c)
        return [
            pltpu.VMEM((2, chips * 2 * size, width), BF16),
            pltpu.VMEM((2 * n, chips, size, width), BF16),
            pltpu.VMEM((rows, far, size, width), BF16),
            pltpu.VMEM((n, chips, size, width), BF16),
            pltpu.VMEM((n, 2, size, width), BF16),
            dma((2 * n, chips)),
            dma((2 * n, chips)),
            dma((2 * n, far)),
            dma((2 * n, far)),
            dma((n,)),
            dma((n,)),
            dma((n, 2)),
            dma((n, 2)),
        ]

    def copy(self, src, dst, send_sem, recv_sem, device):
        return pltpu.make_async_remote_copy(
            src_ref=src,
            dst_ref=dst,
            send_sem=send_sem,
            recv_sem=recv_sem,
            device_id=device,
            device_id_type=MESH,
        )

    def crosses(self, i):
        return self.cross_first[i % self.n]

    def travels(self, i):
        return i >= self.n or not self.crosses(i)

    def mine_of(self, y, core):
        size = self.got.shape[2]
        return pl.ds(pl.multiple_of((2 * y + core) * size, 16), size)

    def by_core(self, i, slot, y):
        p = self.p
        return self.copy(
            self.mine.at[slot, self.mine_of(y, 1 - p.core), :],
            self.got.at[i, y],
            self.sc.at[i, y],
            self.rc.at[i, y],
            p.mate(),
        )

    def row_slot(self, i):
        return sum(1 for e in range(i) if self.travels(e))

    def by_row(self, i, k):
        p = self.p
        return self.copy(
            self.got.at[i, p.chip_after(k)],
            self.row.at[self.row_slot(i), k - 1],
            self.sy.at[i, k - 1],
            self.ry.at[i, k - 1],
            p.row(k),
        )

    def by_tp(self, j):
        p = self.p
        part = slice(None) if self.crosses(j) else p.chip
        return self.copy(
            self.got.at[j, part], self.acr.at[j, part], self.sx.at[j], self.rx.at[j], p.across()
        )

    def inward(self, j):
        slot = jnp.where(self.centre, 1, 0)
        return self.copy(
            self.got.at[self.n + j, self.p.chip],
            self.zin.at[j, slot],
            self.sz.at[j, 0],
            self.rz.at[j, slot],
            self.p.at(ctx=self.inner_at),
        )

    def outward(self, j):
        return self.copy(
            self.got.at[self.n + j, self.p.chip],
            self.zin.at[j, 1],
            self.sz.at[j, 1],
            self.rz.at[j, 1],
            self.p.at(ctx=self.outer_at),
        )

    def add(self, i, y, other):
        self.got[i, y] = (self.got[i, y].astype(F32) + other.astype(F32)).astype(BF16)

    def cores_send(self, i, slot):
        for y in range(self.p.chips):
            self.by_core(i, slot, y).start()

    def cores_sent(self, i, slot):
        for y in range(self.p.chips):
            self.by_core(i, slot, y).wait_send()

    def rows_send(self, i):
        for k in range(1, self.p.chips):
            self.by_row(i, k).start()

    def cores_sum(self, i, slot):
        p = self.p
        for y in range(p.chips):
            self.by_core(i, slot, y).wait_recv()
            self.add(i, y, self.mine[slot, self.mine_of(y, p.core), :])
        if not self.crosses(i):
            self.rows_send(i)
        elif i < self.n:
            self.by_tp(i).start()

    def cross_sum(self, j):
        self.by_tp(j).wait_recv()
        for y in range(self.p.chips):
            self.add(self.n + j, y, self.acr[j, y])
        self.rows_send(self.n + j)

    def rows_sum(self, i):
        p = self.p
        for k in range(1, p.chips):
            self.by_row(i, k).wait_recv()
            self.add(i, p.chip, self.row[self.row_slot(i), k - 1])
        if i < self.n:
            self.by_tp(i).start()
            return
        j = i - self.n
        if not self.crosses(i):
            self.by_tp(j).wait_recv()
            self.add(i, p.chip, self.acr[j, p.chip])

        @pl.when(jnp.logical_not(self.outer))
        def _():
            self.inward(j).start()

    def ctx_in(self, j):
        @pl.when(self.outer)
        def _():
            pltpu.make_async_copy(self.zin.at[j, 0], self.zin.at[j, 0], self.rz.at[j, 0]).wait()
            self.add(self.n + j, self.p.chip, self.zin[j, 0])
            self.inward(j).start()

    def ctx_mid(self, j):
        @pl.when(self.centre)
        def _():
            self.from_inner(j)
            self.add(self.n + j, self.p.chip, self.zin[j, 1])

            @pl.when(self.outer)
            def _():
                self.outward(j).start()

    def ctx_end(self, j):
        @pl.when(jnp.logical_not(self.centre))
        def _():
            self.from_inner(j)
            self.got[self.n + j, self.p.chip] = self.zin[j, 1]

            @pl.when(self.outer)
            def _():
                self.outward(j).start()

    def from_inner(self, j):
        pltpu.make_async_copy(self.zin.at[j, 1], self.zin.at[j, 1], self.rz.at[j, 1]).wait()
        self.inward(j).wait_send()

    def result(self, j):
        return self.got[self.n + j, self.p.chip].astype(F32)

    def drain(self):
        p = self.p
        for i in range(2 * self.n):
            if self.travels(i):
                for k in range(1, p.chips):
                    self.by_row(i, k).wait_send()
        for j in range(self.n):
            self.by_tp(j).wait_send()

            @pl.when(self.outer)
            def _():
                self.outward(j).wait_send()


def small_sum(p, sm, near, rows, across, planes, ss, rc, ry, rx, rz):
    copies = []

    def go(src, dst, recv_sem, device):
        copies.append(send(src, dst, ss.at[len(copies)], recv_sem, device))

    go(sm, near, rc, p.mate())
    copies[-1].wait_recv()
    rows[p.chip] = sm[...] + near[...]
    for k in range(1, p.chips):
        go(rows.at[p.chip], rows.at[p.chip], ry.at[k - 1], p.row(k))
    for k in range(1, p.chips):
        arrived(rows.at[p.chip_before(k)], ry.at[k - 1], p)
    total = rows[0]
    for y in range(1, p.chips):
        total += rows[y]
    across[0] = total
    go(across.at[0], across.at[1], rx, p.across())
    copies[-1].wait_recv()
    planes[p.ctx] = across[0] + across[1]
    for k in range(1, p.ctxs):
        go(planes.at[p.ctx], planes.at[p.ctx], rz.at[k - 1], p.plane(k))
    for k in range(1, p.ctxs):
        arrived(planes.at[p.ctx_before(k)], rz.at[k - 1], p)
    total = planes[0]
    for z in range(1, p.ctxs):
        total += planes[z]
    for copy in copies:
        copy.wait_send()
    return total


def schedule(ra, rb, on, pairs, planes):
    n, nb = ra.n, rb.n
    for i in range(2 * n - 1):
        if i == 2:
            on(("m", 3), partial(ra.rows_sum, 0))
        on(("m", i + 1), partial(ra.cores_sum, (i % 2) * n + i // 2, i % 2))
    on(("e", 0), partial(ra.rows_sum, n))
    on(("e", 0), partial(ra.cores_sum, 2 * n - 1, 1))
    on(("a", 0), partial(rb.cores_sum, 0, 0))
    on(("a", 0), partial(rb.cores_sum, nb, 1))
    on(("a", 2), partial(ra.rows_sum, 2))
    on(("a", 3), partial(rb.cross_sum, 0))
    on(("a", 4), partial(ra.ctx_in, 0))
    on(("a", 5), partial(ra.cross_sum, 1))
    last = pairs
    on(("a", last - 1), partial(rb.rows_sum, nb))
    on(("a", last), partial(ra.ctx_mid, 0))
    on(("a", last + 1), partial(ra.rows_sum, n + 1))
    on(("a", last + 1), partial(ra.rows_sum, n + 2))
    on(("a", last + 1), partial(rb.ctx_in, 0))
    on(("a", last + 3), partial(rb.ctx_mid, 0))
    on(("a", last + 5), partial(ra.ctx_in, 1))
    for i in range(pairs - 1):
        on(("a", last + 1 + i), partial(rb.cores_sum, (i % 2) * nb + 1 + i // 2, i % 2))
    on(("a", last + 3), partial(rb.cross_sum, 1))
    on(("a", last + 5), partial(rb.cross_sum, 2))
    on(("a", last + 5), partial(rb.rows_sum, nb + 1))
    on(("p", planes), partial(rb.cores_sum, 2 * nb - 1, 1))
    on(("p", planes), partial(rb.rows_sum, nb - 1))
    on(("p", planes + 1), partial(rb.rows_sum, nb + 2))
    on(("p", planes + 1), partial(rb.ctx_in, 1))
    on(("p", planes + 2), partial(ra.ctx_in, 2))
    on(("p", planes + 2), partial(ra.ctx_mid, 1))
    on(("t", 0), partial(rb.rows_sum, 2 * nb - 1))
    on(("t", 1), partial(rb.ctx_in, 2))
    on(("t", 2), partial(rb.ctx_mid, 1))
    on(("t", 3), partial(ra.ctx_mid, 2))
    on(("t", 4), partial(rb.ctx_in, 3))
    on(("t", 5), partial(rb.ctx_mid, 2))
    on(("t", 11), partial(rb.ctx_mid, 3))


def backward_kernel(
    dm,
    T,
    FC,
    plan_a,
    plan_b,
    mix,
    att,
    own_p,
    own_c,
    cot_p,
    cot_c,
    ln,
    q,
    lse,
    cos,
    sin,
    wm,
    k_hbm,
    v_hbm,
    nt_hbm,
    own_nt_hbm,
    wq_hbm,
    home_arrays_p,
    home_arrays_c,
    early_p,
    early_c,
    home_cot_p,
    home_cot_c,
    out_p,
    out_c,
    gin_p,
    gin_c,
    gq_out,
    go_out,
    gu_out,
    gd_out,
    small_out,
    resid,
    blk,
    gh,
    wo,
    ring,
    gatt,
    nt,
    own_nt,
    maskp,
    maskx,
    kbuf,
    vbuf,
    dk,
    dv,
    dq,
    dxm,
    dxz,
    dxcm,
    blk_away,
    blk_home,
    gin_home,
    put_sem,
    ring_sem,
    wo_sem,
    kv_sem,
    nt_sem,
    wq_sem,
    home_sem,
    b_send,
    b_recv,
    g_send,
    g_recv,
    m_send,
    m_recv,
    z_send,
    z_recv,
    c_send,
    c_recv,
    sm,
    sm_near,
    sm_rows,
    sm_across,
    sm_planes,
    sm_ss,
    sm_rc,
    sm_ry,
    sm_rx,
    sm_rz,
    *refs,
):
    G, R, PB, NCH, D, NX, NP, NT = dm.G, dm.R, dm.PB, dm.NCH, dm.D, dm.NX, dm.NP, dm.NT
    TP, HC = wo.shape[0], wo.shape[2]
    PT = dm.PAIRS // TP
    p = Peers()
    n_a, NB = len(plan_a), len(plan_b)
    ra = Reduce(p, plan_a, refs[: Reduce.REFS])
    rb = Reduce(p, plan_b, refs[Reduce.REFS :])
    block = block_index()
    TILE = 256
    tiles = dm.P // TILE
    chips = p.chips
    S = D // (2 * chips)

    def begin(copies):
        for copy in copies:
            copy.start()

    def ready(copies):
        for copy in copies:
            copy.wait()

    def load_tile(i, slot):
        t = jnp.where(lax.rem(i, 2) == 0, 1 - p.tp, p.tp)
        first = pl.multiple_of(HC + i // 2 * T, 128)
        return [
            pltpu.make_async_copy(
                wm.at[t, :, pl.ds(first, T)], ring.at[slot, :, pl.ds(0, T)], ring_sem.at[0, slot]
            ),
            pltpu.make_async_copy(
                wm.at[t, :, pl.ds(first + FC, T)], ring.at[slot, :, pl.ds(T, T)], ring_sem.at[1, slot]
            ),
        ]

    def pair_at(it):
        turn = it % dm.PAIRS
        return jnp.where(turn % 2 == 0, 1 - p.tp, p.tp) * PT + turn // 2

    def load_kv(it, slot):
        pair, g = pair_at(it), it // dm.PAIRS
        lanes = pl.ds(pl.multiple_of(pair * 128, 128), 128)
        return [
            pltpu.make_async_copy(k_hbm.at[g, :, lanes], kbuf.at[slot], kv_sem.at[0, slot]),
            pltpu.make_async_copy(v_hbm.at[g, :, lanes], vbuf.at[slot], kv_sem.at[1, slot]),
        ]

    wo_load = pltpu.make_async_copy(wm.at[:, :, pl.ds(0, HC)], wo, wo_sem)
    wo_load.start()
    begin(load_tile(0, 0))
    begin(load_kv(0, 0))
    p.greet(trades=True)
    fill_masks(dm, maskp, maskx)
    gain_two, bias_two = ln[2:3, :], ln[3:4, :]

    hn, gd = slice(0, NT), slice(NT, 2 * NT)
    STEP = 128

    def by_rows(step):
        def prompt_part(i, carry):
            rows = pl.ds(pl.multiple_of(i * STEP, STEP), STEP)
            step(own_p[rows, :], cot_p[rows, :], i * STEP)
            return carry

        def cont_part(i, carry):
            rows = pl.ds(pl.multiple_of(i * STEP, STEP), STEP)
            step(own_c[rows, :], cot_c[rows, :], NP + i * STEP)
            return carry

        lax.fori_loop(0, NP // STEP, prompt_part, 0)
        lax.fori_loop(0, (NT - NP) // STEP, cont_part, 0)

    def shifted(first, row):
        return pl.ds(pl.multiple_of(first + row, STEP), STEP)

    wo_load.wait()

    def enter(x, cot, row):
        rows = shifted(0, row)
        r = x.astype(F32)
        for t in range(TP):
            r += dot_nt(att[rows, t * HC : (t + 1) * HC], wo[t])
        resid[rows, :] = r
        blk[rows, :] = r
        h, _ = norm_stats(r)
        n = (h * gain_two + bias_two).astype(BF16)
        dk[rows, :] = n
        nt[:, rows] = transpose(n)
        g = (mix[4] * cot.astype(F32)).astype(BF16)
        dk[shifted(NT, row), :] = g
        nt[:, shifted(NT, row)] = transpose(g)
        gh[rows, :] = jnp.zeros((STEP, D), F32)

    by_rows(enter)

    during = {}

    def on(stage, step):
        during.setdefault(stage, []).append(step)

    def run_when(index, name):
        for (kind, when), steps in during.items():
            if kind == name:

                @pl.when(index == when)
                def _():
                    for step in steps:
                        step()

    schedule(ra, rb, on, dm.PAIRS, p.ctxs)

    def run(name):
        for kind, when in sorted(key for key in during if key[0] == name):
            for step in during[kind, when]:
                step()

    def feed(i, carry):
        slot = lax.rem(i, 2)

        @pl.when(i + 1 < 2 * n_a)
        def _():
            begin(load_tile(i + 1, 1 - slot))

        ready(load_tile(i, slot))
        up, dn = ring[slot, :, :T], ring[slot, :, T : 2 * T]
        c0 = 0.7978845608028654
        HALF = NT // 2
        for e in range(2):
            rows = slice(e * HALF, (e + 1) * HALF)
            u = dot(dk[rows, :], up)
            if e == 1:
                run_when(i, "m")
            u2 = u * u
            th = jnp.tanh(c0 * u * (1.0 + 0.044715 * u2))
            half = 0.5 * (1.0 + th)
            act = (u * half).astype(BF16)
            slope = half + 0.5 * u * (1.0 - th * th) * (c0 * (1.0 + 3 * 0.044715 * u2))
            dv[rows, :T] = act
            blk[rows, :] += dot_nt(act, dn)
            gu = (dot(dk[NT + e * HALF : NT + (e + 1) * HALF, :], dn) * slope).astype(BF16)
            dv[NT + e * HALF : NT + (e + 1) * HALF, :T] = gu
            gh[rows, :] += dot_nt(gu, up)

        @pl.when(i >= 2)
        def _():
            ra.cores_sent(slot * n_a + i // 2 - 1, slot)

        for y in range(chips):
            mine = slice(y * 2 * S, (y + 1) * 2 * S)
            ra.mine[slot, mine, :T] = dot(nt[mine, hn], dv[gd, :T]).astype(BF16)
            ra.mine[slot, mine, T:] = dot(nt[mine, gd], dv[hn, :T]).astype(BF16)
        ra.cores_send(slot * n_a + i // 2, slot)
        return carry

    lax.fori_loop(0, 2 * n_a, feed, 0)
    run("e")
    blk_away[:NT, :] = blk[...].astype(BF16)
    away = ra.copy(blk_away.at[pl.ds(0, NT), :], blk_home, b_send, b_recv, p.partner())

    @pl.when(p.core != p.tp)
    def _():
        away.start()

    @pl.when(p.core == p.tp)
    def _():
        blk_home[...] = blk_away[:NT, :]

    sm[...] = jnp.zeros_like(sm)

    def leave(x, cot, row):
        rows = shifted(0, row)
        cot = cot.astype(F32)
        sm[2:3, :] += jnp.sum(cot * blk[rows, :], axis=0, keepdims=True)
        h, scale = norm_stats(resid[rows, :])
        g = gh[rows, :]
        sm[0:1, :] += jnp.sum(g * h, axis=0, keepdims=True)
        sm[1:2, :] += jnp.sum(g, axis=0, keepdims=True)
        gr = mix[4] * cot + norm_back(g, gain_two, h, scale)
        resid[rows, :] = gr
        gb = gr.astype(BF16)
        nt[:, shifted(NT, row)] = transpose(gb)
        for t in range(TP):
            gatt[rows, t * HC : (t + 1) * HC] = dot(gb, wo[t]).astype(BF16)

    by_rows(leave)
    for slot, i in enumerate((0, NB)):
        t = p.tp if slot else 1 - p.tp
        lanes = pl.ds(pl.multiple_of(t * HC, 128), HC)
        for y in range(chips):
            mine = slice(y * 2 * S, (y + 1) * 2 * S)
            rb.mine[slot, mine, :] = dot(nt[mine, gd], att[:, lanes]).astype(BF16)
        rb.cores_send(i, slot)
    nt_load = [
        pltpu.make_async_copy(nt_hbm, nt, nt_sem.at[0]),
        pltpu.make_async_copy(own_nt_hbm, own_nt, nt_sem.at[1]),
    ]
    begin(nt_load)
    wq_load = pltpu.make_async_copy(wq_hbm.at[:, :, pl.ds(0, 3 * HC)], ring.at[:, :, pl.ds(0, 3 * HC)], wq_sem)
    wq_load.start()
    during.setdefault(("a", dm.PAIRS), []).insert(0, partial(ready, nt_load))

    def attend(turn, g):
        it = g * dm.PAIRS + turn
        pair = pair_at(it)
        slot = it % 2

        @pl.when(it + 1 < G * dm.PAIRS)
        def _():
            begin(load_kv(it + 1, 1 - slot))

        lanes = pl.ds(pl.multiple_of(pair * 128, 128), 128)
        rp = pl.ds(pl.multiple_of(g * PB, PB), PB)
        rc = pl.ds(pl.multiple_of(dm.NP + g * NCH, NCH), NCH)
        qp, qc = q[rp, lanes], q[rc, lanes]
        gp, gc = gatt[rp, lanes], gatt[rc, lanes]
        ap, ac = att[rp, lanes].astype(F32), att[rc, lanes].astype(F32)
        qt = heads_columns(transpose(qp), transpose(qc))
        gpt, gct = gp.astype(F32).T, gc.astype(F32).T
        gt = heads_columns(gpt.astype(BF16), gct.astype(BF16))
        qs, gs = heads_rows(qp, qc), heads_rows(gp, gc)
        prodp, prodc = gpt * ap.T, gct * ac.T
        delta = jnp.concatenate(
            [
                jnp.sum(prodp[:HD], axis=0, keepdims=True),
                jnp.sum(prodp[HD:], axis=0, keepdims=True),
                jnp.sum(prodc[:HD], axis=0, keepdims=True),
                jnp.sum(prodc[HD:], axis=0, keepdims=True),
            ],
            axis=1,
        )
        stat = lse[g * dm.PAIRS + pair]
        ready(load_kv(it, slot))

        def grads(s, kt, vt, cols):
            pr = jnp.exp(s - stat[:, cols:])
            dp = dot(vt, gt[:, cols:])
            ds = (pr * (dp - delta[:, cols:])).astype(BF16)
            gv = dot(pr.astype(BF16), gs[cols:])
            gk = dot(ds, qs[cols:])
            gq = dot(transpose(kt), ds)
            return gk, gv, gq

        acc = None
        for j in range(tiles):
            rows = slice(j * TILE, (j + 1) * TILE)
            kt = kbuf[slot, rows, :]
            s = dot(kt, qt)
            s = jnp.concatenate([s[:, : 2 * PB] + twice(maskp[rows, :]), s[:, 2 * PB :]], axis=1)
            gk, gv, gq = grads(s, kt, vbuf[slot, rows, :], 0)
            gk = rotate_back(gk, cos[rows, :], sin[rows, :]).astype(BF16)
            gv = gv.astype(BF16)
            out = pl.ds(pl.multiple_of(g * R + j * TILE, 128), TILE)
            dk[out, lanes] = gk
            dv[out, lanes] = gv
            if j == tiles // 2:
                run_when(it, "a")
            acc = gq if acc is None else acc + gq
        kt = kbuf[slot, dm.P :, :]
        s = dot(kt, qt[:, 2 * PB :]) + maskx[...]
        gk, gv, gq = grads(s, kt, vbuf[slot, dm.P :, :], 2 * PB)
        for c in range(dm.NC):
            rows = slice(dm.P, dm.P + CL)
            out = pl.ds(pl.multiple_of(g * R + dm.P + c * CL, CL), CL)
            part = rotate_back(gk[c * CL : (c + 1) * CL], cos[rows, :], sin[rows, :])
            dk[out, lanes] = part.astype(BF16)
            dv[out, lanes] = gv[c * CL : (c + 1) * CL].astype(BF16)
        accp = acc[:, : 2 * PB] * 0.125
        accc = (acc[:, 2 * PB :] + gq) * 0.125
        outp = jnp.where(sublane_pick((128, PB), True), accp[:, :PB], accp[:, PB:]).T
        outc = jnp.where(sublane_pick((128, NCH), True), accc[:, :NCH], accc[:, NCH:]).T
        tab = pl.ds(pl.multiple_of(block * PB, PB), PB)
        dq[rp, lanes] = rotate_back(outp, cos[tab, :], sin[tab, :]).astype(BF16)
        tab = pl.ds(pl.multiple_of(dm.P + p.core * dm.CH, dm.CH), dm.CH)
        for c in range(dm.NC):
            part = rotate_back(outc[c * dm.CH : (c + 1) * dm.CH], cos[tab, :], sin[tab, :])
            rows = pl.ds(pl.multiple_of(dm.NP + g * NCH + c * dm.CH, dm.CH), dm.CH)
            dq[rows, lanes] = part.astype(BF16)

        @pl.when(g == G - 1)
        def _():
            put = turn % 2
            index = put * NB + 1 + turn // 2
            rb.cores_sent(index - 1, put)
            both = jnp.concatenate([dk[:, lanes], dv[:, lanes]], axis=1)
            for y in range(chips):
                mine = slice(y * 2 * S, (y + 1) * 2 * S)
                rb.mine[put, mine, 128:] = dot(nt[mine, :], both).astype(BF16)
                rb.mine[put, mine, :128] = dot(own_nt[mine, :], dq[:, lanes]).astype(BF16)
            rb.cores_send(index, put)

        return g

    w = ring

    def project(rows):
        total = None
        for t in range(TP):
            part = dot_nt(dk[rows, t * HC : (t + 1) * HC], w[t, :, HC : 2 * HC])
            total = part if total is None else total + part
            total += dot_nt(dv[rows, t * HC : (t + 1) * HC], w[t, :, 2 * HC : 3 * HC])
        return total

    NCONT = NT - NP
    gain_one = ln[0:1, :]
    halves = lambda core, g: pl.ds(pl.multiple_of(core * NCONT + g * NCH, 16), NCH)

    def dx_at(g, k, first, count):
        c = p.ctx_after(k)
        if g == G - 1:
            return dk.at[pl.ds(pl.multiple_of(g * R + c * 2 * PB + first, PB), count), :]
        fit = D // (2 * PB)
        row = pl.multiple_of(c % fit * 2 * PB + first, PB)
        return ra.mine.at[c // fit, pl.ds(row, count), pl.ds(0, D)]

    def dx_rows(g, k, core):
        return dx_at(g, k, core * PB, PB)

    def to_mate(g, k):
        i = g * p.ctxs + k
        return ra.copy(dx_rows(g, k, 1 - p.core), dxm.at[i], m_send.at[i], m_recv.at[i], p.mate())

    def to_plane(g, k):
        i = g * (p.ctxs - 1) + k - 1
        return ra.copy(
            dx_rows(g, k, p.core), dxz.at[i], z_send.at[i], z_recv.at[i], p.at(ctx=p.ctx_after(k))
        )

    def each_group(g, step):
        for e in range(G):

            @pl.when(g == e)
            def _():
                step(e)

    def cont_copy(g):
        return ra.copy(
            blk_away.at[halves(1 - p.core, g), :],
            dxcm.at[pl.ds(pl.multiple_of(g * NCH, 16), NCH), :],
            c_send.at[g],
            c_recv.at[g],
            p.mate(),
        )

    def group(g, carry):
        lax.fori_loop(0, dm.PAIRS, attend, g)

        @pl.when(g == 0)
        def _():
            wq_load.wait()
            ra.cores_sent(n_a - 1, 0)
            ra.cores_sent(2 * n_a - 1, 1)

            @pl.when(p.core != p.tp)
            def _():
                away.wait_send()

        def planes(i, carry):
            k = lax.rem(i + 1, p.ctxs)
            both = pl.ds(pl.multiple_of(g * R + p.ctx_after(k) * 2 * PB, 2 * PB), 2 * PB)
            total = project(both).astype(BF16)

            def out(e):
                dx_at(e, k, 0, 2 * PB)[...] = total
                to_mate(e, k).start()

            each_group(g, out)
            run_when(g * p.ctxs + i, "p")

            def back(e):
                to_mate(e, k).wait_recv()
                mine = dx_rows(e, k, p.core)
                mine[...] = (mine[...].astype(F32) + dxm[e * p.ctxs + k].astype(F32)).astype(BF16)

                @pl.when(k > 0)
                def _():
                    to_plane(e, k).start()

            each_group(g, back)
            return carry

        lax.fori_loop(0, p.ctxs, planes, 0)
        rows = pl.ds(pl.multiple_of(g * R + dm.P, CL), NX)
        total = project(rows).astype(BF16)
        for c in range(dm.NC):
            for e in range(2):
                out = pl.ds(pl.multiple_of(e * NCONT + g * NCH + c * dm.CH, dm.CH), dm.CH)
                blk_away[out, :] = total[c * CL + e * dm.CH : c * CL + (e + 1) * dm.CH]
        cont_copy(g).start()
        for first, count in ((g * PB, PB), (NP + g * NCH, NCH)):
            rows = pl.ds(pl.multiple_of(first, 16), count)
            total = dot_nt(dq[rows, :HC], w[0, :, :HC])
            for t in range(1, TP):
                total += dot_nt(dq[rows, t * HC : (t + 1) * HC], w[t, :, :HC])
            blk[rows, :] = total
        return carry

    def enter_back(gn, x, rows):
        gn += blk[rows, :]
        hat, scale = norm_stats(x.astype(F32))
        gatt[rows, :] = (resid[rows, :] + norm_back(gn, gain_one, hat, scale)).astype(BF16)
        sm[7:8, :] += jnp.sum(gn * hat, axis=0, keepdims=True)
        sm[8:9, :] += jnp.sum(gn, axis=0, keepdims=True)

    def gin_away(part):
        rows = pl.ds(0, NP) if part == 0 else pl.ds(NP, NT - NP)
        return ra.copy(gatt.at[rows, :], gin_home.at[rows, :], g_send.at[part], g_recv.at[part], p.partner())

    def give(part):
        rows = slice(0, NP) if part == 0 else slice(NP, NT)

        @pl.when(p.core != p.tp)
        def _():
            gin_away(part).start()

        @pl.when(p.core == p.tp)
        def _():
            gin_home[rows, :] = gatt[rows, :]

    lax.fori_loop(0, G, group, 0)
    homes = []
    for i, (a, c) in enumerate(
        [(home_arrays_p, home_arrays_c)]
        + [(early_p.at[e], early_c.at[e]) for e in range(3)]
        + [(home_cot_p, home_cot_c)]
    ):
        homes.append(pltpu.make_async_copy(a, dv.at[pl.ds(i * NT, NP), :], home_sem.at[0, i]))
        homes.append(pltpu.make_async_copy(c, dv.at[pl.ds(i * NT + NP, NT - NP), :], home_sem.at[1, i]))
    begin(homes)

    def cont_back(g, carry):
        cont_copy(g).wait_recv()
        here = pl.ds(pl.multiple_of(g * NCH, 16), NCH)
        gn = blk_away[halves(p.core, g), :].astype(F32) + dxcm[here, :].astype(F32)
        enter_back(gn, own_c[here, :], pl.ds(pl.multiple_of(NP + g * NCH, 16), NCH))
        return carry

    lax.fori_loop(0, G, cont_back, 0)
    give(1)

    ready(homes)

    @pl.when(p.core != p.tp)
    def _():
        away.wait_recv()

    def blend(i, carry):
        rows = shifted(0, i * STEP)
        res = mix[4] * blk_home[rows, :].astype(F32)
        c = dv[shifted(4 * NT, i * STEP), :].astype(F32)
        for e in range(4):
            a = dv[shifted(e * NT, i * STEP), :].astype(F32)
            res += mix[e] * a
            sm[3 + e : 4 + e, :] += jnp.sum(c * a, axis=0, keepdims=True)
        blk_home[rows, :] = res.astype(BF16)
        return carry

    lax.fori_loop(0, NT // STEP, blend, 0)
    puts = [
        pltpu.make_async_copy(blk_home.at[pl.ds(0, NP), :], out_p, put_sem.at[0]),
        pltpu.make_async_copy(blk_home.at[pl.ds(NP, NT - NP), :], out_c, put_sem.at[1]),
    ]
    begin(puts)
    for when in range(10):
        for step in during.get(("t", when), []):
            step()

    for g in range(G):
        gn = dx_rows(g, 0, p.core)[...].astype(F32)
        for k in range(1, p.ctxs):
            to_plane(g, k).wait_recv()
            gn += dxz[g * (p.ctxs - 1) + k - 1].astype(F32)
        here = slice(g * PB, (g + 1) * PB)
        enter_back(gn, own_p[here, :], here)
    give(0)
    for when in range(10, 20):
        for step in during.get(("t", when), []):
            step()
    small_out[...] = small_sum(
        p, sm, sm_near, sm_rows, sm_across, sm_planes, sm_ss, sm_rc, sm_ry, sm_rx, sm_rz
    )
    gu_puts = []
    for j in range(n_a):
        ra.ctx_end(j)
        total = ra.result(j)
        gd_out[j * T : (j + 1) * T, :] = total[:, T:].T
        if len(gu_puts) > 0:
            gu_puts[-1].wait()
        gh[:S, :T] = total[:, :T]
        gu_puts.append(
            pltpu.make_async_copy(
                gh.at[pl.ds(0, S), pl.ds(0, T)], gu_out.at[:, pl.ds(j * T, T)], put_sem.at[2]
            )
        )
        gu_puts[-1].start()
    gu_puts[-1].wait()
    for j in range(NB):
        rb.ctx_end(j)
        total = rb.result(j)
        if j == 0:
            go_out[...] = total.T
        else:
            for c in range(3):
                first = c * HC + (j - 1) * 128
                gq_out[:, first : first + 128] = total[:, c * 128 : (c + 1) * 128]

    @pl.when(p.core != p.tp)
    def _():
        for part in range(2):
            gin_away(part).wait_recv()
            gin_away(part).wait_send()

    more = [
        pltpu.make_async_copy(gin_home.at[pl.ds(0, NP), :], gin_p, put_sem.at[2]),
        pltpu.make_async_copy(gin_home.at[pl.ds(NP, NT - NP), :], gin_c, put_sem.at[3]),
    ]
    begin(more)
    ready(puts + more)
    rb.cores_sent(NB - 1, 0)
    rb.cores_sent(2 * NB - 1, 1)
    for g in range(G):
        for k in range(p.ctxs):
            to_mate(g, k).wait_send()
        for k in range(1, p.ctxs):
            to_plane(g, k).wait_send()
        cont_copy(g).wait_send()
    ra.drain()
    rb.drain()


def params(**more):
    return pltpu.CompilerParams(vmem_limit_bytes=VMEM_LIMIT, **more)


def per_device(
    prompt_in,
    cont_in,
    prompt_embed,
    cont_embed,
    prompt_earlier,
    cont_earlier,
    ln1_gain,
    ln1_bias,
    ln2_gain,
    ln2_bias,
    w_qkv,
    w_out,
    w_up,
    w_down,
    mix_weights,
    prompt_cot,
    cont_cot,
):
    G, PB, D = prompt_in.shape
    NC, CH = cont_in.shape[1], cont_in.shape[2]
    TP = lax.axis_size("tp")
    PROMPT = PB * TP * lax.axis_size("ctx")
    HC, FC = w_qkv.shape[2], w_up.shape[1]
    S = w_qkv.shape[0]
    dm = Dims(G, PROMPT, PB, NC, CH, D, HC * TP // HD)
    R, NT, NP = dm.R, dm.NT, dm.NP

    sds = jax.ShapeDtypeStruct
    chips, ctxs = lax.axis_size("dp") // 2, lax.axis_size("ctx")
    swap = [(4 * y + 2 * c + t, 4 * y + 2 * t + c) for y in range(chips) for c in (0, 1) for t in (0, 1)]

    def trade(x):
        return lax.ppermute(x, ("dp", "tp"), swap)

    own_p, own_c = trade(prompt_in), trade(cont_in)
    cot_p, cot_c = trade(prompt_cot), trade(cont_cot)
    norms = jnp.stack([ln1_gain, ln1_bias, ln2_gain, ln2_bias], axis=1)
    norms = jnp.pad(norms, ((0, 0), (0, 124)))
    wq_shard = jnp.concatenate([w_qkv.reshape(S, 3 * HC), norms], axis=1)
    wm_shard = jnp.concatenate([w_out.T, w_up, w_down.T], axis=1)

    positions = jnp.arange(PROMPT + CL, dtype=jnp.int32).astype(F32)
    lane = jnp.arange(128, dtype=jnp.int32)
    freq = 10000.0 ** (-((lane % 32).astype(F32) / 32))
    angles = positions[:, None] * freq[None, :]
    cos, sin = jnp.cos(angles), jnp.sin(angles)
    second = (lane % 64) >= 32
    sin = jnp.where(second[None, :], sin, -sin)

    any_ = pl.BlockSpec(memory_space=pl.ANY)
    vmem = pl.BlockSpec(memory_space=pltpu.VMEM)
    dma = pltpu.SemaphoreType.DMA
    nt, own_nt, k, v, q, att, lse, wq, ln, wm = pl.pallas_call(
        partial(forward_kernel, dm),
        out_shape=(
            sds((D, G * R), BF16),
            sds((D, NT), BF16),
            sds((G, R, D), BF16),
            sds((G, R, D), BF16),
            sds((NT, D), BF16),
            sds((NT, D), BF16),
            sds((G * dm.PAIRS, 1, dm.COLS), F32),
            sds((TP, D, 3 * HC + 128), BF16),
            sds((8, D), F32),
            sds((TP, D, HC + 2 * FC), BF16),
        ),
        in_specs=[vmem] * 5 + [any_],
        out_specs=(vmem,) * 7 + (any_, vmem, any_),
        scratch_shapes=[
            pltpu.VMEM((PROMPT, PB), F32),
            pltpu.VMEM((dm.NX, 2 * dm.NCH), F32),
            pltpu.VMEM((PROMPT, dm.COLS), F32),
            pltpu.VMEM((G * R, D), BF16),
            pltpu.VMEM((NT, D), BF16),
            pltpu.VMEM((2 * ctxs, G, PB, D), BF16),
            pltpu.VMEM((2, G, NC, CH, D), BF16),
            pltpu.VMEM((TP, D, 3 * HC + 128), BF16),
            dma,
            dma((2 * ctxs - 1,)),
            dma((ctxs - 1,)),
            dma((ctxs,)),
            dma,
            dma,
            dma((4,)),
        ]
        + WeightGather.semaphores(chips)
        + WeightGather.semaphores(chips),
        compiler_params=params(collective_id=0, has_side_effects=True),
        name="forward",
    )(own_p, own_c, cos, sin, wq_shard, wm_shard)
    T = 512 if FC % 512 == 0 else 256
    plan_a = [j == 1 for j in range(FC // T)]
    plan_b = [j < dm.PAIRS // TP for j in range(1 + dm.PAIRS // TP)]
    far = max(chips - 1, 1)
    rows = lambda x: x.reshape(-1, D)
    out_p, out_c, gin_p, gin_c, gq, go, gu, gd, small = pl.pallas_call(
        partial(backward_kernel, dm, T, FC, plan_a, plan_b),
        out_shape=(
            sds((NP, D), BF16),
            sds((NT - NP, D), BF16),
            sds((NP, D), BF16),
            sds((NT - NP, D), BF16),
            sds((S, 3 * HC), F32),
            sds((HC, S), F32),
            sds((S, FC), F32),
            sds((FC, S), F32),
            sds((16, D), F32),
        ),
        in_specs=[pl.BlockSpec(memory_space=pltpu.SMEM)] + [vmem] * 10 + [any_] * 12,
        out_specs=(any_,) * 4 + (vmem, vmem, any_, vmem, vmem),
        scratch_shapes=[
            pltpu.VMEM((NT, D), F32),
            pltpu.VMEM((NT, D), F32),
            pltpu.VMEM((NT, D), F32),
            pltpu.VMEM((TP, D, HC), BF16),
            pltpu.VMEM((2, D, max(2 * T, 3 * HC)), BF16),
            pltpu.VMEM((NT, D), BF16),
            pltpu.VMEM((D, G * R), BF16),
            pltpu.VMEM((D, NT), BF16),
            pltpu.VMEM((PROMPT, PB), F32),
            pltpu.VMEM((dm.NX, 2 * dm.NCH), F32),
            pltpu.VMEM((2, R, 128), BF16),
            pltpu.VMEM((2, R, 128), BF16),
            pltpu.VMEM((G * R, D), BF16),
            pltpu.VMEM((G * R, D), BF16),
            pltpu.VMEM((NT, D), BF16),
            pltpu.VMEM((G * ctxs, PB, D), BF16),
            pltpu.VMEM((G * (ctxs - 1), PB, D), BF16),
            pltpu.VMEM((NT - NP, D), BF16),
            pltpu.VMEM((max(NT, 2 * (NT - NP)), D), BF16),
            pltpu.VMEM((NT, D), BF16),
            pltpu.VMEM((NT, D), BF16),
            dma((4,)),
            dma((2, 2)),
            dma,
            dma((2, 2)),
            dma((2,)),
            dma,
            dma((2, 5)),
            dma,
            dma,
            dma((2,)),
            dma((2,)),
            dma((G * ctxs,)),
            dma((G * ctxs,)),
            dma((G * (ctxs - 1),)),
            dma((G * (ctxs - 1),)),
            dma((G,)),
            dma((G,)),
            pltpu.VMEM((16, D), F32),
            pltpu.VMEM((16, D), F32),
            pltpu.VMEM((chips, 16, D), F32),
            pltpu.VMEM((2, 16, D), F32),
            pltpu.VMEM((ctxs, 16, D), F32),
            dma((1 + chips + ctxs,)),
            dma,
            dma((far,)),
            dma,
            dma((ctxs - 1,)),
        ]
        + Reduce.scratch(plan_a, chips, S, 2 * T)
        + Reduce.scratch(plan_b, chips, S, HC),
        compiler_params=params(collective_id=1, has_side_effects=True),
        name="backward",
    )(
        mix_weights,
        att,
        rows(own_p),
        rows(own_c),
        rows(cot_p),
        rows(cot_c),
        ln,
        q,
        lse,
        cos,
        sin,
        wm,
        k,
        v,
        nt,
        own_nt,
        wq,
        rows(prompt_embed),
        rows(cont_embed),
        prompt_earlier.reshape(3, NP, D),
        cont_earlier.reshape(3, NT - NP, D),
        rows(prompt_cot),
        rows(cont_cot),
    )
    start = lax.axis_index("dp") * S
    mine = lax.dynamic_slice_in_dim(small, start, S, axis=1)
    return (
        out_p.reshape(prompt_in.shape),
        out_c.reshape(cont_in.shape),
        gin_p.reshape(prompt_in.shape),
        gin_c.reshape(cont_in.shape),
        mine[7],
        mine[8],
        mine[0],
        mine[1],
        gq.reshape(S, 3, HC),
        go,
        gu,
        gd,
        jnp.sum(jnp.concatenate([small[3:7], small[2:3]]), axis=1),
    )


def solution(mesh):
    tokens = P("dp", ("ctx", "tp"), None)
    conts = P("dp", "ctx", "tp", None)
    weights = (P("dp", None, "tp"), P("tp", "dp"), P("dp", "tp"), P("tp", "dp"))
    in_specs = (
        tokens,
        conts,
        tokens,
        conts,
        P(None, "dp", ("ctx", "tp"), None),
        P(None, "dp", "ctx", "tp", None),
        P("dp"),
        P("dp"),
        P("dp"),
        P("dp"),
        *weights,
        P(),
        tokens,
        conts,
    )
    out_specs = (
        tokens,
        conts,
        tokens,
        conts,
        P("dp"),
        P("dp"),
        P("dp"),
        P("dp"),
        *weights,
        P(),
    )
    return jax.shard_map(
        per_device, mesh=mesh, in_specs=in_specs, out_specs=out_specs, check_vma=False
    )
```

```python
from functools import partial

import jax
import jax.numpy as jnp
import numpy as np
from jax import lax
from jax.experimental import pallas as pl
from jax.experimental.pallas import tpu as pltpu
from jax.sharding import PartitionSpec as P

HD = 64
CL = 128
EPS = 1e-05
NEG = -1e30
F32 = jnp.float32
BF16 = jnp.bfloat16
VMEM_LIMIT = 67043328


def dot(a, b):
    return lax.dot_general(a, b, (((1,), (0,)), ((), ())), preferred_element_type=F32)


def dot_nt(a, b):
    return lax.dot_general(a, b, (((1,), (1,)), ((), ())), preferred_element_type=F32)


def norm_stats(x):
    mean = jnp.mean(x, axis=-1, keepdims=True)
    centered = x - mean
    var = jnp.mean(centered * centered, axis=-1, keepdims=True)
    scale = lax.rsqrt(var + EPS)
    return centered * scale, scale


def norm_back(grad, gain, hat, scale):
    gh = grad * gain
    return scale * (
        gh
        - jnp.mean(gh, axis=-1, keepdims=True)
        - hat * jnp.mean(gh * hat, axis=-1, keepdims=True)
    )


def swap_halves(x):
    second = lax.broadcasted_iota(jnp.int32, x.shape, 1) % HD >= HD // 2
    return jnp.where(second, pltpu.roll(x, 32, 1), pltpu.roll(x, 96, 1))


def rotate(x, cos, sin):
    return x * cos + swap_halves(x) * sin


def rotate_back(x, cos, sin):
    return x * cos - swap_halves(x) * sin


def lane_pick(shape, low):
    lanes = lax.broadcasted_iota(jnp.int32, shape, 1)
    return lanes < HD if low else lanes >= HD


def sublane_pick(shape, low):
    rows = lax.broadcasted_iota(jnp.int32, shape, 0)
    return rows < HD if low else rows >= HD


def transpose(x):
    return x.astype(F32).T.astype(x.dtype)


class Dims:
    def __init__(self, groups, prompt, pb, nc, ch, d, heads):
        self.G, self.P, self.PB, self.NC, self.CH, self.D = groups, prompt, pb, nc, ch, d
        self.NCH = nc * ch
        self.R = prompt + nc * CL
        self.NX = nc * CL
        self.NR = pb + self.NCH
        self.NP = groups * pb
        self.NT = groups * self.NR
        self.PAIRS = heads // 2
        self.COLS = 2 * self.NR


MESH = pl.DeviceIdType.MESH


def half_index():
    return lax.axis_index("dp") % 2


def block_index():
    return lax.axis_index("ctx") * 2 + half_index()


class Peers:
    def __init__(self):
        self.ctxs = lax.axis_size("ctx")
        self.chips = lax.axis_size("dp") // 2
        self.tps = lax.axis_size("tp")
        self.dp = lax.axis_index("dp")
        self.ctx = lax.axis_index("ctx")
        self.tp = lax.axis_index("tp")
        self.core = self.dp % 2
        self.chip = self.dp // 2

    def at(self, dp=None, ctx=None, tp=None):
        return {
            "dp": self.dp if dp is None else dp,
            "ctx": self.ctx if ctx is None else ctx,
            "tp": self.tp if tp is None else tp,
        }

    def across(self):
        return self.at(tp=1 - self.tp)

    def mate(self):
        return self.at(dp=self.chip * 2 + 1 - self.core)

    def chip_after(self, k):
        return lax.rem(self.chip + k, self.chips)

    def chip_before(self, k):
        return lax.rem(self.chip + self.chips - k, self.chips)

    def row(self, k):
        return self.at(dp=self.chip_after(k) * 2 + self.core)

    def ctx_after(self, k):
        return lax.rem(self.ctx + k, self.ctxs)

    def ctx_before(self, k):
        return lax.rem(self.ctx + self.ctxs - k, self.ctxs)

    def plane(self, k):
        return self.at(ctx=self.ctx_after(k))

    def partner(self):
        return self.at(dp=self.chip * 2 + self.tp, tp=self.core)

    def greet(self, trades=False):
        barrier = pltpu.get_barrier_semaphore()
        peers = [self.across(), self.mate()]
        peers += [self.row(k) for k in range(1, self.chips)]
        peers += [self.plane(k) for k in range(1, self.ctxs)]
        for peer in peers:
            pl.semaphore_signal(barrier, inc=1, device_id=peer, device_id_type=MESH)
        count = len(peers)
        if trades:
            away = self.core != self.tp

            @pl.when(away)
            def _():
                pl.semaphore_signal(
                    barrier, inc=1, device_id=self.partner(), device_id_type=MESH
                )

            count += jnp.where(away, 1, 0)
        pl.semaphore_wait(barrier, count)


def send(src, dst, send_sem, recv_sem, device):
    copy = pltpu.make_async_remote_copy(
        src_ref=src,
        dst_ref=dst,
        send_sem=send_sem,
        recv_sem=recv_sem,
        device_id=device,
        device_id_type=MESH,
    )
    copy.start()
    return copy


def arrived(ref, sem, peers):
    pltpu.make_async_remote_copy(
        src_ref=ref,
        dst_ref=ref,
        send_sem=sem,
        recv_sem=sem,
        device_id=peers.mate(),
        device_id_type=MESH,
    ).wait_recv()


class WeightGather:
    def __init__(self, peers, shard, full, left, sends, across, rows, mate):
        self.p, self.shard, self.full, self.left = peers, shard, full, left
        self.sends, self.across, self.rows, self.from_mate = sends, across, rows, mate
        self.copies = []
        self.size, self.cols = shard.shape

    @staticmethod
    def semaphores(chips):
        far = chips - 1
        return [
            pltpu.SemaphoreType.DMA((3 + 6 * far,)),
            pltpu.SemaphoreType.DMA((chips,)),
            pltpu.SemaphoreType.DMA((2, max(far, 1))),
            pltpu.SemaphoreType.DMA((2, chips)),
        ]

    def piece(self, tp, dp, cols=slice(None)):
        rows = pl.ds(pl.multiple_of(dp * self.size, 16), self.size)
        if cols == slice(None):
            return self.full.at[tp, rows, :]
        return self.full.at[tp, rows, pl.ds(cols.start, cols.stop - cols.start)]

    def go(self, src, dst, recv_sem, device):
        self.copies.append(send(src, dst, self.sends.at[len(self.copies)], recv_sem, device))

    def start(self):
        p = self.p
        self.go(self.shard, self.piece(p.tp, p.dp), self.across.at[0], p.across())
        for k in range(1, p.chips):
            self.go(self.shard, self.piece(p.tp, p.dp), self.rows.at[0, k - 1], p.row(k))
        self.go(self.shard, self.piece(p.tp, p.dp), self.from_mate.at[0, 0], p.mate())

    def relay_across(self):
        p = self.p
        got = self.piece(1 - p.tp, p.dp)
        arrived(got, self.across.at[0], p)
        part = self.piece(1 - p.tp, p.dp, slice(0, self.left))
        for k in range(1, p.chips):
            self.go(part, part, self.rows.at[1, k - 1], p.row(k))
        self.go(got, got, self.from_mate.at[1, 0], p.mate())

    def relay_rows(self):
        p = self.p
        for k in range(1, p.chips):
            dp = p.chip_before(k) * 2 + p.core
            got = self.piece(p.tp, dp)
            arrived(got, self.rows.at[0, k - 1], p)
            if self.left < self.cols:
                part = self.piece(p.tp, dp, slice(self.left, self.cols))
                self.go(part, part, self.across.at[k], p.across())
            self.go(got, got, self.from_mate.at[0, k], p.mate())

    def relay_last(self):
        p = self.p
        for k in range(1, p.chips):
            dp = p.chip_before(k) * 2 + p.core
            arrived(self.piece(1 - p.tp, dp, slice(0, self.left)), self.rows.at[1, k - 1], p)
            if self.left < self.cols:
                part = self.piece(1 - p.tp, dp, slice(self.left, self.cols))
                arrived(part, self.across.at[k], p)
            got = self.piece(1 - p.tp, dp)
            self.go(got, got, self.from_mate.at[1, k], p.mate())

    def finish(self):
        p = self.p
        for part in range(2):
            tp = p.tp if part == 0 else 1 - p.tp
            for k in range(p.chips):
                dp = p.chip_before(k) * 2 + 1 - p.core
                arrived(self.piece(tp, dp), self.from_mate.at[part, k], p)

    def drain(self):
        for copy in self.copies:
            copy.wait_send()


def twice(x):
    return jnp.concatenate([x, x], axis=1)


def fill_masks(dm, maskp, maskx):
    block = block_index()
    keys = lax.broadcasted_iota(jnp.int32, maskp.shape, 0)
    cols = lax.broadcasted_iota(jnp.int32, maskp.shape, 1) % dm.PB
    maskp[...] = jnp.where(keys <= cols + block * dm.PB, 0.0, NEG)
    keys = lax.broadcasted_iota(jnp.int32, maskx.shape, 0)
    cols = lax.broadcasted_iota(jnp.int32, maskx.shape, 1) % dm.NCH
    seen = (keys // CL == cols // dm.CH) & (
        keys % CL <= cols % dm.CH + half_index() * dm.CH
    )
    maskx[...] = jnp.where(seen, 0.0, NEG)


def heads_columns(a, b):
    lo_a, lo_b = sublane_pick(a.shape, True), sublane_pick(b.shape, True)
    zero_a, zero_b = jnp.zeros_like(a), jnp.zeros_like(b)
    return jnp.concatenate(
        [
            jnp.where(lo_a, a, zero_a),
            jnp.where(lo_a, zero_a, a),
            jnp.where(lo_b, b, zero_b),
            jnp.where(lo_b, zero_b, b),
        ],
        axis=1,
    )


def heads_rows(a, b):
    lo_a, lo_b = lane_pick(a.shape, True), lane_pick(b.shape, True)
    zero_a, zero_b = jnp.zeros_like(a), jnp.zeros_like(b)
    return jnp.concatenate(
        [
            jnp.where(lo_a, a, zero_a),
            jnp.where(lo_a, zero_a, a),
            jnp.where(lo_b, b, zero_b),
            jnp.where(lo_b, zero_b, b),
        ],
        axis=0,
    )


def forward_kernel(
    dm,
    left,
    prompt,
    cont,
    cos,
    sin,
    wq,
    wm,
    cot_p,
    cot_c,
    q_out,
    att_out,
    lse_out,
    ln_out,
    nt_hbm,
    own_nt_hbm,
    k_hbm,
    v_hbm,
    w_hbm,
    wm_out,
    own_p_hbm,
    own_c_hbm,
    cot_p_out,
    cot_c_out,
    nt_out,
    own_out,
    k_out,
    v_out,
    maskp,
    maskx,
    sbuf,
    all_rows,
    own_rows,
    xp,
    xc,
    w,
    put_sem,
    trade_send,
    trade_recv,
    x_send,
    x_plane,
    x_mate,
    c_send,
    c_mate,
    own_sem,
    *sems,
):
    G, R, PB, NCH, D, NP, NT = dm.G, dm.R, dm.PB, dm.NCH, dm.D, dm.NP, dm.NT
    NC, CH = dm.NC, dm.CH
    HC = (w.shape[2] - 128) // 3
    TP = w.shape[0]
    p = Peers()
    block = block_index()
    gq = WeightGather(p, wq, w, wq.shape[1], *sems[:4])
    gm = WeightGather(p, wm, wm_out, left, *sems[4:])
    size = wq.shape[0]
    mine = pl.ds(pl.multiple_of(p.dp * size, 16), size)

    landing = [xp.at[p.ctx * 2 + p.tp], xc.at[p.tp], cot_p_out, cot_c_out]

    def moved(i):
        src = [prompt, cont, cot_p, cot_c][i]
        return pltpu.make_async_remote_copy(
            src_ref=src,
            dst_ref=landing[i],
            send_sem=trade_send.at[i],
            recv_sem=trade_recv.at[i],
            device_id=p.partner(),
            device_id_type=MESH,
        )

    def kept(i):
        return pltpu.make_async_copy([prompt, cont, cot_p, cot_c][i], landing[i], trade_send.at[i])

    moves = p.core != p.tp

    def trade(i):
        @pl.when(moves)
        def _():
            moved(i).start()

        @pl.when(jnp.logical_not(moves))
        def _():
            kept(i).start()

    def traded(i):
        @pl.when(moves)
        def _():
            moved(i).wait_recv()

        @pl.when(jnp.logical_not(moves))
        def _():
            kept(i).wait()

    local = [
        pltpu.make_async_copy(wq, w.at[p.tp, mine, :], own_sem.at[0]),
        pltpu.make_async_copy(wm, wm_out.at[p.tp, mine, :], own_sem.at[1]),
    ]
    for copy in local:
        copy.start()
    p.greet(trades=True)
    trade(0)
    gq.start()
    trade(1)
    fill_masks(dm, maskp, maskx)
    traded(0)
    own = xp.at[block]
    sent = []
    for k in range(1, p.ctxs):
        sent.append(send(own, own, x_send.at[k - 1], x_plane.at[k - 1], p.plane(k)))
    sent.append(send(own, own, x_send.at[p.ctxs - 1], x_mate.at[0], p.mate()))
    gq.relay_across()
    gq.relay_rows()
    traded(1)
    sent.append(send(xc.at[p.core], xc.at[p.core], c_send, c_mate, p.mate()))
    gq.relay_last()
    gm.start()
    trade(2)
    trade(3)
    gq.finish()
    local[0].wait()
    puts = [
        pltpu.make_async_copy(w, w_hbm, put_sem.at[0]),
        pltpu.make_async_copy(xp.at[block], own_p_hbm, put_sem.at[1]),
        pltpu.make_async_copy(xc.at[p.core], own_c_hbm, put_sem.at[2]),
    ]
    for put in puts:
        put.start()
    ln = w[0, :, 3 * HC :].astype(F32).T[:8, :]
    ln_out[...] = ln
    gain, bias = ln[0:1, :], ln[1:2, :]

    def normed(x):
        hat, _ = norm_stats(x.astype(F32))
        return (hat * gain + bias).astype(BF16)

    def turned(x, table):
        rows = x.shape[0]
        return rotate(x, cos[pl.ds(table, rows), :], sin[pl.ds(table, rows), :])

    x = jnp.concatenate([xp[block].reshape(NP, D), xc[p.core].reshape(NT - NP, D)], axis=0)
    n = normed(x)
    own_rows[...] = n
    places = [(g * PB, PB, pl.multiple_of(block * PB, PB)) for g in range(G)]
    places += [
        (NP + i * CH, CH, pl.multiple_of(dm.P + p.core * CH, CH)) for i in range(G * NC)
    ]
    for t in range(TP):
        qq = dot(n, w[t, :, :HC])
        for first, count, table in places:
            for j in range(HC // 128):
                tile = turned(qq[first : first + count, j * 128 : (j + 1) * 128], table).astype(BF16)
                q_out[first : first + count, t * HC + j * 128 : t * HC + (j + 1) * 128] = (
                    tile.astype(F32) * 0.125
                ).astype(BF16)
    own_out[...] = transpose(own_rows[...])

    def keys_values(x, places):
        n = normed(x)
        for first, count, g, row, table in places:
            all_rows[pl.ds(pl.multiple_of(g * R + row, 16), count), :] = n[first : first + count]
        for t in range(TP):
            kk = dot(n, w[t, :, HC : 2 * HC])
            for first, count, g, row, table in places:
                for j in range(HC // 128):
                    tile = turned(kk[first : first + count, j * 128 : (j + 1) * 128], table)
                    k_out[g, pl.ds(row, count), t * HC + j * 128 : t * HC + (j + 1) * 128] = tile.astype(BF16)
            vv = dot(n, w[t, :, 2 * HC : 3 * HC]).astype(BF16)
            for first, count, g, row, table in places:
                v_out[g, pl.ds(row, count), t * HC : (t + 1) * HC] = vv[first : first + count]

    arrived(xc.at[1 - p.core], c_mate, p)
    x = [xc[e, g, c] for g in range(G) for c in range(NC) for e in range(2)]
    keys_values(
        jnp.concatenate(x, axis=0),
        [((g * NC + c) * CL, CL, g, dm.P + c * CL, dm.P) for g in range(G) for c in range(NC)],
    )

    def relay(k):
        b = p.ctx_before(k) * 2 + p.core
        return pltpu.make_async_remote_copy(
            src_ref=xp.at[b],
            dst_ref=xp.at[b],
            send_sem=x_send.at[p.ctxs + k - 1],
            recv_sem=x_mate.at[k],
            device_id=p.mate(),
            device_id_type=MESH,
        )

    def plane(k, carry):
        c = p.ctx_before(k)

        @pl.when(k > 0)
        def _():
            arrived(xp.at[c * 2 + p.core], x_plane.at[k - 1], p)
            relay(k).start()

        arrived(xp.at[c * 2 + 1 - p.core], x_mate.at[k], p)
        x = xp[pl.ds(c * 2, 2)].reshape(2 * NP, D)
        places = []
        for e in range(2):
            row = pl.multiple_of((c * 2 + e) * PB, PB)
            places += [((e * G + g) * PB, PB, g, row, row) for g in range(G)]
        keys_values(x, places)
        return carry

    lax.fori_loop(0, p.ctxs, plane, 0)
    puts += [
        pltpu.make_async_copy(k_out, k_hbm, put_sem.at[3]),
        pltpu.make_async_copy(v_out, v_hbm, put_sem.at[4]),
    ]
    for put in puts[3:]:
        put.start()

    def turn(i, carry):
        rows = pl.ds(pl.multiple_of(i * 256, 256), 256)
        nt_out[:, rows] = transpose(all_rows[rows, :])
        return carry

    lax.fori_loop(0, G * R // 256, turn, 0)
    puts += [
        pltpu.make_async_copy(nt_out, nt_hbm, put_sem.at[5]),
        pltpu.make_async_copy(own_out, own_nt_hbm, put_sem.at[6]),
    ]
    for put in puts[5:]:
        put.start()
    gm.relay_across()
    gm.relay_rows()

    TILE = 256
    tiles = dm.P // TILE

    def attend(i, carry):
        g, pair = i // dm.PAIRS, i % dm.PAIRS
        lanes = pl.ds(pl.multiple_of(pair * 128, 128), 128)
        qp = q_out[pl.ds(pl.multiple_of(g * PB, PB), PB), lanes]
        qc = q_out[pl.ds(pl.multiple_of(dm.NP + g * NCH, NCH), NCH), lanes]
        qt = heads_columns(transpose(qp), transpose(qc))
        top = None
        for j in range(tiles):
            s = dot(k_out[g, j * TILE : (j + 1) * TILE, lanes], qt)
            sbuf[j * TILE : (j + 1) * TILE, : 2 * PB] = (
                s[:, : 2 * PB] + twice(maskp[j * TILE : (j + 1) * TILE, :])
            )
            sbuf[j * TILE : (j + 1) * TILE, 2 * PB :] = s[:, 2 * PB :]
            here = jnp.max(sbuf[j * TILE : (j + 1) * TILE, :], axis=0, keepdims=True)
            top = here if top is None else jnp.maximum(top, here)
        sx = dot(k_out[g, dm.P :, lanes], qt[:, 2 * PB :]) + maskx[...]
        topx = jnp.max(sx, axis=0, keepdims=True)
        top = jnp.concatenate([top[:, : 2 * PB], jnp.maximum(top[:, 2 * PB :], topx)], axis=1)
        total, acc = None, None
        for j in range(tiles):
            e = jnp.exp(sbuf[j * TILE : (j + 1) * TILE, :] - top)
            here = jnp.sum(e, axis=0, keepdims=True)
            vt = transpose(v_out[g, j * TILE : (j + 1) * TILE, lanes])
            part = dot(vt, e.astype(BF16))
            total = here if total is None else total + here
            acc = part if acc is None else acc + part
        ex = jnp.exp(sx - top[:, 2 * PB :])
        partx = dot(transpose(v_out[g, dm.P :, lanes]), ex.astype(BF16))
        totalx = jnp.sum(ex, axis=0, keepdims=True)
        total = jnp.concatenate([total[:, : 2 * PB], total[:, 2 * PB :] + totalx], axis=1)
        acc_p = acc[:, : 2 * PB] / total[:, : 2 * PB]
        acc_c = (acc[:, 2 * PB :] + partx) / total[:, 2 * PB :]
        lse_out[i] = top + jnp.log(total)
        outp = jnp.where(sublane_pick((128, PB), True), acc_p[:, :PB], acc_p[:, PB:])
        outc = jnp.where(sublane_pick((128, NCH), True), acc_c[:, :NCH], acc_c[:, NCH:])
        att_out[pl.ds(pl.multiple_of(g * PB, PB), PB), lanes] = outp.T.astype(BF16)
        att_out[pl.ds(pl.multiple_of(dm.NP + g * NCH, NCH), NCH), lanes] = outc.T.astype(BF16)
        return carry

    lax.fori_loop(0, G * dm.PAIRS, attend, 0)
    gm.relay_last()
    gm.finish()
    gq.drain()
    gm.drain()
    for copy in sent:
        copy.wait_send()
    for k in range(1, p.ctxs):
        relay(k).wait_send()
    local[1].wait()
    for i in (2, 3):
        traded(i)

    @pl.when(moves)
    def _():
        for i in range(4):
            moved(i).wait_send()

    for put in puts:
        put.wait()


class Reduce:
    REFS = 13

    def __init__(self, p, cross_first, refs):
        self.p, self.n, self.cross_first = p, len(cross_first), cross_first
        self.mine, self.got, self.row, self.acr, self.zin = refs[:5]
        self.sc, self.rc, self.sy, self.ry, self.sx, self.rx, self.sz, self.rz = refs[5:13]
        mid = p.ctxs // 2
        self.centre = (p.ctx == mid - 1) | (p.ctx == mid)
        self.outer = (p.ctx > 0) & (p.ctx < p.ctxs - 1)
        step = jnp.where(p.ctx < mid, 1, -1)
        self.inner_at = p.ctx + step
        self.outer_at = jnp.clip(p.ctx - step, 0, p.ctxs - 1)

    @staticmethod
    def scratch(cross_first, chips, size, width):
        n = len(cross_first)
        dma = pltpu.SemaphoreType.DMA
        far = max(chips - 1, 1)
        rows = n + sum(1 for c in cross_first if not c)
        return [
            pltpu.VMEM((2, chips * 2 * size, width), BF16),
            pltpu.VMEM((2 * n, chips, size, width), BF16),
            pltpu.VMEM((rows, far, size, width), BF16),
            pltpu.VMEM((n, chips, size, width), BF16),
            pltpu.VMEM((n, 2, size, width), BF16),
            dma((2 * n, chips)),
            dma((2 * n, chips)),
            dma((2 * n, far)),
            dma((2 * n, far)),
            dma((n,)),
            dma((n,)),
            dma((n, 2)),
            dma((n, 2)),
        ]

    def copy(self, src, dst, send_sem, recv_sem, device):
        return pltpu.make_async_remote_copy(
            src_ref=src,
            dst_ref=dst,
            send_sem=send_sem,
            recv_sem=recv_sem,
            device_id=device,
            device_id_type=MESH,
        )

    def crosses(self, i):
        return self.cross_first[i % self.n]

    def travels(self, i):
        return i >= self.n or not self.crosses(i)

    def mine_of(self, y, core):
        size = self.got.shape[2]
        return pl.ds(pl.multiple_of((2 * y + core) * size, 16), size)

    def by_core(self, i, slot, y):
        p = self.p
        return self.copy(
            self.mine.at[slot, self.mine_of(y, 1 - p.core), :],
            self.got.at[i, y],
            self.sc.at[i, y],
            self.rc.at[i, y],
            p.mate(),
        )

    def row_slot(self, i):
        return sum(1 for e in range(i) if self.travels(e))

    def by_row(self, i, k):
        p = self.p
        return self.copy(
            self.got.at[i, p.chip_after(k)],
            self.row.at[self.row_slot(i), k - 1],
            self.sy.at[i, k - 1],
            self.ry.at[i, k - 1],
            p.row(k),
        )

    def by_tp(self, j):
        p = self.p
        part = slice(None) if self.crosses(j) else p.chip
        return self.copy(
            self.got.at[j, part], self.acr.at[j, part], self.sx.at[j], self.rx.at[j], p.across()
        )

    def inward(self, j):
        slot = jnp.where(self.centre, 1, 0)
        return self.copy(
            self.got.at[self.n + j, self.p.chip],
            self.zin.at[j, slot],
            self.sz.at[j, 0],
            self.rz.at[j, slot],
            self.p.at(ctx=self.inner_at),
        )

    def outward(self, j):
        return self.copy(
            self.got.at[self.n + j, self.p.chip],
            self.zin.at[j, 1],
            self.sz.at[j, 1],
            self.rz.at[j, 1],
            self.p.at(ctx=self.outer_at),
        )

    def add(self, i, y, other):
        self.got[i, y] = (self.got[i, y].astype(F32) + other.astype(F32)).astype(BF16)

    def cores_send(self, i, slot):
        for y in range(self.p.chips):
            self.by_core(i, slot, y).start()

    def cores_sent(self, i, slot):
        for y in range(self.p.chips):
            self.by_core(i, slot, y).wait_send()

    def rows_send(self, i):
        for k in range(1, self.p.chips):
            self.by_row(i, k).start()

    def cores_sum(self, i, slot):
        p = self.p
        for y in range(p.chips):
            self.by_core(i, slot, y).wait_recv()
            self.add(i, y, self.mine[slot, self.mine_of(y, p.core), :])
        if not self.crosses(i):
            self.rows_send(i)
        elif i < self.n:
            self.by_tp(i).start()

    def cross_sum(self, j):
        self.by_tp(j).wait_recv()
        for y in range(self.p.chips):
            self.add(self.n + j, y, self.acr[j, y])
        self.rows_send(self.n + j)

    def rows_sum(self, i):
        p = self.p
        for k in range(1, p.chips):
            self.by_row(i, k).wait_recv()
            self.add(i, p.chip, self.row[self.row_slot(i), k - 1])
        if i < self.n:
            self.by_tp(i).start()
            return
        j = i - self.n
        if not self.crosses(i):
            self.by_tp(j).wait_recv()
            self.add(i, p.chip, self.acr[j, p.chip])

        @pl.when(jnp.logical_not(self.outer))
        def _():
            self.inward(j).start()

    def ctx_in(self, j):
        @pl.when(self.outer)
        def _():
            pltpu.make_async_copy(self.zin.at[j, 0], self.zin.at[j, 0], self.rz.at[j, 0]).wait()
            self.add(self.n + j, self.p.chip, self.zin[j, 0])
            self.inward(j).start()

    def ctx_mid(self, j):
        @pl.when(self.centre)
        def _():
            self.from_inner(j)
            self.add(self.n + j, self.p.chip, self.zin[j, 1])

            @pl.when(self.outer)
            def _():
                self.outward(j).start()

    def ctx_end(self, j):
        @pl.when(jnp.logical_not(self.centre))
        def _():
            self.from_inner(j)
            self.got[self.n + j, self.p.chip] = self.zin[j, 1]

            @pl.when(self.outer)
            def _():
                self.outward(j).start()

    def from_inner(self, j):
        pltpu.make_async_copy(self.zin.at[j, 1], self.zin.at[j, 1], self.rz.at[j, 1]).wait()
        self.inward(j).wait_send()

    def result(self, j):
        return self.got[self.n + j, self.p.chip].astype(F32)

    def drain(self):
        p = self.p
        for i in range(2 * self.n):
            if self.travels(i):
                for k in range(1, p.chips):
                    self.by_row(i, k).wait_send()
        for j in range(self.n):
            self.by_tp(j).wait_send()

            @pl.when(self.outer)
            def _():
                self.outward(j).wait_send()


def small_sum(p, sm, near, rows, across, planes, ss, rc, ry, rx, rz):
    copies = []

    def go(src, dst, recv_sem, device):
        copies.append(send(src, dst, ss.at[len(copies)], recv_sem, device))

    go(sm, near, rc, p.mate())
    copies[-1].wait_recv()
    rows[p.chip] = sm[...] + near[...]
    for k in range(1, p.chips):
        go(rows.at[p.chip], rows.at[p.chip], ry.at[k - 1], p.row(k))
    for k in range(1, p.chips):
        arrived(rows.at[p.chip_before(k)], ry.at[k - 1], p)
    total = rows[0]
    for y in range(1, p.chips):
        total += rows[y]
    across[0] = total
    go(across.at[0], across.at[1], rx, p.across())
    copies[-1].wait_recv()
    planes[p.ctx] = across[0] + across[1]
    for k in range(1, p.ctxs):
        go(planes.at[p.ctx], planes.at[p.ctx], rz.at[k - 1], p.plane(k))
    for k in range(1, p.ctxs):
        arrived(planes.at[p.ctx_before(k)], rz.at[k - 1], p)
    total = planes[0]
    for z in range(1, p.ctxs):
        total += planes[z]
    for copy in copies:
        copy.wait_send()
    return total


def schedule(ra, rb, on, pairs, planes):
    n, nb = ra.n, rb.n
    for i in range(2 * n - 1):
        if i == 2:
            on(("m", 3), partial(ra.rows_sum, 0))
        on(("m", i + 1), partial(ra.cores_sum, (i % 2) * n + i // 2, i % 2))
    on(("e", 0), partial(ra.rows_sum, n))
    on(("e", 0), partial(ra.cores_sum, 2 * n - 1, 1))
    on(("a", 0), partial(rb.cores_sum, 0, 0))
    on(("a", 0), partial(rb.cores_sum, nb, 1))
    on(("a", 2), partial(ra.rows_sum, 2))
    on(("a", 3), partial(rb.cross_sum, 0))
    on(("a", 4), partial(ra.ctx_in, 0))
    on(("a", 5), partial(ra.cross_sum, 1))
    last = pairs
    on(("a", last - 1), partial(rb.rows_sum, nb))
    on(("a", last), partial(ra.ctx_mid, 0))
    on(("a", last + 1), partial(ra.rows_sum, n + 1))
    on(("a", last + 1), partial(ra.rows_sum, n + 2))
    on(("a", last + 1), partial(rb.ctx_in, 0))
    on(("a", last + 3), partial(rb.ctx_mid, 0))
    on(("a", last + 5), partial(ra.ctx_in, 1))
    for i in range(pairs - 1):
        on(("a", last + 1 + i), partial(rb.cores_sum, (i % 2) * nb + 1 + i // 2, i % 2))
    on(("a", last + 3), partial(rb.cross_sum, 1))
    on(("a", last + 5), partial(rb.cross_sum, 2))
    on(("a", last + 5), partial(rb.rows_sum, nb + 1))
    on(("p", planes), partial(rb.cores_sum, 2 * nb - 1, 1))
    on(("p", planes), partial(rb.rows_sum, nb - 1))
    on(("p", planes + 1), partial(rb.rows_sum, nb + 2))
    on(("p", planes + 1), partial(rb.ctx_in, 1))
    on(("p", planes + 2), partial(ra.ctx_in, 2))
    on(("p", planes + 2), partial(ra.ctx_mid, 1))
    on(("t", 0), partial(rb.rows_sum, 2 * nb - 1))
    on(("t", 1), partial(rb.ctx_in, 2))
    on(("t", 2), partial(rb.ctx_mid, 1))
    on(("t", 3), partial(ra.ctx_mid, 2))
    on(("t", 4), partial(rb.ctx_in, 3))
    on(("t", 5), partial(rb.ctx_mid, 2))
    on(("t", 11), partial(rb.ctx_mid, 3))


def backward_kernel(
    dm,
    T,
    FC,
    plan_a,
    plan_b,
    mix,
    att,
    own_p,
    own_c,
    cot_p,
    cot_c,
    ln,
    q,
    lse,
    cos,
    sin,
    wm,
    k_hbm,
    v_hbm,
    nt_hbm,
    own_nt_hbm,
    wq_hbm,
    home_arrays_p,
    home_arrays_c,
    early_p,
    early_c,
    home_cot_p,
    home_cot_c,
    out_p,
    out_c,
    gin_p,
    gin_c,
    gq_out,
    go_out,
    gu_out,
    gd_out,
    small_out,
    resid,
    blk,
    gh,
    wo,
    ring,
    gatt,
    nt,
    own_nt,
    maskp,
    maskx,
    kbuf,
    vbuf,
    dk,
    dv,
    dq,
    dxm,
    dxz,
    dxcm,
    blk_away,
    blk_home,
    gin_home,
    put_sem,
    ring_sem,
    wo_sem,
    kv_sem,
    nt_sem,
    wq_sem,
    home_sem,
    b_send,
    b_recv,
    g_send,
    g_recv,
    m_send,
    m_recv,
    z_send,
    z_recv,
    c_send,
    c_recv,
    sm,
    sm_near,
    sm_rows,
    sm_across,
    sm_planes,
    sm_ss,
    sm_rc,
    sm_ry,
    sm_rx,
    sm_rz,
    *refs,
):
    G, R, PB, NCH, D, NX, NP, NT = dm.G, dm.R, dm.PB, dm.NCH, dm.D, dm.NX, dm.NP, dm.NT
    TP, HC = wo.shape[0], wo.shape[2]
    PT = dm.PAIRS // TP
    p = Peers()
    n_a, NB = len(plan_a), len(plan_b)
    ra = Reduce(p, plan_a, refs[: Reduce.REFS])
    rb = Reduce(p, plan_b, refs[Reduce.REFS :])
    block = block_index()
    TILE = 256
    tiles = dm.P // TILE
    chips = p.chips
    S = D // (2 * chips)

    def begin(copies):
        for copy in copies:
            copy.start()

    def ready(copies):
        for copy in copies:
            copy.wait()

    def load_tile(i, slot):
        t = jnp.where(lax.rem(i, 2) == 0, 1 - p.tp, p.tp)
        first = pl.multiple_of(HC + i // 2 * T, 128)
        return [
            pltpu.make_async_copy(
                wm.at[t, :, pl.ds(first, T)], ring.at[slot, :, pl.ds(0, T)], ring_sem.at[0, slot]
            ),
            pltpu.make_async_copy(
                wm.at[t, :, pl.ds(first + FC, T)], ring.at[slot, :, pl.ds(T, T)], ring_sem.at[1, slot]
            ),
        ]

    def pair_at(it):
        turn = it % dm.PAIRS
        return jnp.where(turn % 2 == 0, 1 - p.tp, p.tp) * PT + turn // 2

    def load_kv(it, slot):
        pair, g = pair_at(it), it // dm.PAIRS
        lanes = pl.ds(pl.multiple_of(pair * 128, 128), 128)
        return [
            pltpu.make_async_copy(k_hbm.at[g, :, lanes], kbuf.at[slot], kv_sem.at[0, slot]),
            pltpu.make_async_copy(v_hbm.at[g, :, lanes], vbuf.at[slot], kv_sem.at[1, slot]),
        ]

    wo_load = pltpu.make_async_copy(wm.at[:, :, pl.ds(0, HC)], wo, wo_sem)
    wo_load.start()
    begin(load_tile(0, 0))
    begin(load_kv(0, 0))
    p.greet(trades=True)
    fill_masks(dm, maskp, maskx)
    gain_two, bias_two = ln[2:3, :], ln[3:4, :]

    hn, gd = slice(0, NT), slice(NT, 2 * NT)
    STEP = 128

    def by_rows(step):
        def prompt_part(i, carry):
            rows = pl.ds(pl.multiple_of(i * STEP, STEP), STEP)
            step(own_p[rows, :], cot_p[rows, :], i * STEP)
            return carry

        def cont_part(i, carry):
            rows = pl.ds(pl.multiple_of(i * STEP, STEP), STEP)
            step(own_c[rows, :], cot_c[rows, :], NP + i * STEP)
            return carry

        lax.fori_loop(0, NP // STEP, prompt_part, 0)
        lax.fori_loop(0, (NT - NP) // STEP, cont_part, 0)

    def shifted(first, row):
        return pl.ds(pl.multiple_of(first + row, STEP), STEP)

    wo_load.wait()

    def enter(x, cot, row):
        rows = shifted(0, row)
        r = x.astype(F32)
        for t in range(TP):
            r += dot_nt(att[rows, t * HC : (t + 1) * HC], wo[t])
        resid[rows, :] = r
        blk[rows, :] = r
        h, _ = norm_stats(r)
        n = (h * gain_two + bias_two).astype(BF16)
        dk[rows, :] = n
        nt[:, rows] = transpose(n)
        g = (mix[4] * cot.astype(F32)).astype(BF16)
        dk[shifted(NT, row), :] = g
        nt[:, shifted(NT, row)] = transpose(g)
        gh[rows, :] = jnp.zeros((STEP, D), F32)

    by_rows(enter)

    during = {}

    def on(stage, step):
        during.setdefault(stage, []).append(step)

    def run_when(index, name):
        for (kind, when), steps in during.items():
            if kind == name:

                @pl.when(index == when)
                def _():
                    for step in steps:
                        step()

    schedule(ra, rb, on, dm.PAIRS, p.ctxs)

    def run(name):
        for kind, when in sorted(key for key in during if key[0] == name):
            for step in during[kind, when]:
                step()

    def feed(i, carry):
        slot = lax.rem(i, 2)

        @pl.when(i + 1 < 2 * n_a)
        def _():
            begin(load_tile(i + 1, 1 - slot))

        ready(load_tile(i, slot))
        up, dn = ring[slot, :, :T], ring[slot, :, T : 2 * T]
        c0 = 0.7978845608028654
        HALF = NT // 2
        for e in range(2):
            rows = slice(e * HALF, (e + 1) * HALF)
            u = dot(dk[rows, :], up)
            if e == 1:
                run_when(i, "m")
            u2 = u * u
            th = jnp.tanh(c0 * u * (1.0 + 0.044715 * u2))
            half = 0.5 * (1.0 + th)
            act = (u * half).astype(BF16)
            slope = half + 0.5 * u * (1.0 - th * th) * (c0 * (1.0 + 3 * 0.044715 * u2))
            dv[rows, :T] = act
            blk[rows, :] += dot_nt(act, dn)
            gu = (dot(dk[NT + e * HALF : NT + (e + 1) * HALF, :], dn) * slope).astype(BF16)
            dv[NT + e * HALF : NT + (e + 1) * HALF, :T] = gu
            gh[rows, :] += dot_nt(gu, up)

        @pl.when(i >= 2)
        def _():
            ra.cores_sent(slot * n_a + i // 2 - 1, slot)

        for y in range(chips):
            mine = slice(y * 2 * S, (y + 1) * 2 * S)
            ra.mine[slot, mine, :T] = dot(nt[mine, hn], dv[gd, :T]).astype(BF16)
            ra.mine[slot, mine, T:] = dot(nt[mine, gd], dv[hn, :T]).astype(BF16)
        ra.cores_send(slot * n_a + i // 2, slot)
        return carry

    lax.fori_loop(0, 2 * n_a, feed, 0)
    run("e")
    blk_away[:NT, :] = blk[...].astype(BF16)
    away = ra.copy(blk_away.at[pl.ds(0, NT), :], blk_home, b_send, b_recv, p.partner())

    @pl.when(p.core != p.tp)
    def _():
        away.start()

    @pl.when(p.core == p.tp)
    def _():
        blk_home[...] = blk_away[:NT, :]

    sm[...] = jnp.zeros_like(sm)

    def leave(x, cot, row):
        rows = shifted(0, row)
        cot = cot.astype(F32)
        sm[2:3, :] += jnp.sum(cot * blk[rows, :], axis=0, keepdims=True)
        h, scale = norm_stats(resid[rows, :])
        g = gh[rows, :]
        sm[0:1, :] += jnp.sum(g * h, axis=0, keepdims=True)
        sm[1:2, :] += jnp.sum(g, axis=0, keepdims=True)
        gr = mix[4] * cot + norm_back(g, gain_two, h, scale)
        resid[rows, :] = gr
        gb = gr.astype(BF16)
        nt[:, shifted(NT, row)] = transpose(gb)
        for t in range(TP):
            gatt[rows, t * HC : (t + 1) * HC] = dot(gb, wo[t]).astype(BF16)

    by_rows(leave)
    for slot, i in enumerate((0, NB)):
        t = p.tp if slot else 1 - p.tp
        lanes = pl.ds(pl.multiple_of(t * HC, 128), HC)
        for y in range(chips):
            mine = slice(y * 2 * S, (y + 1) * 2 * S)
            rb.mine[slot, mine, :] = dot(nt[mine, gd], att[:, lanes]).astype(BF16)
        rb.cores_send(i, slot)
    nt_load = [
        pltpu.make_async_copy(nt_hbm, nt, nt_sem.at[0]),
        pltpu.make_async_copy(own_nt_hbm, own_nt, nt_sem.at[1]),
    ]
    begin(nt_load)
    wq_load = pltpu.make_async_copy(wq_hbm.at[:, :, pl.ds(0, 3 * HC)], ring.at[:, :, pl.ds(0, 3 * HC)], wq_sem)
    wq_load.start()
    during.setdefault(("a", dm.PAIRS), []).insert(0, partial(ready, nt_load))

    def attend(turn, g):
        it = g * dm.PAIRS + turn
        pair = pair_at(it)
        slot = it % 2

        @pl.when(it + 1 < G * dm.PAIRS)
        def _():
            begin(load_kv(it + 1, 1 - slot))

        lanes = pl.ds(pl.multiple_of(pair * 128, 128), 128)
        rp = pl.ds(pl.multiple_of(g * PB, PB), PB)
        rc = pl.ds(pl.multiple_of(dm.NP + g * NCH, NCH), NCH)
        qp, qc = q[rp, lanes], q[rc, lanes]
        gp, gc = gatt[rp, lanes], gatt[rc, lanes]
        ap, ac = att[rp, lanes].astype(F32), att[rc, lanes].astype(F32)
        qt = heads_columns(transpose(qp), transpose(qc))
        gpt, gct = gp.astype(F32).T, gc.astype(F32).T
        gt = heads_columns(gpt.astype(BF16), gct.astype(BF16))
        qs, gs = heads_rows(qp, qc), heads_rows(gp, gc)
        prodp, prodc = gpt * ap.T, gct * ac.T
        delta = jnp.concatenate(
            [
                jnp.sum(prodp[:HD], axis=0, keepdims=True),
                jnp.sum(prodp[HD:], axis=0, keepdims=True),
                jnp.sum(prodc[:HD], axis=0, keepdims=True),
                jnp.sum(prodc[HD:], axis=0, keepdims=True),
            ],
            axis=1,
        )
        stat = lse[g * dm.PAIRS + pair]
        ready(load_kv(it, slot))

        def grads(s, kt, vt, cols):
            pr = jnp.exp(s - stat[:, cols:])
            dp = dot(vt, gt[:, cols:])
            ds = (pr * (dp - delta[:, cols:])).astype(BF16)
            gv = dot(pr.astype(BF16), gs[cols:])
            gk = dot(ds, qs[cols:])
            gq = dot(transpose(kt), ds)
            return gk, gv, gq

        acc = None
        for j in range(tiles):
            rows = slice(j * TILE, (j + 1) * TILE)
            kt = kbuf[slot, rows, :]
            s = dot(kt, qt)
            s = jnp.concatenate([s[:, : 2 * PB] + twice(maskp[rows, :]), s[:, 2 * PB :]], axis=1)
            gk, gv, gq = grads(s, kt, vbuf[slot, rows, :], 0)
            gk = rotate_back(gk, cos[rows, :], sin[rows, :]).astype(BF16)
            gv = gv.astype(BF16)
            out = pl.ds(pl.multiple_of(g * R + j * TILE, 128), TILE)
            dk[out, lanes] = gk
            dv[out, lanes] = gv
            if j == tiles // 2:
                run_when(it, "a")
            acc = gq if acc is None else acc + gq
        kt = kbuf[slot, dm.P :, :]
        s = dot(kt, qt[:, 2 * PB :]) + maskx[...]
        gk, gv, gq = grads(s, kt, vbuf[slot, dm.P :, :], 2 * PB)
        for c in range(dm.NC):
            rows = slice(dm.P, dm.P + CL)
            out = pl.ds(pl.multiple_of(g * R + dm.P + c * CL, CL), CL)
            part = rotate_back(gk[c * CL : (c + 1) * CL], cos[rows, :], sin[rows, :])
            dk[out, lanes] = part.astype(BF16)
            dv[out, lanes] = gv[c * CL : (c + 1) * CL].astype(BF16)
        accp = acc[:, : 2 * PB] * 0.125
        accc = (acc[:, 2 * PB :] + gq) * 0.125
        outp = jnp.where(sublane_pick((128, PB), True), accp[:, :PB], accp[:, PB:]).T
        outc = jnp.where(sublane_pick((128, NCH), True), accc[:, :NCH], accc[:, NCH:]).T
        tab = pl.ds(pl.multiple_of(block * PB, PB), PB)
        dq[rp, lanes] = rotate_back(outp, cos[tab, :], sin[tab, :]).astype(BF16)
        tab = pl.ds(pl.multiple_of(dm.P + p.core * dm.CH, dm.CH), dm.CH)
        for c in range(dm.NC):
            part = rotate_back(outc[c * dm.CH : (c + 1) * dm.CH], cos[tab, :], sin[tab, :])
            rows = pl.ds(pl.multiple_of(dm.NP + g * NCH + c * dm.CH, dm.CH), dm.CH)
            dq[rows, lanes] = part.astype(BF16)

        @pl.when(g == G - 1)
        def _():
            put = turn % 2
            index = put * NB + 1 + turn // 2
            rb.cores_sent(index - 1, put)
            both = jnp.concatenate([dk[:, lanes], dv[:, lanes]], axis=1)
            for y in range(chips):
                mine = slice(y * 2 * S, (y + 1) * 2 * S)
                rb.mine[put, mine, 128:] = dot(nt[mine, :], both).astype(BF16)
                rb.mine[put, mine, :128] = dot(own_nt[mine, :], dq[:, lanes]).astype(BF16)
            rb.cores_send(index, put)

        return g

    w = ring

    def project(rows):
        total = None
        for t in range(TP):
            part = dot_nt(dk[rows, t * HC : (t + 1) * HC], w[t, :, HC : 2 * HC])
            total = part if total is None else total + part
            total += dot_nt(dv[rows, t * HC : (t + 1) * HC], w[t, :, 2 * HC : 3 * HC])
        return total

    NCONT = NT - NP
    gain_one = ln[0:1, :]
    halves = lambda core, g: pl.ds(pl.multiple_of(core * NCONT + g * NCH, 16), NCH)

    def dx_at(g, k, first, count):
        c = p.ctx_after(k)
        if g == G - 1:
            return dk.at[pl.ds(pl.multiple_of(g * R + c * 2 * PB + first, PB), count), :]
        fit = D // (2 * PB)
        row = pl.multiple_of(c % fit * 2 * PB + first, PB)
        return ra.mine.at[c // fit, pl.ds(row, count), pl.ds(0, D)]

    def dx_rows(g, k, core):
        return dx_at(g, k, core * PB, PB)

    def to_mate(g, k):
        i = g * p.ctxs + k
        return ra.copy(dx_rows(g, k, 1 - p.core), dxm.at[i], m_send.at[i], m_recv.at[i], p.mate())

    def to_plane(g, k):
        i = g * (p.ctxs - 1) + k - 1
        return ra.copy(
            dx_rows(g, k, p.core), dxz.at[i], z_send.at[i], z_recv.at[i], p.at(ctx=p.ctx_after(k))
        )

    def each_group(g, step):
        for e in range(G):

            @pl.when(g == e)
            def _():
                step(e)

    def cont_copy(g):
        return ra.copy(
            blk_away.at[halves(1 - p.core, g), :],
            dxcm.at[pl.ds(pl.multiple_of(g * NCH, 16), NCH), :],
            c_send.at[g],
            c_recv.at[g],
            p.mate(),
        )

    def group(g, carry):
        lax.fori_loop(0, dm.PAIRS, attend, g)

        @pl.when(g == 0)
        def _():
            wq_load.wait()
            ra.cores_sent(n_a - 1, 0)
            ra.cores_sent(2 * n_a - 1, 1)

            @pl.when(p.core != p.tp)
            def _():
                away.wait_send()

        def planes(i, carry):
            k = lax.rem(i + 1, p.ctxs)
            both = pl.ds(pl.multiple_of(g * R + p.ctx_after(k) * 2 * PB, 2 * PB), 2 * PB)
            total = project(both).astype(BF16)

            def out(e):
                dx_at(e, k, 0, 2 * PB)[...] = total
                to_mate(e, k).start()

            each_group(g, out)
            run_when(g * p.ctxs + i, "p")

            def back(e):
                to_mate(e, k).wait_recv()
                mine = dx_rows(e, k, p.core)
                mine[...] = (mine[...].astype(F32) + dxm[e * p.ctxs + k].astype(F32)).astype(BF16)

                @pl.when(k > 0)
                def _():
                    to_plane(e, k).start()

            each_group(g, back)
            return carry

        lax.fori_loop(0, p.ctxs, planes, 0)
        rows = pl.ds(pl.multiple_of(g * R + dm.P, CL), NX)
        total = project(rows).astype(BF16)
        for c in range(dm.NC):
            for e in range(2):
                out = pl.ds(pl.multiple_of(e * NCONT + g * NCH + c * dm.CH, dm.CH), dm.CH)
                blk_away[out, :] = total[c * CL + e * dm.CH : c * CL + (e + 1) * dm.CH]
        cont_copy(g).start()
        for first, count in ((g * PB, PB), (NP + g * NCH, NCH)):
            rows = pl.ds(pl.multiple_of(first, 16), count)
            total = dot_nt(dq[rows, :HC], w[0, :, :HC])
            for t in range(1, TP):
                total += dot_nt(dq[rows, t * HC : (t + 1) * HC], w[t, :, :HC])
            blk[rows, :] = total
        return carry

    def enter_back(gn, x, rows):
        gn += blk[rows, :]
        hat, scale = norm_stats(x.astype(F32))
        gatt[rows, :] = (resid[rows, :] + norm_back(gn, gain_one, hat, scale)).astype(BF16)
        sm[7:8, :] += jnp.sum(gn * hat, axis=0, keepdims=True)
        sm[8:9, :] += jnp.sum(gn, axis=0, keepdims=True)

    def gin_away(part):
        rows = pl.ds(0, NP) if part == 0 else pl.ds(NP, NT - NP)
        return ra.copy(gatt.at[rows, :], gin_home.at[rows, :], g_send.at[part], g_recv.at[part], p.partner())

    def give(part):
        rows = slice(0, NP) if part == 0 else slice(NP, NT)

        @pl.when(p.core != p.tp)
        def _():
            gin_away(part).start()

        @pl.when(p.core == p.tp)
        def _():
            gin_home[rows, :] = gatt[rows, :]

    lax.fori_loop(0, G, group, 0)
    homes = []
    for i, (a, c) in enumerate(
        [(home_arrays_p, home_arrays_c)]
        + [(early_p.at[e], early_c.at[e]) for e in range(3)]
        + [(home_cot_p, home_cot_c)]
    ):
        homes.append(pltpu.make_async_copy(a, dv.at[pl.ds(i * NT, NP), :], home_sem.at[0, i]))
        homes.append(pltpu.make_async_copy(c, dv.at[pl.ds(i * NT + NP, NT - NP), :], home_sem.at[1, i]))
    begin(homes)

    def cont_back(g, carry):
        cont_copy(g).wait_recv()
        here = pl.ds(pl.multiple_of(g * NCH, 16), NCH)
        gn = blk_away[halves(p.core, g), :].astype(F32) + dxcm[here, :].astype(F32)
        enter_back(gn, own_c[here, :], pl.ds(pl.multiple_of(NP + g * NCH, 16), NCH))
        return carry

    lax.fori_loop(0, G, cont_back, 0)
    give(1)

    ready(homes)

    @pl.when(p.core != p.tp)
    def _():
        away.wait_recv()

    def blend(i, carry):
        rows = shifted(0, i * STEP)
        res = mix[4] * blk_home[rows, :].astype(F32)
        c = dv[shifted(4 * NT, i * STEP), :].astype(F32)
        for e in range(4):
            a = dv[shifted(e * NT, i * STEP), :].astype(F32)
            res += mix[e] * a
            sm[3 + e : 4 + e, :] += jnp.sum(c * a, axis=0, keepdims=True)
        blk_home[rows, :] = res.astype(BF16)
        return carry

    lax.fori_loop(0, NT // STEP, blend, 0)
    puts = [
        pltpu.make_async_copy(blk_home.at[pl.ds(0, NP), :], out_p, put_sem.at[0]),
        pltpu.make_async_copy(blk_home.at[pl.ds(NP, NT - NP), :], out_c, put_sem.at[1]),
    ]
    begin(puts)
    for when in range(10):
        for step in during.get(("t", when), []):
            step()

    for g in range(G):
        gn = dx_rows(g, 0, p.core)[...].astype(F32)
        for k in range(1, p.ctxs):
            to_plane(g, k).wait_recv()
            gn += dxz[g * (p.ctxs - 1) + k - 1].astype(F32)
        here = slice(g * PB, (g + 1) * PB)
        enter_back(gn, own_p[here, :], here)
    give(0)
    for when in range(10, 20):
        for step in during.get(("t", when), []):
            step()
    small_out[...] = small_sum(
        p, sm, sm_near, sm_rows, sm_across, sm_planes, sm_ss, sm_rc, sm_ry, sm_rx, sm_rz
    )
    gu_puts = []
    for j in range(n_a):
        ra.ctx_end(j)
        total = ra.result(j)
        gd_out[j * T : (j + 1) * T, :] = total[:, T:].T
        if len(gu_puts) > 0:
            gu_puts[-1].wait()
        gh[:S, :T] = total[:, :T]
        gu_puts.append(
            pltpu.make_async_copy(
                gh.at[pl.ds(0, S), pl.ds(0, T)], gu_out.at[:, pl.ds(j * T, T)], put_sem.at[2]
            )
        )
        gu_puts[-1].start()
    gu_puts[-1].wait()
    for j in range(NB):
        rb.ctx_end(j)
        total = rb.result(j)
        if j == 0:
            go_out[...] = total.T
        else:
            for c in range(3):
                first = c * HC + (j - 1) * 128
                gq_out[:, first : first + 128] = total[:, c * 128 : (c + 1) * 128]

    @pl.when(p.core != p.tp)
    def _():
        for part in range(2):
            gin_away(part).wait_recv()
            gin_away(part).wait_send()

    more = [
        pltpu.make_async_copy(gin_home.at[pl.ds(0, NP), :], gin_p, put_sem.at[2]),
        pltpu.make_async_copy(gin_home.at[pl.ds(NP, NT - NP), :], gin_c, put_sem.at[3]),
    ]
    begin(more)
    ready(puts + more)
    rb.cores_sent(NB - 1, 0)
    rb.cores_sent(2 * NB - 1, 1)
    for g in range(G):
        for k in range(p.ctxs):
            to_mate(g, k).wait_send()
        for k in range(1, p.ctxs):
            to_plane(g, k).wait_send()
        cont_copy(g).wait_send()
    ra.drain()
    rb.drain()


def params(**more):
    return pltpu.CompilerParams(vmem_limit_bytes=VMEM_LIMIT, **more)


def per_device(
    prompt_in,
    cont_in,
    prompt_embed,
    cont_embed,
    prompt_earlier,
    cont_earlier,
    ln1_gain,
    ln1_bias,
    ln2_gain,
    ln2_bias,
    w_qkv,
    w_out,
    w_up,
    w_down,
    mix_weights,
    prompt_cot,
    cont_cot,
):
    G, PB, D = prompt_in.shape
    NC, CH = cont_in.shape[1], cont_in.shape[2]
    TP = lax.axis_size("tp")
    PROMPT = PB * TP * lax.axis_size("ctx")
    HC, FC = w_qkv.shape[2], w_up.shape[1]
    S = w_qkv.shape[0]
    dm = Dims(G, PROMPT, PB, NC, CH, D, HC * TP // HD)
    R, NT, NP = dm.R, dm.NT, dm.NP

    sds = jax.ShapeDtypeStruct
    chips, ctxs = lax.axis_size("dp") // 2, lax.axis_size("ctx")
    norms = jnp.stack([ln1_gain, ln1_bias, ln2_gain, ln2_bias], axis=1)
    norms = jnp.pad(norms, ((0, 0), (0, 124)))
    wq_shard = jnp.concatenate([w_qkv.reshape(S, 3 * HC), norms], axis=1)
    wm_shard = jnp.concatenate([w_out.T, w_up, w_down.T], axis=1)

    positions = jnp.arange(PROMPT + CL, dtype=jnp.int32).astype(F32)
    lane = jnp.arange(128, dtype=jnp.int32)
    freq = 10000.0 ** (-((lane % 32).astype(F32) / 32))
    angles = positions[:, None] * freq[None, :]
    cos, sin = jnp.cos(angles), jnp.sin(angles)
    second = (lane % 64) >= 32
    sin = jnp.where(second[None, :], sin, -sin)

    any_ = pl.BlockSpec(memory_space=pl.ANY)
    vmem = pl.BlockSpec(memory_space=pltpu.VMEM)
    dma = pltpu.SemaphoreType.DMA
    left = (HC + 2 * FC) // 128 * 2 // 3 * 128
    q, att, lse, ln, nt, own_nt, k, v, wq, wm, own_p, own_c, cot_p, cot_c = pl.pallas_call(
        partial(forward_kernel, dm, left),
        out_shape=(
            sds((NT, D), BF16),
            sds((NT, D), BF16),
            sds((G * dm.PAIRS, 1, dm.COLS), F32),
            sds((8, D), F32),
            sds((D, G * R), BF16),
            sds((D, NT), BF16),
            sds((G, R, D), BF16),
            sds((G, R, D), BF16),
            sds((TP, D, 3 * HC + 128), BF16),
            sds((TP, D, HC + 2 * FC), BF16),
            sds(prompt_in.shape, BF16),
            sds(cont_in.shape, BF16),
            sds(prompt_in.shape, BF16),
            sds(cont_in.shape, BF16),
        ),
        in_specs=[vmem] * 5 + [any_] * 3,
        out_specs=(vmem,) * 4 + (any_,) * 10,
        scratch_shapes=[
            pltpu.VMEM((D, G * R), BF16),
            pltpu.VMEM((D, NT), BF16),
            pltpu.VMEM((G, R, D), BF16),
            pltpu.VMEM((G, R, D), BF16),
            pltpu.VMEM((PROMPT, PB), F32),
            pltpu.VMEM((dm.NX, 2 * dm.NCH), F32),
            pltpu.VMEM((PROMPT, dm.COLS), F32),
            pltpu.VMEM((G * R, D), BF16),
            pltpu.VMEM((NT, D), BF16),
            pltpu.VMEM((2 * ctxs, G, PB, D), BF16),
            pltpu.VMEM((2, G, NC, CH, D), BF16),
            pltpu.VMEM((TP, D, 3 * HC + 128), BF16),
            dma((7,)),
            dma((4,)),
            dma((4,)),
            dma((2 * ctxs - 1,)),
            dma((ctxs - 1,)),
            dma((ctxs,)),
            dma,
            dma,
            dma((2,)),
        ]
        + WeightGather.semaphores(chips)
        + WeightGather.semaphores(chips),
        compiler_params=params(collective_id=0, has_side_effects=True),
        name="forward",
    )(prompt_in, cont_in, cos, sin, wq_shard, wm_shard, prompt_cot, cont_cot)
    T = 512 if FC % 512 == 0 else 256
    plan_a = [j == 1 for j in range(FC // T)]
    plan_b = [j < dm.PAIRS // TP for j in range(1 + dm.PAIRS // TP)]
    far = max(chips - 1, 1)
    rows = lambda x: x.reshape(-1, D)
    out_p, out_c, gin_p, gin_c, gq, go, gu, gd, small = pl.pallas_call(
        partial(backward_kernel, dm, T, FC, plan_a, plan_b),
        out_shape=(
            sds((NP, D), BF16),
            sds((NT - NP, D), BF16),
            sds((NP, D), BF16),
            sds((NT - NP, D), BF16),
            sds((S, 3 * HC), F32),
            sds((HC, S), F32),
            sds((S, FC), F32),
            sds((FC, S), F32),
            sds((16, D), F32),
        ),
        in_specs=[pl.BlockSpec(memory_space=pltpu.SMEM)] + [vmem] * 10 + [any_] * 12,
        out_specs=(any_,) * 4 + (vmem, vmem, any_, vmem, vmem),
        scratch_shapes=[
            pltpu.VMEM((NT, D), F32),
            pltpu.VMEM((NT, D), F32),
            pltpu.VMEM((NT, D), F32),
            pltpu.VMEM((TP, D, HC), BF16),
            pltpu.VMEM((2, D, max(2 * T, 3 * HC)), BF16),
            pltpu.VMEM((NT, D), BF16),
            pltpu.VMEM((D, G * R), BF16),
            pltpu.VMEM((D, NT), BF16),
            pltpu.VMEM((PROMPT, PB), F32),
            pltpu.VMEM((dm.NX, 2 * dm.NCH), F32),
            pltpu.VMEM((2, R, 128), BF16),
            pltpu.VMEM((2, R, 128), BF16),
            pltpu.VMEM((G * R, D), BF16),
            pltpu.VMEM((G * R, D), BF16),
            pltpu.VMEM((NT, D), BF16),
            pltpu.VMEM((G * ctxs, PB, D), BF16),
            pltpu.VMEM((G * (ctxs - 1), PB, D), BF16),
            pltpu.VMEM((NT - NP, D), BF16),
            pltpu.VMEM((max(NT, 2 * (NT - NP)), D), BF16),
            pltpu.VMEM((NT, D), BF16),
            pltpu.VMEM((NT, D), BF16),
            dma((4,)),
            dma((2, 2)),
            dma,
            dma((2, 2)),
            dma((2,)),
            dma,
            dma((2, 5)),
            dma,
            dma,
            dma((2,)),
            dma((2,)),
            dma((G * ctxs,)),
            dma((G * ctxs,)),
            dma((G * (ctxs - 1),)),
            dma((G * (ctxs - 1),)),
            dma((G,)),
            dma((G,)),
            pltpu.VMEM((16, D), F32),
            pltpu.VMEM((16, D), F32),
            pltpu.VMEM((chips, 16, D), F32),
            pltpu.VMEM((2, 16, D), F32),
            pltpu.VMEM((ctxs, 16, D), F32),
            dma((1 + chips + ctxs,)),
            dma,
            dma((far,)),
            dma,
            dma((ctxs - 1,)),
        ]
        + Reduce.scratch(plan_a, chips, S, 2 * T)
        + Reduce.scratch(plan_b, chips, S, HC),
        compiler_params=params(collective_id=1, has_side_effects=True),
        name="backward",
    )(
        mix_weights,
        att,
        rows(own_p),
        rows(own_c),
        rows(cot_p),
        rows(cot_c),
        ln,
        q,
        lse,
        cos,
        sin,
        wm,
        k,
        v,
        nt,
        own_nt,
        wq,
        rows(prompt_embed),
        rows(cont_embed),
        prompt_earlier.reshape(3, NP, D),
        cont_earlier.reshape(3, NT - NP, D),
        rows(prompt_cot),
        rows(cont_cot),
    )
    start = lax.axis_index("dp") * S
    mine = lax.dynamic_slice_in_dim(small, start, S, axis=1)
    return (
        out_p.reshape(prompt_in.shape),
        out_c.reshape(cont_in.shape),
        gin_p.reshape(prompt_in.shape),
        gin_c.reshape(cont_in.shape),
        mine[7],
        mine[8],
        mine[0],
        mine[1],
        gq.reshape(S, 3, HC),
        go,
        gu,
        gd,
        jnp.sum(jnp.concatenate([small[3:7], small[2:3]]), axis=1),
    )


def solution(mesh):
    tokens = P("dp", ("ctx", "tp"), None)
    conts = P("dp", "ctx", "tp", None)
    weights = (P("dp", None, "tp"), P("tp", "dp"), P("dp", "tp"), P("tp", "dp"))
    in_specs = (
        tokens,
        conts,
        tokens,
        conts,
        P(None, "dp", ("ctx", "tp"), None),
        P(None, "dp", "ctx", "tp", None),
        P("dp"),
        P("dp"),
        P("dp"),
        P("dp"),
        *weights,
        P(),
        tokens,
        conts,
    )
    out_specs = (
        tokens,
        conts,
        tokens,
        conts,
        P("dp"),
        P("dp"),
        P("dp"),
        P("dp"),
        *weights,
        P(),
    )
    return jax.shard_map(
        per_device, mesh=mesh, in_specs=in_specs, out_specs=out_specs, check_vma=False
    )
```

```python
from functools import partial

import jax
import jax.numpy as jnp
import numpy as np
from jax import lax
from jax.experimental import pallas as pl
from jax.experimental.pallas import tpu as pltpu
from jax.sharding import PartitionSpec as P

HD = 64
CL = 128
EPS = 1e-05
NEG = -1e30
F32 = jnp.float32
BF16 = jnp.bfloat16
VMEM_LIMIT = 67043328


def dot(a, b):
    return lax.dot_general(a, b, (((1,), (0,)), ((), ())), preferred_element_type=F32)


def dot_nt(a, b):
    return lax.dot_general(a, b, (((1,), (1,)), ((), ())), preferred_element_type=F32)


def norm_stats(x):
    mean = jnp.mean(x, axis=-1, keepdims=True)
    centered = x - mean
    var = jnp.mean(centered * centered, axis=-1, keepdims=True)
    scale = lax.rsqrt(var + EPS)
    return centered * scale, scale


def norm_back(grad, gain, hat, scale):
    gh = grad * gain
    return scale * (
        gh
        - jnp.mean(gh, axis=-1, keepdims=True)
        - hat * jnp.mean(gh * hat, axis=-1, keepdims=True)
    )


def swap_halves(x):
    second = lax.broadcasted_iota(jnp.int32, x.shape, 1) % HD >= HD // 2
    return jnp.where(second, pltpu.roll(x, 32, 1), pltpu.roll(x, 96, 1))


def rotate(x, cos, sin):
    return x * cos + swap_halves(x) * sin


def rotate_back(x, cos, sin):
    return x * cos - swap_halves(x) * sin


def lane_pick(shape, low):
    lanes = lax.broadcasted_iota(jnp.int32, shape, 1)
    return lanes < HD if low else lanes >= HD


def sublane_pick(shape, low):
    rows = lax.broadcasted_iota(jnp.int32, shape, 0)
    return rows < HD if low else rows >= HD


def transpose(x):
    return x.astype(F32).T.astype(x.dtype)


class Dims:
    def __init__(self, groups, prompt, pb, nc, ch, d, heads):
        self.G, self.P, self.PB, self.NC, self.CH, self.D = groups, prompt, pb, nc, ch, d
        self.NCH = nc * ch
        self.R = prompt + nc * CL
        self.NX = nc * CL
        self.NR = pb + self.NCH
        self.NP = groups * pb
        self.NT = groups * self.NR
        self.PAIRS = heads // 2
        self.COLS = 2 * self.NR


MESH = pl.DeviceIdType.MESH


def half_index():
    return lax.axis_index("dp") % 2


def block_index():
    return lax.axis_index("ctx") * 2 + half_index()


class Peers:
    def __init__(self):
        self.ctxs = lax.axis_size("ctx")
        self.chips = lax.axis_size("dp") // 2
        self.tps = lax.axis_size("tp")
        self.dp = lax.axis_index("dp")
        self.ctx = lax.axis_index("ctx")
        self.tp = lax.axis_index("tp")
        self.core = self.dp % 2
        self.chip = self.dp // 2

    def at(self, dp=None, ctx=None, tp=None):
        return {
            "dp": self.dp if dp is None else dp,
            "ctx": self.ctx if ctx is None else ctx,
            "tp": self.tp if tp is None else tp,
        }

    def across(self):
        return self.at(tp=1 - self.tp)

    def mate(self):
        return self.at(dp=self.chip * 2 + 1 - self.core)

    def chip_after(self, k):
        return lax.rem(self.chip + k, self.chips)

    def chip_before(self, k):
        return lax.rem(self.chip + self.chips - k, self.chips)

    def row(self, k):
        return self.at(dp=self.chip_after(k) * 2 + self.core)

    def ctx_after(self, k):
        return lax.rem(self.ctx + k, self.ctxs)

    def ctx_before(self, k):
        return lax.rem(self.ctx + self.ctxs - k, self.ctxs)

    def plane(self, k):
        return self.at(ctx=self.ctx_after(k))

    def partner(self):
        return self.at(dp=self.chip * 2 + self.tp, tp=self.core)

    def greet(self, trades=False):
        barrier = pltpu.get_barrier_semaphore()
        peers = [self.across(), self.mate()]
        peers += [self.row(k) for k in range(1, self.chips)]
        peers += [self.plane(k) for k in range(1, self.ctxs)]
        for peer in peers:
            pl.semaphore_signal(barrier, inc=1, device_id=peer, device_id_type=MESH)
        count = len(peers)
        if trades:
            away = self.core != self.tp

            @pl.when(away)
            def _():
                pl.semaphore_signal(
                    barrier, inc=1, device_id=self.partner(), device_id_type=MESH
                )

            count += jnp.where(away, 1, 0)
        pl.semaphore_wait(barrier, count)


def send(src, dst, send_sem, recv_sem, device):
    copy = pltpu.make_async_remote_copy(
        src_ref=src,
        dst_ref=dst,
        send_sem=send_sem,
        recv_sem=recv_sem,
        device_id=device,
        device_id_type=MESH,
    )
    copy.start()
    return copy


def arrived(ref, sem, peers):
    pltpu.make_async_remote_copy(
        src_ref=ref,
        dst_ref=ref,
        send_sem=sem,
        recv_sem=sem,
        device_id=peers.mate(),
        device_id_type=MESH,
    ).wait_recv()


class WeightGather:
    def __init__(self, peers, shard, full, left, sends, across, rows, mate):
        self.p, self.shard, self.full, self.left = peers, shard, full, left
        self.sends, self.across, self.rows, self.from_mate = sends, across, rows, mate
        self.copies = []
        self.size, self.cols = shard.shape

    @staticmethod
    def semaphores(chips):
        far = chips - 1
        return [
            pltpu.SemaphoreType.DMA((3 + 6 * far,)),
            pltpu.SemaphoreType.DMA((chips,)),
            pltpu.SemaphoreType.DMA((2, max(far, 1))),
            pltpu.SemaphoreType.DMA((2, chips)),
        ]

    def piece(self, tp, dp, cols=slice(None)):
        rows = pl.ds(pl.multiple_of(dp * self.size, 16), self.size)
        if cols == slice(None):
            return self.full.at[tp, rows, :]
        return self.full.at[tp, rows, pl.ds(cols.start, cols.stop - cols.start)]

    def go(self, src, dst, recv_sem, device):
        self.copies.append(send(src, dst, self.sends.at[len(self.copies)], recv_sem, device))

    def start(self):
        p = self.p
        self.go(self.shard, self.piece(p.tp, p.dp), self.across.at[0], p.across())
        for k in range(1, p.chips):
            self.go(self.shard, self.piece(p.tp, p.dp), self.rows.at[0, k - 1], p.row(k))
        self.go(self.shard, self.piece(p.tp, p.dp), self.from_mate.at[0, 0], p.mate())

    def relay_across(self):
        p = self.p
        got = self.piece(1 - p.tp, p.dp)
        arrived(got, self.across.at[0], p)
        part = self.piece(1 - p.tp, p.dp, slice(0, self.left))
        for k in range(1, p.chips):
            self.go(part, part, self.rows.at[1, k - 1], p.row(k))
        self.go(got, got, self.from_mate.at[1, 0], p.mate())

    def relay_rows(self):
        p = self.p
        for k in range(1, p.chips):
            dp = p.chip_before(k) * 2 + p.core
            got = self.piece(p.tp, dp)
            arrived(got, self.rows.at[0, k - 1], p)
            if self.left < self.cols:
                part = self.piece(p.tp, dp, slice(self.left, self.cols))
                self.go(part, part, self.across.at[k], p.across())
            self.go(got, got, self.from_mate.at[0, k], p.mate())

    def relay_last(self):
        p = self.p
        for k in range(1, p.chips):
            dp = p.chip_before(k) * 2 + p.core
            arrived(self.piece(1 - p.tp, dp, slice(0, self.left)), self.rows.at[1, k - 1], p)
            if self.left < self.cols:
                part = self.piece(1 - p.tp, dp, slice(self.left, self.cols))
                arrived(part, self.across.at[k], p)
            got = self.piece(1 - p.tp, dp)
            self.go(got, got, self.from_mate.at[1, k], p.mate())

    def finish(self):
        p = self.p
        for part in range(2):
            tp = p.tp if part == 0 else 1 - p.tp
            for k in range(p.chips):
                dp = p.chip_before(k) * 2 + 1 - p.core
                arrived(self.piece(tp, dp), self.from_mate.at[part, k], p)

    def drain(self):
        for copy in self.copies:
            copy.wait_send()


def twice(x):
    return jnp.concatenate([x, x], axis=1)


def fill_masks(dm, maskp, maskx):
    block = block_index()
    keys = lax.broadcasted_iota(jnp.int32, maskp.shape, 0)
    cols = lax.broadcasted_iota(jnp.int32, maskp.shape, 1) % dm.PB
    maskp[...] = jnp.where(keys <= cols + block * dm.PB, 0.0, NEG)
    keys = lax.broadcasted_iota(jnp.int32, maskx.shape, 0)
    cols = lax.broadcasted_iota(jnp.int32, maskx.shape, 1) % dm.NCH
    seen = (keys // CL == cols // dm.CH) & (
        keys % CL <= cols % dm.CH + half_index() * dm.CH
    )
    maskx[...] = jnp.where(seen, 0.0, NEG)


def heads_columns(a, b):
    lo_a, lo_b = sublane_pick(a.shape, True), sublane_pick(b.shape, True)
    zero_a, zero_b = jnp.zeros_like(a), jnp.zeros_like(b)
    return jnp.concatenate(
        [
            jnp.where(lo_a, a, zero_a),
            jnp.where(lo_a, zero_a, a),
            jnp.where(lo_b, b, zero_b),
            jnp.where(lo_b, zero_b, b),
        ],
        axis=1,
    )


def heads_rows(a, b):
    lo_a, lo_b = lane_pick(a.shape, True), lane_pick(b.shape, True)
    zero_a, zero_b = jnp.zeros_like(a), jnp.zeros_like(b)
    return jnp.concatenate(
        [
            jnp.where(lo_a, a, zero_a),
            jnp.where(lo_a, zero_a, a),
            jnp.where(lo_b, b, zero_b),
            jnp.where(lo_b, zero_b, b),
        ],
        axis=0,
    )


def forward_kernel(
    dm,
    left,
    prompt,
    cont,
    cos,
    sin,
    wq,
    wm,
    cot_p,
    cot_c,
    q_out,
    att_out,
    lse_out,
    ln_out,
    nt_hbm,
    own_nt_hbm,
    k_hbm,
    v_hbm,
    w_hbm,
    wm_out,
    own_p_hbm,
    own_c_hbm,
    cot_p_out,
    cot_c_out,
    nt_out,
    own_out,
    k_out,
    v_out,
    maskp,
    maskx,
    sbuf,
    all_rows,
    own_rows,
    xp,
    xc,
    w,
    put_sem,
    trade_send,
    trade_recv,
    x_send,
    x_plane,
    x_mate,
    c_send,
    c_mate,
    own_sem,
    *sems,
):
    G, R, PB, NCH, D, NP, NT = dm.G, dm.R, dm.PB, dm.NCH, dm.D, dm.NP, dm.NT
    NC, CH = dm.NC, dm.CH
    HC = (w.shape[2] - 128) // 3
    TP = w.shape[0]
    p = Peers()
    block = block_index()
    gq = WeightGather(p, wq, w, wq.shape[1], *sems[:4])
    gm = WeightGather(p, wm, wm_out, left, *sems[4:])
    size = wq.shape[0]
    mine = pl.ds(pl.multiple_of(p.dp * size, 16), size)

    landing = [xp.at[p.ctx * 2 + p.tp], xc.at[p.tp], cot_p_out, cot_c_out]

    def moved(i):
        src = [prompt, cont, cot_p, cot_c][i]
        return pltpu.make_async_remote_copy(
            src_ref=src,
            dst_ref=landing[i],
            send_sem=trade_send.at[i],
            recv_sem=trade_recv.at[i],
            device_id=p.partner(),
            device_id_type=MESH,
        )

    def kept(i):
        return pltpu.make_async_copy([prompt, cont, cot_p, cot_c][i], landing[i], trade_send.at[i])

    moves = p.core != p.tp

    def trade(i):
        @pl.when(moves)
        def _():
            moved(i).start()

        @pl.when(jnp.logical_not(moves))
        def _():
            kept(i).start()

    def traded(i):
        @pl.when(moves)
        def _():
            moved(i).wait_recv()

        @pl.when(jnp.logical_not(moves))
        def _():
            kept(i).wait()

    local = [
        pltpu.make_async_copy(wq, w.at[p.tp, mine, :], own_sem.at[0]),
        pltpu.make_async_copy(wm, wm_out.at[p.tp, mine, :], own_sem.at[1]),
    ]
    for copy in local:
        copy.start()
    p.greet(trades=True)
    trade(0)
    gq.start()
    trade(1)
    fill_masks(dm, maskp, maskx)
    traded(0)
    own = xp.at[block]
    sent = []
    for k in range(1, p.ctxs):
        sent.append(send(own, own, x_send.at[k - 1], x_plane.at[k - 1], p.plane(k)))
    sent.append(send(own, own, x_send.at[p.ctxs - 1], x_mate.at[0], p.mate()))
    gq.relay_across()
    gq.relay_rows()
    traded(1)
    sent.append(send(xc.at[p.core], xc.at[p.core], c_send, c_mate, p.mate()))
    gq.relay_last()
    gm.start()
    trade(2)
    trade(3)
    gq.finish()
    local[0].wait()
    puts = [
        pltpu.make_async_copy(w, w_hbm, put_sem.at[0]),
        pltpu.make_async_copy(xp.at[block], own_p_hbm, put_sem.at[1]),
        pltpu.make_async_copy(xc.at[p.core], own_c_hbm, put_sem.at[2]),
    ]
    for put in puts:
        put.start()
    ln = w[0, :, 3 * HC :].astype(F32).T[:8, :]
    ln_out[...] = ln
    gain, bias = ln[0:1, :], ln[1:2, :]

    def normed(x):
        hat, _ = norm_stats(x.astype(F32))
        return (hat * gain + bias).astype(BF16)

    def turned(x, table):
        rows = x.shape[0]
        return rotate(x, cos[pl.ds(table, rows), :], sin[pl.ds(table, rows), :])

    x = jnp.concatenate([xp[block].reshape(NP, D), xc[p.core].reshape(NT - NP, D)], axis=0)
    n = normed(x)
    own_rows[...] = n
    places = [(g * PB, PB, pl.multiple_of(block * PB, PB)) for g in range(G)]
    places += [
        (NP + i * CH, CH, pl.multiple_of(dm.P + p.core * CH, CH)) for i in range(G * NC)
    ]
    for t in range(TP):
        qq = dot(n, w[t, :, :HC])
        for first, count, table in places:
            for j in range(HC // 128):
                tile = turned(qq[first : first + count, j * 128 : (j + 1) * 128], table).astype(BF16)
                q_out[first : first + count, t * HC + j * 128 : t * HC + (j + 1) * 128] = (
                    tile.astype(F32) * 0.125
                ).astype(BF16)
    own_out[...] = transpose(own_rows[...])

    def keys_values(x, places):
        n = normed(x)
        for first, count, g, row, table in places:
            all_rows[pl.ds(pl.multiple_of(g * R + row, 16), count), :] = n[first : first + count]
        for t in range(TP):
            kk = dot(n, w[t, :, HC : 2 * HC])
            for first, count, g, row, table in places:
                for j in range(HC // 128):
                    tile = turned(kk[first : first + count, j * 128 : (j + 1) * 128], table)
                    k_out[g, pl.ds(row, count), t * HC + j * 128 : t * HC + (j + 1) * 128] = tile.astype(BF16)
            vv = dot(n, w[t, :, 2 * HC : 3 * HC]).astype(BF16)
            for first, count, g, row, table in places:
                v_out[g, pl.ds(row, count), t * HC : (t + 1) * HC] = vv[first : first + count]

    arrived(xc.at[1 - p.core], c_mate, p)
    x = [xc[e, g, c] for g in range(G) for c in range(NC) for e in range(2)]
    keys_values(
        jnp.concatenate(x, axis=0),
        [((g * NC + c) * CL, CL, g, dm.P + c * CL, dm.P) for g in range(G) for c in range(NC)],
    )

    def relay(k):
        b = p.ctx_before(k) * 2 + p.core
        return pltpu.make_async_remote_copy(
            src_ref=xp.at[b],
            dst_ref=xp.at[b],
            send_sem=x_send.at[p.ctxs + k - 1],
            recv_sem=x_mate.at[k],
            device_id=p.mate(),
            device_id_type=MESH,
        )

    def plane(k, carry):
        c = p.ctx_before(k)

        @pl.when(k > 0)
        def _():
            arrived(xp.at[c * 2 + p.core], x_plane.at[k - 1], p)
            relay(k).start()

        arrived(xp.at[c * 2 + 1 - p.core], x_mate.at[k], p)
        x = xp[pl.ds(c * 2, 2)].reshape(2 * NP, D)
        places = []
        for e in range(2):
            row = pl.multiple_of((c * 2 + e) * PB, PB)
            places += [((e * G + g) * PB, PB, g, row, row) for g in range(G)]
        keys_values(x, places)
        return carry

    lax.fori_loop(0, p.ctxs, plane, 0)
    puts += [
        pltpu.make_async_copy(k_out, k_hbm, put_sem.at[3]),
        pltpu.make_async_copy(v_out, v_hbm, put_sem.at[4]),
    ]
    for put in puts[3:]:
        put.start()

    def turn(i, carry):
        rows = pl.ds(pl.multiple_of(i * 256, 256), 256)
        nt_out[:, rows] = transpose(all_rows[rows, :])
        return carry

    lax.fori_loop(0, G * R // 256, turn, 0)
    puts += [
        pltpu.make_async_copy(nt_out, nt_hbm, put_sem.at[5]),
        pltpu.make_async_copy(own_out, own_nt_hbm, put_sem.at[6]),
    ]
    for put in puts[5:]:
        put.start()
    gm.relay_across()
    gm.relay_rows()

    TILE = 256
    tiles = dm.P // TILE

    def attend(i, carry):
        g, pair = i // dm.PAIRS, i % dm.PAIRS
        lanes = pl.ds(pl.multiple_of(pair * 128, 128), 128)
        qp = q_out[pl.ds(pl.multiple_of(g * PB, PB), PB), lanes]
        qc = q_out[pl.ds(pl.multiple_of(dm.NP + g * NCH, NCH), NCH), lanes]
        qt = heads_columns(transpose(qp), transpose(qc))
        top = None
        for j in range(tiles):
            s = dot(k_out[g, j * TILE : (j + 1) * TILE, lanes], qt)
            sbuf[j * TILE : (j + 1) * TILE, : 2 * PB] = (
                s[:, : 2 * PB] + twice(maskp[j * TILE : (j + 1) * TILE, :])
            )
            sbuf[j * TILE : (j + 1) * TILE, 2 * PB :] = s[:, 2 * PB :]
            here = jnp.max(sbuf[j * TILE : (j + 1) * TILE, :], axis=0, keepdims=True)
            top = here if top is None else jnp.maximum(top, here)
        sx = dot(k_out[g, dm.P :, lanes], qt[:, 2 * PB :]) + maskx[...]
        topx = jnp.max(sx, axis=0, keepdims=True)
        top = jnp.concatenate([top[:, : 2 * PB], jnp.maximum(top[:, 2 * PB :], topx)], axis=1)
        total, acc = None, None
        for j in range(tiles):
            e = jnp.exp(sbuf[j * TILE : (j + 1) * TILE, :] - top)
            here = jnp.sum(e, axis=0, keepdims=True)
            vt = transpose(v_out[g, j * TILE : (j + 1) * TILE, lanes])
            part = dot(vt, e.astype(BF16))
            total = here if total is None else total + here
            acc = part if acc is None else acc + part
        ex = jnp.exp(sx - top[:, 2 * PB :])
        partx = dot(transpose(v_out[g, dm.P :, lanes]), ex.astype(BF16))
        totalx = jnp.sum(ex, axis=0, keepdims=True)
        total = jnp.concatenate([total[:, : 2 * PB], total[:, 2 * PB :] + totalx], axis=1)
        acc_p = acc[:, : 2 * PB] / total[:, : 2 * PB]
        acc_c = (acc[:, 2 * PB :] + partx) / total[:, 2 * PB :]
        lse_out[i] = top + jnp.log(total)
        outp = jnp.where(sublane_pick((128, PB), True), acc_p[:, :PB], acc_p[:, PB:])
        outc = jnp.where(sublane_pick((128, NCH), True), acc_c[:, :NCH], acc_c[:, NCH:])
        att_out[pl.ds(pl.multiple_of(g * PB, PB), PB), lanes] = outp.T.astype(BF16)
        att_out[pl.ds(pl.multiple_of(dm.NP + g * NCH, NCH), NCH), lanes] = outc.T.astype(BF16)
        return carry

    lax.fori_loop(0, G * dm.PAIRS, attend, 0)
    gm.relay_last()
    gm.finish()
    gq.drain()
    gm.drain()
    for copy in sent:
        copy.wait_send()
    for k in range(1, p.ctxs):
        relay(k).wait_send()
    local[1].wait()
    for i in (2, 3):
        traded(i)

    @pl.when(moves)
    def _():
        for i in range(4):
            moved(i).wait_send()

    for put in puts:
        put.wait()


class Reduce:
    REFS = 13

    def __init__(self, p, cross_first, refs):
        self.p, self.n, self.cross_first = p, len(cross_first), cross_first
        self.mine, self.got, self.row, self.acr, self.zin = refs[:5]
        self.sc, self.rc, self.sy, self.ry, self.sx, self.rx, self.sz, self.rz = refs[5:13]
        mid = p.ctxs // 2
        self.centre = (p.ctx == mid - 1) | (p.ctx == mid)
        self.outer = (p.ctx > 0) & (p.ctx < p.ctxs - 1)
        step = jnp.where(p.ctx < mid, 1, -1)
        self.inner_at = p.ctx + step
        self.outer_at = jnp.clip(p.ctx - step, 0, p.ctxs - 1)

    @staticmethod
    def scratch(cross_first, chips, size, width):
        n = len(cross_first)
        dma = pltpu.SemaphoreType.DMA
        far = max(chips - 1, 1)
        rows = n + sum(1 for c in cross_first if not c)
        return [
            pltpu.VMEM((2, chips * 2 * size, width), BF16),
            pltpu.VMEM((2 * n, chips, size, width), BF16),
            pltpu.VMEM((rows, far, size, width), BF16),
            pltpu.VMEM((n, chips, size, width), BF16),
            pltpu.VMEM((n, 2, size, width), BF16),
            dma((2 * n, chips)),
            dma((2 * n, chips)),
            dma((2 * n, far)),
            dma((2 * n, far)),
            dma((n,)),
            dma((n,)),
            dma((n, 2)),
            dma((n, 2)),
        ]

    def copy(self, src, dst, send_sem, recv_sem, device):
        return pltpu.make_async_remote_copy(
            src_ref=src,
            dst_ref=dst,
            send_sem=send_sem,
            recv_sem=recv_sem,
            device_id=device,
            device_id_type=MESH,
        )

    def slot(self, whose, j):
        return 0 if whose == "other" else 1

    def crosses(self, i):
        return self.cross_first[i % self.n]

    def travels(self, i):
        return i >= self.n or not self.crosses(i)

    def mine_of(self, y, core):
        size = self.got.shape[2]
        return pl.ds(pl.multiple_of((2 * y + core) * size, 16), size)

    def by_core(self, i, slot, y):
        p = self.p
        return self.copy(
            self.mine.at[slot, self.mine_of(y, 1 - p.core), :],
            self.got.at[i, y],
            self.sc.at[i, y],
            self.rc.at[i, y],
            p.mate(),
        )

    def row_slot(self, i):
        return sum(1 for e in range(i) if self.travels(e))

    def by_row(self, i, k):
        p = self.p
        return self.copy(
            self.got.at[i, p.chip_after(k)],
            self.row.at[self.row_slot(i), k - 1],
            self.sy.at[i, k - 1],
            self.ry.at[i, k - 1],
            p.row(k),
        )

    def by_tp(self, j):
        p = self.p
        part = slice(None) if self.crosses(j) else p.chip
        return self.copy(
            self.got.at[j, part], self.acr.at[j, part], self.sx.at[j], self.rx.at[j], p.across()
        )

    def inward(self, j):
        slot = jnp.where(self.centre, 1, 0)
        return self.copy(
            self.got.at[self.n + j, self.p.chip],
            self.zin.at[j, slot],
            self.sz.at[j, 0],
            self.rz.at[j, slot],
            self.p.at(ctx=self.inner_at),
        )

    def outward(self, j):
        return self.copy(
            self.got.at[self.n + j, self.p.chip],
            self.zin.at[j, 1],
            self.sz.at[j, 1],
            self.rz.at[j, 1],
            self.p.at(ctx=self.outer_at),
        )

    def add(self, i, y, other):
        self.got[i, y] = (self.got[i, y].astype(F32) + other.astype(F32)).astype(BF16)

    def cores_send(self, i, slot):
        for y in range(self.p.chips):
            self.by_core(i, slot, y).start()

    def cores_sent(self, i, slot):
        for y in range(self.p.chips):
            self.by_core(i, slot, y).wait_send()

    def rows_send(self, i):
        for k in range(1, self.p.chips):
            self.by_row(i, k).start()

    def cores_sum(self, i, slot):
        p = self.p
        for y in range(p.chips):
            self.by_core(i, slot, y).wait_recv()
            self.add(i, y, self.mine[slot, self.mine_of(y, p.core), :])
        if not self.crosses(i):
            self.rows_send(i)
        elif i < self.n:
            self.by_tp(i).start()

    def cross_sum(self, j):
        self.by_tp(j).wait_recv()
        for y in range(self.p.chips):
            self.add(self.n + j, y, self.acr[j, y])
        self.rows_send(self.n + j)

    def rows_sum(self, i):
        p = self.p
        for k in range(1, p.chips):
            self.by_row(i, k).wait_recv()
            self.add(i, p.chip, self.row[self.row_slot(i), k - 1])
        if i < self.n:
            self.by_tp(i).start()
            return
        j = i - self.n
        if not self.crosses(i):
            self.by_tp(j).wait_recv()
            self.add(i, p.chip, self.acr[j, p.chip])

        @pl.when(jnp.logical_not(self.outer))
        def _():
            self.inward(j).start()

    def ctx_in(self, j):
        @pl.when(self.outer)
        def _():
            pltpu.make_async_copy(self.zin.at[j, 0], self.zin.at[j, 0], self.rz.at[j, 0]).wait()
            self.add(self.n + j, self.p.chip, self.zin[j, 0])
            self.inward(j).start()

    def ctx_mid(self, j):
        @pl.when(self.centre)
        def _():
            self.from_inner(j)
            self.add(self.n + j, self.p.chip, self.zin[j, 1])

            @pl.when(self.outer)
            def _():
                self.outward(j).start()

    def ctx_end(self, j):
        @pl.when(jnp.logical_not(self.centre))
        def _():
            self.from_inner(j)
            self.got[self.n + j, self.p.chip] = self.zin[j, 1]

            @pl.when(self.outer)
            def _():
                self.outward(j).start()

    def from_inner(self, j):
        pltpu.make_async_copy(self.zin.at[j, 1], self.zin.at[j, 1], self.rz.at[j, 1]).wait()
        self.inward(j).wait_send()

    def result(self, j):
        return self.got[self.n + j, self.p.chip].astype(F32)

    def drain(self):
        p = self.p
        for i in range(2 * self.n):
            if self.travels(i):
                for k in range(1, p.chips):
                    self.by_row(i, k).wait_send()
        for j in range(self.n):
            self.by_tp(j).wait_send()

            @pl.when(self.outer)
            def _():
                self.outward(j).wait_send()


def small_sum(p, sm, near, rows, across, planes, ss, rc, ry, rx, rz):
    copies = []

    def go(src, dst, recv_sem, device):
        copies.append(send(src, dst, ss.at[len(copies)], recv_sem, device))

    go(sm, near, rc, p.mate())
    copies[-1].wait_recv()
    rows[p.chip] = sm[...] + near[...]
    for k in range(1, p.chips):
        go(rows.at[p.chip], rows.at[p.chip], ry.at[k - 1], p.row(k))
    for k in range(1, p.chips):
        arrived(rows.at[p.chip_before(k)], ry.at[k - 1], p)
    total = rows[0]
    for y in range(1, p.chips):
        total += rows[y]
    across[0] = total
    go(across.at[0], across.at[1], rx, p.across())
    copies[-1].wait_recv()
    planes[p.ctx] = across[0] + across[1]
    for k in range(1, p.ctxs):
        go(planes.at[p.ctx], planes.at[p.ctx], rz.at[k - 1], p.plane(k))
    for k in range(1, p.ctxs):
        arrived(planes.at[p.ctx_before(k)], rz.at[k - 1], p)
    total = planes[0]
    for z in range(1, p.ctxs):
        total += planes[z]
    for copy in copies:
        copy.wait_send()
    return total


PLAN = {
    ("m", 2): [("a", "cores_sum", "other", 0)],
    ("m", 3): [("a", "cores_sum", "own", 0)],
    ("m", 4): [("a", "cores_sum", "other", 1)],
    ("m", 5): [("a", "cores_sum", "own", 1)],
    ("e", 0): [("a", "rows_sum", "other", 0)],
    ("a", 1): [("a", "cores_sum", "own", 2), ("a", "cores_sum", "other", 2)],
    ("a", 3): [("a", "rows_sum", "own", 0)],
    ("p", 0, 1): [("a", "rows_sum", "other", 1)],
    ("a", 6): [("a", "ctx_in", "own", 0), ("b", "cores_sum", "other", 0)],
    ("a", 7): [("a", "rows_sum", "own", 1), ("b", "cores_sum", "own", 0)],
    ("a", 8): [("b", "cores_sum", "other", 1)],
    ("a", 9): [("b", "cores_sum", "own", 1)],
    ("a", 10): [("b", "cores_sum", "other", 2)],
    ("a", 11): [("b", "cross_sum", "own", 0), ("b", "cores_sum", "own", 2)],
    ("p", 1, 0): [("b", "cross_sum", "own", 1)],
    ("p", 1, 2): [("a", "rows_sum", "other", 2)],
    ("p", 1, 3): [("a", "ctx_in", "own", 1), ("b", "rows_sum", "own", 0), ("b", "cores_sum", "other", 3)],
    ("t", 0): [("b", "ctx_in", "own", 0)],
    ("t", 1): [("b", "cross_sum", "own", 2)],
    ("t", 2): [("a", "rows_sum", "own", 2), ("a", "ctx_mid", "own", 0), ("a", "ctx_mid", "own", 1)],
    ("t", 10): [("b", "rows_sum", "own", 2)],
    ("t", 11): [("b", "rows_sum", "own", 1)],
    ("t", 12): [("a", "ctx_in", "own", 2)],
    ("t", 13): [("b", "rows_sum", "other", 3)],
    ("t", 14): [("b", "ctx_mid", "own", 0)],
    ("t", 16): [("small",)],
    ("t", 17): [("a", "ctx_mid", "own", 2), ("b", "ctx_in", "own", 1)],
    ("t", 18): [("b", "cores_sum", "own", 3), ("b", "rows_sum", "own", 3)],
    ("t", 19): [("b", "ctx_in", "own", 2), ("b", "ctx_mid", "own", 1), ("b", "ctx_in", "own", 3), ("b", "ctx_mid", "own", 2), ("b", "ctx_mid", "own", 3)],
}


def schedule(ra, rb, on, planes, small):
    for stage, steps in PLAN.items():
        if stage[0] == "p":
            stage = ("p", stage[1] * planes + stage[2])
        for step in steps:
            if step[0] == "small":
                on(stage, small)
                continue
            name, what, whose, j = step
            r = ra if name == "a" else rb
            if what == "cores_sum":
                on(stage, partial(r.cores_sum, j if whose == "other" else r.n + j, r.slot(whose, j)))
            elif what == "rows_sum":
                on(stage, partial(r.rows_sum, j if whose == "other" else r.n + j))
            else:
                on(stage, partial(getattr(r, what), j))


def backward_kernel(
    dm,
    T,
    FC,
    plan_a,
    plan_b,
    mix,
    att,
    own_p,
    own_c,
    cot_p,
    cot_c,
    ln,
    q,
    lse,
    cos,
    sin,
    wm,
    k_hbm,
    v_hbm,
    nt_hbm,
    own_nt_hbm,
    wq_hbm,
    home_arrays_p,
    home_arrays_c,
    early_p,
    early_c,
    home_cot_p,
    home_cot_c,
    out_p,
    out_c,
    gin_p,
    gin_c,
    gq_out,
    go_out,
    gu_out,
    gd_out,
    small_out,
    resid,
    blk,
    gh,
    wo,
    ring,
    gatt,
    nt,
    own_nt,
    maskp,
    maskx,
    kbuf,
    vbuf,
    dk,
    dv,
    dq,
    dxm,
    dxz,
    dxcm,
    blk_away,
    blk_home,
    gin_home,
    put_sem,
    ring_sem,
    wo_sem,
    kv_sem,
    nt_sem,
    wq_sem,
    home_sem,
    b_send,
    b_recv,
    g_send,
    g_recv,
    m_send,
    m_recv,
    z_send,
    z_recv,
    c_send,
    c_recv,
    sm,
    sm_near,
    sm_rows,
    sm_across,
    sm_planes,
    sm_ss,
    sm_rc,
    sm_ry,
    sm_rx,
    sm_rz,
    *refs,
):
    G, R, PB, NCH, D, NX, NP, NT = dm.G, dm.R, dm.PB, dm.NCH, dm.D, dm.NX, dm.NP, dm.NT
    TP, HC = wo.shape[0], wo.shape[2]
    PT = dm.PAIRS // TP
    p = Peers()
    n_a, NB = len(plan_a), len(plan_b)
    ra = Reduce(p, plan_a, refs[: Reduce.REFS])
    rb = Reduce(p, plan_b, refs[Reduce.REFS :])
    block = block_index()
    TILE = 256
    tiles = dm.P // TILE
    chips = p.chips
    S = D // (2 * chips)

    def begin(copies):
        for copy in copies:
            copy.start()

    def ready(copies):
        for copy in copies:
            copy.wait()

    def load_tile(i, slot):
        t = jnp.where(lax.rem(i, 2) == 0, 1 - p.tp, p.tp)
        first = pl.multiple_of(HC + i // 2 * T, 128)
        return [
            pltpu.make_async_copy(
                wm.at[t, :, pl.ds(first, T)], ring.at[slot, :, pl.ds(0, T)], ring_sem.at[0, slot]
            ),
            pltpu.make_async_copy(
                wm.at[t, :, pl.ds(first + FC, T)], ring.at[slot, :, pl.ds(T, T)], ring_sem.at[1, slot]
            ),
        ]

    def pair_at(it):
        turn = it % dm.PAIRS
        return jnp.where(turn % 2 == 0, 1 - p.tp, p.tp) * PT + turn // 2

    def load_kv(it, slot):
        pair, g = pair_at(it), it // dm.PAIRS
        lanes = pl.ds(pl.multiple_of(pair * 128, 128), 128)
        return [
            pltpu.make_async_copy(k_hbm.at[g, :, lanes], kbuf.at[slot], kv_sem.at[0, slot]),
            pltpu.make_async_copy(v_hbm.at[g, :, lanes], vbuf.at[slot], kv_sem.at[1, slot]),
        ]

    wo_load = pltpu.make_async_copy(wm.at[:, :, pl.ds(0, HC)], wo, wo_sem)
    wo_load.start()
    begin(load_tile(0, 0))
    begin(load_kv(0, 0))
    p.greet(trades=True)
    fill_masks(dm, maskp, maskx)
    gain_two, bias_two = ln[2:3, :], ln[3:4, :]

    hn, gd = slice(0, NT), slice(NT, 2 * NT)
    STEP = 128

    def by_rows(step):
        def prompt_part(i, carry):
            rows = pl.ds(pl.multiple_of(i * STEP, STEP), STEP)
            step(own_p[rows, :], cot_p[rows, :], i * STEP)
            return carry

        def cont_part(i, carry):
            rows = pl.ds(pl.multiple_of(i * STEP, STEP), STEP)
            step(own_c[rows, :], cot_c[rows, :], NP + i * STEP)
            return carry

        lax.fori_loop(0, NP // STEP, prompt_part, 0)
        lax.fori_loop(0, (NT - NP) // STEP, cont_part, 0)

    def shifted(first, row):
        return pl.ds(pl.multiple_of(first + row, STEP), STEP)

    wo_load.wait()

    def enter(x, cot, row):
        rows = shifted(0, row)
        r = x.astype(F32)
        for t in range(TP):
            r += dot_nt(att[rows, t * HC : (t + 1) * HC], wo[t])
        resid[rows, :] = r
        blk[rows, :] = r
        h, _ = norm_stats(r)
        n = (h * gain_two + bias_two).astype(BF16)
        dk[rows, :] = n
        nt[:, rows] = transpose(n)
        g = (mix[4] * cot.astype(F32)).astype(BF16)
        dk[shifted(NT, row), :] = g
        nt[:, shifted(NT, row)] = transpose(g)
        gh[rows, :] = jnp.zeros((STEP, D), F32)

    by_rows(enter)

    during = {}

    def on(stage, step):
        during.setdefault(stage, []).append(step)

    def run_when(index, name):
        for (kind, when), steps in during.items():
            if kind == name:

                @pl.when(index == when)
                def _():
                    for step in steps:
                        step()


    def small():
        small_out[...] = small_sum(
            p, sm, sm_near, sm_rows, sm_across, sm_planes, sm_ss, sm_rc, sm_ry, sm_rx, sm_rz
        )

    schedule(ra, rb, on, p.ctxs, small)

    def run(name):
        for kind, when in sorted(key for key in during if key[0] == name):
            for step in during[kind, when]:
                step()

    def feed(i, carry):
        slot = lax.rem(i, 2)

        @pl.when(i + 1 < 2 * n_a)
        def _():
            begin(load_tile(i + 1, 1 - slot))

        ready(load_tile(i, slot))
        up, dn = ring[slot, :, :T], ring[slot, :, T : 2 * T]
        c0 = 0.7978845608028654
        HALF = NT // 2
        for e in range(2):
            rows = slice(e * HALF, (e + 1) * HALF)
            u = dot(dk[rows, :], up)
            if e == 1:
                run_when(i, "m")
            u2 = u * u
            th = jnp.tanh(c0 * u * (1.0 + 0.044715 * u2))
            half = 0.5 * (1.0 + th)
            act = (u * half).astype(BF16)
            slope = half + 0.5 * u * (1.0 - th * th) * (c0 * (1.0 + 3 * 0.044715 * u2))
            dv[rows, :T] = act
            blk[rows, :] += dot_nt(act, dn)
            gu = (dot(dk[NT + e * HALF : NT + (e + 1) * HALF, :], dn) * slope).astype(BF16)
            dv[NT + e * HALF : NT + (e + 1) * HALF, :T] = gu
            gh[rows, :] += dot_nt(gu, up)

        @pl.when(i >= 2)
        def _():
            ra.cores_sent(slot * n_a + i // 2 - 1, slot)

        for y in range(chips):
            mine = slice(y * 2 * S, (y + 1) * 2 * S)
            ra.mine[slot, mine, :T] = dot(nt[mine, hn], dv[gd, :T]).astype(BF16)
            ra.mine[slot, mine, T:] = dot(nt[mine, gd], dv[hn, :T]).astype(BF16)
        ra.cores_send(slot * n_a + i // 2, slot)
        return carry

    lax.fori_loop(0, 2 * n_a, feed, 0)
    run("e")
    blk_away[:NT, :] = blk[...].astype(BF16)
    away = ra.copy(blk_away.at[pl.ds(0, NT), :], blk_home, b_send, b_recv, p.partner())

    @pl.when(p.core != p.tp)
    def _():
        away.start()

    @pl.when(p.core == p.tp)
    def _():
        blk_home[...] = blk_away[:NT, :]

    sm[...] = jnp.zeros_like(sm)

    def leave(x, cot, row):
        rows = shifted(0, row)
        cot = cot.astype(F32)
        sm[2:3, :] += jnp.sum(cot * blk[rows, :], axis=0, keepdims=True)
        h, scale = norm_stats(resid[rows, :])
        g = gh[rows, :]
        sm[0:1, :] += jnp.sum(g * h, axis=0, keepdims=True)
        sm[1:2, :] += jnp.sum(g, axis=0, keepdims=True)
        gr = mix[4] * cot + norm_back(g, gain_two, h, scale)
        resid[rows, :] = gr
        gb = gr.astype(BF16)
        nt[:, shifted(NT, row)] = transpose(gb)
        for t in range(TP):
            gatt[rows, t * HC : (t + 1) * HC] = dot(gb, wo[t]).astype(BF16)

    by_rows(leave)
    for slot, i in enumerate((0, NB)):
        t = p.tp if slot else 1 - p.tp
        lanes = pl.ds(pl.multiple_of(t * HC, 128), HC)
        for y in range(chips):
            mine = slice(y * 2 * S, (y + 1) * 2 * S)
            rb.mine[slot, mine, :] = dot(nt[mine, gd], att[:, lanes]).astype(BF16)
        rb.cores_send(i, slot)
    nt_load = [
        pltpu.make_async_copy(nt_hbm, nt, nt_sem.at[0]),
        pltpu.make_async_copy(own_nt_hbm, own_nt, nt_sem.at[1]),
    ]
    begin(nt_load)
    wq_load = pltpu.make_async_copy(wq_hbm.at[:, :, pl.ds(0, 3 * HC)], ring.at[:, :, pl.ds(0, 3 * HC)], wq_sem)
    wq_load.start()
    during.setdefault(("a", dm.PAIRS), []).insert(0, partial(ready, nt_load))

    def attend(turn, g):
        it = g * dm.PAIRS + turn
        pair = pair_at(it)
        slot = it % 2

        @pl.when(it + 1 < G * dm.PAIRS)
        def _():
            begin(load_kv(it + 1, 1 - slot))

        lanes = pl.ds(pl.multiple_of(pair * 128, 128), 128)
        rp = pl.ds(pl.multiple_of(g * PB, PB), PB)
        rc = pl.ds(pl.multiple_of(dm.NP + g * NCH, NCH), NCH)
        qp, qc = q[rp, lanes], q[rc, lanes]
        gp, gc = gatt[rp, lanes], gatt[rc, lanes]
        ap, ac = att[rp, lanes].astype(F32), att[rc, lanes].astype(F32)
        qt = heads_columns(transpose(qp), transpose(qc))
        gpt, gct = gp.astype(F32).T, gc.astype(F32).T
        gt = heads_columns(gpt.astype(BF16), gct.astype(BF16))
        qs, gs = heads_rows(qp, qc), heads_rows(gp, gc)
        prodp, prodc = gpt * ap.T, gct * ac.T
        delta = jnp.concatenate(
            [
                jnp.sum(prodp[:HD], axis=0, keepdims=True),
                jnp.sum(prodp[HD:], axis=0, keepdims=True),
                jnp.sum(prodc[:HD], axis=0, keepdims=True),
                jnp.sum(prodc[HD:], axis=0, keepdims=True),
            ],
            axis=1,
        )
        stat = lse[g * dm.PAIRS + pair]
        ready(load_kv(it, slot))

        def grads(s, kt, vt, cols):
            pr = jnp.exp(s - stat[:, cols:])
            dp = dot(vt, gt[:, cols:])
            ds = (pr * (dp - delta[:, cols:])).astype(BF16)
            gv = dot(pr.astype(BF16), gs[cols:])
            gk = dot(ds, qs[cols:])
            gq = dot(transpose(kt), ds)
            return gk, gv, gq

        acc = None
        for j in range(tiles):
            rows = slice(j * TILE, (j + 1) * TILE)
            kt = kbuf[slot, rows, :]
            s = dot(kt, qt)
            s = jnp.concatenate([s[:, : 2 * PB] + twice(maskp[rows, :]), s[:, 2 * PB :]], axis=1)
            gk, gv, gq = grads(s, kt, vbuf[slot, rows, :], 0)
            gk = rotate_back(gk, cos[rows, :], sin[rows, :]).astype(BF16)
            gv = gv.astype(BF16)
            out = pl.ds(pl.multiple_of(g * R + j * TILE, 128), TILE)
            dk[out, lanes] = gk
            dv[out, lanes] = gv
            if j == tiles // 2:
                run_when(it, "a")
            acc = gq if acc is None else acc + gq
        kt = kbuf[slot, dm.P :, :]
        s = dot(kt, qt[:, 2 * PB :]) + maskx[...]
        gk, gv, gq = grads(s, kt, vbuf[slot, dm.P :, :], 2 * PB)
        for c in range(dm.NC):
            rows = slice(dm.P, dm.P + CL)
            out = pl.ds(pl.multiple_of(g * R + dm.P + c * CL, CL), CL)
            part = rotate_back(gk[c * CL : (c + 1) * CL], cos[rows, :], sin[rows, :])
            dk[out, lanes] = part.astype(BF16)
            dv[out, lanes] = gv[c * CL : (c + 1) * CL].astype(BF16)
        accp = acc[:, : 2 * PB] * 0.125
        accc = (acc[:, 2 * PB :] + gq) * 0.125
        outp = jnp.where(sublane_pick((128, PB), True), accp[:, :PB], accp[:, PB:]).T
        outc = jnp.where(sublane_pick((128, NCH), True), accc[:, :NCH], accc[:, NCH:]).T
        tab = pl.ds(pl.multiple_of(block * PB, PB), PB)
        dq[rp, lanes] = rotate_back(outp, cos[tab, :], sin[tab, :]).astype(BF16)
        tab = pl.ds(pl.multiple_of(dm.P + p.core * dm.CH, dm.CH), dm.CH)
        for c in range(dm.NC):
            part = rotate_back(outc[c * dm.CH : (c + 1) * dm.CH], cos[tab, :], sin[tab, :])
            rows = pl.ds(pl.multiple_of(dm.NP + g * NCH + c * dm.CH, dm.CH), dm.CH)
            dq[rows, lanes] = part.astype(BF16)

        @pl.when(g == G - 1)
        def _():
            put = turn % 2
            index = put * NB + 1 + turn // 2
            rb.cores_sent(index - 1, put)
            both = jnp.concatenate([dk[:, lanes], dv[:, lanes]], axis=1)
            for y in range(chips):
                mine = slice(y * 2 * S, (y + 1) * 2 * S)
                rb.mine[put, mine, 128:] = dot(nt[mine, :], both).astype(BF16)
                rb.mine[put, mine, :128] = dot(own_nt[mine, :], dq[:, lanes]).astype(BF16)
            rb.cores_send(index, put)

        return g

    w = ring

    def project(rows):
        total = None
        for t in range(TP):
            part = dot_nt(dk[rows, t * HC : (t + 1) * HC], w[t, :, HC : 2 * HC])
            total = part if total is None else total + part
            total += dot_nt(dv[rows, t * HC : (t + 1) * HC], w[t, :, 2 * HC : 3 * HC])
        return total

    NCONT = NT - NP
    gain_one = ln[0:1, :]
    halves = lambda core, g: pl.ds(pl.multiple_of(core * NCONT + g * NCH, 16), NCH)

    def dx_at(g, k, first, count):
        c = p.ctx_after(k)
        if g == G - 1:
            return dk.at[pl.ds(pl.multiple_of(g * R + c * 2 * PB + first, PB), count), :]
        fit = D // (2 * PB)
        row = pl.multiple_of(c % fit * 2 * PB + first, PB)
        return ra.mine.at[c // fit, pl.ds(row, count), pl.ds(0, D)]

    def dx_rows(g, k, core):
        return dx_at(g, k, core * PB, PB)

    def to_mate(g, k):
        i = g * p.ctxs + k
        return ra.copy(dx_rows(g, k, 1 - p.core), dxm.at[i], m_send.at[i], m_recv.at[i], p.mate())

    def to_plane(g, k):
        i = g * (p.ctxs - 1) + k - 1
        return ra.copy(
            dx_rows(g, k, p.core), dxz.at[i], z_send.at[i], z_recv.at[i], p.at(ctx=p.ctx_after(k))
        )

    def each_group(g, step):
        for e in range(G):

            @pl.when(g == e)
            def _():
                step(e)

    def cont_copy(g):
        return ra.copy(
            blk_away.at[halves(1 - p.core, g), :],
            dxcm.at[pl.ds(pl.multiple_of(g * NCH, 16), NCH), :],
            c_send.at[g],
            c_recv.at[g],
            p.mate(),
        )

    def group(g, carry):
        lax.fori_loop(0, dm.PAIRS, attend, g)

        @pl.when(g == 0)
        def _():
            wq_load.wait()
            ra.cores_sent(n_a - 1, 0)
            ra.cores_sent(2 * n_a - 1, 1)

            @pl.when(p.core != p.tp)
            def _():
                away.wait_send()

        def planes(i, carry):
            @pl.when(i < p.ctxs)
            def _():
                k = lax.rem(i + 1, p.ctxs)
                both = pl.ds(pl.multiple_of(g * R + p.ctx_after(k) * 2 * PB, 2 * PB), 2 * PB)
                total = project(both).astype(BF16)

                def out(e):
                    dx_at(e, k, 0, 2 * PB)[...] = total
                    to_mate(e, k).start()

                each_group(g, out)
                run_when(g * p.ctxs + i, "p")

            @pl.when(i > 0)
            def _():
                k = lax.rem(i, p.ctxs)

                def back(e):
                    to_mate(e, k).wait_recv()
                    mine = dx_rows(e, k, p.core)
                    mine[...] = (mine[...].astype(F32) + dxm[e * p.ctxs + k].astype(F32)).astype(BF16)

                    @pl.when(k > 0)
                    def _():
                        to_plane(e, k).start()

                each_group(g, back)

            return carry

        lax.fori_loop(0, p.ctxs + 1, planes, 0)
        rows = pl.ds(pl.multiple_of(g * R + dm.P, CL), NX)
        total = project(rows).astype(BF16)
        for c in range(dm.NC):
            for e in range(2):
                out = pl.ds(pl.multiple_of(e * NCONT + g * NCH + c * dm.CH, dm.CH), dm.CH)
                blk_away[out, :] = total[c * CL + e * dm.CH : c * CL + (e + 1) * dm.CH]
        cont_copy(g).start()
        for first, count in ((g * PB, PB), (NP + g * NCH, NCH)):
            rows = pl.ds(pl.multiple_of(first, 16), count)
            total = dot_nt(dq[rows, :HC], w[0, :, :HC])
            for t in range(1, TP):
                total += dot_nt(dq[rows, t * HC : (t + 1) * HC], w[t, :, :HC])
            blk[rows, :] = total
        return carry

    def enter_back(gn, x, rows):
        gn += blk[rows, :]
        hat, scale = norm_stats(x.astype(F32))
        gatt[rows, :] = (resid[rows, :] + norm_back(gn, gain_one, hat, scale)).astype(BF16)
        sm[7:8, :] += jnp.sum(gn * hat, axis=0, keepdims=True)
        sm[8:9, :] += jnp.sum(gn, axis=0, keepdims=True)

    def gin_away(part):
        rows = pl.ds(0, NP) if part == 0 else pl.ds(NP, NT - NP)
        return ra.copy(gatt.at[rows, :], gin_home.at[rows, :], g_send.at[part], g_recv.at[part], p.partner())

    def give(part):
        rows = slice(0, NP) if part == 0 else slice(NP, NT)

        @pl.when(p.core != p.tp)
        def _():
            gin_away(part).start()

        @pl.when(p.core == p.tp)
        def _():
            gin_home[rows, :] = gatt[rows, :]

    lax.fori_loop(0, G, group, 0)
    homes = []
    for i, (a, c) in enumerate(
        [(home_arrays_p, home_arrays_c)]
        + [(early_p.at[e], early_c.at[e]) for e in range(3)]
        + [(home_cot_p, home_cot_c)]
    ):
        homes.append(pltpu.make_async_copy(a, dv.at[pl.ds(i * NT, NP), :], home_sem.at[0, i]))
        homes.append(pltpu.make_async_copy(c, dv.at[pl.ds(i * NT + NP, NT - NP), :], home_sem.at[1, i]))
    begin(homes)

    def cont_back(g, carry):
        cont_copy(g).wait_recv()
        here = pl.ds(pl.multiple_of(g * NCH, 16), NCH)
        gn = blk_away[halves(p.core, g), :].astype(F32) + dxcm[here, :].astype(F32)
        enter_back(gn, own_c[here, :], pl.ds(pl.multiple_of(NP + g * NCH, 16), NCH))
        return carry

    lax.fori_loop(0, G, cont_back, 0)
    give(1)

    ready(homes)

    @pl.when(p.core != p.tp)
    def _():
        away.wait_recv()

    def blend(i, carry):
        rows = shifted(0, i * STEP)
        res = mix[4] * blk_home[rows, :].astype(F32)
        c = dv[shifted(4 * NT, i * STEP), :].astype(F32)
        for e in range(4):
            a = dv[shifted(e * NT, i * STEP), :].astype(F32)
            res += mix[e] * a
            sm[3 + e : 4 + e, :] += jnp.sum(c * a, axis=0, keepdims=True)
        blk_home[rows, :] = res.astype(BF16)
        return carry

    lax.fori_loop(0, NT // STEP, blend, 0)
    puts = [
        pltpu.make_async_copy(blk_home.at[pl.ds(0, NP), :], out_p, put_sem.at[0]),
        pltpu.make_async_copy(blk_home.at[pl.ds(NP, NT - NP), :], out_c, put_sem.at[1]),
    ]
    begin(puts)
    for when in range(10):
        for step in during.get(("t", when), []):
            step()

    for g in range(G):
        gn = dx_rows(g, 0, p.core)[...].astype(F32)
        for k in range(1, p.ctxs):
            to_plane(g, k).wait_recv()
            gn += dxz[g * (p.ctxs - 1) + k - 1].astype(F32)
        here = slice(g * PB, (g + 1) * PB)
        enter_back(gn, own_p[here, :], here)
    give(0)
    for when in range(10, 20):
        for step in during.get(("t", when), []):
            step()
    gu_puts = []
    for j in range(n_a):
        ra.ctx_end(j)
        total = ra.result(j)
        gd_out[j * T : (j + 1) * T, :] = total[:, T:].T
        if len(gu_puts) > 0:
            gu_puts[-1].wait()
        gh[:S, :T] = total[:, :T]
        gu_puts.append(
            pltpu.make_async_copy(
                gh.at[pl.ds(0, S), pl.ds(0, T)], gu_out.at[:, pl.ds(j * T, T)], put_sem.at[2]
            )
        )
        gu_puts[-1].start()
    gu_puts[-1].wait()
    for j in range(NB):
        rb.ctx_end(j)
        total = rb.result(j)
        if j == 0:
            go_out[...] = total.T
        else:
            for c in range(3):
                first = c * HC + (j - 1) * 128
                gq_out[:, first : first + 128] = total[:, c * 128 : (c + 1) * 128]

    @pl.when(p.core != p.tp)
    def _():
        for part in range(2):
            gin_away(part).wait_recv()
            gin_away(part).wait_send()

    more = [
        pltpu.make_async_copy(gin_home.at[pl.ds(0, NP), :], gin_p, put_sem.at[2]),
        pltpu.make_async_copy(gin_home.at[pl.ds(NP, NT - NP), :], gin_c, put_sem.at[3]),
    ]
    begin(more)
    ready(puts + more)
    rb.cores_sent(NB - 1, 0)
    rb.cores_sent(2 * NB - 1, 1)
    for g in range(G):
        for k in range(p.ctxs):
            to_mate(g, k).wait_send()
        for k in range(1, p.ctxs):
            to_plane(g, k).wait_send()
        cont_copy(g).wait_send()
    ra.drain()
    rb.drain()


def params(**more):
    return pltpu.CompilerParams(vmem_limit_bytes=VMEM_LIMIT, **more)


def per_device(
    prompt_in,
    cont_in,
    prompt_embed,
    cont_embed,
    prompt_earlier,
    cont_earlier,
    ln1_gain,
    ln1_bias,
    ln2_gain,
    ln2_bias,
    w_qkv,
    w_out,
    w_up,
    w_down,
    mix_weights,
    prompt_cot,
    cont_cot,
):
    G, PB, D = prompt_in.shape
    NC, CH = cont_in.shape[1], cont_in.shape[2]
    TP = lax.axis_size("tp")
    PROMPT = PB * TP * lax.axis_size("ctx")
    HC, FC = w_qkv.shape[2], w_up.shape[1]
    S = w_qkv.shape[0]
    dm = Dims(G, PROMPT, PB, NC, CH, D, HC * TP // HD)
    R, NT, NP = dm.R, dm.NT, dm.NP

    sds = jax.ShapeDtypeStruct
    chips, ctxs = lax.axis_size("dp") // 2, lax.axis_size("ctx")
    norms = jnp.stack([ln1_gain, ln1_bias, ln2_gain, ln2_bias], axis=1)
    norms = jnp.pad(norms, ((0, 0), (0, 124)))
    wq_shard = jnp.concatenate([w_qkv.reshape(S, 3 * HC), norms], axis=1)
    wm_shard = jnp.concatenate([w_out.T, w_up, w_down.T], axis=1)

    positions = jnp.arange(PROMPT + CL, dtype=jnp.int32).astype(F32)
    lane = jnp.arange(128, dtype=jnp.int32)
    freq = 10000.0 ** (-((lane % 32).astype(F32) / 32))
    angles = positions[:, None] * freq[None, :]
    cos, sin = jnp.cos(angles), jnp.sin(angles)
    second = (lane % 64) >= 32
    sin = jnp.where(second[None, :], sin, -sin)

    any_ = pl.BlockSpec(memory_space=pl.ANY)
    vmem = pl.BlockSpec(memory_space=pltpu.VMEM)
    dma = pltpu.SemaphoreType.DMA
    left = (HC + 2 * FC) // 128 * 2 // 3 * 128
    q, att, lse, ln, nt, own_nt, k, v, wq, wm, own_p, own_c, cot_p, cot_c = pl.pallas_call(
        partial(forward_kernel, dm, left),
        out_shape=(
            sds((NT, D), BF16),
            sds((NT, D), BF16),
            sds((G * dm.PAIRS, 1, dm.COLS), F32),
            sds((8, D), F32),
            sds((D, G * R), BF16),
            sds((D, NT), BF16),
            sds((G, R, D), BF16),
            sds((G, R, D), BF16),
            sds((TP, D, 3 * HC + 128), BF16),
            sds((TP, D, HC + 2 * FC), BF16),
            sds(prompt_in.shape, BF16),
            sds(cont_in.shape, BF16),
            sds(prompt_in.shape, BF16),
            sds(cont_in.shape, BF16),
        ),
        in_specs=[vmem] * 5 + [any_] * 3,
        out_specs=(vmem,) * 4 + (any_,) * 10,
        scratch_shapes=[
            pltpu.VMEM((D, G * R), BF16),
            pltpu.VMEM((D, NT), BF16),
            pltpu.VMEM((G, R, D), BF16),
            pltpu.VMEM((G, R, D), BF16),
            pltpu.VMEM((PROMPT, PB), F32),
            pltpu.VMEM((dm.NX, 2 * dm.NCH), F32),
            pltpu.VMEM((PROMPT, dm.COLS), F32),
            pltpu.VMEM((G * R, D), BF16),
            pltpu.VMEM((NT, D), BF16),
            pltpu.VMEM((2 * ctxs, G, PB, D), BF16),
            pltpu.VMEM((2, G, NC, CH, D), BF16),
            pltpu.VMEM((TP, D, 3 * HC + 128), BF16),
            dma((7,)),
            dma((4,)),
            dma((4,)),
            dma((2 * ctxs - 1,)),
            dma((ctxs - 1,)),
            dma((ctxs,)),
            dma,
            dma,
            dma((2,)),
        ]
        + WeightGather.semaphores(chips)
        + WeightGather.semaphores(chips),
        compiler_params=params(collective_id=0, has_side_effects=True),
        name="forward",
    )(prompt_in, cont_in, cos, sin, wq_shard, wm_shard, prompt_cot, cont_cot)
    T = 512 if FC % 512 == 0 else 256
    plan_a, plan_b = [False, False, False], [True, True, True, False]
    far = max(chips - 1, 1)
    rows = lambda x: x.reshape(-1, D)
    out_p, out_c, gin_p, gin_c, gq, go, gu, gd, small = pl.pallas_call(
        partial(backward_kernel, dm, T, FC, plan_a, plan_b),
        out_shape=(
            sds((NP, D), BF16),
            sds((NT - NP, D), BF16),
            sds((NP, D), BF16),
            sds((NT - NP, D), BF16),
            sds((S, 3 * HC), F32),
            sds((HC, S), F32),
            sds((S, FC), F32),
            sds((FC, S), F32),
            sds((16, D), F32),
        ),
        in_specs=[pl.BlockSpec(memory_space=pltpu.SMEM)] + [vmem] * 10 + [any_] * 12,
        out_specs=(any_,) * 4 + (vmem, vmem, any_, vmem, vmem),
        scratch_shapes=[
            pltpu.VMEM((NT, D), F32),
            pltpu.VMEM((NT, D), F32),
            pltpu.VMEM((NT, D), F32),
            pltpu.VMEM((TP, D, HC), BF16),
            pltpu.VMEM((2, D, max(2 * T, 3 * HC)), BF16),
            pltpu.VMEM((NT, D), BF16),
            pltpu.VMEM((D, G * R), BF16),
            pltpu.VMEM((D, NT), BF16),
            pltpu.VMEM((PROMPT, PB), F32),
            pltpu.VMEM((dm.NX, 2 * dm.NCH), F32),
            pltpu.VMEM((2, R, 128), BF16),
            pltpu.VMEM((2, R, 128), BF16),
            pltpu.VMEM((G * R, D), BF16),
            pltpu.VMEM((G * R, D), BF16),
            pltpu.VMEM((NT, D), BF16),
            pltpu.VMEM((G * ctxs, PB, D), BF16),
            pltpu.VMEM((G * (ctxs - 1), PB, D), BF16),
            pltpu.VMEM((NT - NP, D), BF16),
            pltpu.VMEM((max(NT, 2 * (NT - NP)), D), BF16),
            pltpu.VMEM((NT, D), BF16),
            pltpu.VMEM((NT, D), BF16),
            dma((4,)),
            dma((2, 2)),
            dma,
            dma((2, 2)),
            dma((2,)),
            dma,
            dma((2, 5)),
            dma,
            dma,
            dma((2,)),
            dma((2,)),
            dma((G * ctxs,)),
            dma((G * ctxs,)),
            dma((G * (ctxs - 1),)),
            dma((G * (ctxs - 1),)),
            dma((G,)),
            dma((G,)),
            pltpu.VMEM((16, D), F32),
            pltpu.VMEM((16, D), F32),
            pltpu.VMEM((chips, 16, D), F32),
            pltpu.VMEM((2, 16, D), F32),
            pltpu.VMEM((ctxs, 16, D), F32),
            dma((1 + chips + ctxs,)),
            dma,
            dma((far,)),
            dma,
            dma((ctxs - 1,)),
        ]
        + Reduce.scratch(plan_a, chips, S, 2 * T)
        + Reduce.scratch(plan_b, chips, S, HC),
        compiler_params=params(collective_id=1, has_side_effects=True),
        name="backward",
    )(
        mix_weights,
        att,
        rows(own_p),
        rows(own_c),
        rows(cot_p),
        rows(cot_c),
        ln,
        q,
        lse,
        cos,
        sin,
        wm,
        k,
        v,
        nt,
        own_nt,
        wq,
        rows(prompt_embed),
        rows(cont_embed),
        prompt_earlier.reshape(3, NP, D),
        cont_earlier.reshape(3, NT - NP, D),
        rows(prompt_cot),
        rows(cont_cot),
    )
    start = lax.axis_index("dp") * S
    mine = lax.dynamic_slice_in_dim(small, start, S, axis=1)
    return (
        out_p.reshape(prompt_in.shape),
        out_c.reshape(cont_in.shape),
        gin_p.reshape(prompt_in.shape),
        gin_c.reshape(cont_in.shape),
        mine[7],
        mine[8],
        mine[0],
        mine[1],
        gq.reshape(S, 3, HC),
        go,
        gu,
        gd,
        jnp.sum(jnp.concatenate([small[3:7], small[2:3]]), axis=1),
    )


def solution(mesh):
    tokens = P("dp", ("ctx", "tp"), None)
    conts = P("dp", "ctx", "tp", None)
    weights = (P("dp", None, "tp"), P("tp", "dp"), P("dp", "tp"), P("tp", "dp"))
    in_specs = (
        tokens,
        conts,
        tokens,
        conts,
        P(None, "dp", ("ctx", "tp"), None),
        P(None, "dp", "ctx", "tp", None),
        P("dp"),
        P("dp"),
        P("dp"),
        P("dp"),
        *weights,
        P(),
        tokens,
        conts,
    )
    out_specs = (
        tokens,
        conts,
        tokens,
        conts,
        P("dp"),
        P("dp"),
        P("dp"),
        P("dp"),
        *weights,
        P(),
    )
    return jax.shard_map(
        per_device, mesh=mesh, in_specs=in_specs, out_specs=out_specs, check_vma=False
    )
```

```python
from functools import partial

import jax
import jax.numpy as jnp
import numpy as np
from jax import lax
from jax.experimental import pallas as pl
from jax.experimental.pallas import tpu as pltpu
from jax.sharding import PartitionSpec as P

HD = 64
CL = 128
EPS = 1e-05
NEG = -1e30
F32 = jnp.float32
BF16 = jnp.bfloat16
VMEM_LIMIT = 67043328


def dot(a, b):
    return lax.dot_general(a, b, (((1,), (0,)), ((), ())), preferred_element_type=F32)


def dot_nt(a, b):
    return lax.dot_general(a, b, (((1,), (1,)), ((), ())), preferred_element_type=F32)


def norm_stats(x):
    mean = jnp.mean(x, axis=-1, keepdims=True)
    centered = x - mean
    var = jnp.mean(centered * centered, axis=-1, keepdims=True)
    scale = lax.rsqrt(var + EPS)
    return centered * scale, scale


def norm_back(grad, gain, hat, scale):
    gh = grad * gain
    return scale * (
        gh
        - jnp.mean(gh, axis=-1, keepdims=True)
        - hat * jnp.mean(gh * hat, axis=-1, keepdims=True)
    )


def swap_halves(x):
    second = lax.broadcasted_iota(jnp.int32, x.shape, 1) % HD >= HD // 2
    return jnp.where(second, pltpu.roll(x, 32, 1), pltpu.roll(x, 96, 1))


def rotate(x, cos, sin):
    return x * cos + swap_halves(x) * sin


def rotate_back(x, cos, sin):
    return x * cos - swap_halves(x) * sin


def lane_pick(shape, low):
    lanes = lax.broadcasted_iota(jnp.int32, shape, 1)
    return lanes < HD if low else lanes >= HD


def sublane_pick(shape, low):
    rows = lax.broadcasted_iota(jnp.int32, shape, 0)
    return rows < HD if low else rows >= HD


def transpose(x):
    return x.astype(F32).T.astype(x.dtype)


class Dims:
    def __init__(self, groups, prompt, pb, nc, ch, d, heads):
        self.G, self.P, self.PB, self.NC, self.CH, self.D = groups, prompt, pb, nc, ch, d
        self.NCH = nc * ch
        self.R = prompt + nc * CL
        self.NX = nc * CL
        self.NR = pb + self.NCH
        self.NP = groups * pb
        self.NT = groups * self.NR
        self.PAIRS = heads // 2
        self.COLS = 2 * self.NR


MESH = pl.DeviceIdType.MESH


def half_index():
    return lax.axis_index("dp") % 2


def block_index():
    return lax.axis_index("ctx") * 2 + half_index()


class Peers:
    def __init__(self):
        self.ctxs = lax.axis_size("ctx")
        self.chips = lax.axis_size("dp") // 2
        self.tps = lax.axis_size("tp")
        self.dp = lax.axis_index("dp")
        self.ctx = lax.axis_index("ctx")
        self.tp = lax.axis_index("tp")
        self.core = self.dp % 2
        self.chip = self.dp // 2

    def at(self, dp=None, ctx=None, tp=None):
        return {
            "dp": self.dp if dp is None else dp,
            "ctx": self.ctx if ctx is None else ctx,
            "tp": self.tp if tp is None else tp,
        }

    def across(self):
        return self.at(tp=1 - self.tp)

    def mate(self):
        return self.at(dp=self.chip * 2 + 1 - self.core)

    def chip_after(self, k):
        return lax.rem(self.chip + k, self.chips)

    def chip_before(self, k):
        return lax.rem(self.chip + self.chips - k, self.chips)

    def row(self, k):
        return self.at(dp=self.chip_after(k) * 2 + self.core)

    def ctx_after(self, k):
        return lax.rem(self.ctx + k, self.ctxs)

    def ctx_before(self, k):
        return lax.rem(self.ctx + self.ctxs - k, self.ctxs)

    def plane(self, k):
        return self.at(ctx=self.ctx_after(k))

    def partner(self):
        return self.at(dp=self.chip * 2 + self.tp, tp=self.core)

    def greet(self, trades=False):
        barrier = pltpu.get_barrier_semaphore()
        peers = [self.across(), self.mate()]
        peers += [self.row(k) for k in range(1, self.chips)]
        peers += [self.plane(k) for k in range(1, self.ctxs)]
        for peer in peers:
            pl.semaphore_signal(barrier, inc=1, device_id=peer, device_id_type=MESH)
        count = len(peers)
        if trades:
            away = self.core != self.tp

            @pl.when(away)
            def _():
                pl.semaphore_signal(
                    barrier, inc=1, device_id=self.partner(), device_id_type=MESH
                )

            count += jnp.where(away, 1, 0)
        pl.semaphore_wait(barrier, count)


def send(src, dst, send_sem, recv_sem, device):
    copy = pltpu.make_async_remote_copy(
        src_ref=src,
        dst_ref=dst,
        send_sem=send_sem,
        recv_sem=recv_sem,
        device_id=device,
        device_id_type=MESH,
    )
    copy.start()
    return copy


def arrived(ref, sem, peers):
    pltpu.make_async_remote_copy(
        src_ref=ref,
        dst_ref=ref,
        send_sem=sem,
        recv_sem=sem,
        device_id=peers.mate(),
        device_id_type=MESH,
    ).wait_recv()


class WeightGather:
    def __init__(self, peers, shard, full, left, sends, across, rows, mate):
        self.p, self.shard, self.full, self.left = peers, shard, full, left
        self.sends, self.across, self.rows, self.from_mate = sends, across, rows, mate
        self.copies = []
        self.size, self.cols = shard.shape

    @staticmethod
    def semaphores(chips):
        far = chips - 1
        return [
            pltpu.SemaphoreType.DMA((3 + 6 * far,)),
            pltpu.SemaphoreType.DMA((chips,)),
            pltpu.SemaphoreType.DMA((2, max(far, 1))),
            pltpu.SemaphoreType.DMA((2, chips)),
        ]

    def piece(self, tp, dp, cols=slice(None)):
        rows = pl.ds(pl.multiple_of(dp * self.size, 16), self.size)
        if cols == slice(None):
            return self.full.at[tp, rows, :]
        return self.full.at[tp, rows, pl.ds(cols.start, cols.stop - cols.start)]

    def go(self, src, dst, recv_sem, device):
        self.copies.append(send(src, dst, self.sends.at[len(self.copies)], recv_sem, device))

    def start(self):
        p = self.p
        self.go(self.shard, self.piece(p.tp, p.dp), self.across.at[0], p.across())
        for k in range(1, p.chips):
            self.go(self.shard, self.piece(p.tp, p.dp), self.rows.at[0, k - 1], p.row(k))
        self.go(self.shard, self.piece(p.tp, p.dp), self.from_mate.at[0, 0], p.mate())

    def relay_across(self):
        p = self.p
        got = self.piece(1 - p.tp, p.dp)
        arrived(got, self.across.at[0], p)
        part = self.piece(1 - p.tp, p.dp, slice(0, self.left))
        for k in range(1, p.chips):
            self.go(part, part, self.rows.at[1, k - 1], p.row(k))
        self.go(got, got, self.from_mate.at[1, 0], p.mate())

    def relay_rows(self):
        p = self.p
        for k in range(1, p.chips):
            dp = p.chip_before(k) * 2 + p.core
            got = self.piece(p.tp, dp)
            arrived(got, self.rows.at[0, k - 1], p)
            if self.left < self.cols:
                part = self.piece(p.tp, dp, slice(self.left, self.cols))
                self.go(part, part, self.across.at[k], p.across())
            self.go(got, got, self.from_mate.at[0, k], p.mate())

    def relay_last(self):
        p = self.p
        for k in range(1, p.chips):
            dp = p.chip_before(k) * 2 + p.core
            arrived(self.piece(1 - p.tp, dp, slice(0, self.left)), self.rows.at[1, k - 1], p)
            if self.left < self.cols:
                part = self.piece(1 - p.tp, dp, slice(self.left, self.cols))
                arrived(part, self.across.at[k], p)
            got = self.piece(1 - p.tp, dp)
            self.go(got, got, self.from_mate.at[1, k], p.mate())

    def finish(self):
        p = self.p
        for part in range(2):
            tp = p.tp if part == 0 else 1 - p.tp
            for k in range(p.chips):
                dp = p.chip_before(k) * 2 + 1 - p.core
                arrived(self.piece(tp, dp), self.from_mate.at[part, k], p)

    def drain(self):
        for copy in self.copies:
            copy.wait_send()


def twice(x):
    return jnp.concatenate([x, x], axis=1)


def fill_masks(dm, maskp, maskx):
    block = block_index()
    keys = lax.broadcasted_iota(jnp.int32, maskp.shape, 0)
    cols = lax.broadcasted_iota(jnp.int32, maskp.shape, 1) % dm.PB
    maskp[...] = jnp.where(keys <= cols + block * dm.PB, 0.0, NEG)
    keys = lax.broadcasted_iota(jnp.int32, maskx.shape, 0)
    cols = lax.broadcasted_iota(jnp.int32, maskx.shape, 1) % dm.NCH
    seen = (keys // CL == cols // dm.CH) & (
        keys % CL <= cols % dm.CH + half_index() * dm.CH
    )
    maskx[...] = jnp.where(seen, 0.0, NEG)


def heads_columns(a, b):
    lo_a, lo_b = sublane_pick(a.shape, True), sublane_pick(b.shape, True)
    zero_a, zero_b = jnp.zeros_like(a), jnp.zeros_like(b)
    return jnp.concatenate(
        [
            jnp.where(lo_a, a, zero_a),
            jnp.where(lo_a, zero_a, a),
            jnp.where(lo_b, b, zero_b),
            jnp.where(lo_b, zero_b, b),
        ],
        axis=1,
    )


def heads_rows(a, b):
    lo_a, lo_b = lane_pick(a.shape, True), lane_pick(b.shape, True)
    zero_a, zero_b = jnp.zeros_like(a), jnp.zeros_like(b)
    return jnp.concatenate(
        [
            jnp.where(lo_a, a, zero_a),
            jnp.where(lo_a, zero_a, a),
            jnp.where(lo_b, b, zero_b),
            jnp.where(lo_b, zero_b, b),
        ],
        axis=0,
    )


def forward_kernel(
    dm,
    left,
    prompt,
    cont,
    cos,
    sin,
    wq,
    wm,
    cot_p,
    cot_c,
    q_out,
    att_out,
    lse_out,
    ln_out,
    nt_hbm,
    own_nt_hbm,
    k_hbm,
    v_hbm,
    w_hbm,
    wm_out,
    own_p_hbm,
    own_c_hbm,
    cot_p_out,
    cot_c_out,
    nt_out,
    own_out,
    k_out,
    v_out,
    maskp,
    maskx,
    sbuf,
    all_rows,
    own_rows,
    xp,
    xc,
    w,
    put_sem,
    trade_send,
    trade_recv,
    x_send,
    x_plane,
    x_mate,
    c_send,
    c_mate,
    own_sem,
    *sems,
):
    G, R, PB, NCH, D, NP, NT = dm.G, dm.R, dm.PB, dm.NCH, dm.D, dm.NP, dm.NT
    NC, CH = dm.NC, dm.CH
    HC = (w.shape[2] - 128) // 3
    TP = w.shape[0]
    p = Peers()
    block = block_index()
    gq = WeightGather(p, wq, w, wq.shape[1], *sems[:4])
    gm = WeightGather(p, wm, wm_out, left, *sems[4:])
    size = wq.shape[0]
    mine = pl.ds(pl.multiple_of(p.dp * size, 16), size)

    landing = [xp.at[p.ctx * 2 + p.tp], xc.at[p.tp], cot_p_out, cot_c_out]

    def moved(i):
        src = [prompt, cont, cot_p, cot_c][i]
        return pltpu.make_async_remote_copy(
            src_ref=src,
            dst_ref=landing[i],
            send_sem=trade_send.at[i],
            recv_sem=trade_recv.at[i],
            device_id=p.partner(),
            device_id_type=MESH,
        )

    def kept(i):
        return pltpu.make_async_copy([prompt, cont, cot_p, cot_c][i], landing[i], trade_send.at[i])

    moves = p.core != p.tp

    def trade(i):
        @pl.when(moves)
        def _():
            moved(i).start()

        @pl.when(jnp.logical_not(moves))
        def _():
            kept(i).start()

    def traded(i):
        @pl.when(moves)
        def _():
            moved(i).wait_recv()

        @pl.when(jnp.logical_not(moves))
        def _():
            kept(i).wait()

    local = [
        pltpu.make_async_copy(wq, w.at[p.tp, mine, :], own_sem.at[0]),
        pltpu.make_async_copy(wm, wm_out.at[p.tp, mine, :], own_sem.at[1]),
    ]
    for copy in local:
        copy.start()
    p.greet(trades=True)
    trade(0)
    gq.start()
    trade(1)
    fill_masks(dm, maskp, maskx)
    traded(0)
    own = xp.at[block]
    sent = []
    for k in range(1, p.ctxs):
        sent.append(send(own, own, x_send.at[k - 1], x_plane.at[k - 1], p.plane(k)))
    sent.append(send(own, own, x_send.at[p.ctxs - 1], x_mate.at[0], p.mate()))
    gq.relay_across()
    gq.relay_rows()
    traded(1)
    sent.append(send(xc.at[p.core], xc.at[p.core], c_send, c_mate, p.mate()))
    gq.relay_last()
    gm.start()
    trade(2)
    trade(3)
    gq.finish()
    local[0].wait()
    puts = [
        pltpu.make_async_copy(w, w_hbm, put_sem.at[0]),
        pltpu.make_async_copy(xp.at[block], own_p_hbm, put_sem.at[1]),
        pltpu.make_async_copy(xc.at[p.core], own_c_hbm, put_sem.at[2]),
    ]
    for put in puts:
        put.start()
    ln = w[0, :, 3 * HC :].astype(F32).T[:8, :]
    ln_out[...] = ln
    gain, bias = ln[0:1, :], ln[1:2, :]

    def normed(x):
        hat, _ = norm_stats(x.astype(F32))
        return (hat * gain + bias).astype(BF16)

    def turned(x, table):
        rows = x.shape[0]
        return rotate(x, cos[pl.ds(table, rows), :], sin[pl.ds(table, rows), :])

    x = jnp.concatenate([xp[block].reshape(NP, D), xc[p.core].reshape(NT - NP, D)], axis=0)
    n = normed(x)
    own_rows[...] = n
    places = [(g * PB, PB, pl.multiple_of(block * PB, PB)) for g in range(G)]
    places += [
        (NP + i * CH, CH, pl.multiple_of(dm.P + p.core * CH, CH)) for i in range(G * NC)
    ]
    for t in range(TP):
        qq = dot(n, w[t, :, :HC])
        for first, count, table in places:
            for j in range(HC // 128):
                tile = turned(qq[first : first + count, j * 128 : (j + 1) * 128], table).astype(BF16)
                q_out[first : first + count, t * HC + j * 128 : t * HC + (j + 1) * 128] = (
                    tile.astype(F32) * 0.125
                ).astype(BF16)
    own_out[...] = transpose(own_rows[...])

    def keys_values(x, places):
        n = normed(x)
        for first, count, g, row, table in places:
            all_rows[pl.ds(pl.multiple_of(g * R + row, 16), count), :] = n[first : first + count]
        for t in range(TP):
            kk = dot(n, w[t, :, HC : 2 * HC])
            for first, count, g, row, table in places:
                for j in range(HC // 128):
                    tile = turned(kk[first : first + count, j * 128 : (j + 1) * 128], table)
                    k_out[g, pl.ds(row, count), t * HC + j * 128 : t * HC + (j + 1) * 128] = tile.astype(BF16)
            vv = dot(n, w[t, :, 2 * HC : 3 * HC]).astype(BF16)
            for first, count, g, row, table in places:
                v_out[g, pl.ds(row, count), t * HC : (t + 1) * HC] = vv[first : first + count]

    arrived(xc.at[1 - p.core], c_mate, p)
    x = [xc[e, g, c] for g in range(G) for c in range(NC) for e in range(2)]
    keys_values(
        jnp.concatenate(x, axis=0),
        [((g * NC + c) * CL, CL, g, dm.P + c * CL, dm.P) for g in range(G) for c in range(NC)],
    )

    def relay(k):
        b = p.ctx_before(k) * 2 + p.core
        return pltpu.make_async_remote_copy(
            src_ref=xp.at[b],
            dst_ref=xp.at[b],
            send_sem=x_send.at[p.ctxs + k - 1],
            recv_sem=x_mate.at[k],
            device_id=p.mate(),
            device_id_type=MESH,
        )

    def plane(k, carry):
        c = p.ctx_before(k)

        @pl.when(k > 0)
        def _():
            arrived(xp.at[c * 2 + p.core], x_plane.at[k - 1], p)
            relay(k).start()

        arrived(xp.at[c * 2 + 1 - p.core], x_mate.at[k], p)
        x = xp[pl.ds(c * 2, 2)].reshape(2 * NP, D)
        places = []
        for e in range(2):
            row = pl.multiple_of((c * 2 + e) * PB, PB)
            places += [((e * G + g) * PB, PB, g, row, row) for g in range(G)]
        keys_values(x, places)
        return carry

    lax.fori_loop(0, p.ctxs, plane, 0)
    puts += [
        pltpu.make_async_copy(k_out, k_hbm, put_sem.at[3]),
        pltpu.make_async_copy(v_out, v_hbm, put_sem.at[4]),
    ]
    for put in puts[3:]:
        put.start()

    def turn(i, carry):
        rows = pl.ds(pl.multiple_of(i * 256, 256), 256)
        nt_out[:, rows] = transpose(all_rows[rows, :])
        return carry

    lax.fori_loop(0, G * R // 256, turn, 0)
    puts += [
        pltpu.make_async_copy(nt_out, nt_hbm, put_sem.at[5]),
        pltpu.make_async_copy(own_out, own_nt_hbm, put_sem.at[6]),
    ]
    for put in puts[5:]:
        put.start()
    gm.relay_across()
    gm.relay_rows()

    TILE = 256
    tiles = dm.P // TILE

    def attend(i, carry):
        g, pair = i // dm.PAIRS, i % dm.PAIRS
        lanes = pl.ds(pl.multiple_of(pair * 128, 128), 128)
        qp = q_out[pl.ds(pl.multiple_of(g * PB, PB), PB), lanes]
        qc = q_out[pl.ds(pl.multiple_of(dm.NP + g * NCH, NCH), NCH), lanes]
        qt = heads_columns(transpose(qp), transpose(qc))
        top = None
        for j in range(tiles):
            s = dot(k_out[g, j * TILE : (j + 1) * TILE, lanes], qt)
            sbuf[j * TILE : (j + 1) * TILE, : 2 * PB] = (
                s[:, : 2 * PB] + twice(maskp[j * TILE : (j + 1) * TILE, :])
            )
            sbuf[j * TILE : (j + 1) * TILE, 2 * PB :] = s[:, 2 * PB :]
            here = jnp.max(sbuf[j * TILE : (j + 1) * TILE, :], axis=0, keepdims=True)
            top = here if top is None else jnp.maximum(top, here)
        sx = dot(k_out[g, dm.P :, lanes], qt[:, 2 * PB :]) + maskx[...]
        topx = jnp.max(sx, axis=0, keepdims=True)
        top = jnp.concatenate([top[:, : 2 * PB], jnp.maximum(top[:, 2 * PB :], topx)], axis=1)
        total, acc = None, None
        for j in range(tiles):
            e = jnp.exp(sbuf[j * TILE : (j + 1) * TILE, :] - top)
            here = jnp.sum(e, axis=0, keepdims=True)
            vt = transpose(v_out[g, j * TILE : (j + 1) * TILE, lanes])
            part = dot(vt, e.astype(BF16))
            total = here if total is None else total + here
            acc = part if acc is None else acc + part
        ex = jnp.exp(sx - top[:, 2 * PB :])
        partx = dot(transpose(v_out[g, dm.P :, lanes]), ex.astype(BF16))
        totalx = jnp.sum(ex, axis=0, keepdims=True)
        total = jnp.concatenate([total[:, : 2 * PB], total[:, 2 * PB :] + totalx], axis=1)
        acc_p = acc[:, : 2 * PB] / total[:, : 2 * PB]
        acc_c = (acc[:, 2 * PB :] + partx) / total[:, 2 * PB :]
        lse_out[i] = top + jnp.log(total)
        outp = jnp.where(sublane_pick((128, PB), True), acc_p[:, :PB], acc_p[:, PB:])
        outc = jnp.where(sublane_pick((128, NCH), True), acc_c[:, :NCH], acc_c[:, NCH:])
        att_out[pl.ds(pl.multiple_of(g * PB, PB), PB), lanes] = outp.T.astype(BF16)
        att_out[pl.ds(pl.multiple_of(dm.NP + g * NCH, NCH), NCH), lanes] = outc.T.astype(BF16)
        return carry

    lax.fori_loop(0, G * dm.PAIRS, attend, 0)
    gm.relay_last()
    gm.finish()
    gq.drain()
    gm.drain()
    for copy in sent:
        copy.wait_send()
    for k in range(1, p.ctxs):
        relay(k).wait_send()
    local[1].wait()
    for i in (2, 3):
        traded(i)

    @pl.when(moves)
    def _():
        for i in range(4):
            moved(i).wait_send()

    for put in puts:
        put.wait()


class Reduce:
    REFS = 13

    def __init__(self, p, cross_first, refs):
        self.p, self.n, self.cross_first = p, len(cross_first), cross_first
        self.mine, self.got, self.row, self.acr, self.zin = refs[:5]
        self.sc, self.rc, self.sy, self.ry, self.sx, self.rx, self.sz, self.rz = refs[5:13]
        mid = p.ctxs // 2
        self.centre = (p.ctx == mid - 1) | (p.ctx == mid)
        self.outer = (p.ctx > 0) & (p.ctx < p.ctxs - 1)
        step = jnp.where(p.ctx < mid, 1, -1)
        self.inner_at = p.ctx + step
        self.outer_at = jnp.clip(p.ctx - step, 0, p.ctxs - 1)

    @staticmethod
    def scratch(cross_first, chips, size, width):
        n = len(cross_first)
        dma = pltpu.SemaphoreType.DMA
        far = max(chips - 1, 1)
        rows = n + sum(1 for c in cross_first if not c)
        parts = sum(chips if c else 1 for c in cross_first)
        return [
            pltpu.VMEM((2, chips * 2 * size, width), BF16),
            pltpu.VMEM((2 * n, chips, size, width), BF16),
            pltpu.VMEM((rows, far, size, width), BF16),
            pltpu.VMEM((parts, size, width), BF16),
            pltpu.VMEM((n, 2, size, width), BF16),
            dma((2 * n, chips)),
            dma((2 * n, chips)),
            dma((2 * n, far)),
            dma((2 * n, far)),
            dma((n,)),
            dma((n,)),
            dma((n, 2)),
            dma((n, 2)),
        ]

    def copy(self, src, dst, send_sem, recv_sem, device):
        return pltpu.make_async_remote_copy(
            src_ref=src,
            dst_ref=dst,
            send_sem=send_sem,
            recv_sem=recv_sem,
            device_id=device,
            device_id_type=MESH,
        )

    def slot(self, whose, j):
        return 0 if whose == "other" else 1

    def crosses(self, i):
        return self.cross_first[i % self.n]

    def travels(self, i):
        return i >= self.n or not self.crosses(i)

    def mine_of(self, y, core):
        size = self.got.shape[2]
        return pl.ds(pl.multiple_of((2 * y + core) * size, 16), size)

    def by_core(self, i, slot, y):
        p = self.p
        return self.copy(
            self.mine.at[slot, self.mine_of(y, 1 - p.core), :],
            self.got.at[i, y],
            self.sc.at[i, y],
            self.rc.at[i, y],
            p.mate(),
        )

    def row_slot(self, i):
        return sum(1 for e in range(i) if self.travels(e))

    def by_row(self, i, k):
        p = self.p
        return self.copy(
            self.got.at[i, p.chip_after(k)],
            self.row.at[self.row_slot(i), k - 1],
            self.sy.at[i, k - 1],
            self.ry.at[i, k - 1],
            p.row(k),
        )

    def by_tp(self, j):
        p = self.p
        slot = self.acr_slot(j)
        if self.crosses(j):
            src, dst = self.got.at[j], self.acr.at[pl.ds(slot, p.chips)]
        else:
            src, dst = self.got.at[j, p.chip], self.acr.at[slot]
        return self.copy(src, dst, self.sx.at[j], self.rx.at[j], p.across())

    def acr_slot(self, j):
        return sum(self.p.chips if c else 1 for c in self.cross_first[:j])

    def inward(self, j):
        slot = jnp.where(self.centre, 1, 0)
        return self.copy(
            self.got.at[self.n + j, self.p.chip],
            self.zin.at[j, slot],
            self.sz.at[j, 0],
            self.rz.at[j, slot],
            self.p.at(ctx=self.inner_at),
        )

    def outward(self, j):
        return self.copy(
            self.got.at[self.n + j, self.p.chip],
            self.zin.at[j, 1],
            self.sz.at[j, 1],
            self.rz.at[j, 1],
            self.p.at(ctx=self.outer_at),
        )

    def add(self, i, y, other):
        self.got[i, y] = (self.got[i, y].astype(F32) + other.astype(F32)).astype(BF16)

    def cores_send(self, i, slot):
        for y in range(self.p.chips):
            self.by_core(i, slot, y).start()

    def cores_sent(self, i, slot):
        for y in range(self.p.chips):
            self.by_core(i, slot, y).wait_send()

    def rows_send(self, i):
        for k in range(1, self.p.chips):
            self.by_row(i, k).start()

    def cores_sum(self, i, slot):
        p = self.p
        for y in range(p.chips):
            self.by_core(i, slot, y).wait_recv()
            self.add(i, y, self.mine[slot, self.mine_of(y, p.core), :])
        if not self.crosses(i):
            self.rows_send(i)
        elif i < self.n:
            self.by_tp(i).start()

    def cross_sum(self, j):
        self.by_tp(j).wait_recv()
        for y in range(self.p.chips):
            self.add(self.n + j, y, self.acr[self.acr_slot(j) + y])
        self.rows_send(self.n + j)

    def rows_sum(self, i):
        p = self.p
        for k in range(1, p.chips):
            self.by_row(i, k).wait_recv()
            self.add(i, p.chip, self.row[self.row_slot(i), k - 1])
        if i < self.n:
            self.by_tp(i).start()
            return
        j = i - self.n
        if not self.crosses(i):
            self.by_tp(j).wait_recv()
            self.add(i, p.chip, self.acr[self.acr_slot(j)])

        @pl.when(jnp.logical_not(self.outer))
        def _():
            self.inward(j).start()

    def ctx_in(self, j):
        @pl.when(self.outer)
        def _():
            pltpu.make_async_copy(self.zin.at[j, 0], self.zin.at[j, 0], self.rz.at[j, 0]).wait()
            self.add(self.n + j, self.p.chip, self.zin[j, 0])
            self.inward(j).start()

    def ctx_mid(self, j):
        @pl.when(self.centre)
        def _():
            self.from_inner(j)
            self.add(self.n + j, self.p.chip, self.zin[j, 1])

            @pl.when(self.outer)
            def _():
                self.outward(j).start()

    def ctx_end(self, j):
        @pl.when(jnp.logical_not(self.centre))
        def _():
            self.from_inner(j)
            self.got[self.n + j, self.p.chip] = self.zin[j, 1]

            @pl.when(self.outer)
            def _():
                self.outward(j).start()

    def from_inner(self, j):
        pltpu.make_async_copy(self.zin.at[j, 1], self.zin.at[j, 1], self.rz.at[j, 1]).wait()
        self.inward(j).wait_send()

    def result(self, j):
        return self.got[self.n + j, self.p.chip].astype(F32)

    def drain(self):
        p = self.p
        for i in range(2 * self.n):
            if self.travels(i):
                for k in range(1, p.chips):
                    self.by_row(i, k).wait_send()
        for j in range(self.n):
            self.by_tp(j).wait_send()

            @pl.when(self.outer)
            def _():
                self.outward(j).wait_send()


class SmallSum:
    def __init__(self, p, sm, near, rows, across, planes, ss, rc, ry, rx, rz):
        self.p, self.sm, self.near, self.rows, self.across, self.planes = p, sm, near, rows, across, planes
        self.ss, self.rc, self.ry, self.rx, self.rz = ss, rc, ry, rx, rz

    def copy(self, index, src, dst, recv_sem, device):
        return pltpu.make_async_remote_copy(
            src_ref=src,
            dst_ref=dst,
            send_sem=self.ss.at[index],
            recv_sem=recv_sem,
            device_id=device,
            device_id_type=MESH,
        )

    def to_mate(self):
        return self.copy(0, self.sm, self.near, self.rc, self.p.mate())

    def to_row(self, k):
        mine = self.rows.at[self.p.chip]
        return self.copy(1 + k, mine, mine, self.ry.at[k - 1], self.p.row(k))

    def to_across(self):
        return self.copy(1, self.across.at[0], self.across.at[1], self.rx, self.p.across())

    def to_plane(self, k):
        mine = self.planes.at[self.p.ctx]
        return self.copy(self.p.chips + k, mine, mine, self.rz.at[k - 1], self.p.plane(k))

    def step(self, which):
        p = self.p
        if which == 0:
            self.to_mate().start()
        elif which == 1:
            self.to_mate().wait_recv()
            self.rows[p.chip] = self.sm[...] + self.near[...]
            for k in range(1, p.chips):
                self.to_row(k).start()
        elif which == 2:
            for k in range(1, p.chips):
                arrived(self.rows.at[p.chip_before(k)], self.ry.at[k - 1], p)
            total = self.rows[0]
            for y in range(1, p.chips):
                total += self.rows[y]
            self.across[0] = total
            self.to_across().start()
        elif which == 3:
            self.to_across().wait_recv()
            self.planes[p.ctx] = self.across[0] + self.across[1]
            for k in range(1, p.ctxs):
                self.to_plane(k).start()

    def result(self):
        p = self.p
        for k in range(1, p.ctxs):
            arrived(self.planes.at[p.ctx_before(k)], self.rz.at[k - 1], p)
        total = self.planes[0]
        for z in range(1, p.ctxs):
            total += self.planes[z]
        self.to_mate().wait_send()
        self.to_across().wait_send()
        for k in range(1, p.chips):
            self.to_row(k).wait_send()
        for k in range(1, p.ctxs):
            self.to_plane(k).wait_send()
        return total


SMALL_AT = {2: 1, 5: 2, 8: 3}
PLAN = {
    ("m", 1): [("a", "cores_sum", "other", 0)],
    ("m", 3): [("a", "cores_sum", "own", 0)],
    ("m", 4): [("a", "cores_sum", "other", 1), ("a", "rows_sum", "other", 0)],
    ("m", 5): [("a", "cores_sum", "own", 1)],
    ("e", 0): [("a", "cores_sum", "other", 2)],
    ("a", 0): [("a", "rows_sum", "own", 0)],
    ("a", 1): [("a", "cores_sum", "own", 2)],
    ("p", 0, 0): [("a", "ctx_in", "own", 0)],
    ("p", 0, 1): [("b", "cores_sum", "own", 0), ("b", "cores_sum", "other", 0)],
    ("p", 0, 3): [("a", "cross_sum", "own", 2), ("a", "rows_sum", "other", 1)],
    ("a", 7): [("a", "ctx_mid", "own", 0)],
    ("a", 8): [("a", "rows_sum", "own", 2), ("hop", 0, 0), ("b", "cores_sum", "other", 1)],
    ("a", 9): [("a", "rows_sum", "own", 1), ("b", "cores_sum", "own", 1), ("b", "cores_sum", "other", 2), ("hop", 0, 1)],
    ("a", 10): [("a", "ctx_in", "own", 2), ("b", "cross_sum", "own", 0)],
    ("a", 11): [("b", "cores_sum", "own", 2), ("hop", 0, 2)],
    ("p", 1, 1): [("b", "cores_sum", "other", 3), ("a", "ctx_in", "own", 1), ("b", "cross_sum", "own", 1)],
    ("p", 1, 3): [("a", "ctx_mid", "own", 2)],
    ("t", 0): [("hop", 1, 0)],
    ("t", 2): [("b", "rows_sum", "other", 3), ("a", "ctx_mid", "own", 1)],
    ("t", 3): [("b", "cross_sum", "own", 2), ("b", "rows_sum", "own", 0), ("b", "cores_sum", "own", 3)],
    ("t", 4): [("b", "rows_sum", "own", 1)],
    ("t", 5): [("hop", 1, 1)],
    ("t", 6): [("b", "ctx_in", "own", 0), ("b", "rows_sum", "own", 3)],
    ("t", 8): [("b", "ctx_in", "own", 1)],
    ("t", 9): [("hop", 1, 2), ("b", "ctx_in", "own", 3), ("b", "rows_sum", "own", 2)],
    ("t", 10): [("b", "ctx_mid", "own", 0)],
    ("t", 11): [("b", "ctx_in", "own", 2)],
    ("t", 14): [("b", "ctx_mid", "own", 1), ("b", "ctx_mid", "own", 3)],
    ("t", 18): [("b", "ctx_mid", "own", 2)],
}


def schedule(ra, rb, on, planes, hop):
    for stage, steps in PLAN.items():
        if stage[0] == "p":
            stage = ("p", stage[1] * planes + stage[2])
        for step in steps:
            if step[0] == "hop":
                on(stage, partial(hop, step[1], step[2]))
                continue
            name, what, whose, j = step
            r = ra if name == "a" else rb
            if what == "cores_sum":
                on(stage, partial(r.cores_sum, j if whose == "other" else r.n + j, r.slot(whose, j)))
            elif what == "rows_sum":
                on(stage, partial(r.rows_sum, j if whose == "other" else r.n + j))
            else:
                on(stage, partial(getattr(r, what), j))


def backward_kernel(
    dm,
    T,
    FC,
    plan_a,
    plan_b,
    mix,
    att,
    own_p,
    own_c,
    cot_p,
    cot_c,
    ln,
    q,
    lse,
    cos,
    sin,
    wm,
    k_hbm,
    v_hbm,
    nt_hbm,
    own_nt_hbm,
    wq_hbm,
    home_arrays_p,
    home_arrays_c,
    early_p,
    early_c,
    home_cot_p,
    home_cot_c,
    out_p,
    out_c,
    gin_p,
    gin_c,
    gq_out,
    go_out,
    gu_out,
    gd_out,
    small_out,
    resid,
    blk,
    gh,
    wo,
    ring,
    gatt,
    nt,
    own_nt,
    maskp,
    maskx,
    kbuf,
    vbuf,
    dk,
    dv,
    dq,
    dxm,
    dxz,
    dxcm,
    blk_away,
    blk_home,
    gin_home,
    put_sem,
    ring_sem,
    wo_sem,
    kv_sem,
    nt_sem,
    wq_sem,
    home_sem,
    b_send,
    b_recv,
    g_send,
    g_recv,
    m_send,
    m_recv,
    z_send,
    z_recv,
    c_send,
    c_recv,
    sm,
    sm_near,
    sm_rows,
    sm_across,
    sm_planes,
    sm_ss,
    sm_rc,
    sm_ry,
    sm_rx,
    sm_rz,
    *refs,
):
    G, R, PB, NCH, D, NX, NP, NT = dm.G, dm.R, dm.PB, dm.NCH, dm.D, dm.NX, dm.NP, dm.NT
    TP, HC = wo.shape[0], wo.shape[2]
    PT = dm.PAIRS // TP
    p = Peers()
    n_a, NB = len(plan_a), len(plan_b)
    ra = Reduce(p, plan_a, refs[: Reduce.REFS])
    rb = Reduce(p, plan_b, refs[Reduce.REFS :])
    block = block_index()
    TILE = 256
    tiles = dm.P // TILE
    chips = p.chips
    S = D // (2 * chips)

    def begin(copies):
        for copy in copies:
            copy.start()

    def ready(copies):
        for copy in copies:
            copy.wait()

    def load_tile(i, slot):
        t = jnp.where(lax.rem(i, 2) == 0, 1 - p.tp, p.tp)
        first = pl.multiple_of(HC + i // 2 * T, 128)
        return [
            pltpu.make_async_copy(
                wm.at[t, :, pl.ds(first, T)], ring.at[slot, :, pl.ds(0, T)], ring_sem.at[0, slot]
            ),
            pltpu.make_async_copy(
                wm.at[t, :, pl.ds(first + FC, T)], ring.at[slot, :, pl.ds(T, T)], ring_sem.at[1, slot]
            ),
        ]

    def pair_at(it):
        turn = it % dm.PAIRS
        return jnp.where(turn % 2 == 0, 1 - p.tp, p.tp) * PT + turn // 2

    def load_kv(it, slot):
        pair, g = pair_at(it), it // dm.PAIRS
        lanes = pl.ds(pl.multiple_of(pair * 128, 128), 128)
        return [
            pltpu.make_async_copy(k_hbm.at[g, :, lanes], kbuf.at[slot], kv_sem.at[0, slot]),
            pltpu.make_async_copy(v_hbm.at[g, :, lanes], vbuf.at[slot], kv_sem.at[1, slot]),
        ]

    wo_load = pltpu.make_async_copy(wm.at[:, :, pl.ds(0, HC)], wo, wo_sem)
    wo_load.start()
    begin(load_tile(0, 0))
    begin(load_kv(0, 0))
    p.greet(trades=True)
    fill_masks(dm, maskp, maskx)
    gain_two, bias_two = ln[2:3, :], ln[3:4, :]

    hn, gd = slice(0, NT), slice(NT, 2 * NT)
    STEP = 128

    def by_rows(step):
        def prompt_part(i, carry):
            rows = pl.ds(pl.multiple_of(i * STEP, STEP), STEP)
            step(own_p[rows, :], cot_p[rows, :], i * STEP)
            return carry

        def cont_part(i, carry):
            rows = pl.ds(pl.multiple_of(i * STEP, STEP), STEP)
            step(own_c[rows, :], cot_c[rows, :], NP + i * STEP)
            return carry

        lax.fori_loop(0, NP // STEP, prompt_part, 0)
        lax.fori_loop(0, (NT - NP) // STEP, cont_part, 0)

    def shifted(first, row):
        return pl.ds(pl.multiple_of(first + row, STEP), STEP)

    wo_load.wait()

    def enter(x, cot, row):
        rows = shifted(0, row)
        r = x.astype(F32)
        for t in range(TP):
            r += dot_nt(att[rows, t * HC : (t + 1) * HC], wo[t])
        resid[rows, :] = r
        blk[rows, :] = r
        h, _ = norm_stats(r)
        n = (h * gain_two + bias_two).astype(BF16)
        dk[rows, :] = n
        nt[:, rows] = transpose(n)
        g = (mix[4] * cot.astype(F32)).astype(BF16)
        dk[shifted(NT, row), :] = g
        nt[:, shifted(NT, row)] = transpose(g)
        gh[rows, :] = jnp.zeros((STEP, D), F32)

    by_rows(enter)

    during = {}

    def on(stage, step):
        during.setdefault(stage, []).append(step)

    def run_when(index, name):
        for (kind, when), steps in during.items():
            if kind == name:

                @pl.when(index == when)
                def _():
                    for step in steps:
                        step()


    sums = SmallSum(p, sm, sm_near, sm_rows, sm_across, sm_planes, sm_ss, sm_rc, sm_ry, sm_rx, sm_rz)
    hops = [(c, b) for c in range(1, p.ctxs - 1) for b in range(c + 1, p.ctxs)]

    def hop(g, part):
        third = pl.cdiv(len(hops), 3)
        for c, b in hops[part * third : (part + 1) * third]:

            @pl.when(p.ctx == c)
            def _():
                at = b - c
                landed(g, at)
                mine = dx_rows(g, b, p.core)[...].astype(F32)
                dxz[g, at] = (dxz[g, at].astype(F32) + mine).astype(BF16)
                rightward(g, dxz.at[g, at], c, b).start()

            far, to = p.ctxs - 1 - c, p.ctxs - 1 - b

            @pl.when(p.ctx == far)
            def _():
                at = p.ctxs - far + to
                landed(g, at)
                mine = dx_rows(g, to, p.core)[...].astype(F32)
                dxz[g, at] = (dxz[g, at].astype(F32) + mine).astype(BF16)
                leftward(g, dxz.at[g, at], far, to).start()

    schedule(ra, rb, on, p.ctxs, hop)

    def run(name):
        for kind, when in sorted(key for key in during if key[0] == name):
            for step in during[kind, when]:
                step()

    def feed(i, carry):
        slot = lax.rem(i, 2)

        @pl.when(i + 1 < 2 * n_a)
        def _():
            begin(load_tile(i + 1, 1 - slot))

        ready(load_tile(i, slot))
        up, dn = ring[slot, :, :T], ring[slot, :, T : 2 * T]
        c0 = 0.7978845608028654
        HALF = NT // 2
        for e in range(2):
            rows = slice(e * HALF, (e + 1) * HALF)
            u = dot(dk[rows, :], up)
            if e == 1:
                run_when(i, "m")
            u2 = u * u
            th = jnp.tanh(c0 * u * (1.0 + 0.044715 * u2))
            half = 0.5 * (1.0 + th)
            act = (u * half).astype(BF16)
            slope = half + 0.5 * u * (1.0 - th * th) * (c0 * (1.0 + 3 * 0.044715 * u2))
            dv[rows, :T] = act
            blk[rows, :] += dot_nt(act, dn)
            gu = (dot(dk[NT + e * HALF : NT + (e + 1) * HALF, :], dn) * slope).astype(BF16)
            dv[NT + e * HALF : NT + (e + 1) * HALF, :T] = gu
            gh[rows, :] += dot_nt(gu, up)

        @pl.when(i >= 2)
        def _():
            ra.cores_sent(slot * n_a + i // 2 - 1, slot)

        for y in range(chips):
            mine = slice(y * 2 * S, (y + 1) * 2 * S)
            ra.mine[slot, mine, :T] = dot(nt[mine, hn], dv[gd, :T]).astype(BF16)
            ra.mine[slot, mine, T:] = dot(nt[mine, gd], dv[hn, :T]).astype(BF16)
        ra.cores_send(slot * n_a + i // 2, slot)
        return carry

    lax.fori_loop(0, 2 * n_a, feed, 0)
    run("e")
    blk_away[:NT, :] = blk[...].astype(BF16)
    away = ra.copy(blk_away.at[pl.ds(0, NT), :], blk_home, b_send, b_recv, p.partner())

    @pl.when(p.core != p.tp)
    def _():
        away.start()

    @pl.when(p.core == p.tp)
    def _():
        blk_home[...] = blk_away[:NT, :]

    sm[...] = jnp.zeros_like(sm)

    def leave(x, cot, row):
        rows = shifted(0, row)
        cot = cot.astype(F32)
        sm[2:3, :] += jnp.sum(cot * blk[rows, :], axis=0, keepdims=True)
        h, scale = norm_stats(resid[rows, :])
        g = gh[rows, :]
        sm[0:1, :] += jnp.sum(g * h, axis=0, keepdims=True)
        sm[1:2, :] += jnp.sum(g, axis=0, keepdims=True)
        gr = mix[4] * cot + norm_back(g, gain_two, h, scale)
        resid[rows, :] = gr
        gb = gr.astype(BF16)
        nt[:, shifted(NT, row)] = transpose(gb)
        for t in range(TP):
            gatt[rows, t * HC : (t + 1) * HC] = dot(gb, wo[t]).astype(BF16)

    by_rows(leave)
    for slot, i in enumerate((0, NB)):
        t = p.tp if slot else 1 - p.tp
        lanes = pl.ds(pl.multiple_of(t * HC, 128), HC)
        for y in range(chips):
            mine = slice(y * 2 * S, (y + 1) * 2 * S)
            rb.mine[slot, mine, :] = dot(nt[mine, gd], att[:, lanes]).astype(BF16)
        rb.cores_send(i, slot)
    nt_load = [
        pltpu.make_async_copy(nt_hbm, nt, nt_sem.at[0]),
        pltpu.make_async_copy(own_nt_hbm, own_nt, nt_sem.at[1]),
    ]
    begin(nt_load)
    wq_load = pltpu.make_async_copy(wq_hbm.at[:, :, pl.ds(0, 3 * HC)], ring.at[:, :, pl.ds(0, 3 * HC)], wq_sem)
    wq_load.start()
    during.setdefault(("a", dm.PAIRS - 1), []).insert(0, partial(ready, nt_load))

    def attend(turn, g):
        it = g * dm.PAIRS + turn
        pair = pair_at(it)
        slot = it % 2

        @pl.when(it + 1 < G * dm.PAIRS)
        def _():
            begin(load_kv(it + 1, 1 - slot))

        lanes = pl.ds(pl.multiple_of(pair * 128, 128), 128)
        rp = pl.ds(pl.multiple_of(g * PB, PB), PB)
        rc = pl.ds(pl.multiple_of(dm.NP + g * NCH, NCH), NCH)
        qp, qc = q[rp, lanes], q[rc, lanes]
        gp, gc = gatt[rp, lanes], gatt[rc, lanes]
        ap, ac = att[rp, lanes].astype(F32), att[rc, lanes].astype(F32)
        qt = heads_columns(transpose(qp), transpose(qc))
        gpt, gct = gp.astype(F32).T, gc.astype(F32).T
        gt = heads_columns(gpt.astype(BF16), gct.astype(BF16))
        qs, gs = heads_rows(qp, qc), heads_rows(gp, gc)
        prodp, prodc = gpt * ap.T, gct * ac.T
        delta = jnp.concatenate(
            [
                jnp.sum(prodp[:HD], axis=0, keepdims=True),
                jnp.sum(prodp[HD:], axis=0, keepdims=True),
                jnp.sum(prodc[:HD], axis=0, keepdims=True),
                jnp.sum(prodc[HD:], axis=0, keepdims=True),
            ],
            axis=1,
        )
        stat = lse[g * dm.PAIRS + pair]
        ready(load_kv(it, slot))

        def grads(s, kt, vt, cols):
            pr = jnp.exp(s - stat[:, cols:])
            dp = dot(vt, gt[:, cols:])
            ds = (pr * (dp - delta[:, cols:])).astype(BF16)
            gv = dot(pr.astype(BF16), gs[cols:])
            gk = dot(ds, qs[cols:])
            gq = dot(transpose(kt), ds)
            return gk, gv, gq

        acc = None
        for j in range(tiles):
            rows = slice(j * TILE, (j + 1) * TILE)
            kt = kbuf[slot, rows, :]
            s = dot(kt, qt)
            s = jnp.concatenate([s[:, : 2 * PB] + twice(maskp[rows, :]), s[:, 2 * PB :]], axis=1)
            gk, gv, gq = grads(s, kt, vbuf[slot, rows, :], 0)
            gk = rotate_back(gk, cos[rows, :], sin[rows, :]).astype(BF16)
            gv = gv.astype(BF16)
            out = pl.ds(pl.multiple_of(g * R + j * TILE, 128), TILE)
            dk[out, lanes] = gk
            dv[out, lanes] = gv
            if j == tiles // 2:
                run_when(it, "a")
            acc = gq if acc is None else acc + gq
        kt = kbuf[slot, dm.P :, :]
        s = dot(kt, qt[:, 2 * PB :]) + maskx[...]
        gk, gv, gq = grads(s, kt, vbuf[slot, dm.P :, :], 2 * PB)
        for c in range(dm.NC):
            rows = slice(dm.P, dm.P + CL)
            out = pl.ds(pl.multiple_of(g * R + dm.P + c * CL, CL), CL)
            part = rotate_back(gk[c * CL : (c + 1) * CL], cos[rows, :], sin[rows, :])
            dk[out, lanes] = part.astype(BF16)
            dv[out, lanes] = gv[c * CL : (c + 1) * CL].astype(BF16)
        accp = acc[:, : 2 * PB] * 0.125
        accc = (acc[:, 2 * PB :] + gq) * 0.125
        outp = jnp.where(sublane_pick((128, PB), True), accp[:, :PB], accp[:, PB:]).T
        outc = jnp.where(sublane_pick((128, NCH), True), accc[:, :NCH], accc[:, NCH:]).T
        tab = pl.ds(pl.multiple_of(block * PB, PB), PB)
        dq[rp, lanes] = rotate_back(outp, cos[tab, :], sin[tab, :]).astype(BF16)
        tab = pl.ds(pl.multiple_of(dm.P + p.core * dm.CH, dm.CH), dm.CH)
        for c in range(dm.NC):
            part = rotate_back(outc[c * dm.CH : (c + 1) * dm.CH], cos[tab, :], sin[tab, :])
            rows = pl.ds(pl.multiple_of(dm.NP + g * NCH + c * dm.CH, dm.CH), dm.CH)
            dq[rows, lanes] = part.astype(BF16)

        @pl.when(g == G - 1)
        def _():
            put = turn % 2
            index = put * NB + 1 + turn // 2
            rb.cores_sent(index - 1, put)
            both = jnp.concatenate([dk[:, lanes], dv[:, lanes]], axis=1)
            for y in range(chips):
                mine = slice(y * 2 * S, (y + 1) * 2 * S)
                rb.mine[put, mine, 128:] = dot(nt[mine, :], both).astype(BF16)
                rb.mine[put, mine, :128] = dot(own_nt[mine, :], dq[:, lanes]).astype(BF16)
            rb.cores_send(index, put)

        return g

    w = ring

    def project(rows):
        total = None
        for t in range(TP):
            part = dot_nt(dk[rows, t * HC : (t + 1) * HC], w[t, :, HC : 2 * HC])
            total = part if total is None else total + part
            total += dot_nt(dv[rows, t * HC : (t + 1) * HC], w[t, :, 2 * HC : 3 * HC])
        return total

    NCONT = NT - NP
    gain_one = ln[0:1, :]
    halves = lambda core, g: pl.ds(pl.multiple_of(core * NCONT + g * NCH, 16), NCH)

    def dx_at(g, c, first, count):
        if g == G - 1:
            return dk.at[pl.ds(pl.multiple_of(g * R + c * 2 * PB + first, PB), count), :]
        fit = D // (2 * PB)
        row = pl.multiple_of(c % fit * 2 * PB + first, PB)
        return ra.mine.at[c // fit, pl.ds(row, count), pl.ds(0, D)]

    def dx_rows(g, c, core):
        return dx_at(g, c, core * PB, PB)

    def to_mate(g, k):
        i = g * p.ctxs + k
        rows = dx_rows(g, p.ctx_after(k), 1 - p.core)
        return ra.copy(rows, dxm.at[i], m_send.at[i], m_recv.at[i], p.mate())

    def rightward(g, src, c, b):
        i = b - c - 1
        return ra.copy(src, dxz.at[g, i], z_send.at[g, b], z_recv.at[g, i], p.at(ctx=c + 1))

    def leftward(g, src, c, b):
        i = p.ctxs - c + 1 + b
        return ra.copy(src, dxz.at[g, i], z_send.at[g, b], z_recv.at[g, i], p.at(ctx=c - 1))

    def landed(g, i):
        pltpu.make_async_copy(dxz.at[g, i], dxz.at[g, i], z_recv.at[g, i]).wait()

    def each_group(g, step):
        for e in range(G):

            @pl.when(g == e)
            def _():
                step(e)

    def cont_copy(g):
        return ra.copy(
            blk_away.at[halves(1 - p.core, g), :],
            dxcm.at[pl.ds(pl.multiple_of(g * NCH, 16), NCH), :],
            c_send.at[g],
            c_recv.at[g],
            p.mate(),
        )

    def norm_sums(x, turned, rows):
        sm[8:9, :] += jnp.sum(x.astype(F32), axis=0, keepdims=True)
        for d in range(0, D, 128):
            gh[:128, d : d + 128] += dot(turned[d : d + 128, rows], x[:, d : d + 128])

    def norm_grads():
        same = lax.broadcasted_iota(jnp.int32, (128, 128), 0) == lax.broadcasted_iota(
            jnp.int32, (128, 128), 1
        )
        for d in range(0, D, 128):
            cols = slice(d, d + 128)
            x = blk[:, cols].astype(BF16)
            sm[8:9, cols] += jnp.sum(x.astype(F32), axis=0, keepdims=True)
            gh[:128, cols] += dot(own_nt[cols, :], x)
            total = jnp.sum(jnp.where(same, gh[:128, cols], 0.0), axis=0, keepdims=True)
            sm[7:8, cols] = (total - ln[1:2, cols] * sm[8:9, cols]) / ln[0:1, cols]

    gh[:128, :] = jnp.zeros((128, D), F32)

    def group(g, carry):
        lax.fori_loop(0, dm.PAIRS, attend, g)

        @pl.when(g == 0)
        def _():
            wq_load.wait()
            ra.cores_sent(n_a - 1, 0)
            ra.cores_sent(2 * n_a - 1, 1)

            @pl.when(p.core != p.tp)
            def _():
                away.wait_send()

        def planes(i, carry):
            @pl.when(i < p.ctxs)
            def _():
                k = lax.rem(i + 1, p.ctxs)
                both = pl.ds(pl.multiple_of(g * R + p.ctx_after(k) * 2 * PB, 2 * PB), 2 * PB)
                total = project(both).astype(BF16)
                norm_sums(total, nt, both)

                def out(e):
                    dx_at(e, p.ctx_after(k), 0, 2 * PB)[...] = total
                    to_mate(e, k).start()

                each_group(g, out)
                run_when(g * p.ctxs + i, "p")

            @pl.when(i > 0)
            def _():
                k = lax.rem(i, p.ctxs)

                def back(e):
                    to_mate(e, k).wait_recv()
                    b = p.ctx_after(k)
                    mine = dx_rows(e, b, p.core)
                    mine[...] = (mine[...].astype(F32) + dxm[e * p.ctxs + k].astype(F32)).astype(BF16)

                    @pl.when((k > 0) & (p.ctx == 0))
                    def _():
                        rightward(e, mine, 0, b).start()

                    @pl.when((k > 0) & (p.ctx == p.ctxs - 1))
                    def _():
                        leftward(e, mine, p.ctxs - 1, b).start()

                each_group(g, back)

            return carry

        lax.fori_loop(0, p.ctxs + 1, planes, 0)
        rows = pl.ds(pl.multiple_of(g * R + dm.P, CL), NX)
        total = project(rows).astype(BF16)
        norm_sums(total, nt, rows)
        for c in range(dm.NC):
            for e in range(2):
                out = pl.ds(pl.multiple_of(e * NCONT + g * NCH + c * dm.CH, dm.CH), dm.CH)
                blk_away[out, :] = total[c * CL + e * dm.CH : c * CL + (e + 1) * dm.CH]
        cont_copy(g).start()
        for first, count in ((g * PB, PB), (NP + g * NCH, NCH)):
            rows = pl.ds(pl.multiple_of(first, 16), count)
            total = dot_nt(dq[rows, :HC], w[0, :, :HC])
            for t in range(1, TP):
                total += dot_nt(dq[rows, t * HC : (t + 1) * HC], w[t, :, :HC])
            blk[rows, :] = total
        return carry

    def enter_back(gn, x, rows):
        gn += blk[rows, :]
        hat, scale = norm_stats(x.astype(F32))
        gatt[rows, :] = (resid[rows, :] + norm_back(gn, gain_one, hat, scale)).astype(BF16)

    def gin_away(part):
        rows = pl.ds(0, NP) if part == 0 else pl.ds(NP, NT - NP)
        return ra.copy(gatt.at[rows, :], gin_home.at[rows, :], g_send.at[part], g_recv.at[part], p.partner())

    def give(part):
        rows = slice(0, NP) if part == 0 else slice(NP, NT)

        @pl.when(p.core != p.tp)
        def _():
            gin_away(part).start()

        @pl.when(p.core == p.tp)
        def _():
            gin_home[rows, :] = gatt[rows, :]

    lax.fori_loop(0, G, group, 0)
    homes = []
    for i, (a, c) in enumerate(
        [(home_arrays_p, home_arrays_c)]
        + [(early_p.at[e], early_c.at[e]) for e in range(3)]
        + [(home_cot_p, home_cot_c)]
    ):
        homes.append(pltpu.make_async_copy(a, dv.at[pl.ds(i * NT, NP), :], home_sem.at[0, i]))
        homes.append(pltpu.make_async_copy(c, dv.at[pl.ds(i * NT + NP, NT - NP), :], home_sem.at[1, i]))
    begin(homes)

    def cont_back(g, carry):
        cont_copy(g).wait_recv()
        here = pl.ds(pl.multiple_of(g * NCH, 16), NCH)
        gn = blk_away[halves(p.core, g), :].astype(F32) + dxcm[here, :].astype(F32)
        enter_back(gn, own_c[here, :], pl.ds(pl.multiple_of(NP + g * NCH, 16), NCH))
        return carry

    lax.fori_loop(0, G, cont_back, 0)
    give(1)

    ready(homes)

    @pl.when(p.core != p.tp)
    def _():
        away.wait_recv()

    def blend(i, carry):
        rows = shifted(0, i * STEP)
        res = mix[4] * blk_home[rows, :].astype(F32)
        c = dv[shifted(4 * NT, i * STEP), :].astype(F32)
        for e in range(4):
            a = dv[shifted(e * NT, i * STEP), :].astype(F32)
            res += mix[e] * a
            sm[3 + e : 4 + e, :] += jnp.sum(c * a, axis=0, keepdims=True)
        blk_home[rows, :] = res.astype(BF16)
        return carry

    lax.fori_loop(0, NT // STEP, blend, 0)
    puts = [
        pltpu.make_async_copy(blk_home.at[pl.ds(0, NP), :], out_p, put_sem.at[0]),
        pltpu.make_async_copy(blk_home.at[pl.ds(NP, NT - NP), :], out_c, put_sem.at[1]),
    ]
    begin(puts)
    norm_grads()
    sums.step(0)
    for when in range(10):
        for step in during.get(("t", when), []):
            step()
        if SMALL_AT.get(when):
            sums.step(SMALL_AT[when])

    for g in range(G):
        here = slice(g * PB, (g + 1) * PB)

        @pl.when(p.ctx > 0)
        def _():
            landed(g, 0)
            blk[here, :] += dxz[g, 0].astype(F32)

        @pl.when(p.ctx < p.ctxs - 1)
        def _():
            landed(g, p.ctxs)
            blk[here, :] += dxz[g, p.ctxs].astype(F32)

        enter_back(dx_rows(g, p.ctx, p.core)[...].astype(F32), own_p[here, :], here)
    give(0)
    for when in range(10, 20):
        for step in during.get(("t", when), []):
            step()
    small_out[...] = sums.result()
    gu_puts = []
    for j in range(n_a):
        ra.ctx_end(j)
        total = ra.result(j)
        gd_out[:, j * T : (j + 1) * T] = total[:, T:]
        if len(gu_puts) > 0:
            gu_puts[-1].wait()
        gh[:S, :T] = total[:, :T]
        gu_puts.append(
            pltpu.make_async_copy(
                gh.at[pl.ds(0, S), pl.ds(0, T)], gu_out.at[:, pl.ds(j * T, T)], put_sem.at[2]
            )
        )
        gu_puts[-1].start()
    gu_puts[-1].wait()
    for j in range(NB):
        rb.ctx_end(j)
        total = rb.result(j)
        if j == 0:
            go_out[...] = total
        else:
            for c in range(3):
                gq_out[c, :, (j - 1) * 128 : j * 128] = total[:, c * 128 : (c + 1) * 128]

    @pl.when(p.core != p.tp)
    def _():
        for part in range(2):
            gin_away(part).wait_recv()
            gin_away(part).wait_send()

    more = [
        pltpu.make_async_copy(gin_home.at[pl.ds(0, NP), :], gin_p, put_sem.at[2]),
        pltpu.make_async_copy(gin_home.at[pl.ds(NP, NT - NP), :], gin_c, put_sem.at[3]),
    ]
    begin(more)
    ready(puts + more)
    rb.cores_sent(NB - 1, 0)
    rb.cores_sent(2 * NB - 1, 1)
    for g in range(G):
        for k in range(p.ctxs):
            to_mate(g, k).wait_send()
        for k in range(1, p.ctxs):
            b = p.ctx_after(k)
            ra.copy(dxz.at[g, 0], dxz.at[g, 0], z_send.at[g, b], z_send.at[g, b], p.mate()).wait_send()
        cont_copy(g).wait_send()
    ra.drain()
    rb.drain()


def deliver_kernel(count, *refs):
    sources, small, targets = refs[:count], refs[count], refs[count + 1 : 2 * count + 1]
    outs = refs[2 * count + 1 : 2 * count + 6]
    kept = refs[2 * count + 6 : 3 * count + 6]
    in_sem, out_sem, parts = refs[3 * count + 6 :]
    loads = [pltpu.make_async_copy(sources[i], kept[i], in_sem.at[i]) for i in range(count)]
    puts = [pltpu.make_async_copy(kept[i], targets[i], out_sem.at[i]) for i in range(count)]
    for load in loads:
        load.start()
    S = parts.shape[2]
    norms = jnp.concatenate([small[7:9, :], small[0:2, :], jnp.zeros((4, small.shape[1]), F32)], axis=0)
    for d in range(parts.shape[0]):
        parts[d] = norms[:, d * S : (d + 1) * S]
    mine = parts[lax.axis_index("dp")]
    for i in range(4):
        outs[i][...] = mine[i : i + 1, :]
    sums = jnp.sum(small[...], axis=1, keepdims=True)
    order = (3, 4, 5, 6, 2)
    lanes = lax.broadcasted_iota(jnp.int32, (1, 8), 1)
    mix = jnp.zeros((1, 8), F32)
    for i, row in enumerate(order):
        mix = jnp.where(lanes == i, sums[row : row + 1, :], mix)
    outs[4][...] = mix
    for i in range(count):
        loads[i].wait()
        puts[i].start()
    for put in puts:
        put.wait()


def params(**more):
    return pltpu.CompilerParams(vmem_limit_bytes=VMEM_LIMIT, **more)


def per_device(
    prompt_in,
    cont_in,
    prompt_embed,
    cont_embed,
    prompt_earlier,
    cont_earlier,
    ln1_gain,
    ln1_bias,
    ln2_gain,
    ln2_bias,
    w_qkv,
    w_out,
    w_up,
    w_down,
    mix_weights,
    prompt_cot,
    cont_cot,
):
    G, PB, D = prompt_in.shape
    NC, CH = cont_in.shape[1], cont_in.shape[2]
    TP = lax.axis_size("tp")
    PROMPT = PB * TP * lax.axis_size("ctx")
    HC, FC = w_qkv.shape[2], w_up.shape[1]
    S = w_qkv.shape[0]
    dm = Dims(G, PROMPT, PB, NC, CH, D, HC * TP // HD)
    R, NT, NP = dm.R, dm.NT, dm.NP

    sds = jax.ShapeDtypeStruct
    chips, ctxs = lax.axis_size("dp") // 2, lax.axis_size("ctx")
    norms = jnp.stack([ln1_gain, ln1_bias, ln2_gain, ln2_bias], axis=1)
    norms = jnp.pad(norms, ((0, 0), (0, 124)))
    wq_shard = jnp.concatenate([w_qkv.reshape(S, 3 * HC), norms], axis=1)
    wm_shard = jnp.concatenate([w_out.T, w_up, w_down.T], axis=1)

    positions = jnp.arange(PROMPT + CL, dtype=jnp.int32).astype(F32)
    lane = jnp.arange(128, dtype=jnp.int32)
    freq = 10000.0 ** (-((lane % 32).astype(F32) / 32))
    angles = positions[:, None] * freq[None, :]
    cos, sin = jnp.cos(angles), jnp.sin(angles)
    second = (lane % 64) >= 32
    sin = jnp.where(second[None, :], sin, -sin)

    any_ = pl.BlockSpec(memory_space=pl.ANY)
    vmem = pl.BlockSpec(memory_space=pltpu.VMEM)
    dma = pltpu.SemaphoreType.DMA
    left = (HC + 2 * FC) // 128 * 2 // 3 * 128
    q, att, lse, ln, nt, own_nt, k, v, wq, wm, own_p, own_c, cot_p, cot_c = pl.pallas_call(
        partial(forward_kernel, dm, left),
        out_shape=(
            sds((NT, D), BF16),
            sds((NT, D), BF16),
            sds((G * dm.PAIRS, 1, dm.COLS), F32),
            sds((8, D), F32),
            sds((D, G * R), BF16),
            sds((D, NT), BF16),
            sds((G, R, D), BF16),
            sds((G, R, D), BF16),
            sds((TP, D, 3 * HC + 128), BF16),
            sds((TP, D, HC + 2 * FC), BF16),
            sds(prompt_in.shape, BF16),
            sds(cont_in.shape, BF16),
            sds(prompt_in.shape, BF16),
            sds(cont_in.shape, BF16),
        ),
        in_specs=[vmem] * 5 + [any_] * 3,
        out_specs=(vmem,) * 4 + (any_,) * 10,
        scratch_shapes=[
            pltpu.VMEM((D, G * R), BF16),
            pltpu.VMEM((D, NT), BF16),
            pltpu.VMEM((G, R, D), BF16),
            pltpu.VMEM((G, R, D), BF16),
            pltpu.VMEM((PROMPT, PB), F32),
            pltpu.VMEM((dm.NX, 2 * dm.NCH), F32),
            pltpu.VMEM((PROMPT, dm.COLS), F32),
            pltpu.VMEM((G * R, D), BF16),
            pltpu.VMEM((NT, D), BF16),
            pltpu.VMEM((2 * ctxs, G, PB, D), BF16),
            pltpu.VMEM((2, G, NC, CH, D), BF16),
            pltpu.VMEM((TP, D, 3 * HC + 128), BF16),
            dma((7,)),
            dma((4,)),
            dma((4,)),
            dma((2 * ctxs - 1,)),
            dma((ctxs - 1,)),
            dma((ctxs,)),
            dma,
            dma,
            dma((2,)),
        ]
        + WeightGather.semaphores(chips)
        + WeightGather.semaphores(chips),
        compiler_params=params(collective_id=0, has_side_effects=True),
        name="forward",
    )(prompt_in, cont_in, cos, sin, wq_shard, wm_shard, prompt_cot, cont_cot)
    T = 512 if FC % 512 == 0 else 256
    plan_a, plan_b = [False, False, True], [True, True, True, False]
    far = max(chips - 1, 1)
    rows = lambda x: x.reshape(-1, D)
    out_p, out_c, gin_p, gin_c, gq, go, gu, gd, small = pl.pallas_call(
        partial(backward_kernel, dm, T, FC, plan_a, plan_b),
        out_shape=(
            sds((NP, D), BF16),
            sds((NT - NP, D), BF16),
            sds((NP, D), BF16),
            sds((NT - NP, D), BF16),
            sds((3, S, HC), F32),
            sds((S, HC), F32),
            sds((S, FC), F32),
            sds((S, FC), F32),
            sds((16, D), F32),
        ),
        in_specs=[pl.BlockSpec(memory_space=pltpu.SMEM)] + [vmem] * 10 + [any_] * 12,
        out_specs=(any_,) * 4 + (vmem, vmem, any_, vmem, vmem),
        scratch_shapes=[
            pltpu.VMEM((NT, D), F32),
            pltpu.VMEM((NT, D), F32),
            pltpu.VMEM((NT, D), F32),
            pltpu.VMEM((TP, D, HC), BF16),
            pltpu.VMEM((2, D, max(2 * T, 3 * HC)), BF16),
            pltpu.VMEM((NT, D), BF16),
            pltpu.VMEM((D, G * R), BF16),
            pltpu.VMEM((D, NT), BF16),
            pltpu.VMEM((PROMPT, PB), F32),
            pltpu.VMEM((dm.NX, 2 * dm.NCH), F32),
            pltpu.VMEM((2, R, 128), BF16),
            pltpu.VMEM((2, R, 128), BF16),
            pltpu.VMEM((G * R, D), BF16),
            pltpu.VMEM((G * R, D), BF16),
            pltpu.VMEM((NT, D), BF16),
            pltpu.VMEM((G * ctxs, PB, D), BF16),
            pltpu.VMEM((G, ctxs + 1, PB, D), BF16),
            pltpu.VMEM((NT - NP, D), BF16),
            pltpu.VMEM((max(NT, 2 * (NT - NP)), D), BF16),
            pltpu.VMEM((NT, D), BF16),
            pltpu.VMEM((NT, D), BF16),
            dma((4,)),
            dma((2, 2)),
            dma,
            dma((2, 2)),
            dma((2,)),
            dma,
            dma((2, 5)),
            dma,
            dma,
            dma((2,)),
            dma((2,)),
            dma((G * ctxs,)),
            dma((G * ctxs,)),
            dma((G, ctxs)),
            dma((G, ctxs + 1)),
            dma((G,)),
            dma((G,)),
            pltpu.VMEM((16, D), F32),
            pltpu.VMEM((16, D), F32),
            pltpu.VMEM((chips, 16, D), F32),
            pltpu.VMEM((2, 16, D), F32),
            pltpu.VMEM((ctxs, 16, D), F32),
            dma((1 + chips + ctxs,)),
            dma,
            dma((far,)),
            dma,
            dma((ctxs - 1,)),
        ]
        + Reduce.scratch(plan_a, chips, S, 2 * T)
        + Reduce.scratch(plan_b, chips, S, HC),
        compiler_params=params(collective_id=1, has_side_effects=True),
        name="backward",
    )(
        mix_weights,
        att,
        rows(own_p),
        rows(own_c),
        rows(cot_p),
        rows(cot_c),
        ln,
        q,
        lse,
        cos,
        sin,
        wm,
        k,
        v,
        nt,
        own_nt,
        wq,
        rows(prompt_embed),
        rows(cont_embed),
        prompt_earlier.reshape(3, NP, D),
        cont_earlier.reshape(3, NT - NP, D),
        rows(prompt_cot),
        rows(cont_cot),
    )
    results = (out_p, out_c, gin_p, gin_c, gq, go, gu, gd)
    shapes = tuple(sds(x.shape, x.dtype) for x in results)
    out = pl.pallas_call(
        partial(deliver_kernel, len(results)),
        out_shape=shapes + (sds((1, S), F32),) * 4 + (sds((1, 8), F32),),
        in_specs=[any_] * len(results) + [vmem],
        out_specs=(any_,) * len(results) + (vmem,) * 5,
        scratch_shapes=[pltpu.VMEM(x.shape, x.dtype) for x in results]
        + [dma((len(results),)), dma((len(results),)), pltpu.VMEM((2 * chips, 8, S), F32)],
        compiler_params=params(),
        name="deliver",
    )(*results, small)
    out_p, out_c, gin_p, gin_c, gq, go, gu, gd = out[:8]
    gains = [x.reshape(S) for x in out[8:12]]
    return (
        out_p.reshape(prompt_in.shape),
        out_c.reshape(cont_in.shape),
        gin_p.reshape(prompt_in.shape),
        gin_c.reshape(cont_in.shape),
        *gains,
        jnp.transpose(gq, (1, 0, 2)),
        go.T,
        gu,
        gd.T,
        out[12][0, :5],
    )


def solution(mesh):
    tokens = P("dp", ("ctx", "tp"), None)
    conts = P("dp", "ctx", "tp", None)
    weights = (P("dp", None, "tp"), P("tp", "dp"), P("dp", "tp"), P("tp", "dp"))
    in_specs = (
        tokens,
        conts,
        tokens,
        conts,
        P(None, "dp", ("ctx", "tp"), None),
        P(None, "dp", "ctx", "tp", None),
        P("dp"),
        P("dp"),
        P("dp"),
        P("dp"),
        *weights,
        P(),
        tokens,
        conts,
    )
    out_specs = (
        tokens,
        conts,
        tokens,
        conts,
        P("dp"),
        P("dp"),
        P("dp"),
        P("dp"),
        *weights,
        P(),
    )
    return jax.shard_map(
        per_device, mesh=mesh, in_specs=in_specs, out_specs=out_specs, check_vma=False
    )
```

```python
from functools import partial

import jax
import jax.numpy as jnp
import numpy as np
from jax import lax
from jax.experimental import pallas as pl
from jax.experimental.pallas import tpu as pltpu
from jax.sharding import PartitionSpec as P

HD = 64
CL = 128
EPS = 1e-05
NEG = -1e30
F32 = jnp.float32
BF16 = jnp.bfloat16
VMEM_LIMIT = 67043328


def dot(a, b):
    return lax.dot_general(a, b, (((1,), (0,)), ((), ())), preferred_element_type=F32)


def dot_nt(a, b):
    return lax.dot_general(a, b, (((1,), (1,)), ((), ())), preferred_element_type=F32)


def norm_stats(x):
    mean = jnp.mean(x, axis=-1, keepdims=True)
    centered = x - mean
    var = jnp.mean(centered * centered, axis=-1, keepdims=True)
    scale = lax.rsqrt(var + EPS)
    return centered * scale, scale


def norm_back(grad, gain, hat, scale):
    gh = grad * gain
    return scale * (
        gh
        - jnp.mean(gh, axis=-1, keepdims=True)
        - hat * jnp.mean(gh * hat, axis=-1, keepdims=True)
    )


def swap_halves(x):
    second = lax.broadcasted_iota(jnp.int32, x.shape, 1) % HD >= HD // 2
    return jnp.where(second, pltpu.roll(x, 32, 1), pltpu.roll(x, 96, 1))


def rotate(x, cos, sin):
    return x * cos + swap_halves(x) * sin


def rotate_back(x, cos, sin):
    return x * cos - swap_halves(x) * sin


def lane_pick(shape, low):
    lanes = lax.broadcasted_iota(jnp.int32, shape, 1)
    return lanes < HD if low else lanes >= HD


def sublane_pick(shape, low):
    rows = lax.broadcasted_iota(jnp.int32, shape, 0)
    return rows < HD if low else rows >= HD


def transpose(x):
    return x.astype(F32).T.astype(x.dtype)


class Dims:
    def __init__(self, groups, prompt, pb, nc, ch, d, heads):
        self.G, self.P, self.PB, self.NC, self.CH, self.D = groups, prompt, pb, nc, ch, d
        self.NCH = nc * ch
        self.R = prompt + nc * CL
        self.NX = nc * CL
        self.NR = pb + self.NCH
        self.NP = groups * pb
        self.NT = groups * self.NR
        self.PAIRS = heads // 2
        self.COLS = 2 * self.NR


MESH = pl.DeviceIdType.MESH


def half_index():
    return lax.axis_index("dp") % 2


def block_index():
    return lax.axis_index("ctx") * 2 + half_index()


class Peers:
    def __init__(self):
        self.ctxs = lax.axis_size("ctx")
        self.chips = lax.axis_size("dp") // 2
        self.tps = lax.axis_size("tp")
        self.dp = lax.axis_index("dp")
        self.ctx = lax.axis_index("ctx")
        self.tp = lax.axis_index("tp")
        self.core = self.dp % 2
        self.chip = self.dp // 2

    def at(self, dp=None, ctx=None, tp=None):
        return {
            "dp": self.dp if dp is None else dp,
            "ctx": self.ctx if ctx is None else ctx,
            "tp": self.tp if tp is None else tp,
        }

    def across(self):
        return self.at(tp=1 - self.tp)

    def mate(self):
        return self.at(dp=self.chip * 2 + 1 - self.core)

    def chip_after(self, k):
        return lax.rem(self.chip + k, self.chips)

    def chip_before(self, k):
        return lax.rem(self.chip + self.chips - k, self.chips)

    def row(self, k):
        return self.at(dp=self.chip_after(k) * 2 + self.core)

    def ctx_after(self, k):
        return lax.rem(self.ctx + k, self.ctxs)

    def ctx_before(self, k):
        return lax.rem(self.ctx + self.ctxs - k, self.ctxs)

    def plane(self, k):
        return self.at(ctx=self.ctx_after(k))

    def partner(self):
        return self.at(dp=self.chip * 2 + self.tp, tp=self.core)

    def greet(self, trades=False):
        barrier = pltpu.get_barrier_semaphore()
        peers = [self.across(), self.mate()]
        peers += [self.row(k) for k in range(1, self.chips)]
        peers += [self.plane(k) for k in range(1, self.ctxs)]
        for peer in peers:
            pl.semaphore_signal(barrier, inc=1, device_id=peer, device_id_type=MESH)
        count = len(peers)
        if trades:
            away = self.core != self.tp

            @pl.when(away)
            def _():
                pl.semaphore_signal(
                    barrier, inc=1, device_id=self.partner(), device_id_type=MESH
                )

            count += jnp.where(away, 1, 0)
        pl.semaphore_wait(barrier, count)


def send(src, dst, send_sem, recv_sem, device):
    copy = pltpu.make_async_remote_copy(
        src_ref=src,
        dst_ref=dst,
        send_sem=send_sem,
        recv_sem=recv_sem,
        device_id=device,
        device_id_type=MESH,
    )
    copy.start()
    return copy


def arrived(ref, sem, peers):
    pltpu.make_async_remote_copy(
        src_ref=ref,
        dst_ref=ref,
        send_sem=sem,
        recv_sem=sem,
        device_id=peers.mate(),
        device_id_type=MESH,
    ).wait_recv()


class WeightGather:
    def __init__(self, peers, shard, full, left, sends, across, rows, mate):
        self.p, self.shard, self.full, self.left = peers, shard, full, left
        self.sends, self.across, self.rows, self.from_mate = sends, across, rows, mate
        self.copies = []
        self.size, self.cols = shard.shape

    @staticmethod
    def semaphores(chips):
        far = chips - 1
        return [
            pltpu.SemaphoreType.DMA((3 + 6 * far,)),
            pltpu.SemaphoreType.DMA((chips,)),
            pltpu.SemaphoreType.DMA((2, max(far, 1))),
            pltpu.SemaphoreType.DMA((2, chips)),
        ]

    def piece(self, tp, dp, cols=slice(None)):
        rows = pl.ds(pl.multiple_of(dp * self.size, 16), self.size)
        if cols == slice(None):
            return self.full.at[tp, rows, :]
        return self.full.at[tp, rows, pl.ds(cols.start, cols.stop - cols.start)]

    def go(self, src, dst, recv_sem, device):
        self.copies.append(send(src, dst, self.sends.at[len(self.copies)], recv_sem, device))

    def start(self):
        p = self.p
        self.go(self.shard, self.piece(p.tp, p.dp), self.across.at[0], p.across())
        for k in range(1, p.chips):
            self.go(self.shard, self.piece(p.tp, p.dp), self.rows.at[0, k - 1], p.row(k))
        self.go(self.shard, self.piece(p.tp, p.dp), self.from_mate.at[0, 0], p.mate())

    def relay_across(self):
        p = self.p
        got = self.piece(1 - p.tp, p.dp)
        arrived(got, self.across.at[0], p)
        part = self.piece(1 - p.tp, p.dp, slice(0, self.left))
        for k in range(1, p.chips):
            self.go(part, part, self.rows.at[1, k - 1], p.row(k))
        self.go(got, got, self.from_mate.at[1, 0], p.mate())

    def relay_rows(self):
        p = self.p
        for k in range(1, p.chips):
            dp = p.chip_before(k) * 2 + p.core
            got = self.piece(p.tp, dp)
            arrived(got, self.rows.at[0, k - 1], p)
            if self.left < self.cols:
                part = self.piece(p.tp, dp, slice(self.left, self.cols))
                self.go(part, part, self.across.at[k], p.across())
            self.go(got, got, self.from_mate.at[0, k], p.mate())

    def relay_last(self):
        p = self.p
        for k in range(1, p.chips):
            dp = p.chip_before(k) * 2 + p.core
            arrived(self.piece(1 - p.tp, dp, slice(0, self.left)), self.rows.at[1, k - 1], p)
            if self.left < self.cols:
                part = self.piece(1 - p.tp, dp, slice(self.left, self.cols))
                arrived(part, self.across.at[k], p)
            got = self.piece(1 - p.tp, dp)
            self.go(got, got, self.from_mate.at[1, k], p.mate())

    def finish(self):
        p = self.p
        for part in range(2):
            tp = p.tp if part == 0 else 1 - p.tp
            for k in range(p.chips):
                dp = p.chip_before(k) * 2 + 1 - p.core
                arrived(self.piece(tp, dp), self.from_mate.at[part, k], p)

    def drain(self):
        for copy in self.copies:
            copy.wait_send()


def twice(x):
    return jnp.concatenate([x, x], axis=1)


def fill_masks(dm, maskp, maskx):
    block = block_index()
    keys = lax.broadcasted_iota(jnp.int32, maskp.shape, 0)
    cols = lax.broadcasted_iota(jnp.int32, maskp.shape, 1) % dm.PB
    maskp[...] = jnp.where(keys <= cols + block * dm.PB, 0.0, NEG)
    keys = lax.broadcasted_iota(jnp.int32, maskx.shape, 0)
    cols = lax.broadcasted_iota(jnp.int32, maskx.shape, 1) % dm.NCH
    seen = (keys // CL == cols // dm.CH) & (
        keys % CL <= cols % dm.CH + half_index() * dm.CH
    )
    maskx[...] = jnp.where(seen, 0.0, NEG)


def heads_columns(a, b):
    lo_a, lo_b = sublane_pick(a.shape, True), sublane_pick(b.shape, True)
    zero_a, zero_b = jnp.zeros_like(a), jnp.zeros_like(b)
    return jnp.concatenate(
        [
            jnp.where(lo_a, a, zero_a),
            jnp.where(lo_a, zero_a, a),
            jnp.where(lo_b, b, zero_b),
            jnp.where(lo_b, zero_b, b),
        ],
        axis=1,
    )


def heads_rows(a, b):
    lo_a, lo_b = lane_pick(a.shape, True), lane_pick(b.shape, True)
    zero_a, zero_b = jnp.zeros_like(a), jnp.zeros_like(b)
    return jnp.concatenate(
        [
            jnp.where(lo_a, a, zero_a),
            jnp.where(lo_a, zero_a, a),
            jnp.where(lo_b, b, zero_b),
            jnp.where(lo_b, zero_b, b),
        ],
        axis=0,
    )


def forward_kernel(
    dm,
    left,
    prompt,
    cont,
    cos_few,
    sin_few,
    wq,
    wm,
    cot_p,
    cot_c,
    q_out,
    att_out,
    lse_out,
    ln_out,
    cos,
    sin,
    nt_hbm,
    own_nt_hbm,
    k_hbm,
    v_hbm,
    w_hbm,
    wm_out,
    own_p_hbm,
    own_c_hbm,
    cot_p_out,
    cot_c_out,
    nt_out,
    own_out,
    k_out,
    v_out,
    maskp,
    maskx,
    sbuf,
    all_rows,
    own_rows,
    xp,
    xc,
    w,
    put_sem,
    trade_send,
    trade_recv,
    x_send,
    x_plane,
    x_mate,
    c_send,
    c_mate,
    own_sem,
    *sems,
):
    G, R, PB, NCH, D, NP, NT = dm.G, dm.R, dm.PB, dm.NCH, dm.D, dm.NP, dm.NT
    NC, CH = dm.NC, dm.CH
    HC = (w.shape[2] - 128) // 3
    TP = w.shape[0]
    p = Peers()
    block = block_index()
    gq = WeightGather(p, wq, w, wq.shape[1] // 256 * 128, *sems[:4])
    gm = WeightGather(p, wm, wm_out, left, *sems[4:])
    size = wq.shape[0]
    mine = pl.ds(pl.multiple_of(p.dp * size, 16), size)

    landing = [xp.at[p.ctx * 2 + p.tp], xc.at[p.tp], cot_p_out, cot_c_out]

    def moved(i):
        src = [prompt, cont, cot_p, cot_c][i]
        return pltpu.make_async_remote_copy(
            src_ref=src,
            dst_ref=landing[i],
            send_sem=trade_send.at[i],
            recv_sem=trade_recv.at[i],
            device_id=p.partner(),
            device_id_type=MESH,
        )

    def kept(i):
        return pltpu.make_async_copy([prompt, cont, cot_p, cot_c][i], landing[i], trade_send.at[i])

    moves = p.core != p.tp

    def trade(i):
        @pl.when(moves)
        def _():
            moved(i).start()

        @pl.when(jnp.logical_not(moves))
        def _():
            kept(i).start()

    def traded(i):
        @pl.when(moves)
        def _():
            moved(i).wait_recv()

        @pl.when(jnp.logical_not(moves))
        def _():
            kept(i).wait()

    local = [
        pltpu.make_async_copy(wq, w.at[p.tp, mine, :], own_sem.at[0]),
        pltpu.make_async_copy(wm, wm_out.at[p.tp, mine, :], own_sem.at[1]),
    ]
    for copy in local:
        copy.start()
    p.greet(trades=True)
    trade(0)
    gq.start()
    traded(0)
    own = xp.at[block]
    sent = []
    for k in range(1, p.ctxs):
        sent.append(send(own, own, x_send.at[k - 1], x_plane.at[k - 1], p.plane(k)))
    sent.append(send(own, own, x_send.at[p.ctxs - 1], x_mate.at[0], p.mate()))
    fill_masks(dm, maskp, maskx)
    second = lax.broadcasted_iota(jnp.int32, (128, 128), 1) % HD >= HD // 2
    for i in range(0, dm.P + CL, 128):
        part = cos_few[:, i : i + 128]
        cos[i : i + 128, :] = jnp.concatenate([part] * 4, axis=0).T
        part = sin_few[:, i : i + 128]
        part = jnp.concatenate([part] * 4, axis=0).T
        sin[i : i + 128, :] = jnp.where(second, part, -part)
    gq.relay_rows()
    gq.relay_across()
    trade(1)
    gm.start()
    gq.relay_last()
    traded(1)
    sent.append(send(xc.at[p.core], xc.at[p.core], c_send, c_mate, p.mate()))
    trade(2)
    trade(3)
    gq.finish()
    local[0].wait()
    puts = [
        pltpu.make_async_copy(w, w_hbm, put_sem.at[0]),
        pltpu.make_async_copy(xp.at[block], own_p_hbm, put_sem.at[1]),
        pltpu.make_async_copy(xc.at[p.core], own_c_hbm, put_sem.at[2]),
    ]
    for put in puts:
        put.start()
    ln = w[0, :, 3 * HC :].astype(F32).T[:8, :]
    ln_out[...] = ln
    gain, bias = ln[0:1, :], ln[1:2, :]

    def normed(x):
        hat, _ = norm_stats(x.astype(F32))
        return (hat * gain + bias).astype(BF16)

    def turned(x, table):
        rows = x.shape[0]
        return rotate(x, cos[pl.ds(table, rows), :], sin[pl.ds(table, rows), :])

    x = jnp.concatenate([xp[block].reshape(NP, D), xc[p.core].reshape(NT - NP, D)], axis=0)
    n = normed(x)
    own_rows[...] = n
    places = [(g * PB, PB, pl.multiple_of(block * PB, PB)) for g in range(G)]
    places += [
        (NP + i * CH, CH, pl.multiple_of(dm.P + p.core * CH, CH)) for i in range(G * NC)
    ]
    for t in range(TP):
        qq = dot(n, w[t, :, :HC])
        for first, count, table in places:
            for j in range(HC // 128):
                tile = turned(qq[first : first + count, j * 128 : (j + 1) * 128], table).astype(BF16)
                q_out[first : first + count, t * HC + j * 128 : t * HC + (j + 1) * 128] = (
                    tile.astype(F32) * 0.125
                ).astype(BF16)
    own_out[...] = transpose(own_rows[...])

    def keys_values(x, places):
        n = normed(x)
        for first, count, g, row, table in places:
            all_rows[pl.ds(pl.multiple_of(g * R + row, 16), count), :] = n[first : first + count]
        for t in range(TP):
            kk = dot(n, w[t, :, HC : 2 * HC])
            for first, count, g, row, table in places:
                for j in range(HC // 128):
                    tile = turned(kk[first : first + count, j * 128 : (j + 1) * 128], table)
                    k_out[g, pl.ds(row, count), t * HC + j * 128 : t * HC + (j + 1) * 128] = tile.astype(BF16)
            vv = dot(n, w[t, :, 2 * HC : 3 * HC]).astype(BF16)
            for first, count, g, row, table in places:
                v_out[g, pl.ds(row, count), t * HC : (t + 1) * HC] = vv[first : first + count]

    arrived(xc.at[1 - p.core], c_mate, p)
    x = [xc[e, g, c] for g in range(G) for c in range(NC) for e in range(2)]
    keys_values(
        jnp.concatenate(x, axis=0),
        [((g * NC + c) * CL, CL, g, dm.P + c * CL, dm.P) for g in range(G) for c in range(NC)],
    )

    def relay(k):
        b = p.ctx_before(k) * 2 + p.core
        return pltpu.make_async_remote_copy(
            src_ref=xp.at[b],
            dst_ref=xp.at[b],
            send_sem=x_send.at[p.ctxs + k - 1],
            recv_sem=x_mate.at[k],
            device_id=p.mate(),
            device_id_type=MESH,
        )

    def plane(k, carry):
        c = p.ctx_before(k)

        @pl.when(k > 0)
        def _():
            arrived(xp.at[c * 2 + p.core], x_plane.at[k - 1], p)
            relay(k).start()

        arrived(xp.at[c * 2 + 1 - p.core], x_mate.at[k], p)
        x = xp[pl.ds(c * 2, 2)].reshape(2 * NP, D)
        places = []
        for e in range(2):
            row = pl.multiple_of((c * 2 + e) * PB, PB)
            places += [((e * G + g) * PB, PB, g, row, row) for g in range(G)]
        keys_values(x, places)
        return carry

    lax.fori_loop(0, p.ctxs, plane, 0)
    puts += [
        pltpu.make_async_copy(k_out, k_hbm, put_sem.at[3]),
        pltpu.make_async_copy(v_out, v_hbm, put_sem.at[4]),
    ]
    for put in puts[3:]:
        put.start()

    def turn(i, carry):
        rows = pl.ds(pl.multiple_of(i * 256, 256), 256)
        nt_out[:, rows] = transpose(all_rows[rows, :])
        return carry

    lax.fori_loop(0, G * R // 256, turn, 0)
    puts += [
        pltpu.make_async_copy(nt_out, nt_hbm, put_sem.at[5]),
        pltpu.make_async_copy(own_out, own_nt_hbm, put_sem.at[6]),
    ]
    for put in puts[5:]:
        put.start()
    gm.relay_across()
    gm.relay_rows()

    TILE = 256
    tiles = dm.P // TILE

    def attend(i, carry):
        g, pair = i // dm.PAIRS, i % dm.PAIRS
        lanes = pl.ds(pl.multiple_of(pair * 128, 128), 128)
        qp = q_out[pl.ds(pl.multiple_of(g * PB, PB), PB), lanes]
        qc = q_out[pl.ds(pl.multiple_of(dm.NP + g * NCH, NCH), NCH), lanes]
        qt = heads_columns(transpose(qp), transpose(qc))
        top = None
        for j in range(tiles):
            s = dot(k_out[g, j * TILE : (j + 1) * TILE, lanes], qt)
            sbuf[j * TILE : (j + 1) * TILE, : 2 * PB] = (
                s[:, : 2 * PB] + twice(maskp[j * TILE : (j + 1) * TILE, :])
            )
            sbuf[j * TILE : (j + 1) * TILE, 2 * PB :] = s[:, 2 * PB :]
            here = jnp.max(sbuf[j * TILE : (j + 1) * TILE, :], axis=0, keepdims=True)
            top = here if top is None else jnp.maximum(top, here)
        sx = dot(k_out[g, dm.P :, lanes], qt[:, 2 * PB :]) + maskx[...]
        topx = jnp.max(sx, axis=0, keepdims=True)
        top = jnp.concatenate([top[:, : 2 * PB], jnp.maximum(top[:, 2 * PB :], topx)], axis=1)
        total, acc = None, None
        for j in range(tiles):
            e = jnp.exp(sbuf[j * TILE : (j + 1) * TILE, :] - top)
            here = jnp.sum(e, axis=0, keepdims=True)
            vt = transpose(v_out[g, j * TILE : (j + 1) * TILE, lanes])
            part = dot(vt, e.astype(BF16))
            total = here if total is None else total + here
            acc = part if acc is None else acc + part
        ex = jnp.exp(sx - top[:, 2 * PB :])
        partx = dot(transpose(v_out[g, dm.P :, lanes]), ex.astype(BF16))
        totalx = jnp.sum(ex, axis=0, keepdims=True)
        total = jnp.concatenate([total[:, : 2 * PB], total[:, 2 * PB :] + totalx], axis=1)
        acc_p = acc[:, : 2 * PB] / total[:, : 2 * PB]
        acc_c = (acc[:, 2 * PB :] + partx) / total[:, 2 * PB :]
        lse_out[i] = top + jnp.log(total)
        outp = jnp.where(sublane_pick((128, PB), True), acc_p[:, :PB], acc_p[:, PB:])
        outc = jnp.where(sublane_pick((128, NCH), True), acc_c[:, :NCH], acc_c[:, NCH:])
        att_out[pl.ds(pl.multiple_of(g * PB, PB), PB), lanes] = outp.T.astype(BF16)
        att_out[pl.ds(pl.multiple_of(dm.NP + g * NCH, NCH), NCH), lanes] = outc.T.astype(BF16)
        return carry

    lax.fori_loop(0, G * dm.PAIRS, attend, 0)
    gm.relay_last()
    gm.finish()
    gq.drain()
    gm.drain()
    for copy in sent:
        copy.wait_send()
    for k in range(1, p.ctxs):
        relay(k).wait_send()
    local[1].wait()
    for i in (2, 3):
        traded(i)

    @pl.when(moves)
    def _():
        for i in range(4):
            moved(i).wait_send()

    for put in puts:
        put.wait()


class Reduce:
    REFS = 13

    def __init__(self, p, cross_first, refs):
        self.p, self.n, self.cross_first = p, len(cross_first), cross_first
        self.mine, self.got, self.row, self.acr, self.zin = refs[:5]
        self.sc, self.rc, self.sy, self.ry, self.sx, self.rx, self.sz, self.rz = refs[5:13]
        mid = p.ctxs // 2
        self.centre = (p.ctx == mid - 1) | (p.ctx == mid)
        self.outer = (p.ctx > 0) & (p.ctx < p.ctxs - 1)
        step = jnp.where(p.ctx < mid, 1, -1)
        self.inner_at = p.ctx + step
        self.outer_at = jnp.clip(p.ctx - step, 0, p.ctxs - 1)

    @staticmethod
    def scratch(cross_first, chips, size, width):
        n = len(cross_first)
        dma = pltpu.SemaphoreType.DMA
        far = max(chips - 1, 1)
        rows = n + sum(1 for c in cross_first if not c)
        parts = sum(chips if c else 1 for c in cross_first)
        return [
            pltpu.VMEM((2, chips * 2 * size, width), BF16),
            pltpu.VMEM((2 * n, chips, size, width), BF16),
            pltpu.VMEM((rows, far, size, width), BF16),
            pltpu.VMEM((parts, size, width), BF16),
            pltpu.VMEM((n, 2, size, width), BF16),
            dma((2 * n, chips)),
            dma((2 * n, chips)),
            dma((2 * n, far)),
            dma((2 * n, far)),
            dma((n,)),
            dma((n,)),
            dma((n, 2)),
            dma((n, 2)),
        ]

    def copy(self, src, dst, send_sem, recv_sem, device):
        return pltpu.make_async_remote_copy(
            src_ref=src,
            dst_ref=dst,
            send_sem=send_sem,
            recv_sem=recv_sem,
            device_id=device,
            device_id_type=MESH,
        )

    def slot(self, whose, j):
        return 0 if whose == "other" else 1

    def crosses(self, i):
        return self.cross_first[i % self.n]

    def travels(self, i):
        return i >= self.n or not self.crosses(i)

    def mine_of(self, y, core):
        size = self.got.shape[2]
        return pl.ds(pl.multiple_of((2 * y + core) * size, 16), size)

    def by_core(self, i, slot, y):
        p = self.p
        return self.copy(
            self.mine.at[slot, self.mine_of(y, 1 - p.core), :],
            self.got.at[i, y],
            self.sc.at[i, y],
            self.rc.at[i, y],
            p.mate(),
        )

    def row_slot(self, i):
        return sum(1 for e in range(i) if self.travels(e))

    def by_row(self, i, k):
        p = self.p
        return self.copy(
            self.got.at[i, p.chip_after(k)],
            self.row.at[self.row_slot(i), k - 1],
            self.sy.at[i, k - 1],
            self.ry.at[i, k - 1],
            p.row(k),
        )

    def by_tp(self, j):
        p = self.p
        slot = self.acr_slot(j)
        if self.crosses(j):
            src, dst = self.got.at[j], self.acr.at[pl.ds(slot, p.chips)]
        else:
            src, dst = self.got.at[j, p.chip], self.acr.at[slot]
        return self.copy(src, dst, self.sx.at[j], self.rx.at[j], p.across())

    def acr_slot(self, j):
        return sum(self.p.chips if c else 1 for c in self.cross_first[:j])

    def inward(self, j):
        slot = jnp.where(self.centre, 1, 0)
        return self.copy(
            self.got.at[self.n + j, self.p.chip],
            self.zin.at[j, slot],
            self.sz.at[j, 0],
            self.rz.at[j, slot],
            self.p.at(ctx=self.inner_at),
        )

    def outward(self, j):
        return self.copy(
            self.got.at[self.n + j, self.p.chip],
            self.zin.at[j, 1],
            self.sz.at[j, 1],
            self.rz.at[j, 1],
            self.p.at(ctx=self.outer_at),
        )

    def add(self, i, y, other):
        self.got[i, y] = (self.got[i, y].astype(F32) + other.astype(F32)).astype(BF16)

    def cores_send(self, i, slot):
        for y in range(self.p.chips):
            self.by_core(i, slot, y).start()

    def cores_sent(self, i, slot):
        for y in range(self.p.chips):
            self.by_core(i, slot, y).wait_send()

    def rows_send(self, i):
        for k in range(1, self.p.chips):
            self.by_row(i, k).start()

    def cores_sum(self, i, slot):
        p = self.p
        for y in range(p.chips):
            self.by_core(i, slot, y).wait_recv()
            self.add(i, y, self.mine[slot, self.mine_of(y, p.core), :])
        if not self.crosses(i):
            self.rows_send(i)
        elif i < self.n:
            self.by_tp(i).start()

    def cross_sum(self, j):
        self.by_tp(j).wait_recv()
        for y in range(self.p.chips):
            self.add(self.n + j, y, self.acr[self.acr_slot(j) + y])
        self.rows_send(self.n + j)

    def rows_sum(self, i):
        p = self.p
        for k in range(1, p.chips):
            self.by_row(i, k).wait_recv()
            self.add(i, p.chip, self.row[self.row_slot(i), k - 1])
        if i < self.n:
            self.by_tp(i).start()
            return
        j = i - self.n
        if not self.crosses(i):
            self.by_tp(j).wait_recv()
            self.add(i, p.chip, self.acr[self.acr_slot(j)])

        @pl.when(jnp.logical_not(self.outer))
        def _():
            self.inward(j).start()

    def ctx_in(self, j):
        @pl.when(self.outer)
        def _():
            pltpu.make_async_copy(self.zin.at[j, 0], self.zin.at[j, 0], self.rz.at[j, 0]).wait()
            self.add(self.n + j, self.p.chip, self.zin[j, 0])
            self.inward(j).start()

    def ctx_mid(self, j):
        @pl.when(self.centre)
        def _():
            self.from_inner(j)
            self.add(self.n + j, self.p.chip, self.zin[j, 1])

            @pl.when(self.outer)
            def _():
                self.outward(j).start()

    def ctx_end(self, j):
        @pl.when(jnp.logical_not(self.centre))
        def _():
            self.from_inner(j)
            self.got[self.n + j, self.p.chip] = self.zin[j, 1]

            @pl.when(self.outer)
            def _():
                self.outward(j).start()

    def from_inner(self, j):
        pltpu.make_async_copy(self.zin.at[j, 1], self.zin.at[j, 1], self.rz.at[j, 1]).wait()
        self.inward(j).wait_send()

    def result(self, j):
        return self.got[self.n + j, self.p.chip].astype(F32)

    def drain(self):
        p = self.p
        for i in range(2 * self.n):
            if self.travels(i):
                for k in range(1, p.chips):
                    self.by_row(i, k).wait_send()
        for j in range(self.n):
            self.by_tp(j).wait_send()

            @pl.when(self.outer)
            def _():
                self.outward(j).wait_send()


class SmallSum:
    def __init__(self, p, sm, near, rows, across, planes, ss, rc, ry, rx, rz):
        self.p, self.sm, self.near, self.rows, self.across, self.planes = p, sm, near, rows, across, planes
        self.ss, self.rc, self.ry, self.rx, self.rz = ss, rc, ry, rx, rz

    def copy(self, index, src, dst, recv_sem, device):
        return pltpu.make_async_remote_copy(
            src_ref=src,
            dst_ref=dst,
            send_sem=self.ss.at[index],
            recv_sem=recv_sem,
            device_id=device,
            device_id_type=MESH,
        )

    def to_mate(self):
        return self.copy(0, self.sm, self.near, self.rc, self.p.mate())

    def to_row(self, k):
        mine = self.rows.at[self.p.chip]
        return self.copy(1 + k, mine, mine, self.ry.at[k - 1], self.p.row(k))

    def to_across(self):
        return self.copy(1, self.across.at[0], self.across.at[1], self.rx, self.p.across())

    def to_plane(self, k):
        mine = self.planes.at[self.p.ctx]
        return self.copy(self.p.chips + k, mine, mine, self.rz.at[k - 1], self.p.plane(k))

    def step(self, which):
        p = self.p
        if which == 0:
            self.to_mate().start()
        elif which == 1:
            self.to_mate().wait_recv()
            self.rows[p.chip] = self.sm[...] + self.near[...]
            for k in range(1, p.chips):
                self.to_row(k).start()
        elif which == 2:
            for k in range(1, p.chips):
                arrived(self.rows.at[p.chip_before(k)], self.ry.at[k - 1], p)
            total = self.rows[0]
            for y in range(1, p.chips):
                total += self.rows[y]
            self.across[0] = total
            self.to_across().start()
        elif which == 3:
            self.to_across().wait_recv()
            self.planes[p.ctx] = self.across[0] + self.across[1]
            for k in range(1, p.ctxs):
                self.to_plane(k).start()

    def result(self):
        p = self.p
        for k in range(1, p.ctxs):
            arrived(self.planes.at[p.ctx_before(k)], self.rz.at[k - 1], p)
        total = self.planes[0]
        for z in range(1, p.ctxs):
            total += self.planes[z]
        self.to_mate().wait_send()
        self.to_across().wait_send()
        for k in range(1, p.chips):
            self.to_row(k).wait_send()
        for k in range(1, p.ctxs):
            self.to_plane(k).wait_send()
        return total


SMALL_AT = {2: 1, 5: 2, 8: 3}
PLAN = {
    ("m", 1): [("a", "cores_sum", "other", 0)],
    ("m", 3): [("a", "cores_sum", "own", 0)],
    ("m", 4): [("a", "cores_sum", "other", 1), ("a", "rows_sum", "other", 0)],
    ("m", 5): [("a", "cores_sum", "own", 1)],
    ("e", 0): [("a", "cores_sum", "other", 2)],
    ("a", 0): [("a", "rows_sum", "own", 0)],
    ("a", 1): [("a", "cores_sum", "own", 2)],
    ("p", 0, 0): [("a", "ctx_in", "own", 0)],
    ("p", 0, 1): [("b", "cores_sum", "own", 0), ("b", "cores_sum", "other", 0)],
    ("p", 0, 3): [("a", "cross_sum", "own", 2), ("a", "rows_sum", "other", 1)],
    ("a", 7): [("a", "ctx_mid", "own", 0)],
    ("a", 8): [("a", "rows_sum", "own", 2), ("hop", 0, 0), ("b", "cores_sum", "other", 1)],
    ("a", 9): [("a", "rows_sum", "own", 1), ("b", "cores_sum", "own", 1), ("b", "cores_sum", "other", 2), ("hop", 0, 1)],
    ("a", 10): [("a", "ctx_in", "own", 2), ("b", "cross_sum", "own", 0)],
    ("a", 11): [("b", "cores_sum", "own", 2), ("hop", 0, 2)],
    ("p", 1, 1): [("b", "cores_sum", "other", 3), ("a", "ctx_in", "own", 1), ("b", "cross_sum", "own", 1)],
    ("p", 1, 3): [("a", "ctx_mid", "own", 2)],
    ("t", 0): [("hop", 1, 0)],
    ("t", 2): [("b", "rows_sum", "other", 3), ("a", "ctx_mid", "own", 1)],
    ("t", 3): [("b", "cross_sum", "own", 2), ("b", "rows_sum", "own", 0), ("b", "cores_sum", "own", 3)],
    ("t", 4): [("b", "rows_sum", "own", 1)],
    ("t", 5): [("hop", 1, 1)],
    ("t", 6): [("b", "ctx_in", "own", 0), ("b", "rows_sum", "own", 3)],
    ("t", 8): [("b", "ctx_in", "own", 1)],
    ("t", 9): [("hop", 1, 2), ("b", "ctx_in", "own", 3), ("b", "rows_sum", "own", 2)],
    ("t", 10): [("b", "ctx_mid", "own", 0)],
    ("t", 11): [("b", "ctx_in", "own", 2)],
    ("t", 14): [("b", "ctx_mid", "own", 1), ("b", "ctx_mid", "own", 3)],
    ("t", 18): [("b", "ctx_mid", "own", 2)],
}


def schedule(ra, rb, on, planes, hop):
    for stage, steps in PLAN.items():
        if stage[0] == "p":
            stage = ("p", stage[1] * planes + stage[2])
        for step in steps:
            if step[0] == "hop":
                on(stage, partial(hop, step[1], step[2]))
                continue
            name, what, whose, j = step
            r = ra if name == "a" else rb
            if what == "cores_sum":
                on(stage, partial(r.cores_sum, j if whose == "other" else r.n + j, r.slot(whose, j)))
            elif what == "rows_sum":
                on(stage, partial(r.rows_sum, j if whose == "other" else r.n + j))
            else:
                on(stage, partial(getattr(r, what), j))


def backward_kernel(
    dm,
    T,
    FC,
    plan_a,
    plan_b,
    mix,
    att,
    own_p,
    own_c,
    cot_p,
    cot_c,
    ln,
    q,
    lse,
    cos,
    sin,
    wm,
    k_hbm,
    v_hbm,
    nt_hbm,
    own_nt_hbm,
    wq_hbm,
    home_arrays_p,
    home_arrays_c,
    early_p,
    early_c,
    home_cot_p,
    home_cot_c,
    out_p,
    out_c,
    gin_p,
    gin_c,
    gq_out,
    go_out,
    gu_out,
    gd_out,
    small_out,
    resid,
    blk,
    gh,
    wo,
    ring,
    gatt,
    nt,
    own_nt,
    maskp,
    maskx,
    kbuf,
    vbuf,
    dk,
    dv,
    dq,
    dxm,
    dxz,
    dxcm,
    blk_away,
    blk_home,
    gin_home,
    put_sem,
    ring_sem,
    wo_sem,
    kv_sem,
    nt_sem,
    wq_sem,
    home_sem,
    b_send,
    b_recv,
    g_send,
    g_recv,
    m_send,
    m_recv,
    z_send,
    z_recv,
    c_send,
    c_recv,
    sm,
    sm_near,
    sm_rows,
    sm_across,
    sm_planes,
    sm_ss,
    sm_rc,
    sm_ry,
    sm_rx,
    sm_rz,
    *refs,
):
    G, R, PB, NCH, D, NX, NP, NT = dm.G, dm.R, dm.PB, dm.NCH, dm.D, dm.NX, dm.NP, dm.NT
    TP, HC = wo.shape[0], wo.shape[2]
    PT = dm.PAIRS // TP
    p = Peers()
    n_a, NB = len(plan_a), len(plan_b)
    ra = Reduce(p, plan_a, refs[: Reduce.REFS])
    rb = Reduce(p, plan_b, refs[Reduce.REFS :])
    block = block_index()
    TILE = 256
    tiles = dm.P // TILE
    chips = p.chips
    S = D // (2 * chips)

    def begin(copies):
        for copy in copies:
            copy.start()

    def ready(copies):
        for copy in copies:
            copy.wait()

    def load_tile(i, slot):
        t = jnp.where(lax.rem(i, 2) == 0, 1 - p.tp, p.tp)
        first = pl.multiple_of(HC + i // 2 * T, 128)
        return [
            pltpu.make_async_copy(
                wm.at[t, :, pl.ds(first, T)], ring.at[slot, :, pl.ds(0, T)], ring_sem.at[0, slot]
            ),
            pltpu.make_async_copy(
                wm.at[t, :, pl.ds(first + FC, T)], ring.at[slot, :, pl.ds(T, T)], ring_sem.at[1, slot]
            ),
        ]

    def pair_at(it):
        turn = it % dm.PAIRS
        return jnp.where(turn % 2 == 0, 1 - p.tp, p.tp) * PT + turn // 2

    def load_kv(it, slot):
        pair, g = pair_at(it), it // dm.PAIRS
        lanes = pl.ds(pl.multiple_of(pair * 128, 128), 128)
        return [
            pltpu.make_async_copy(k_hbm.at[g, :, lanes], kbuf.at[slot], kv_sem.at[0, slot]),
            pltpu.make_async_copy(v_hbm.at[g, :, lanes], vbuf.at[slot], kv_sem.at[1, slot]),
        ]

    wo_load = pltpu.make_async_copy(wm.at[:, :, pl.ds(0, HC)], wo, wo_sem)
    wo_load.start()
    begin(load_tile(0, 0))
    begin(load_kv(0, 0))
    p.greet(trades=True)
    fill_masks(dm, maskp, maskx)
    gain_two, bias_two = ln[2:3, :], ln[3:4, :]

    hn, gd = slice(0, NT), slice(NT, 2 * NT)
    STEP = 128

    def by_rows(step):
        def prompt_part(i, carry):
            rows = pl.ds(pl.multiple_of(i * STEP, STEP), STEP)
            step(own_p[rows, :], cot_p[rows, :], i * STEP)
            return carry

        def cont_part(i, carry):
            rows = pl.ds(pl.multiple_of(i * STEP, STEP), STEP)
            step(own_c[rows, :], cot_c[rows, :], NP + i * STEP)
            return carry

        lax.fori_loop(0, NP // STEP, prompt_part, 0)
        lax.fori_loop(0, (NT - NP) // STEP, cont_part, 0)

    def shifted(first, row):
        return pl.ds(pl.multiple_of(first + row, STEP), STEP)

    wo_load.wait()

    def enter(x, cot, row):
        rows = shifted(0, row)
        r = x.astype(F32)
        for t in range(TP):
            r += dot_nt(att[rows, t * HC : (t + 1) * HC], wo[t])
        resid[rows, :] = r
        blk[rows, :] = r
        h, _ = norm_stats(r)
        n = (h * gain_two + bias_two).astype(BF16)
        dk[rows, :] = n
        nt[:, rows] = transpose(n)
        g = (mix[4] * cot.astype(F32)).astype(BF16)
        dk[shifted(NT, row), :] = g
        nt[:, shifted(NT, row)] = transpose(g)
        gh[rows, :] = jnp.zeros((STEP, D), F32)

    by_rows(enter)

    during = {}

    def on(stage, step):
        during.setdefault(stage, []).append(step)

    def run_when(index, name):
        for (kind, when), steps in during.items():
            if kind == name:

                @pl.when(index == when)
                def _():
                    for step in steps:
                        step()


    sums = SmallSum(p, sm, sm_near, sm_rows, sm_across, sm_planes, sm_ss, sm_rc, sm_ry, sm_rx, sm_rz)
    hops = [(c, b) for c in range(1, p.ctxs - 1) for b in range(c + 1, p.ctxs)]

    def hop(g, part):
        third = pl.cdiv(len(hops), 3)
        for c, b in hops[part * third : (part + 1) * third]:

            @pl.when(p.ctx == c)
            def _():
                at = b - c
                landed(g, at)
                mine = dx_rows(g, b, p.core)[...].astype(F32)
                dxz[g, at] = (dxz[g, at].astype(F32) + mine).astype(BF16)
                rightward(g, dxz.at[g, at], c, b).start()

            far, to = p.ctxs - 1 - c, p.ctxs - 1 - b

            @pl.when(p.ctx == far)
            def _():
                at = p.ctxs - far + to
                landed(g, at)
                mine = dx_rows(g, to, p.core)[...].astype(F32)
                dxz[g, at] = (dxz[g, at].astype(F32) + mine).astype(BF16)
                leftward(g, dxz.at[g, at], far, to).start()

    schedule(ra, rb, on, p.ctxs, hop)

    def run(name):
        for kind, when in sorted(key for key in during if key[0] == name):
            for step in during[kind, when]:
                step()

    def feed(i, carry):
        slot = lax.rem(i, 2)

        @pl.when(i + 1 < 2 * n_a)
        def _():
            begin(load_tile(i + 1, 1 - slot))

        ready(load_tile(i, slot))
        up, dn = ring[slot, :, :T], ring[slot, :, T : 2 * T]
        c0 = 0.7978845608028654
        HALF = NT // 2
        for e in range(2):
            rows = slice(e * HALF, (e + 1) * HALF)
            u = dot(dk[rows, :], up)
            if e == 1:
                run_when(i, "m")
            u2 = u * u
            th = jnp.tanh(c0 * u * (1.0 + 0.044715 * u2))
            half = 0.5 * (1.0 + th)
            act = (u * half).astype(BF16)
            slope = half + 0.5 * u * (1.0 - th * th) * (c0 * (1.0 + 3 * 0.044715 * u2))
            dv[rows, :T] = act
            blk[rows, :] += dot_nt(act, dn)
            gu = (dot(dk[NT + e * HALF : NT + (e + 1) * HALF, :], dn) * slope).astype(BF16)
            dv[NT + e * HALF : NT + (e + 1) * HALF, :T] = gu
            gh[rows, :] += dot_nt(gu, up)

        @pl.when(i >= 2)
        def _():
            ra.cores_sent(slot * n_a + i // 2 - 1, slot)

        for y in range(chips):
            mine = slice(y * 2 * S, (y + 1) * 2 * S)
            ra.mine[slot, mine, :T] = dot(nt[mine, hn], dv[gd, :T]).astype(BF16)
            ra.mine[slot, mine, T:] = dot(nt[mine, gd], dv[hn, :T]).astype(BF16)
        ra.cores_send(slot * n_a + i // 2, slot)
        return carry

    lax.fori_loop(0, 2 * n_a, feed, 0)
    run("e")
    blk_away[:NT, :] = blk[...].astype(BF16)
    away = ra.copy(blk_away.at[pl.ds(0, NT), :], blk_home, b_send, b_recv, p.partner())

    @pl.when(p.core != p.tp)
    def _():
        away.start()

    @pl.when(p.core == p.tp)
    def _():
        blk_home[...] = blk_away[:NT, :]

    sm[...] = jnp.zeros_like(sm)

    def leave(x, cot, row):
        rows = shifted(0, row)
        cot = cot.astype(F32)
        sm[2:3, :] += jnp.sum(cot * blk[rows, :], axis=0, keepdims=True)
        h, scale = norm_stats(resid[rows, :])
        g = gh[rows, :]
        sm[0:1, :] += jnp.sum(g * h, axis=0, keepdims=True)
        sm[1:2, :] += jnp.sum(g, axis=0, keepdims=True)
        gr = mix[4] * cot + norm_back(g, gain_two, h, scale)
        resid[rows, :] = gr
        gb = gr.astype(BF16)
        nt[:, shifted(NT, row)] = transpose(gb)
        for t in range(TP):
            gatt[rows, t * HC : (t + 1) * HC] = dot(gb, wo[t]).astype(BF16)

    by_rows(leave)
    for slot, i in enumerate((0, NB)):
        t = p.tp if slot else 1 - p.tp
        lanes = pl.ds(pl.multiple_of(t * HC, 128), HC)
        for y in range(chips):
            mine = slice(y * 2 * S, (y + 1) * 2 * S)
            rb.mine[slot, mine, :] = dot(nt[mine, gd], att[:, lanes]).astype(BF16)
        rb.cores_send(i, slot)
    nt_load = [
        pltpu.make_async_copy(nt_hbm, nt, nt_sem.at[0]),
        pltpu.make_async_copy(own_nt_hbm, own_nt, nt_sem.at[1]),
    ]
    begin(nt_load)
    wq_load = pltpu.make_async_copy(wq_hbm.at[:, :, pl.ds(0, 3 * HC)], ring.at[:, :, pl.ds(0, 3 * HC)], wq_sem)
    wq_load.start()
    during.setdefault(("a", dm.PAIRS - 1), []).insert(0, partial(ready, nt_load))

    def attend(turn, g):
        it = g * dm.PAIRS + turn
        pair = pair_at(it)
        slot = it % 2

        @pl.when(it + 1 < G * dm.PAIRS)
        def _():
            begin(load_kv(it + 1, 1 - slot))

        lanes = pl.ds(pl.multiple_of(pair * 128, 128), 128)
        rp = pl.ds(pl.multiple_of(g * PB, PB), PB)
        rc = pl.ds(pl.multiple_of(dm.NP + g * NCH, NCH), NCH)
        qp, qc = q[rp, lanes], q[rc, lanes]
        gp, gc = gatt[rp, lanes], gatt[rc, lanes]
        ap, ac = att[rp, lanes].astype(F32), att[rc, lanes].astype(F32)
        qt = heads_columns(transpose(qp), transpose(qc))
        gpt, gct = gp.astype(F32).T, gc.astype(F32).T
        gt = heads_columns(gpt.astype(BF16), gct.astype(BF16))
        qs, gs = heads_rows(qp, qc), heads_rows(gp, gc)
        prodp, prodc = gpt * ap.T, gct * ac.T
        delta = jnp.concatenate(
            [
                jnp.sum(prodp[:HD], axis=0, keepdims=True),
                jnp.sum(prodp[HD:], axis=0, keepdims=True),
                jnp.sum(prodc[:HD], axis=0, keepdims=True),
                jnp.sum(prodc[HD:], axis=0, keepdims=True),
            ],
            axis=1,
        )
        stat = lse[g * dm.PAIRS + pair]
        ready(load_kv(it, slot))

        def grads(s, kt, vt, cols):
            pr = jnp.exp(s - stat[:, cols:])
            dp = dot(vt, gt[:, cols:])
            ds = (pr * (dp - delta[:, cols:])).astype(BF16)
            gv = dot(pr.astype(BF16), gs[cols:])
            gk = dot(ds, qs[cols:])
            gq = dot(transpose(kt), ds)
            return gk, gv, gq

        acc = None
        for j in range(tiles):
            rows = slice(j * TILE, (j + 1) * TILE)
            kt = kbuf[slot, rows, :]
            s = dot(kt, qt)
            s = jnp.concatenate([s[:, : 2 * PB] + twice(maskp[rows, :]), s[:, 2 * PB :]], axis=1)
            gk, gv, gq = grads(s, kt, vbuf[slot, rows, :], 0)
            gk = rotate_back(gk, cos[rows, :], sin[rows, :]).astype(BF16)
            gv = gv.astype(BF16)
            out = pl.ds(pl.multiple_of(g * R + j * TILE, 128), TILE)
            dk[out, lanes] = gk
            dv[out, lanes] = gv
            if j == tiles // 2:
                run_when(it, "a")
            acc = gq if acc is None else acc + gq
        kt = kbuf[slot, dm.P :, :]
        s = dot(kt, qt[:, 2 * PB :]) + maskx[...]
        gk, gv, gq = grads(s, kt, vbuf[slot, dm.P :, :], 2 * PB)
        for c in range(dm.NC):
            rows = slice(dm.P, dm.P + CL)
            out = pl.ds(pl.multiple_of(g * R + dm.P + c * CL, CL), CL)
            part = rotate_back(gk[c * CL : (c + 1) * CL], cos[rows, :], sin[rows, :])
            dk[out, lanes] = part.astype(BF16)
            dv[out, lanes] = gv[c * CL : (c + 1) * CL].astype(BF16)
        accp = acc[:, : 2 * PB] * 0.125
        accc = (acc[:, 2 * PB :] + gq) * 0.125
        outp = jnp.where(sublane_pick((128, PB), True), accp[:, :PB], accp[:, PB:]).T
        outc = jnp.where(sublane_pick((128, NCH), True), accc[:, :NCH], accc[:, NCH:]).T
        tab = pl.ds(pl.multiple_of(block * PB, PB), PB)
        dq[rp, lanes] = rotate_back(outp, cos[tab, :], sin[tab, :]).astype(BF16)
        tab = pl.ds(pl.multiple_of(dm.P + p.core * dm.CH, dm.CH), dm.CH)
        for c in range(dm.NC):
            part = rotate_back(outc[c * dm.CH : (c + 1) * dm.CH], cos[tab, :], sin[tab, :])
            rows = pl.ds(pl.multiple_of(dm.NP + g * NCH + c * dm.CH, dm.CH), dm.CH)
            dq[rows, lanes] = part.astype(BF16)

        @pl.when(g == G - 1)
        def _():
            put = turn % 2
            index = put * NB + 1 + turn // 2
            rb.cores_sent(index - 1, put)
            both = jnp.concatenate([dk[:, lanes], dv[:, lanes]], axis=1)
            for y in range(chips):
                mine = slice(y * 2 * S, (y + 1) * 2 * S)
                rb.mine[put, mine, 128:] = dot(nt[mine, :], both).astype(BF16)
                rb.mine[put, mine, :128] = dot(own_nt[mine, :], dq[:, lanes]).astype(BF16)
            rb.cores_send(index, put)

        return g

    w = ring

    def project(rows):
        total = None
        for t in range(TP):
            part = dot_nt(dk[rows, t * HC : (t + 1) * HC], w[t, :, HC : 2 * HC])
            total = part if total is None else total + part
            total += dot_nt(dv[rows, t * HC : (t + 1) * HC], w[t, :, 2 * HC : 3 * HC])
        return total

    NCONT = NT - NP
    gain_one = ln[0:1, :]
    halves = lambda core, g: pl.ds(pl.multiple_of(core * NCONT + g * NCH, 16), NCH)

    def dx_at(g, c, first, count):
        if g == G - 1:
            return dk.at[pl.ds(pl.multiple_of(g * R + c * 2 * PB + first, PB), count), :]
        fit = D // (2 * PB)
        row = pl.multiple_of(c % fit * 2 * PB + first, PB)
        return ra.mine.at[c // fit, pl.ds(row, count), pl.ds(0, D)]

    def dx_rows(g, c, core):
        return dx_at(g, c, core * PB, PB)

    def to_mate(g, k):
        i = g * p.ctxs + k
        rows = dx_rows(g, p.ctx_after(k), 1 - p.core)
        return ra.copy(rows, dxm.at[i], m_send.at[i], m_recv.at[i], p.mate())

    def rightward(g, src, c, b):
        i = b - c - 1
        return ra.copy(src, dxz.at[g, i], z_send.at[g, b], z_recv.at[g, i], p.at(ctx=c + 1))

    def leftward(g, src, c, b):
        i = p.ctxs - c + 1 + b
        return ra.copy(src, dxz.at[g, i], z_send.at[g, b], z_recv.at[g, i], p.at(ctx=c - 1))

    def landed(g, i):
        pltpu.make_async_copy(dxz.at[g, i], dxz.at[g, i], z_recv.at[g, i]).wait()

    def each_group(g, step):
        for e in range(G):

            @pl.when(g == e)
            def _():
                step(e)

    def cont_copy(g):
        return ra.copy(
            blk_away.at[halves(1 - p.core, g), :],
            dxcm.at[pl.ds(pl.multiple_of(g * NCH, 16), NCH), :],
            c_send.at[g],
            c_recv.at[g],
            p.mate(),
        )

    def norm_sums(x, turned, rows):
        sm[8:9, :] += jnp.sum(x.astype(F32), axis=0, keepdims=True)
        for d in range(0, D, 128):
            gh[:128, d : d + 128] += dot(turned[d : d + 128, rows], x[:, d : d + 128])

    def norm_grads():
        same = lax.broadcasted_iota(jnp.int32, (128, 128), 0) == lax.broadcasted_iota(
            jnp.int32, (128, 128), 1
        )
        for d in range(0, D, 128):
            cols = slice(d, d + 128)
            x = blk[:, cols].astype(BF16)
            sm[8:9, cols] += jnp.sum(x.astype(F32), axis=0, keepdims=True)
            gh[:128, cols] += dot(own_nt[cols, :], x)
            total = jnp.sum(jnp.where(same, gh[:128, cols], 0.0), axis=0, keepdims=True)
            sm[7:8, cols] = (total - ln[1:2, cols] * sm[8:9, cols]) / ln[0:1, cols]

    gh[:128, :] = jnp.zeros((128, D), F32)

    def group(g, carry):
        lax.fori_loop(0, dm.PAIRS, attend, g)

        @pl.when(g == 0)
        def _():
            wq_load.wait()
            ra.cores_sent(n_a - 1, 0)
            ra.cores_sent(2 * n_a - 1, 1)

            @pl.when(p.core != p.tp)
            def _():
                away.wait_send()

        def planes(i, carry):
            @pl.when(i < p.ctxs)
            def _():
                k = lax.rem(i + 1, p.ctxs)
                both = pl.ds(pl.multiple_of(g * R + p.ctx_after(k) * 2 * PB, 2 * PB), 2 * PB)
                total = project(both).astype(BF16)
                norm_sums(total, nt, both)

                def out(e):
                    dx_at(e, p.ctx_after(k), 0, 2 * PB)[...] = total
                    to_mate(e, k).start()

                each_group(g, out)
                run_when(g * p.ctxs + i, "p")

            @pl.when(i > 0)
            def _():
                k = lax.rem(i, p.ctxs)

                def back(e):
                    to_mate(e, k).wait_recv()
                    b = p.ctx_after(k)
                    mine = dx_rows(e, b, p.core)
                    mine[...] = (mine[...].astype(F32) + dxm[e * p.ctxs + k].astype(F32)).astype(BF16)

                    @pl.when((k > 0) & (p.ctx == 0))
                    def _():
                        rightward(e, mine, 0, b).start()

                    @pl.when((k > 0) & (p.ctx == p.ctxs - 1))
                    def _():
                        leftward(e, mine, p.ctxs - 1, b).start()

                each_group(g, back)

            return carry

        lax.fori_loop(0, p.ctxs + 1, planes, 0)
        rows = pl.ds(pl.multiple_of(g * R + dm.P, CL), NX)
        total = project(rows).astype(BF16)
        norm_sums(total, nt, rows)
        for c in range(dm.NC):
            for e in range(2):
                out = pl.ds(pl.multiple_of(e * NCONT + g * NCH + c * dm.CH, dm.CH), dm.CH)
                blk_away[out, :] = total[c * CL + e * dm.CH : c * CL + (e + 1) * dm.CH]
        cont_copy(g).start()
        for first, count in ((g * PB, PB), (NP + g * NCH, NCH)):
            rows = pl.ds(pl.multiple_of(first, 16), count)
            total = dot_nt(dq[rows, :HC], w[0, :, :HC])
            for t in range(1, TP):
                total += dot_nt(dq[rows, t * HC : (t + 1) * HC], w[t, :, :HC])
            blk[rows, :] = total
        return carry

    def enter_back(gn, x, rows):
        gn += blk[rows, :]
        hat, scale = norm_stats(x.astype(F32))
        gatt[rows, :] = (resid[rows, :] + norm_back(gn, gain_one, hat, scale)).astype(BF16)

    def gin_away(part):
        rows = pl.ds(0, NP) if part == 0 else pl.ds(NP, NT - NP)
        return ra.copy(gatt.at[rows, :], gin_home.at[rows, :], g_send.at[part], g_recv.at[part], p.partner())

    def give(part):
        rows = slice(0, NP) if part == 0 else slice(NP, NT)

        @pl.when(p.core != p.tp)
        def _():
            gin_away(part).start()

        @pl.when(p.core == p.tp)
        def _():
            gin_home[rows, :] = gatt[rows, :]

    lax.fori_loop(0, G, group, 0)
    homes = []
    for i, (a, c) in enumerate(
        [(home_arrays_p, home_arrays_c)]
        + [(early_p.at[e], early_c.at[e]) for e in range(3)]
        + [(home_cot_p, home_cot_c)]
    ):
        homes.append(pltpu.make_async_copy(a, dv.at[pl.ds(i * NT, NP), :], home_sem.at[0, i]))
        homes.append(pltpu.make_async_copy(c, dv.at[pl.ds(i * NT + NP, NT - NP), :], home_sem.at[1, i]))
    begin(homes)

    def cont_back(g, carry):
        cont_copy(g).wait_recv()
        here = pl.ds(pl.multiple_of(g * NCH, 16), NCH)
        gn = blk_away[halves(p.core, g), :].astype(F32) + dxcm[here, :].astype(F32)
        enter_back(gn, own_c[here, :], pl.ds(pl.multiple_of(NP + g * NCH, 16), NCH))
        return carry

    lax.fori_loop(0, G, cont_back, 0)
    give(1)

    ready(homes)

    @pl.when(p.core != p.tp)
    def _():
        away.wait_recv()

    def blend(i, carry):
        rows = shifted(0, i * STEP)
        res = mix[4] * blk_home[rows, :].astype(F32)
        c = dv[shifted(4 * NT, i * STEP), :].astype(F32)
        for e in range(4):
            a = dv[shifted(e * NT, i * STEP), :].astype(F32)
            res += mix[e] * a
            sm[3 + e : 4 + e, :] += jnp.sum(c * a, axis=0, keepdims=True)
        blk_home[rows, :] = res.astype(BF16)
        return carry

    lax.fori_loop(0, NT // STEP, blend, 0)
    puts = [
        pltpu.make_async_copy(blk_home.at[pl.ds(0, NP), :], out_p, put_sem.at[0]),
        pltpu.make_async_copy(blk_home.at[pl.ds(NP, NT - NP), :], out_c, put_sem.at[1]),
    ]
    begin(puts)
    norm_grads()
    sums.step(0)
    for when in range(10):
        for step in during.get(("t", when), []):
            step()
        if SMALL_AT.get(when):
            sums.step(SMALL_AT[when])

    for g in range(G):
        here = slice(g * PB, (g + 1) * PB)

        @pl.when(p.ctx > 0)
        def _():
            landed(g, 0)
            blk[here, :] += dxz[g, 0].astype(F32)

        @pl.when(p.ctx < p.ctxs - 1)
        def _():
            landed(g, p.ctxs)
            blk[here, :] += dxz[g, p.ctxs].astype(F32)

        enter_back(dx_rows(g, p.ctx, p.core)[...].astype(F32), own_p[here, :], here)
    give(0)
    for when in range(10, 20):
        for step in during.get(("t", when), []):
            step()
    small_out[...] = sums.result()
    gu_puts = []
    for j in range(n_a):
        ra.ctx_end(j)
        total = ra.result(j)
        gd_out[:, j * T : (j + 1) * T] = total[:, T:]
        if len(gu_puts) > 0:
            gu_puts[-1].wait()
        gh[:S, :T] = total[:, :T]
        gu_puts.append(
            pltpu.make_async_copy(
                gh.at[pl.ds(0, S), pl.ds(0, T)], gu_out.at[:, pl.ds(j * T, T)], put_sem.at[2]
            )
        )
        gu_puts[-1].start()
    gu_puts[-1].wait()
    for j in range(NB):
        rb.ctx_end(j)
        total = rb.result(j)
        if j == 0:
            go_out[...] = total
        else:
            for c in range(3):
                gq_out[c, :, (j - 1) * 128 : j * 128] = total[:, c * 128 : (c + 1) * 128]

    @pl.when(p.core != p.tp)
    def _():
        for part in range(2):
            gin_away(part).wait_recv()
            gin_away(part).wait_send()

    more = [
        pltpu.make_async_copy(gin_home.at[pl.ds(0, NP), :], gin_p, put_sem.at[2]),
        pltpu.make_async_copy(gin_home.at[pl.ds(NP, NT - NP), :], gin_c, put_sem.at[3]),
    ]
    begin(more)
    ready(puts + more)
    rb.cores_sent(NB - 1, 0)
    rb.cores_sent(2 * NB - 1, 1)
    for g in range(G):
        for k in range(p.ctxs):
            to_mate(g, k).wait_send()
        for k in range(1, p.ctxs):
            b = p.ctx_after(k)
            ra.copy(dxz.at[g, 0], dxz.at[g, 0], z_send.at[g, b], z_send.at[g, b], p.mate()).wait_send()
        cont_copy(g).wait_send()
    ra.drain()
    rb.drain()


def deliver_kernel(count, *refs):
    sources, small, targets = refs[:count], refs[count], refs[count + 1 : 2 * count + 1]
    outs = refs[2 * count + 1 : 2 * count + 6]
    kept = refs[2 * count + 6 : 3 * count + 6]
    in_sem, out_sem, parts = refs[3 * count + 6 :]
    loads = [pltpu.make_async_copy(sources[i], kept[i], in_sem.at[i]) for i in range(count)]
    puts = [pltpu.make_async_copy(kept[i], targets[i], out_sem.at[i]) for i in range(count)]
    for load in loads:
        load.start()
    S = parts.shape[2]
    norms = jnp.concatenate([small[7:9, :], small[0:2, :], jnp.zeros((4, small.shape[1]), F32)], axis=0)
    for d in range(parts.shape[0]):
        parts[d] = norms[:, d * S : (d + 1) * S]
    mine = parts[lax.axis_index("dp")]
    for i in range(4):
        outs[i][...] = mine[i : i + 1, :]
    sums = jnp.sum(small[...], axis=1, keepdims=True)
    order = (3, 4, 5, 6, 2)
    lanes = lax.broadcasted_iota(jnp.int32, (1, 5), 1)
    mix = jnp.zeros((1, 5), F32)
    for i, row in enumerate(order):
        mix = jnp.where(lanes == i, sums[row : row + 1, :], mix)
    outs[4][...] = mix
    for i in range(count):
        loads[i].wait()
        puts[i].start()
    for put in puts:
        put.wait()


def params(**more):
    return pltpu.CompilerParams(vmem_limit_bytes=VMEM_LIMIT, **more)


def per_device(
    prompt_in,
    cont_in,
    prompt_embed,
    cont_embed,
    prompt_earlier,
    cont_earlier,
    ln1_gain,
    ln1_bias,
    ln2_gain,
    ln2_bias,
    w_qkv,
    w_out,
    w_up,
    w_down,
    mix_weights,
    prompt_cot,
    cont_cot,
):
    G, PB, D = prompt_in.shape
    NC, CH = cont_in.shape[1], cont_in.shape[2]
    TP = lax.axis_size("tp")
    PROMPT = PB * TP * lax.axis_size("ctx")
    HC, FC = w_qkv.shape[2], w_up.shape[1]
    S = w_qkv.shape[0]
    dm = Dims(G, PROMPT, PB, NC, CH, D, HC * TP // HD)
    R, NT, NP = dm.R, dm.NT, dm.NP

    sds = jax.ShapeDtypeStruct
    chips, ctxs = lax.axis_size("dp") // 2, lax.axis_size("ctx")
    norms = jnp.stack([ln1_gain, ln1_bias, ln2_gain, ln2_bias], axis=1)
    norms = jnp.pad(norms, ((0, 0), (0, 124)))
    wq_shard = jnp.concatenate([w_qkv.reshape(S, 3 * HC), norms], axis=1)
    wm_shard = jnp.concatenate([w_out.T, w_up, w_down.T], axis=1)

    positions = jnp.arange(PROMPT + CL, dtype=jnp.int32).astype(F32)
    freq = 10000.0 ** (-(jnp.arange(HD // 2, dtype=jnp.int32).astype(F32) / (HD // 2)))
    angles = freq[:, None] * positions[None, :]
    cos_few, sin_few = jnp.cos(angles), jnp.sin(angles)

    any_ = pl.BlockSpec(memory_space=pl.ANY)
    vmem = pl.BlockSpec(memory_space=pltpu.VMEM)
    dma = pltpu.SemaphoreType.DMA
    left = (HC + 2 * FC) // 128 * 2 // 3 * 128
    q, att, lse, ln, cos, sin, nt, own_nt, k, v, wq, wm, own_p, own_c, cot_p, cot_c = pl.pallas_call(
        partial(forward_kernel, dm, left),
        out_shape=(
            sds((NT, D), BF16),
            sds((NT, D), BF16),
            sds((G * dm.PAIRS, 1, dm.COLS), F32),
            sds((8, D), F32),
            sds((PROMPT + CL, 128), F32),
            sds((PROMPT + CL, 128), F32),
            sds((D, G * R), BF16),
            sds((D, NT), BF16),
            sds((G, R, D), BF16),
            sds((G, R, D), BF16),
            sds((TP, D, 3 * HC + 128), BF16),
            sds((TP, D, HC + 2 * FC), BF16),
            sds(prompt_in.shape, BF16),
            sds(cont_in.shape, BF16),
            sds(prompt_in.shape, BF16),
            sds(cont_in.shape, BF16),
        ),
        in_specs=[vmem] * 5 + [any_] * 3,
        out_specs=(vmem,) * 6 + (any_,) * 10,
        scratch_shapes=[
            pltpu.VMEM((D, G * R), BF16),
            pltpu.VMEM((D, NT), BF16),
            pltpu.VMEM((G, R, D), BF16),
            pltpu.VMEM((G, R, D), BF16),
            pltpu.VMEM((PROMPT, PB), F32),
            pltpu.VMEM((dm.NX, 2 * dm.NCH), F32),
            pltpu.VMEM((PROMPT, dm.COLS), F32),
            pltpu.VMEM((G * R, D), BF16),
            pltpu.VMEM((NT, D), BF16),
            pltpu.VMEM((2 * ctxs, G, PB, D), BF16),
            pltpu.VMEM((2, G, NC, CH, D), BF16),
            pltpu.VMEM((TP, D, 3 * HC + 128), BF16),
            dma((7,)),
            dma((4,)),
            dma((4,)),
            dma((2 * ctxs - 1,)),
            dma((ctxs - 1,)),
            dma((ctxs,)),
            dma,
            dma,
            dma((2,)),
        ]
        + WeightGather.semaphores(chips)
        + WeightGather.semaphores(chips),
        compiler_params=params(collective_id=0, has_side_effects=True),
        name="forward",
    )(prompt_in, cont_in, cos_few, sin_few, wq_shard, wm_shard, prompt_cot, cont_cot)
    T = 512 if FC % 512 == 0 else 256
    plan_a, plan_b = [False, False, True], [True, True, True, False]
    far = max(chips - 1, 1)
    rows = lambda x: x.reshape(-1, D)
    out_p, out_c, gin_p, gin_c, gq, go, gu, gd, small = pl.pallas_call(
        partial(backward_kernel, dm, T, FC, plan_a, plan_b),
        out_shape=(
            sds((NP, D), BF16),
            sds((NT - NP, D), BF16),
            sds((NP, D), BF16),
            sds((NT - NP, D), BF16),
            sds((3, S, HC), F32),
            sds((S, HC), F32),
            sds((S, FC), F32),
            sds((S, FC), F32),
            sds((16, D), F32),
        ),
        in_specs=[pl.BlockSpec(memory_space=pltpu.SMEM)] + [vmem] * 10 + [any_] * 12,
        out_specs=(any_,) * 4 + (vmem, vmem, any_, vmem, vmem),
        scratch_shapes=[
            pltpu.VMEM((NT, D), F32),
            pltpu.VMEM((NT, D), F32),
            pltpu.VMEM((NT, D), F32),
            pltpu.VMEM((TP, D, HC), BF16),
            pltpu.VMEM((2, D, max(2 * T, 3 * HC)), BF16),
            pltpu.VMEM((NT, D), BF16),
            pltpu.VMEM((D, G * R), BF16),
            pltpu.VMEM((D, NT), BF16),
            pltpu.VMEM((PROMPT, PB), F32),
            pltpu.VMEM((dm.NX, 2 * dm.NCH), F32),
            pltpu.VMEM((2, R, 128), BF16),
            pltpu.VMEM((2, R, 128), BF16),
            pltpu.VMEM((G * R, D), BF16),
            pltpu.VMEM((G * R, D), BF16),
            pltpu.VMEM((NT, D), BF16),
            pltpu.VMEM((G * ctxs, PB, D), BF16),
            pltpu.VMEM((G, ctxs + 1, PB, D), BF16),
            pltpu.VMEM((NT - NP, D), BF16),
            pltpu.VMEM((max(NT, 2 * (NT - NP)), D), BF16),
            pltpu.VMEM((NT, D), BF16),
            pltpu.VMEM((NT, D), BF16),
            dma((4,)),
            dma((2, 2)),
            dma,
            dma((2, 2)),
            dma((2,)),
            dma,
            dma((2, 5)),
            dma,
            dma,
            dma((2,)),
            dma((2,)),
            dma((G * ctxs,)),
            dma((G * ctxs,)),
            dma((G, ctxs)),
            dma((G, ctxs + 1)),
            dma((G,)),
            dma((G,)),
            pltpu.VMEM((16, D), F32),
            pltpu.VMEM((16, D), F32),
            pltpu.VMEM((chips, 16, D), F32),
            pltpu.VMEM((2, 16, D), F32),
            pltpu.VMEM((ctxs, 16, D), F32),
            dma((1 + chips + ctxs,)),
            dma,
            dma((far,)),
            dma,
            dma((ctxs - 1,)),
        ]
        + Reduce.scratch(plan_a, chips, S, 2 * T)
        + Reduce.scratch(plan_b, chips, S, HC),
        compiler_params=params(collective_id=1, has_side_effects=True),
        name="backward",
    )(
        mix_weights,
        att,
        rows(own_p),
        rows(own_c),
        rows(cot_p),
        rows(cot_c),
        ln,
        q,
        lse,
        cos,
        sin,
        wm,
        k,
        v,
        nt,
        own_nt,
        wq,
        rows(prompt_embed),
        rows(cont_embed),
        prompt_earlier.reshape(3, NP, D),
        cont_earlier.reshape(3, NT - NP, D),
        rows(prompt_cot),
        rows(cont_cot),
    )
    results = (out_p, out_c, gin_p, gin_c, gq, go, gu, gd)
    shapes = tuple(sds(x.shape, x.dtype) for x in results)
    out = pl.pallas_call(
        partial(deliver_kernel, len(results)),
        out_shape=shapes + (sds((1, S), F32),) * 4 + (sds((1, 5), F32),),
        in_specs=[any_] * len(results) + [vmem],
        out_specs=(any_,) * len(results) + (vmem,) * 5,
        scratch_shapes=[pltpu.VMEM(x.shape, x.dtype) for x in results]
        + [dma((len(results),)), dma((len(results),)), pltpu.VMEM((2 * chips, 8, S), F32)],
        compiler_params=params(),
        name="deliver",
    )(*results, small)
    out_p, out_c, gin_p, gin_c, gq, go, gu, gd = out[:8]
    gains = [x.reshape(S) for x in out[8:12]]
    return (
        out_p.reshape(prompt_in.shape),
        out_c.reshape(cont_in.shape),
        gin_p.reshape(prompt_in.shape),
        gin_c.reshape(cont_in.shape),
        *gains,
        jnp.transpose(gq, (1, 0, 2)),
        go.T,
        gu,
        gd.T,
        out[12].reshape(5),
    )


def solution(mesh):
    tokens = P("dp", ("ctx", "tp"), None)
    conts = P("dp", "ctx", "tp", None)
    weights = (P("dp", None, "tp"), P("tp", "dp"), P("dp", "tp"), P("tp", "dp"))
    in_specs = (
        tokens,
        conts,
        tokens,
        conts,
        P(None, "dp", ("ctx", "tp"), None),
        P(None, "dp", "ctx", "tp", None),
        P("dp"),
        P("dp"),
        P("dp"),
        P("dp"),
        *weights,
        P(),
        tokens,
        conts,
    )
    out_specs = (
        tokens,
        conts,
        tokens,
        conts,
        P("dp"),
        P("dp"),
        P("dp"),
        P("dp"),
        *weights,
        P(),
    )
    return jax.shard_map(
        per_device, mesh=mesh, in_specs=in_specs, out_specs=out_specs, check_vma=False
    )
```

```python
from functools import partial

import jax
import jax.numpy as jnp
import numpy as np
from jax import lax
from jax.experimental import pallas as pl
from jax.experimental.pallas import tpu as pltpu
from jax.sharding import PartitionSpec as P

HD = 64
CL = 128
EPS = 1e-05
NEG = -1e30
F32 = jnp.float32
BF16 = jnp.bfloat16
VMEM_LIMIT = 67043328


def dot(a, b):
    return lax.dot_general(a, b, (((1,), (0,)), ((), ())), preferred_element_type=F32)


def dot_nt(a, b):
    return lax.dot_general(a, b, (((1,), (1,)), ((), ())), preferred_element_type=F32)


def norm_stats(x):
    mean = jnp.mean(x, axis=-1, keepdims=True)
    centered = x - mean
    var = jnp.mean(centered * centered, axis=-1, keepdims=True)
    scale = lax.rsqrt(var + EPS)
    return centered * scale, scale


def norm_back(grad, gain, hat, scale):
    gh = grad * gain
    return scale * (
        gh
        - jnp.mean(gh, axis=-1, keepdims=True)
        - hat * jnp.mean(gh * hat, axis=-1, keepdims=True)
    )


def swap_halves(x):
    second = lax.broadcasted_iota(jnp.int32, x.shape, 1) % HD >= HD // 2
    return jnp.where(second, pltpu.roll(x, 32, 1), pltpu.roll(x, 96, 1))


def rotate(x, cos, sin):
    return x * cos + swap_halves(x) * sin


def rotate_back(x, cos, sin):
    return x * cos - swap_halves(x) * sin


def lane_pick(shape, low):
    lanes = lax.broadcasted_iota(jnp.int32, shape, 1)
    return lanes < HD if low else lanes >= HD


def sublane_pick(shape, low):
    rows = lax.broadcasted_iota(jnp.int32, shape, 0)
    return rows < HD if low else rows >= HD


def transpose(x):
    return x.astype(F32).T.astype(x.dtype)


class Dims:
    def __init__(self, groups, prompt, pb, nc, ch, d, heads):
        self.G, self.P, self.PB, self.NC, self.CH, self.D = groups, prompt, pb, nc, ch, d
        self.NCH = nc * ch
        self.R = prompt + nc * CL
        self.NX = nc * CL
        self.NR = pb + self.NCH
        self.NP = groups * pb
        self.NT = groups * self.NR
        self.PAIRS = heads // 2
        self.COLS = 2 * self.NR


MESH = pl.DeviceIdType.MESH


def half_index():
    return lax.axis_index("dp") % 2


def block_index():
    return lax.axis_index("ctx") * 2 + half_index()


class Peers:
    def __init__(self):
        self.ctxs = lax.axis_size("ctx")
        self.chips = lax.axis_size("dp") // 2
        self.tps = lax.axis_size("tp")
        self.dp = lax.axis_index("dp")
        self.ctx = lax.axis_index("ctx")
        self.tp = lax.axis_index("tp")
        self.core = self.dp % 2
        self.chip = self.dp // 2

    def at(self, dp=None, ctx=None, tp=None):
        return {
            "dp": self.dp if dp is None else dp,
            "ctx": self.ctx if ctx is None else ctx,
            "tp": self.tp if tp is None else tp,
        }

    def across(self):
        return self.at(tp=1 - self.tp)

    def mate(self):
        return self.at(dp=self.chip * 2 + 1 - self.core)

    def chip_after(self, k):
        return lax.rem(self.chip + k, self.chips)

    def chip_before(self, k):
        return lax.rem(self.chip + self.chips - k, self.chips)

    def row(self, k):
        return self.at(dp=self.chip_after(k) * 2 + self.core)

    def ctx_after(self, k):
        return lax.rem(self.ctx + k, self.ctxs)

    def ctx_before(self, k):
        return lax.rem(self.ctx + self.ctxs - k, self.ctxs)

    def plane(self, k):
        return self.at(ctx=self.ctx_after(k))

    def partner(self):
        return self.at(dp=self.chip * 2 + self.tp, tp=self.core)

    def greet(self, trades=False):
        barrier = pltpu.get_barrier_semaphore()
        peers = [self.across(), self.mate()]
        peers += [self.row(k) for k in range(1, self.chips)]
        peers += [self.plane(k) for k in range(1, self.ctxs)]
        for peer in peers:
            pl.semaphore_signal(barrier, inc=1, device_id=peer, device_id_type=MESH)
        count = len(peers)
        if trades:
            away = self.core != self.tp

            @pl.when(away)
            def _():
                pl.semaphore_signal(
                    barrier, inc=1, device_id=self.partner(), device_id_type=MESH
                )

            count += jnp.where(away, 1, 0)
        pl.semaphore_wait(barrier, count)


def send(src, dst, send_sem, recv_sem, device):
    copy = pltpu.make_async_remote_copy(
        src_ref=src,
        dst_ref=dst,
        send_sem=send_sem,
        recv_sem=recv_sem,
        device_id=device,
        device_id_type=MESH,
    )
    copy.start()
    return copy


def arrived(ref, sem, peers):
    pltpu.make_async_remote_copy(
        src_ref=ref,
        dst_ref=ref,
        send_sem=sem,
        recv_sem=sem,
        device_id=peers.mate(),
        device_id_type=MESH,
    ).wait_recv()


class WeightGather:
    def __init__(self, peers, shard, full, left, sends, across, rows, mate):
        self.p, self.shard, self.full, self.left = peers, shard, full, left
        self.sends, self.across, self.rows, self.from_mate = sends, across, rows, mate
        self.copies = []
        self.size, self.cols = shard.shape

    @staticmethod
    def semaphores(chips):
        far = chips - 1
        return [
            pltpu.SemaphoreType.DMA((3 + 6 * far,)),
            pltpu.SemaphoreType.DMA((chips,)),
            pltpu.SemaphoreType.DMA((2, max(far, 1))),
            pltpu.SemaphoreType.DMA((2, chips)),
        ]

    def piece(self, tp, dp, cols=slice(None)):
        rows = pl.ds(pl.multiple_of(dp * self.size, 16), self.size)
        if cols == slice(None):
            return self.full.at[tp, rows, :]
        return self.full.at[tp, rows, pl.ds(cols.start, cols.stop - cols.start)]

    def go(self, src, dst, recv_sem, device):
        self.copies.append(send(src, dst, self.sends.at[len(self.copies)], recv_sem, device))

    def start(self):
        p = self.p
        self.go(self.shard, self.piece(p.tp, p.dp), self.across.at[0], p.across())
        for k in range(1, p.chips):
            self.go(self.shard, self.piece(p.tp, p.dp), self.rows.at[0, k - 1], p.row(k))
        self.go(self.shard, self.piece(p.tp, p.dp), self.from_mate.at[0, 0], p.mate())

    def relay_across(self):
        p = self.p
        got = self.piece(1 - p.tp, p.dp)
        arrived(got, self.across.at[0], p)
        part = self.piece(1 - p.tp, p.dp, slice(0, self.left))
        for k in range(1, p.chips):
            self.go(part, part, self.rows.at[1, k - 1], p.row(k))
        self.go(got, got, self.from_mate.at[1, 0], p.mate())

    def relay_rows(self):
        p = self.p
        for k in range(1, p.chips):
            dp = p.chip_before(k) * 2 + p.core
            got = self.piece(p.tp, dp)
            arrived(got, self.rows.at[0, k - 1], p)
            if self.left < self.cols:
                part = self.piece(p.tp, dp, slice(self.left, self.cols))
                self.go(part, part, self.across.at[k], p.across())
            self.go(got, got, self.from_mate.at[0, k], p.mate())

    def relay_last(self):
        p = self.p
        for k in range(1, p.chips):
            dp = p.chip_before(k) * 2 + p.core
            arrived(self.piece(1 - p.tp, dp, slice(0, self.left)), self.rows.at[1, k - 1], p)
            if self.left < self.cols:
                part = self.piece(1 - p.tp, dp, slice(self.left, self.cols))
                arrived(part, self.across.at[k], p)
            got = self.piece(1 - p.tp, dp)
            self.go(got, got, self.from_mate.at[1, k], p.mate())

    def finish(self):
        p = self.p
        for part in range(2):
            tp = p.tp if part == 0 else 1 - p.tp
            for k in range(p.chips):
                dp = p.chip_before(k) * 2 + 1 - p.core
                arrived(self.piece(tp, dp), self.from_mate.at[part, k], p)

    def drain(self):
        for copy in self.copies:
            copy.wait_send()


def twice(x):
    return jnp.concatenate([x, x], axis=1)


def fill_masks(dm, maskp, maskx):
    block = block_index()
    keys = lax.broadcasted_iota(jnp.int32, maskp.shape, 0)
    cols = lax.broadcasted_iota(jnp.int32, maskp.shape, 1) % dm.PB
    maskp[...] = jnp.where(keys <= cols + block * dm.PB, 0.0, NEG)
    keys = lax.broadcasted_iota(jnp.int32, maskx.shape, 0)
    cols = lax.broadcasted_iota(jnp.int32, maskx.shape, 1) % dm.NCH
    seen = (keys // CL == cols // dm.CH) & (
        keys % CL <= cols % dm.CH + half_index() * dm.CH
    )
    maskx[...] = jnp.where(seen, 0.0, NEG)


def heads_columns(a, b):
    lo_a, lo_b = sublane_pick(a.shape, True), sublane_pick(b.shape, True)
    zero_a, zero_b = jnp.zeros_like(a), jnp.zeros_like(b)
    return jnp.concatenate(
        [
            jnp.where(lo_a, a, zero_a),
            jnp.where(lo_a, zero_a, a),
            jnp.where(lo_b, b, zero_b),
            jnp.where(lo_b, zero_b, b),
        ],
        axis=1,
    )


def heads_rows(a, b):
    lo_a, lo_b = lane_pick(a.shape, True), lane_pick(b.shape, True)
    zero_a, zero_b = jnp.zeros_like(a), jnp.zeros_like(b)
    return jnp.concatenate(
        [
            jnp.where(lo_a, a, zero_a),
            jnp.where(lo_a, zero_a, a),
            jnp.where(lo_b, b, zero_b),
            jnp.where(lo_b, zero_b, b),
        ],
        axis=0,
    )


def forward_kernel(
    dm,
    left,
    prompt,
    cont,
    cos_few,
    sin_few,
    wq,
    wm,
    cot_p,
    cot_c,
    q_out,
    att_out,
    lse_out,
    ln_out,
    cos,
    sin,
    nt_hbm,
    own_nt_hbm,
    k_hbm,
    v_hbm,
    w_hbm,
    wm_out,
    own_p_hbm,
    own_c_hbm,
    cot_p_out,
    cot_c_out,
    nt_out,
    own_out,
    k_out,
    v_out,
    maskp,
    maskx,
    sbuf,
    all_rows,
    own_rows,
    xp,
    xc,
    w,
    put_sem,
    trade_send,
    trade_recv,
    x_send,
    x_plane,
    x_mate,
    c_send,
    c_mate,
    own_sem,
    *sems,
):
    G, R, PB, NCH, D, NP, NT = dm.G, dm.R, dm.PB, dm.NCH, dm.D, dm.NP, dm.NT
    NC, CH = dm.NC, dm.CH
    HC = (w.shape[2] - 128) // 3
    TP = w.shape[0]
    p = Peers()
    block = block_index()
    gq = WeightGather(p, wq, w, wq.shape[1] // 256 * 128, *sems[:4])
    gm = WeightGather(p, wm, wm_out, left, *sems[4:])
    size = wq.shape[0]
    mine = pl.ds(pl.multiple_of(p.dp * size, 16), size)

    landing = [xp.at[p.ctx * 2 + p.tp], xc.at[p.tp], cot_p_out, cot_c_out]

    def moved(i):
        src = [prompt, cont, cot_p, cot_c][i]
        return pltpu.make_async_remote_copy(
            src_ref=src,
            dst_ref=landing[i],
            send_sem=trade_send.at[i],
            recv_sem=trade_recv.at[i],
            device_id=p.partner(),
            device_id_type=MESH,
        )

    def kept(i):
        return pltpu.make_async_copy([prompt, cont, cot_p, cot_c][i], landing[i], trade_send.at[i])

    moves = p.core != p.tp

    def trade(i):
        @pl.when(moves)
        def _():
            moved(i).start()

        @pl.when(jnp.logical_not(moves))
        def _():
            kept(i).start()

    def traded(i):
        @pl.when(moves)
        def _():
            moved(i).wait_recv()

        @pl.when(jnp.logical_not(moves))
        def _():
            kept(i).wait()

    local = [
        pltpu.make_async_copy(wq, w.at[p.tp, mine, :], own_sem.at[0]),
        pltpu.make_async_copy(wm, wm_out.at[p.tp, mine, :], own_sem.at[1]),
    ]
    for copy in local:
        copy.start()
    p.greet(trades=True)
    trade(0)
    gq.start()
    traded(0)
    own = xp.at[block]
    sent = []
    for k in range(1, p.ctxs):
        sent.append(send(own, own, x_send.at[k - 1], x_plane.at[k - 1], p.plane(k)))
    sent.append(send(own, own, x_send.at[p.ctxs - 1], x_mate.at[0], p.mate()))
    fill_masks(dm, maskp, maskx)
    second = lax.broadcasted_iota(jnp.int32, (128, 128), 1) % HD >= HD // 2
    for i in range(0, dm.P + CL, 128):
        part = cos_few[:, i : i + 128]
        cos[i : i + 128, :] = jnp.concatenate([part] * 4, axis=0).T
        part = sin_few[:, i : i + 128]
        part = jnp.concatenate([part] * 4, axis=0).T
        sin[i : i + 128, :] = jnp.where(second, part, -part)
    gq.relay_rows()
    gq.relay_across()
    trade(1)
    gm.start()
    gq.relay_last()
    traded(1)
    sent.append(send(xc.at[p.core], xc.at[p.core], c_send, c_mate, p.mate()))
    trade(2)
    trade(3)
    gq.finish()
    local[0].wait()
    puts = [
        pltpu.make_async_copy(w, w_hbm, put_sem.at[0]),
        pltpu.make_async_copy(xp.at[block], own_p_hbm, put_sem.at[1]),
        pltpu.make_async_copy(xc.at[p.core], own_c_hbm, put_sem.at[2]),
    ]
    for put in puts:
        put.start()
    ln = w[0, :, 3 * HC :].astype(F32).T[:8, :]
    ln_out[...] = ln
    gain, bias = ln[0:1, :], ln[1:2, :]

    def normed(x):
        hat, _ = norm_stats(x.astype(F32))
        return (hat * gain + bias).astype(BF16)

    def turned(x, table):
        rows = x.shape[0]
        return rotate(x, cos[pl.ds(table, rows), :], sin[pl.ds(table, rows), :])

    x = jnp.concatenate([xp[block].reshape(NP, D), xc[p.core].reshape(NT - NP, D)], axis=0)
    n = normed(x)
    own_rows[...] = n
    places = [(g * PB, PB, pl.multiple_of(block * PB, PB)) for g in range(G)]
    places += [
        (NP + i * CH, CH, pl.multiple_of(dm.P + p.core * CH, CH)) for i in range(G * NC)
    ]
    for t in range(TP):
        qq = dot(n, w[t, :, :HC])
        for first, count, table in places:
            for j in range(HC // 128):
                tile = turned(qq[first : first + count, j * 128 : (j + 1) * 128], table).astype(BF16)
                q_out[first : first + count, t * HC + j * 128 : t * HC + (j + 1) * 128] = (
                    tile.astype(F32) * 0.125
                ).astype(BF16)
    own_out[...] = transpose(own_rows[...])

    def keys_values(x, places):
        n = normed(x)
        for first, count, g, row, table in places:
            all_rows[pl.ds(pl.multiple_of(g * R + row, 16), count), :] = n[first : first + count]
        for t in range(TP):
            kk = dot(n, w[t, :, HC : 2 * HC])
            for first, count, g, row, table in places:
                for j in range(HC // 128):
                    tile = turned(kk[first : first + count, j * 128 : (j + 1) * 128], table)
                    k_out[g, pl.ds(row, count), t * HC + j * 128 : t * HC + (j + 1) * 128] = tile.astype(BF16)
            vv = dot(n, w[t, :, 2 * HC : 3 * HC]).astype(BF16)
            for first, count, g, row, table in places:
                v_out[g, pl.ds(row, count), t * HC : (t + 1) * HC] = vv[first : first + count]

    arrived(xc.at[1 - p.core], c_mate, p)
    x = [xc[e, g, c] for g in range(G) for c in range(NC) for e in range(2)]
    keys_values(
        jnp.concatenate(x, axis=0),
        [((g * NC + c) * CL, CL, g, dm.P + c * CL, dm.P) for g in range(G) for c in range(NC)],
    )

    def relay(k):
        b = p.ctx_before(k) * 2 + p.core
        return pltpu.make_async_remote_copy(
            src_ref=xp.at[b],
            dst_ref=xp.at[b],
            send_sem=x_send.at[p.ctxs + k - 1],
            recv_sem=x_mate.at[k],
            device_id=p.mate(),
            device_id_type=MESH,
        )

    def plane(k, carry):
        c = p.ctx_before(k)

        @pl.when(k > 0)
        def _():
            arrived(xp.at[c * 2 + p.core], x_plane.at[k - 1], p)
            relay(k).start()

        arrived(xp.at[c * 2 + 1 - p.core], x_mate.at[k], p)
        x = xp[pl.ds(c * 2, 2)].reshape(2 * NP, D)
        places = []
        for e in range(2):
            row = pl.multiple_of((c * 2 + e) * PB, PB)
            places += [((e * G + g) * PB, PB, g, row, row) for g in range(G)]
        keys_values(x, places)
        return carry

    lax.fori_loop(0, p.ctxs, plane, 0)
    puts += [
        pltpu.make_async_copy(k_out, k_hbm, put_sem.at[3]),
        pltpu.make_async_copy(v_out, v_hbm, put_sem.at[4]),
    ]
    for put in puts[3:]:
        put.start()

    def turn(i, carry):
        rows = pl.ds(pl.multiple_of(i * 256, 256), 256)
        nt_out[:, rows] = transpose(all_rows[rows, :])
        return carry

    lax.fori_loop(0, G * R // 256, turn, 0)
    puts += [
        pltpu.make_async_copy(nt_out, nt_hbm, put_sem.at[5]),
        pltpu.make_async_copy(own_out, own_nt_hbm, put_sem.at[6]),
    ]
    for put in puts[5:]:
        put.start()
    gm.relay_across()
    gm.relay_rows()

    TILE = 256
    tiles = dm.P // TILE

    def attend(i, carry):
        g, pair = i // dm.PAIRS, i % dm.PAIRS
        lanes = pl.ds(pl.multiple_of(pair * 128, 128), 128)
        qp = q_out[pl.ds(pl.multiple_of(g * PB, PB), PB), lanes]
        qc = q_out[pl.ds(pl.multiple_of(dm.NP + g * NCH, NCH), NCH), lanes]
        qt = heads_columns(transpose(qp), transpose(qc))
        top = None
        for j in range(tiles):
            s = dot(k_out[g, j * TILE : (j + 1) * TILE, lanes], qt)
            sbuf[j * TILE : (j + 1) * TILE, : 2 * PB] = (
                s[:, : 2 * PB] + twice(maskp[j * TILE : (j + 1) * TILE, :])
            )
            sbuf[j * TILE : (j + 1) * TILE, 2 * PB :] = s[:, 2 * PB :]
            here = jnp.max(sbuf[j * TILE : (j + 1) * TILE, :], axis=0, keepdims=True)
            top = here if top is None else jnp.maximum(top, here)
        sx = dot(k_out[g, dm.P :, lanes], qt[:, 2 * PB :]) + maskx[...]
        topx = jnp.max(sx, axis=0, keepdims=True)
        top = jnp.concatenate([top[:, : 2 * PB], jnp.maximum(top[:, 2 * PB :], topx)], axis=1)
        total, acc = None, None
        for j in range(tiles):
            e = jnp.exp(sbuf[j * TILE : (j + 1) * TILE, :] - top)
            here = jnp.sum(e, axis=0, keepdims=True)
            vt = transpose(v_out[g, j * TILE : (j + 1) * TILE, lanes])
            part = dot(vt, e.astype(BF16))
            total = here if total is None else total + here
            acc = part if acc is None else acc + part
        ex = jnp.exp(sx - top[:, 2 * PB :])
        partx = dot(transpose(v_out[g, dm.P :, lanes]), ex.astype(BF16))
        totalx = jnp.sum(ex, axis=0, keepdims=True)
        total = jnp.concatenate([total[:, : 2 * PB], total[:, 2 * PB :] + totalx], axis=1)
        acc_p = acc[:, : 2 * PB] / total[:, : 2 * PB]
        acc_c = (acc[:, 2 * PB :] + partx) / total[:, 2 * PB :]
        lse_out[i] = top + jnp.log(total)
        outp = jnp.where(sublane_pick((128, PB), True), acc_p[:, :PB], acc_p[:, PB:])
        outc = jnp.where(sublane_pick((128, NCH), True), acc_c[:, :NCH], acc_c[:, NCH:])
        att_out[pl.ds(pl.multiple_of(g * PB, PB), PB), lanes] = outp.T.astype(BF16)
        att_out[pl.ds(pl.multiple_of(dm.NP + g * NCH, NCH), NCH), lanes] = outc.T.astype(BF16)
        return carry

    lax.fori_loop(0, G * dm.PAIRS, attend, 0)
    gm.relay_last()
    gm.finish()
    gq.drain()
    gm.drain()
    for copy in sent:
        copy.wait_send()
    for k in range(1, p.ctxs):
        relay(k).wait_send()
    local[1].wait()
    for i in (2, 3):
        traded(i)

    @pl.when(moves)
    def _():
        for i in range(4):
            moved(i).wait_send()

    for put in puts:
        put.wait()


class Reduce:
    REFS = 13

    def __init__(self, p, cross_first, refs):
        self.p, self.n, self.cross_first = p, len(cross_first), cross_first
        self.mine, self.got, self.row, self.acr, self.zin = refs[:5]
        self.sc, self.rc, self.sy, self.ry, self.sx, self.rx, self.sz, self.rz = refs[5:13]
        mid = p.ctxs // 2
        self.centre = (p.ctx == mid - 1) | (p.ctx == mid)
        self.outer = (p.ctx > 0) & (p.ctx < p.ctxs - 1)
        step = jnp.where(p.ctx < mid, 1, -1)
        self.inner_at = p.ctx + step
        self.outer_at = jnp.clip(p.ctx - step, 0, p.ctxs - 1)

    @staticmethod
    def scratch(cross_first, chips, size, width):
        n = len(cross_first)
        dma = pltpu.SemaphoreType.DMA
        far = max(chips - 1, 1)
        rows = n + sum(1 for c in cross_first if not c)
        parts = sum(chips if c else 1 for c in cross_first)
        return [
            pltpu.VMEM((2, chips * 2 * size, width), BF16),
            pltpu.VMEM((2 * n, chips, size, width), BF16),
            pltpu.VMEM((rows, far, size, width), BF16),
            pltpu.VMEM((parts, size, width), BF16),
            pltpu.VMEM((n, 2, size, width), BF16),
            dma((2 * n, chips)),
            dma((2 * n, chips)),
            dma((2 * n, far)),
            dma((2 * n, far)),
            dma((n,)),
            dma((n,)),
            dma((n, 2)),
            dma((n, 2)),
        ]

    def copy(self, src, dst, send_sem, recv_sem, device):
        return pltpu.make_async_remote_copy(
            src_ref=src,
            dst_ref=dst,
            send_sem=send_sem,
            recv_sem=recv_sem,
            device_id=device,
            device_id_type=MESH,
        )

    def slot(self, whose, j):
        return 0 if whose == "other" else 1

    def crosses(self, i):
        return self.cross_first[i % self.n]

    def travels(self, i):
        return i >= self.n or not self.crosses(i)

    def mine_of(self, y, core):
        size = self.got.shape[2]
        return pl.ds(pl.multiple_of((2 * y + core) * size, 16), size)

    def by_core(self, i, slot, y):
        p = self.p
        return self.copy(
            self.mine.at[slot, self.mine_of(y, 1 - p.core), :],
            self.got.at[i, y],
            self.sc.at[i, y],
            self.rc.at[i, y],
            p.mate(),
        )

    def row_slot(self, i):
        return sum(1 for e in range(i) if self.travels(e))

    def by_row(self, i, k):
        p = self.p
        return self.copy(
            self.got.at[i, p.chip_after(k)],
            self.row.at[self.row_slot(i), k - 1],
            self.sy.at[i, k - 1],
            self.ry.at[i, k - 1],
            p.row(k),
        )

    def by_tp(self, j):
        p = self.p
        slot = self.acr_slot(j)
        if self.crosses(j):
            src, dst = self.got.at[j], self.acr.at[pl.ds(slot, p.chips)]
        else:
            src, dst = self.got.at[j, p.chip], self.acr.at[slot]
        return self.copy(src, dst, self.sx.at[j], self.rx.at[j], p.across())

    def acr_slot(self, j):
        return sum(self.p.chips if c else 1 for c in self.cross_first[:j])

    def inward(self, j):
        slot = jnp.where(self.centre, 1, 0)
        return self.copy(
            self.got.at[self.n + j, self.p.chip],
            self.zin.at[j, slot],
            self.sz.at[j, 0],
            self.rz.at[j, slot],
            self.p.at(ctx=self.inner_at),
        )

    def outward(self, j):
        return self.copy(
            self.got.at[self.n + j, self.p.chip],
            self.zin.at[j, 1],
            self.sz.at[j, 1],
            self.rz.at[j, 1],
            self.p.at(ctx=self.outer_at),
        )

    def add(self, i, y, other):
        self.got[i, y] = (self.got[i, y].astype(F32) + other.astype(F32)).astype(BF16)

    def cores_send(self, i, slot):
        for y in range(self.p.chips):
            self.by_core(i, slot, y).start()

    def cores_sent(self, i, slot):
        for y in range(self.p.chips):
            self.by_core(i, slot, y).wait_send()

    def rows_send(self, i):
        for k in range(1, self.p.chips):
            self.by_row(i, k).start()

    def cores_sum(self, i, slot):
        p = self.p
        for y in range(p.chips):
            self.by_core(i, slot, y).wait_recv()
            self.add(i, y, self.mine[slot, self.mine_of(y, p.core), :])
        if not self.crosses(i):
            self.rows_send(i)
        elif i < self.n:
            self.by_tp(i).start()

    def cross_sum(self, j):
        self.by_tp(j).wait_recv()
        for y in range(self.p.chips):
            self.add(self.n + j, y, self.acr[self.acr_slot(j) + y])
        self.rows_send(self.n + j)

    def rows_sum(self, i):
        p = self.p
        for k in range(1, p.chips):
            self.by_row(i, k).wait_recv()
            self.add(i, p.chip, self.row[self.row_slot(i), k - 1])
        if i < self.n:
            self.by_tp(i).start()
            return
        j = i - self.n
        if not self.crosses(i):
            self.by_tp(j).wait_recv()
            self.add(i, p.chip, self.acr[self.acr_slot(j)])

        @pl.when(jnp.logical_not(self.outer))
        def _():
            self.inward(j).start()

    def ctx_in(self, j):
        @pl.when(self.outer)
        def _():
            pltpu.make_async_copy(self.zin.at[j, 0], self.zin.at[j, 0], self.rz.at[j, 0]).wait()
            self.add(self.n + j, self.p.chip, self.zin[j, 0])
            self.inward(j).start()

    def ctx_mid(self, j):
        @pl.when(self.centre)
        def _():
            self.from_inner(j)
            self.add(self.n + j, self.p.chip, self.zin[j, 1])

            @pl.when(self.outer)
            def _():
                self.outward(j).start()

    def ctx_end(self, j):
        @pl.when(jnp.logical_not(self.centre))
        def _():
            self.from_inner(j)
            self.got[self.n + j, self.p.chip] = self.zin[j, 1]

            @pl.when(self.outer)
            def _():
                self.outward(j).start()

    def from_inner(self, j):
        pltpu.make_async_copy(self.zin.at[j, 1], self.zin.at[j, 1], self.rz.at[j, 1]).wait()
        self.inward(j).wait_send()

    def result(self, j):
        return self.got[self.n + j, self.p.chip].astype(F32)

    def drain(self):
        p = self.p
        for i in range(2 * self.n):
            if self.travels(i):
                for k in range(1, p.chips):
                    self.by_row(i, k).wait_send()
        for j in range(self.n):
            self.by_tp(j).wait_send()

            @pl.when(self.outer)
            def _():
                self.outward(j).wait_send()


class SmallSum:
    def __init__(self, p, sm, near, rows, across, planes, ss, rc, ry, rx, rz):
        self.p, self.sm, self.near, self.rows, self.across, self.planes = p, sm, near, rows, across, planes
        self.ss, self.rc, self.ry, self.rx, self.rz = ss, rc, ry, rx, rz

    def copy(self, index, src, dst, recv_sem, device):
        return pltpu.make_async_remote_copy(
            src_ref=src,
            dst_ref=dst,
            send_sem=self.ss.at[index],
            recv_sem=recv_sem,
            device_id=device,
            device_id_type=MESH,
        )

    def to_mate(self):
        return self.copy(0, self.sm, self.near, self.rc, self.p.mate())

    def to_row(self, k):
        mine = self.rows.at[self.p.chip]
        return self.copy(1 + k, mine, mine, self.ry.at[k - 1], self.p.row(k))

    def to_across(self):
        return self.copy(1, self.across.at[0], self.across.at[1], self.rx, self.p.across())

    def to_plane(self, k):
        mine = self.planes.at[self.p.ctx]
        return self.copy(self.p.chips + k, mine, mine, self.rz.at[k - 1], self.p.plane(k))

    def step(self, which):
        p = self.p
        if which == 0:
            self.to_mate().start()
        elif which == 1:
            self.to_mate().wait_recv()
            self.rows[p.chip] = self.sm[...] + self.near[...]
            for k in range(1, p.chips):
                self.to_row(k).start()
        elif which == 2:
            for k in range(1, p.chips):
                arrived(self.rows.at[p.chip_before(k)], self.ry.at[k - 1], p)
            total = self.rows[0]
            for y in range(1, p.chips):
                total += self.rows[y]
            self.across[0] = total
            self.to_across().start()
        elif which == 3:
            self.to_across().wait_recv()
            self.planes[p.ctx] = self.across[0] + self.across[1]
            for k in range(1, p.ctxs):
                self.to_plane(k).start()

    def result(self):
        p = self.p
        for k in range(1, p.ctxs):
            arrived(self.planes.at[p.ctx_before(k)], self.rz.at[k - 1], p)
        total = self.planes[0]
        for z in range(1, p.ctxs):
            total += self.planes[z]
        self.to_mate().wait_send()
        self.to_across().wait_send()
        for k in range(1, p.chips):
            self.to_row(k).wait_send()
        for k in range(1, p.ctxs):
            self.to_plane(k).wait_send()
        return total


SMALL_AT = {2: 1, 5: 2, 8: 3}
PLAN = {
    ("m", 1): [("a", "cores_sum", "other", 0)],
    ("m", 3): [("a", "cores_sum", "own", 0)],
    ("m", 4): [("a", "cores_sum", "other", 1), ("a", "rows_sum", "other", 0)],
    ("m", 5): [("a", "cores_sum", "own", 1)],
    ("e", 0): [("a", "cores_sum", "other", 2)],
    ("a", 0): [("a", "rows_sum", "own", 0)],
    ("a", 1): [("a", "cores_sum", "own", 2)],
    ("p", 0, 0): [("a", "ctx_in", "own", 0)],
    ("p", 0, 1): [("b", "cores_sum", "own", 0), ("b", "cores_sum", "other", 0)],
    ("p", 0, 3): [("a", "cross_sum", "own", 2), ("a", "rows_sum", "other", 1)],
    ("a", 7): [("a", "ctx_mid", "own", 0)],
    ("a", 8): [("a", "rows_sum", "own", 2), ("hop", 0, 0), ("b", "cores_sum", "other", 1)],
    ("a", 9): [("a", "rows_sum", "own", 1), ("b", "cores_sum", "own", 1), ("b", "cores_sum", "other", 2), ("hop", 0, 1)],
    ("a", 10): [("a", "ctx_in", "own", 2), ("b", "cross_sum", "own", 0)],
    ("a", 11): [("b", "cores_sum", "own", 2), ("hop", 0, 2)],
    ("p", 1, 1): [("b", "cores_sum", "other", 3), ("a", "ctx_in", "own", 1), ("b", "cross_sum", "own", 1)],
    ("p", 1, 3): [("a", "ctx_mid", "own", 2)],
    ("t", 0): [("hop", 1, 0)],
    ("t", 2): [("b", "rows_sum", "other", 3), ("a", "ctx_mid", "own", 1)],
    ("t", 3): [("b", "cross_sum", "own", 2), ("b", "rows_sum", "own", 0), ("b", "cores_sum", "own", 3)],
    ("t", 4): [("b", "rows_sum", "own", 1)],
    ("t", 5): [("hop", 1, 1)],
    ("t", 6): [("b", "ctx_in", "own", 0), ("b", "rows_sum", "own", 3)],
    ("t", 8): [("b", "ctx_in", "own", 1)],
    ("t", 9): [("hop", 1, 2), ("b", "ctx_in", "own", 3), ("b", "rows_sum", "own", 2)],
    ("t", 10): [("b", "ctx_mid", "own", 0)],
    ("t", 11): [("b", "ctx_in", "own", 2)],
    ("t", 14): [("b", "ctx_mid", "own", 1), ("b", "ctx_mid", "own", 3)],
    ("t", 18): [("b", "ctx_mid", "own", 2)],
}


def schedule(ra, rb, on, planes, hop):
    for stage, steps in PLAN.items():
        if stage[0] == "p":
            stage = ("p", stage[1] * planes + stage[2])
        for step in steps:
            if step[0] == "hop":
                on(stage, partial(hop, step[1], step[2]))
                continue
            name, what, whose, j = step
            r = ra if name == "a" else rb
            if what == "cores_sum":
                on(stage, partial(r.cores_sum, j if whose == "other" else r.n + j, r.slot(whose, j)))
            elif what == "rows_sum":
                on(stage, partial(r.rows_sum, j if whose == "other" else r.n + j))
            else:
                on(stage, partial(getattr(r, what), j))


def backward_kernel(
    dm,
    T,
    FC,
    plan_a,
    plan_b,
    mix,
    att,
    own_p,
    own_c,
    cot_p,
    cot_c,
    ln,
    q,
    lse,
    cos,
    sin,
    wm,
    k_hbm,
    v_hbm,
    nt_hbm,
    own_nt_hbm,
    wq_hbm,
    home_arrays_p,
    home_arrays_c,
    early_p,
    early_c,
    home_cot_p,
    home_cot_c,
    out_p,
    out_c,
    gin_p,
    gin_c,
    gq_out,
    go_out,
    gu_out,
    gd_out,
    small_out,
    resid,
    blk,
    gh,
    wo,
    ring,
    gatt,
    nt,
    own_nt,
    maskp,
    maskx,
    kbuf,
    vbuf,
    dk,
    dv,
    dq,
    dxm,
    dxz,
    dxcm,
    blk_away,
    blk_home,
    gin_home,
    put_sem,
    ring_sem,
    wo_sem,
    kv_sem,
    nt_sem,
    wq_sem,
    home_sem,
    b_send,
    b_recv,
    g_send,
    g_recv,
    m_send,
    m_recv,
    z_send,
    z_recv,
    c_send,
    c_recv,
    sm,
    sm_near,
    sm_rows,
    sm_across,
    sm_planes,
    sm_ss,
    sm_rc,
    sm_ry,
    sm_rx,
    sm_rz,
    *refs,
):
    G, R, PB, NCH, D, NX, NP, NT = dm.G, dm.R, dm.PB, dm.NCH, dm.D, dm.NX, dm.NP, dm.NT
    TP, HC = wo.shape[0], wo.shape[2]
    PT = dm.PAIRS // TP
    p = Peers()
    n_a, NB = len(plan_a), len(plan_b)
    ra = Reduce(p, plan_a, refs[: Reduce.REFS])
    rb = Reduce(p, plan_b, refs[Reduce.REFS :])
    block = block_index()
    TILE = 256
    tiles = dm.P // TILE
    chips = p.chips
    S = D // (2 * chips)

    def begin(copies):
        for copy in copies:
            copy.start()

    def ready(copies):
        for copy in copies:
            copy.wait()

    def load_tile(i, slot):
        t = jnp.where(lax.rem(i, 2) == 0, 1 - p.tp, p.tp)
        first = pl.multiple_of(HC + i // 2 * T, 128)
        return [
            pltpu.make_async_copy(
                wm.at[t, :, pl.ds(first, T)], ring.at[slot, :, pl.ds(0, T)], ring_sem.at[0, slot]
            ),
            pltpu.make_async_copy(
                wm.at[t, :, pl.ds(first + FC, T)], ring.at[slot, :, pl.ds(T, T)], ring_sem.at[1, slot]
            ),
        ]

    def pair_at(it):
        turn = it % dm.PAIRS
        return jnp.where(turn % 2 == 0, 1 - p.tp, p.tp) * PT + turn // 2

    def load_kv(it, slot):
        pair, g = pair_at(it), it // dm.PAIRS
        lanes = pl.ds(pl.multiple_of(pair * 128, 128), 128)
        return [
            pltpu.make_async_copy(k_hbm.at[g, :, lanes], kbuf.at[slot], kv_sem.at[0, slot]),
            pltpu.make_async_copy(v_hbm.at[g, :, lanes], vbuf.at[slot], kv_sem.at[1, slot]),
        ]

    wo_load = pltpu.make_async_copy(wm.at[:, :, pl.ds(0, HC)], wo, wo_sem)
    wo_load.start()
    begin(load_tile(0, 0))
    begin(load_kv(0, 0))
    p.greet(trades=True)
    fill_masks(dm, maskp, maskx)
    gain_two, bias_two = ln[2:3, :], ln[3:4, :]

    hn, gd = slice(0, NT), slice(NT, 2 * NT)
    STEP = 128

    def by_rows(step):
        def prompt_part(i, carry):
            rows = pl.ds(pl.multiple_of(i * STEP, STEP), STEP)
            step(own_p[rows, :], cot_p[rows, :], i * STEP)
            return carry

        def cont_part(i, carry):
            rows = pl.ds(pl.multiple_of(i * STEP, STEP), STEP)
            step(own_c[rows, :], cot_c[rows, :], NP + i * STEP)
            return carry

        lax.fori_loop(0, NP // STEP, prompt_part, 0)
        lax.fori_loop(0, (NT - NP) // STEP, cont_part, 0)

    def shifted(first, row):
        return pl.ds(pl.multiple_of(first + row, STEP), STEP)

    wo_load.wait()

    def enter(x, cot, row):
        rows = shifted(0, row)
        r = x.astype(F32)
        for t in range(TP):
            r += dot_nt(att[rows, t * HC : (t + 1) * HC], wo[t])
        resid[rows, :] = r
        blk[rows, :] = r
        h, _ = norm_stats(r)
        n = (h * gain_two + bias_two).astype(BF16)
        dk[rows, :] = n
        nt[:, rows] = transpose(n)
        g = (mix[4] * cot.astype(F32)).astype(BF16)
        dk[shifted(NT, row), :] = g
        nt[:, shifted(NT, row)] = transpose(g)
        gh[rows, :] = jnp.zeros((STEP, D), F32)

    by_rows(enter)

    during = {}

    def on(stage, step):
        during.setdefault(stage, []).append(step)

    def run_when(index, name):
        for (kind, when), steps in during.items():
            if kind == name:

                @pl.when(index == when)
                def _():
                    for step in steps:
                        step()


    sums = SmallSum(p, sm, sm_near, sm_rows, sm_across, sm_planes, sm_ss, sm_rc, sm_ry, sm_rx, sm_rz)
    hops = [(c, b) for c in range(1, p.ctxs - 1) for b in range(c + 1, p.ctxs)]

    def hop(g, part):
        third = pl.cdiv(len(hops), 3)
        for c, b in hops[part * third : (part + 1) * third]:

            @pl.when(p.ctx == c)
            def _():
                at = b - c
                landed(g, at)
                mine = dx_rows(g, b, p.core)[...].astype(F32)
                dxz[g, at] = (dxz[g, at].astype(F32) + mine).astype(BF16)
                rightward(g, dxz.at[g, at], c, b).start()

            far, to = p.ctxs - 1 - c, p.ctxs - 1 - b

            @pl.when(p.ctx == far)
            def _():
                at = p.ctxs - far + to
                landed(g, at)
                mine = dx_rows(g, to, p.core)[...].astype(F32)
                dxz[g, at] = (dxz[g, at].astype(F32) + mine).astype(BF16)
                leftward(g, dxz.at[g, at], far, to).start()

    schedule(ra, rb, on, p.ctxs, hop)

    def run(name):
        for kind, when in sorted(key for key in during if key[0] == name):
            for step in during[kind, when]:
                step()

    def feed(i, carry):
        slot = lax.rem(i, 2)

        @pl.when(i + 1 < 2 * n_a)
        def _():
            begin(load_tile(i + 1, 1 - slot))

        ready(load_tile(i, slot))
        up, dn = ring[slot, :, :T], ring[slot, :, T : 2 * T]
        c0 = 0.7978845608028654
        HALF = NT // 2
        for e in range(2):
            rows = slice(e * HALF, (e + 1) * HALF)
            u = dot(dk[rows, :], up)
            if e == 1:
                run_when(i, "m")
            u2 = u * u
            th = jnp.tanh(c0 * u * (1.0 + 0.044715 * u2))
            half = 0.5 * (1.0 + th)
            act = (u * half).astype(BF16)
            slope = half + 0.5 * u * (1.0 - th * th) * (c0 * (1.0 + 3 * 0.044715 * u2))
            dv[rows, :T] = act
            blk[rows, :] += dot_nt(act, dn)
            gu = (dot(dk[NT + e * HALF : NT + (e + 1) * HALF, :], dn) * slope).astype(BF16)
            dv[NT + e * HALF : NT + (e + 1) * HALF, :T] = gu
            gh[rows, :] += dot_nt(gu, up)

        @pl.when(i >= 2)
        def _():
            ra.cores_sent(slot * n_a + i // 2 - 1, slot)

        for y in range(chips):
            mine = slice(y * 2 * S, (y + 1) * 2 * S)
            ra.mine[slot, mine, :T] = dot(nt[mine, hn], dv[gd, :T]).astype(BF16)
            ra.mine[slot, mine, T:] = dot(nt[mine, gd], dv[hn, :T]).astype(BF16)
        ra.cores_send(slot * n_a + i // 2, slot)
        return carry

    lax.fori_loop(0, 2 * n_a, feed, 0)
    run("e")
    blk_away[:NT, :] = blk[...].astype(BF16)
    away = ra.copy(blk_away.at[pl.ds(0, NT), :], blk_home, b_send, b_recv, p.partner())

    @pl.when(p.core != p.tp)
    def _():
        away.start()

    @pl.when(p.core == p.tp)
    def _():
        blk_home[...] = blk_away[:NT, :]

    sm[...] = jnp.zeros_like(sm)

    def leave(x, cot, row):
        rows = shifted(0, row)
        cot = cot.astype(F32)
        sm[2:3, :] += jnp.sum(cot * blk[rows, :], axis=0, keepdims=True)
        h, scale = norm_stats(resid[rows, :])
        g = gh[rows, :]
        sm[0:1, :] += jnp.sum(g * h, axis=0, keepdims=True)
        sm[1:2, :] += jnp.sum(g, axis=0, keepdims=True)
        gr = mix[4] * cot + norm_back(g, gain_two, h, scale)
        resid[rows, :] = gr
        gb = gr.astype(BF16)
        nt[:, shifted(NT, row)] = transpose(gb)
        for t in range(TP):
            gatt[rows, t * HC : (t + 1) * HC] = dot(gb, wo[t]).astype(BF16)

    by_rows(leave)
    for slot, i in enumerate((0, NB)):
        t = p.tp if slot else 1 - p.tp
        lanes = pl.ds(pl.multiple_of(t * HC, 128), HC)
        for y in range(chips):
            mine = slice(y * 2 * S, (y + 1) * 2 * S)
            rb.mine[slot, mine, :] = dot(nt[mine, gd], att[:, lanes]).astype(BF16)
        rb.cores_send(i, slot)
    nt_load = [
        pltpu.make_async_copy(nt_hbm, nt, nt_sem.at[0]),
        pltpu.make_async_copy(own_nt_hbm, own_nt, nt_sem.at[1]),
    ]
    begin(nt_load)
    wq_load = pltpu.make_async_copy(wq_hbm.at[:, :, pl.ds(0, 3 * HC)], ring.at[:, :, pl.ds(0, 3 * HC)], wq_sem)
    wq_load.start()
    during.setdefault(("a", dm.PAIRS - 1), []).insert(0, partial(ready, nt_load))

    def attend(turn, g):
        it = g * dm.PAIRS + turn
        pair = pair_at(it)
        slot = it % 2

        @pl.when(it + 1 < G * dm.PAIRS)
        def _():
            begin(load_kv(it + 1, 1 - slot))

        lanes = pl.ds(pl.multiple_of(pair * 128, 128), 128)
        rp = pl.ds(pl.multiple_of(g * PB, PB), PB)
        rc = pl.ds(pl.multiple_of(dm.NP + g * NCH, NCH), NCH)
        qp, qc = q[rp, lanes], q[rc, lanes]
        gp, gc = gatt[rp, lanes], gatt[rc, lanes]
        ap, ac = att[rp, lanes].astype(F32), att[rc, lanes].astype(F32)
        qt = heads_columns(transpose(qp), transpose(qc))
        gpt, gct = gp.astype(F32).T, gc.astype(F32).T
        gt = heads_columns(gpt.astype(BF16), gct.astype(BF16))
        qs, gs = heads_rows(qp, qc), heads_rows(gp, gc)
        prodp, prodc = gpt * ap.T, gct * ac.T
        delta = jnp.concatenate(
            [
                jnp.sum(prodp[:HD], axis=0, keepdims=True),
                jnp.sum(prodp[HD:], axis=0, keepdims=True),
                jnp.sum(prodc[:HD], axis=0, keepdims=True),
                jnp.sum(prodc[HD:], axis=0, keepdims=True),
            ],
            axis=1,
        )
        stat = lse[g * dm.PAIRS + pair]
        ready(load_kv(it, slot))

        def grads(s, kt, vt, cols):
            pr = jnp.exp(s - stat[:, cols:])
            dp = dot(vt, gt[:, cols:])
            ds = (pr * (dp - delta[:, cols:])).astype(BF16)
            gv = dot(pr.astype(BF16), gs[cols:])
            gk = dot(ds, qs[cols:])
            gq = dot(transpose(kt), ds)
            return gk, gv, gq

        acc = None
        for j in range(tiles):
            rows = slice(j * TILE, (j + 1) * TILE)
            kt = kbuf[slot, rows, :]
            s = dot(kt, qt)
            s = jnp.concatenate([s[:, : 2 * PB] + twice(maskp[rows, :]), s[:, 2 * PB :]], axis=1)
            gk, gv, gq = grads(s, kt, vbuf[slot, rows, :], 0)
            gk = rotate_back(gk, cos[rows, :], sin[rows, :]).astype(BF16)
            gv = gv.astype(BF16)
            out = pl.ds(pl.multiple_of(g * R + j * TILE, 128), TILE)
            dk[out, lanes] = gk
            dv[out, lanes] = gv
            if j == tiles // 2:
                run_when(it, "a")
            acc = gq if acc is None else acc + gq
        kt = kbuf[slot, dm.P :, :]
        s = dot(kt, qt[:, 2 * PB :]) + maskx[...]
        gk, gv, gq = grads(s, kt, vbuf[slot, dm.P :, :], 2 * PB)
        for c in range(dm.NC):
            rows = slice(dm.P, dm.P + CL)
            out = pl.ds(pl.multiple_of(g * R + dm.P + c * CL, CL), CL)
            part = rotate_back(gk[c * CL : (c + 1) * CL], cos[rows, :], sin[rows, :])
            dk[out, lanes] = part.astype(BF16)
            dv[out, lanes] = gv[c * CL : (c + 1) * CL].astype(BF16)
        accp = acc[:, : 2 * PB] * 0.125
        accc = (acc[:, 2 * PB :] + gq) * 0.125
        outp = jnp.where(sublane_pick((128, PB), True), accp[:, :PB], accp[:, PB:]).T
        outc = jnp.where(sublane_pick((128, NCH), True), accc[:, :NCH], accc[:, NCH:]).T
        tab = pl.ds(pl.multiple_of(block * PB, PB), PB)
        dq[rp, lanes] = rotate_back(outp, cos[tab, :], sin[tab, :]).astype(BF16)
        tab = pl.ds(pl.multiple_of(dm.P + p.core * dm.CH, dm.CH), dm.CH)
        for c in range(dm.NC):
            part = rotate_back(outc[c * dm.CH : (c + 1) * dm.CH], cos[tab, :], sin[tab, :])
            rows = pl.ds(pl.multiple_of(dm.NP + g * NCH + c * dm.CH, dm.CH), dm.CH)
            dq[rows, lanes] = part.astype(BF16)

        @pl.when(g == G - 1)
        def _():
            put = turn % 2
            index = put * NB + 1 + turn // 2
            rb.cores_sent(index - 1, put)
            both = jnp.concatenate([dk[:, lanes], dv[:, lanes]], axis=1)
            for y in range(chips):
                mine = slice(y * 2 * S, (y + 1) * 2 * S)
                rb.mine[put, mine, 128:] = dot(nt[mine, :], both).astype(BF16)
                rb.mine[put, mine, :128] = dot(own_nt[mine, :], dq[:, lanes]).astype(BF16)
            rb.cores_send(index, put)

        return g

    w = ring

    def project(rows):
        total = None
        for t in range(TP):
            part = dot_nt(dk[rows, t * HC : (t + 1) * HC], w[t, :, HC : 2 * HC])
            total = part if total is None else total + part
            total += dot_nt(dv[rows, t * HC : (t + 1) * HC], w[t, :, 2 * HC : 3 * HC])
        return total

    NCONT = NT - NP
    gain_one = ln[0:1, :]
    halves = lambda core, g: pl.ds(pl.multiple_of(core * NCONT + g * NCH, 16), NCH)

    def dx_at(g, c, first, count):
        if g == G - 1:
            return dk.at[pl.ds(pl.multiple_of(g * R + c * 2 * PB + first, PB), count), :]
        fit = D // (2 * PB)
        row = pl.multiple_of(c % fit * 2 * PB + first, PB)
        return ra.mine.at[c // fit, pl.ds(row, count), pl.ds(0, D)]

    def dx_rows(g, c, core):
        return dx_at(g, c, core * PB, PB)

    def to_mate(g, k):
        i = g * p.ctxs + k
        rows = dx_rows(g, p.ctx_after(k), 1 - p.core)
        return ra.copy(rows, dxm.at[i], m_send.at[i], m_recv.at[i], p.mate())

    def rightward(g, src, c, b):
        i = b - c - 1
        return ra.copy(src, dxz.at[g, i], z_send.at[g, b], z_recv.at[g, i], p.at(ctx=c + 1))

    def leftward(g, src, c, b):
        i = p.ctxs - c + 1 + b
        return ra.copy(src, dxz.at[g, i], z_send.at[g, b], z_recv.at[g, i], p.at(ctx=c - 1))

    def landed(g, i):
        pltpu.make_async_copy(dxz.at[g, i], dxz.at[g, i], z_recv.at[g, i]).wait()

    def each_group(g, step):
        for e in range(G):

            @pl.when(g == e)
            def _():
                step(e)

    def cont_copy(g):
        return ra.copy(
            blk_away.at[halves(1 - p.core, g), :],
            dxcm.at[pl.ds(pl.multiple_of(g * NCH, 16), NCH), :],
            c_send.at[g],
            c_recv.at[g],
            p.mate(),
        )

    def norm_sums(x, turned, rows):
        sm[8:9, :] += jnp.sum(x.astype(F32), axis=0, keepdims=True)
        for d in range(0, D, 128):
            gh[:128, d : d + 128] += dot(turned[d : d + 128, rows], x[:, d : d + 128])

    def norm_grads():
        same = lax.broadcasted_iota(jnp.int32, (128, 128), 0) == lax.broadcasted_iota(
            jnp.int32, (128, 128), 1
        )
        for d in range(0, D, 128):
            cols = slice(d, d + 128)
            x = blk[:, cols].astype(BF16)
            sm[8:9, cols] += jnp.sum(x.astype(F32), axis=0, keepdims=True)
            gh[:128, cols] += dot(own_nt[cols, :], x)
            total = jnp.sum(jnp.where(same, gh[:128, cols], 0.0), axis=0, keepdims=True)
            sm[7:8, cols] = (total - ln[1:2, cols] * sm[8:9, cols]) / ln[0:1, cols]

    gh[:128, :] = jnp.zeros((128, D), F32)

    def group(g, carry):
        lax.fori_loop(0, dm.PAIRS, attend, g)

        @pl.when(g == 0)
        def _():
            wq_load.wait()
            ra.cores_sent(n_a - 1, 0)
            ra.cores_sent(2 * n_a - 1, 1)

            @pl.when(p.core != p.tp)
            def _():
                away.wait_send()

        def planes(i, carry):
            @pl.when(i < p.ctxs)
            def _():
                k = lax.rem(i + 1, p.ctxs)
                both = pl.ds(pl.multiple_of(g * R + p.ctx_after(k) * 2 * PB, 2 * PB), 2 * PB)
                total = project(both).astype(BF16)
                norm_sums(total, nt, both)

                def out(e):
                    dx_at(e, p.ctx_after(k), 0, 2 * PB)[...] = total
                    to_mate(e, k).start()

                each_group(g, out)
                run_when(g * p.ctxs + i, "p")

            @pl.when(i > 0)
            def _():
                k = lax.rem(i, p.ctxs)

                def back(e):
                    to_mate(e, k).wait_recv()
                    b = p.ctx_after(k)
                    mine = dx_rows(e, b, p.core)
                    mine[...] = (mine[...].astype(F32) + dxm[e * p.ctxs + k].astype(F32)).astype(BF16)

                    @pl.when((k > 0) & (p.ctx == 0))
                    def _():
                        rightward(e, mine, 0, b).start()

                    @pl.when((k > 0) & (p.ctx == p.ctxs - 1))
                    def _():
                        leftward(e, mine, p.ctxs - 1, b).start()

                each_group(g, back)

            return carry

        lax.fori_loop(0, p.ctxs + 1, planes, 0)
        rows = pl.ds(pl.multiple_of(g * R + dm.P, CL), NX)
        total = project(rows).astype(BF16)
        norm_sums(total, nt, rows)
        for c in range(dm.NC):
            for e in range(2):
                out = pl.ds(pl.multiple_of(e * NCONT + g * NCH + c * dm.CH, dm.CH), dm.CH)
                blk_away[out, :] = total[c * CL + e * dm.CH : c * CL + (e + 1) * dm.CH]
        cont_copy(g).start()
        for first, count in ((g * PB, PB), (NP + g * NCH, NCH)):
            rows = pl.ds(pl.multiple_of(first, 16), count)
            total = dot_nt(dq[rows, :HC], w[0, :, :HC])
            for t in range(1, TP):
                total += dot_nt(dq[rows, t * HC : (t + 1) * HC], w[t, :, :HC])
            blk[rows, :] = total
        return carry

    def enter_back(gn, x, rows):
        gn += blk[rows, :]
        hat, scale = norm_stats(x.astype(F32))
        gatt[rows, :] = (resid[rows, :] + norm_back(gn, gain_one, hat, scale)).astype(BF16)

    def gin_away(part):
        rows = pl.ds(0, NP) if part == 0 else pl.ds(NP, NT - NP)
        return ra.copy(gatt.at[rows, :], gin_home.at[rows, :], g_send.at[part], g_recv.at[part], p.partner())

    def give(part):
        rows = slice(0, NP) if part == 0 else slice(NP, NT)

        @pl.when(p.core != p.tp)
        def _():
            gin_away(part).start()

        @pl.when(p.core == p.tp)
        def _():
            gin_home[rows, :] = gatt[rows, :]

    lax.fori_loop(0, G, group, 0)
    homes = []
    for i, (a, c) in enumerate(
        [(home_arrays_p, home_arrays_c)]
        + [(early_p.at[e], early_c.at[e]) for e in range(3)]
        + [(home_cot_p, home_cot_c)]
    ):
        homes.append(pltpu.make_async_copy(a, dv.at[pl.ds(i * NT, NP), :], home_sem.at[0, i]))
        homes.append(pltpu.make_async_copy(c, dv.at[pl.ds(i * NT + NP, NT - NP), :], home_sem.at[1, i]))
    begin(homes)

    def cont_back(g, carry):
        cont_copy(g).wait_recv()
        here = pl.ds(pl.multiple_of(g * NCH, 16), NCH)
        gn = blk_away[halves(p.core, g), :].astype(F32) + dxcm[here, :].astype(F32)
        enter_back(gn, own_c[here, :], pl.ds(pl.multiple_of(NP + g * NCH, 16), NCH))
        return carry

    lax.fori_loop(0, G, cont_back, 0)
    give(1)

    ready(homes)

    @pl.when(p.core != p.tp)
    def _():
        away.wait_recv()

    def blend(i, carry):
        rows = shifted(0, i * STEP)
        res = mix[4] * blk_home[rows, :].astype(F32)
        c = dv[shifted(4 * NT, i * STEP), :].astype(F32)
        for e in range(4):
            a = dv[shifted(e * NT, i * STEP), :].astype(F32)
            res += mix[e] * a
            sm[3 + e : 4 + e, :] += jnp.sum(c * a, axis=0, keepdims=True)
        blk_home[rows, :] = res.astype(BF16)
        return carry

    lax.fori_loop(0, NT // STEP, blend, 0)
    puts = [
        pltpu.make_async_copy(blk_home.at[pl.ds(0, NP), :], out_p, put_sem.at[0]),
        pltpu.make_async_copy(blk_home.at[pl.ds(NP, NT - NP), :], out_c, put_sem.at[1]),
    ]
    begin(puts)
    norm_grads()
    sums.step(0)
    for when in range(10):
        for step in during.get(("t", when), []):
            step()
        if SMALL_AT.get(when):
            sums.step(SMALL_AT[when])

    for g in range(G):
        here = slice(g * PB, (g + 1) * PB)

        @pl.when(p.ctx > 0)
        def _():
            landed(g, 0)
            blk[here, :] += dxz[g, 0].astype(F32)

        @pl.when(p.ctx < p.ctxs - 1)
        def _():
            landed(g, p.ctxs)
            blk[here, :] += dxz[g, p.ctxs].astype(F32)

        enter_back(dx_rows(g, p.ctx, p.core)[...].astype(F32), own_p[here, :], here)
    give(0)
    for when in range(10, 20):
        for step in during.get(("t", when), []):
            step()
    small_out[...] = sums.result()
    gu_puts = []
    for j in range(n_a):
        ra.ctx_end(j)
        total = ra.result(j)
        gd_out[:, j * T : (j + 1) * T] = total[:, T:]
        if len(gu_puts) > 0:
            gu_puts[-1].wait()
        gh[:S, :T] = total[:, :T]
        gu_puts.append(
            pltpu.make_async_copy(
                gh.at[pl.ds(0, S), pl.ds(0, T)], gu_out.at[:, pl.ds(j * T, T)], put_sem.at[2]
            )
        )
        gu_puts[-1].start()
    gu_puts[-1].wait()
    for j in range(NB):
        rb.ctx_end(j)
        total = rb.result(j)
        if j == 0:
            go_out[...] = total
        else:
            for c in range(3):
                gq_out[c, :, (j - 1) * 128 : j * 128] = total[:, c * 128 : (c + 1) * 128]

    @pl.when(p.core != p.tp)
    def _():
        for part in range(2):
            gin_away(part).wait_recv()
            gin_away(part).wait_send()

    more = [
        pltpu.make_async_copy(gin_home.at[pl.ds(0, NP), :], gin_p, put_sem.at[2]),
        pltpu.make_async_copy(gin_home.at[pl.ds(NP, NT - NP), :], gin_c, put_sem.at[3]),
    ]
    begin(more)
    ready(puts + more)
    rb.cores_sent(NB - 1, 0)
    rb.cores_sent(2 * NB - 1, 1)
    for g in range(G):
        for k in range(p.ctxs):
            to_mate(g, k).wait_send()
        for k in range(1, p.ctxs):
            b = p.ctx_after(k)
            ra.copy(dxz.at[g, 0], dxz.at[g, 0], z_send.at[g, b], z_send.at[g, b], p.mate()).wait_send()
        cont_copy(g).wait_send()
    ra.drain()
    rb.drain()


def deliver_kernel(count, *refs):
    sources, small, targets = refs[:count], refs[count], refs[count + 1 : 2 * count + 1]
    outs = refs[2 * count + 1 : 2 * count + 6]
    kept = refs[2 * count + 6 : 3 * count + 6]
    in_sem, out_sem, parts = refs[3 * count + 6 :]
    loads = [pltpu.make_async_copy(sources[i], kept[i], in_sem.at[i]) for i in range(count)]
    puts = [pltpu.make_async_copy(kept[i], targets[i], out_sem.at[i]) for i in range(count)]
    for load in loads:
        load.start()
    S = parts.shape[2]
    norms = jnp.concatenate([small[7:9, :], small[0:2, :], jnp.zeros((4, small.shape[1]), F32)], axis=0)
    for d in range(parts.shape[0]):
        parts[d] = norms[:, d * S : (d + 1) * S]
    mine = parts[lax.axis_index("dp")]
    for i in range(4):
        outs[i][...] = mine[i : i + 1, :]
    sums = jnp.sum(small[...], axis=1, keepdims=True)
    order = (3, 4, 5, 6, 2)
    lanes = lax.broadcasted_iota(jnp.int32, (1, 5), 1)
    mix = jnp.zeros((1, 5), F32)
    for i, row in enumerate(order):
        mix = jnp.where(lanes == i, sums[row : row + 1, :], mix)
    outs[4][...] = mix
    for i in range(count):
        loads[i].wait()
        puts[i].start()
    for put in puts:
        put.wait()


def params(**more):
    return pltpu.CompilerParams(vmem_limit_bytes=VMEM_LIMIT, **more)


def per_device(
    prompt_in,
    cont_in,
    prompt_embed,
    cont_embed,
    prompt_earlier,
    cont_earlier,
    ln1_gain,
    ln1_bias,
    ln2_gain,
    ln2_bias,
    w_qkv,
    w_out,
    w_up,
    w_down,
    mix_weights,
    prompt_cot,
    cont_cot,
):
    G, PB, D = prompt_in.shape
    NC, CH = cont_in.shape[1], cont_in.shape[2]
    TP = lax.axis_size("tp")
    PROMPT = PB * TP * lax.axis_size("ctx")
    HC, FC = w_qkv.shape[2], w_up.shape[1]
    S = w_qkv.shape[0]
    dm = Dims(G, PROMPT, PB, NC, CH, D, HC * TP // HD)
    R, NT, NP = dm.R, dm.NT, dm.NP

    sds = jax.ShapeDtypeStruct
    chips, ctxs = lax.axis_size("dp") // 2, lax.axis_size("ctx")
    norms = jnp.concatenate([ln1_gain, ln1_bias, ln2_gain, ln2_bias]).reshape(4, S)
    norms = jnp.pad(norms, ((0, 124), (0, 0))).T
    wq_shard = jnp.concatenate([w_qkv.reshape(S, 3 * HC), norms], axis=1)
    wm_shard = jnp.concatenate([w_out.T, w_up, w_down.T], axis=1)

    positions = jnp.arange(PROMPT + CL, dtype=jnp.int32).astype(F32)
    freq = 10000.0 ** (-(jnp.arange(HD // 2, dtype=jnp.int32).astype(F32) / (HD // 2)))
    angles = freq[:, None] * positions[None, :]
    cos_few, sin_few = jnp.cos(angles), jnp.sin(angles)

    any_ = pl.BlockSpec(memory_space=pl.ANY)
    vmem = pl.BlockSpec(memory_space=pltpu.VMEM)
    dma = pltpu.SemaphoreType.DMA
    left = (HC + 2 * FC) // 128 * 2 // 3 * 128
    q, att, lse, ln, cos, sin, nt, own_nt, k, v, wq, wm, own_p, own_c, cot_p, cot_c = pl.pallas_call(
        partial(forward_kernel, dm, left),
        out_shape=(
            sds((NT, D), BF16),
            sds((NT, D), BF16),
            sds((G * dm.PAIRS, 1, dm.COLS), F32),
            sds((8, D), F32),
            sds((PROMPT + CL, 128), F32),
            sds((PROMPT + CL, 128), F32),
            sds((D, G * R), BF16),
            sds((D, NT), BF16),
            sds((G, R, D), BF16),
            sds((G, R, D), BF16),
            sds((TP, D, 3 * HC + 128), BF16),
            sds((TP, D, HC + 2 * FC), BF16),
            sds(prompt_in.shape, BF16),
            sds(cont_in.shape, BF16),
            sds(prompt_in.shape, BF16),
            sds(cont_in.shape, BF16),
        ),
        in_specs=[vmem] * 5 + [any_] * 3,
        out_specs=(vmem,) * 6 + (any_,) * 10,
        scratch_shapes=[
            pltpu.VMEM((D, G * R), BF16),
            pltpu.VMEM((D, NT), BF16),
            pltpu.VMEM((G, R, D), BF16),
            pltpu.VMEM((G, R, D), BF16),
            pltpu.VMEM((PROMPT, PB), F32),
            pltpu.VMEM((dm.NX, 2 * dm.NCH), F32),
            pltpu.VMEM((PROMPT, dm.COLS), F32),
            pltpu.VMEM((G * R, D), BF16),
            pltpu.VMEM((NT, D), BF16),
            pltpu.VMEM((2 * ctxs, G, PB, D), BF16),
            pltpu.VMEM((2, G, NC, CH, D), BF16),
            pltpu.VMEM((TP, D, 3 * HC + 128), BF16),
            dma((7,)),
            dma((4,)),
            dma((4,)),
            dma((2 * ctxs - 1,)),
            dma((ctxs - 1,)),
            dma((ctxs,)),
            dma,
            dma,
            dma((2,)),
        ]
        + WeightGather.semaphores(chips)
        + WeightGather.semaphores(chips),
        compiler_params=params(collective_id=0, has_side_effects=True),
        name="forward",
    )(prompt_in, cont_in, cos_few, sin_few, wq_shard, wm_shard, prompt_cot, cont_cot)
    T = 512 if FC % 512 == 0 else 256
    plan_a, plan_b = [False, False, True], [True, True, True, False]
    far = max(chips - 1, 1)
    rows = lambda x: x.reshape(-1, D)
    out_p, out_c, gin_p, gin_c, gq, go, gu, gd, small = pl.pallas_call(
        partial(backward_kernel, dm, T, FC, plan_a, plan_b),
        out_shape=(
            sds((NP, D), BF16),
            sds((NT - NP, D), BF16),
            sds((NP, D), BF16),
            sds((NT - NP, D), BF16),
            sds((3, S, HC), F32),
            sds((S, HC), F32),
            sds((S, FC), F32),
            sds((S, FC), F32),
            sds((16, D), F32),
        ),
        in_specs=[pl.BlockSpec(memory_space=pltpu.SMEM)] + [vmem] * 10 + [any_] * 12,
        out_specs=(any_,) * 4 + (vmem, vmem, any_, vmem, vmem),
        scratch_shapes=[
            pltpu.VMEM((NT, D), F32),
            pltpu.VMEM((NT, D), F32),
            pltpu.VMEM((NT, D), F32),
            pltpu.VMEM((TP, D, HC), BF16),
            pltpu.VMEM((2, D, max(2 * T, 3 * HC)), BF16),
            pltpu.VMEM((NT, D), BF16),
            pltpu.VMEM((D, G * R), BF16),
            pltpu.VMEM((D, NT), BF16),
            pltpu.VMEM((PROMPT, PB), F32),
            pltpu.VMEM((dm.NX, 2 * dm.NCH), F32),
            pltpu.VMEM((2, R, 128), BF16),
            pltpu.VMEM((2, R, 128), BF16),
            pltpu.VMEM((G * R, D), BF16),
            pltpu.VMEM((G * R, D), BF16),
            pltpu.VMEM((NT, D), BF16),
            pltpu.VMEM((G * ctxs, PB, D), BF16),
            pltpu.VMEM((G, ctxs + 1, PB, D), BF16),
            pltpu.VMEM((NT - NP, D), BF16),
            pltpu.VMEM((max(NT, 2 * (NT - NP)), D), BF16),
            pltpu.VMEM((NT, D), BF16),
            pltpu.VMEM((NT, D), BF16),
            dma((4,)),
            dma((2, 2)),
            dma,
            dma((2, 2)),
            dma((2,)),
            dma,
            dma((2, 5)),
            dma,
            dma,
            dma((2,)),
            dma((2,)),
            dma((G * ctxs,)),
            dma((G * ctxs,)),
            dma((G, ctxs)),
            dma((G, ctxs + 1)),
            dma((G,)),
            dma((G,)),
            pltpu.VMEM((16, D), F32),
            pltpu.VMEM((16, D), F32),
            pltpu.VMEM((chips, 16, D), F32),
            pltpu.VMEM((2, 16, D), F32),
            pltpu.VMEM((ctxs, 16, D), F32),
            dma((1 + chips + ctxs,)),
            dma,
            dma((far,)),
            dma,
            dma((ctxs - 1,)),
        ]
        + Reduce.scratch(plan_a, chips, S, 2 * T)
        + Reduce.scratch(plan_b, chips, S, HC),
        compiler_params=params(collective_id=1, has_side_effects=True),
        name="backward",
    )(
        mix_weights,
        att,
        rows(own_p),
        rows(own_c),
        rows(cot_p),
        rows(cot_c),
        ln,
        q,
        lse,
        cos,
        sin,
        wm,
        k,
        v,
        nt,
        own_nt,
        wq,
        rows(prompt_embed),
        rows(cont_embed),
        prompt_earlier.reshape(3, NP, D),
        cont_earlier.reshape(3, NT - NP, D),
        rows(prompt_cot),
        rows(cont_cot),
    )
    results = (out_p, out_c, gin_p, gin_c, gq, go, gu, gd)
    shapes = tuple(sds(x.shape, x.dtype) for x in results)
    out = pl.pallas_call(
        partial(deliver_kernel, len(results)),
        out_shape=shapes + (sds((1, S), F32),) * 4 + (sds((1, 5), F32),),
        in_specs=[any_] * len(results) + [vmem],
        out_specs=(any_,) * len(results) + (vmem,) * 5,
        scratch_shapes=[pltpu.VMEM(x.shape, x.dtype) for x in results]
        + [dma((len(results),)), dma((len(results),)), pltpu.VMEM((2 * chips, 8, S), F32)],
        compiler_params=params(),
        name="deliver",
    )(*results, small)
    out_p, out_c, gin_p, gin_c, gq, go, gu, gd = out[:8]
    gains = [x.reshape(S) for x in out[8:12]]
    return (
        out_p.reshape(prompt_in.shape),
        out_c.reshape(cont_in.shape),
        gin_p.reshape(prompt_in.shape),
        gin_c.reshape(cont_in.shape),
        *gains,
        jnp.transpose(gq, (1, 0, 2)),
        go.T,
        gu,
        gd.T,
        out[12].reshape(5),
    )


def solution(mesh):
    tokens = P("dp", ("ctx", "tp"), None)
    conts = P("dp", "ctx", "tp", None)
    weights = (P("dp", None, "tp"), P("tp", "dp"), P("dp", "tp"), P("tp", "dp"))
    in_specs = (
        tokens,
        conts,
        tokens,
        conts,
        P(None, "dp", ("ctx", "tp"), None),
        P(None, "dp", "ctx", "tp", None),
        P("dp"),
        P("dp"),
        P("dp"),
        P("dp"),
        *weights,
        P(),
        tokens,
        conts,
    )
    out_specs = (
        tokens,
        conts,
        tokens,
        conts,
        P("dp"),
        P("dp"),
        P("dp"),
        P("dp"),
        *weights,
        P(),
    )
    return jax.shard_map(
        per_device, mesh=mesh, in_specs=in_specs, out_specs=out_specs, check_vma=False
    )
```

```python
from functools import partial

import jax
import jax.numpy as jnp
import numpy as np
from jax import lax
from jax.experimental import pallas as pl
from jax.experimental.pallas import tpu as pltpu
from jax.sharding import PartitionSpec as P

HD = 64
CL = 128
EPS = 1e-05
NEG = -1e30
F32 = jnp.float32
BF16 = jnp.bfloat16
VMEM_LIMIT = 67043328


def dot(a, b):
    return lax.dot_general(a, b, (((1,), (0,)), ((), ())), preferred_element_type=F32)


def dot_nt(a, b):
    return lax.dot_general(a, b, (((1,), (1,)), ((), ())), preferred_element_type=F32)


def norm_stats(x):
    mean = jnp.mean(x, axis=-1, keepdims=True)
    centered = x - mean
    var = jnp.mean(centered * centered, axis=-1, keepdims=True)
    scale = lax.rsqrt(var + EPS)
    return centered * scale, scale


def norm_back(grad, gain, hat, scale):
    gh = grad * gain
    return scale * (
        gh
        - jnp.mean(gh, axis=-1, keepdims=True)
        - hat * jnp.mean(gh * hat, axis=-1, keepdims=True)
    )


def swap_halves(x):
    second = lax.broadcasted_iota(jnp.int32, x.shape, 1) % HD >= HD // 2
    return jnp.where(second, pltpu.roll(x, 32, 1), pltpu.roll(x, 96, 1))


def rotate(x, cos, sin):
    return x * cos + swap_halves(x) * sin


def rotate_back(x, cos, sin):
    return x * cos - swap_halves(x) * sin


def lane_pick(shape, low):
    lanes = lax.broadcasted_iota(jnp.int32, shape, 1)
    return lanes < HD if low else lanes >= HD


def sublane_pick(shape, low):
    rows = lax.broadcasted_iota(jnp.int32, shape, 0)
    return rows < HD if low else rows >= HD


def transpose(x):
    return x.astype(F32).T.astype(x.dtype)


class Dims:
    def __init__(self, groups, prompt, pb, nc, ch, d, heads):
        self.G, self.P, self.PB, self.NC, self.CH, self.D = groups, prompt, pb, nc, ch, d
        self.NCH = nc * ch
        self.R = prompt + nc * CL
        self.NX = nc * CL
        self.NR = pb + self.NCH
        self.NP = groups * pb
        self.NT = groups * self.NR
        self.PAIRS = heads // 2
        self.COLS = 2 * self.NR


MESH = pl.DeviceIdType.MESH


def half_index():
    return lax.axis_index("dp") % 2


def block_index():
    return lax.axis_index("ctx") * 2 + half_index()


class Peers:
    def __init__(self):
        self.ctxs = lax.axis_size("ctx")
        self.chips = lax.axis_size("dp") // 2
        self.tps = lax.axis_size("tp")
        self.dp = lax.axis_index("dp")
        self.ctx = lax.axis_index("ctx")
        self.tp = lax.axis_index("tp")
        self.core = self.dp % 2
        self.chip = self.dp // 2

    def at(self, dp=None, ctx=None, tp=None):
        return {
            "dp": self.dp if dp is None else dp,
            "ctx": self.ctx if ctx is None else ctx,
            "tp": self.tp if tp is None else tp,
        }

    def across(self):
        return self.at(tp=1 - self.tp)

    def mate(self):
        return self.at(dp=self.chip * 2 + 1 - self.core)

    def chip_after(self, k):
        return lax.rem(self.chip + k, self.chips)

    def chip_before(self, k):
        return lax.rem(self.chip + self.chips - k, self.chips)

    def row(self, k):
        return self.at(dp=self.chip_after(k) * 2 + self.core)

    def ctx_after(self, k):
        return lax.rem(self.ctx + k, self.ctxs)

    def ctx_before(self, k):
        return lax.rem(self.ctx + self.ctxs - k, self.ctxs)

    def plane(self, k):
        return self.at(ctx=self.ctx_after(k))

    def partner(self):
        return self.at(dp=self.chip * 2 + self.tp, tp=self.core)

    def greet(self, trades=False):
        barrier = pltpu.get_barrier_semaphore()
        peers = [self.across(), self.mate()]
        peers += [self.row(k) for k in range(1, self.chips)]
        peers += [self.plane(k) for k in range(1, self.ctxs)]
        for peer in peers:
            pl.semaphore_signal(barrier, inc=1, device_id=peer, device_id_type=MESH)
        count = len(peers)
        if trades:
            away = self.core != self.tp

            @pl.when(away)
            def _():
                pl.semaphore_signal(
                    barrier, inc=1, device_id=self.partner(), device_id_type=MESH
                )

            count += jnp.where(away, 1, 0)
        pl.semaphore_wait(barrier, count)


def send(src, dst, send_sem, recv_sem, device):
    copy = pltpu.make_async_remote_copy(
        src_ref=src,
        dst_ref=dst,
        send_sem=send_sem,
        recv_sem=recv_sem,
        device_id=device,
        device_id_type=MESH,
    )
    copy.start()
    return copy


def arrived(ref, sem, peers):
    pltpu.make_async_remote_copy(
        src_ref=ref,
        dst_ref=ref,
        send_sem=sem,
        recv_sem=sem,
        device_id=peers.mate(),
        device_id_type=MESH,
    ).wait_recv()


class WeightGather:
    def __init__(self, peers, shard, full, left, sends, across, rows, mate):
        self.p, self.shard, self.full, self.left = peers, shard, full, left
        self.sends, self.across, self.rows, self.from_mate = sends, across, rows, mate
        self.copies = []
        self.size, self.cols = shard.shape

    @staticmethod
    def semaphores(chips):
        far = chips - 1
        return [
            pltpu.SemaphoreType.DMA((3 + 6 * far,)),
            pltpu.SemaphoreType.DMA((chips,)),
            pltpu.SemaphoreType.DMA((2, max(far, 1))),
            pltpu.SemaphoreType.DMA((2, chips)),
        ]

    def piece(self, tp, dp, cols=slice(None)):
        rows = pl.ds(pl.multiple_of(dp * self.size, 16), self.size)
        if cols == slice(None):
            return self.full.at[tp, rows, :]
        return self.full.at[tp, rows, pl.ds(cols.start, cols.stop - cols.start)]

    def go(self, src, dst, recv_sem, device):
        self.copies.append(send(src, dst, self.sends.at[len(self.copies)], recv_sem, device))

    def start(self):
        p = self.p
        self.go(self.shard, self.piece(p.tp, p.dp), self.across.at[0], p.across())
        for k in range(1, p.chips):
            self.go(self.shard, self.piece(p.tp, p.dp), self.rows.at[0, k - 1], p.row(k))
        self.go(self.shard, self.piece(p.tp, p.dp), self.from_mate.at[0, 0], p.mate())

    def relay_across(self):
        p = self.p
        got = self.piece(1 - p.tp, p.dp)
        arrived(got, self.across.at[0], p)
        part = self.piece(1 - p.tp, p.dp, slice(0, self.left))
        for k in range(1, p.chips):
            self.go(part, part, self.rows.at[1, k - 1], p.row(k))
        self.go(got, got, self.from_mate.at[1, 0], p.mate())

    def relay_rows(self):
        p = self.p
        for k in range(1, p.chips):
            dp = p.chip_before(k) * 2 + p.core
            got = self.piece(p.tp, dp)
            arrived(got, self.rows.at[0, k - 1], p)
            if self.left < self.cols:
                part = self.piece(p.tp, dp, slice(self.left, self.cols))
                self.go(part, part, self.across.at[k], p.across())
            self.go(got, got, self.from_mate.at[0, k], p.mate())

    def relay_last(self):
        p = self.p
        for k in range(1, p.chips):
            dp = p.chip_before(k) * 2 + p.core
            arrived(self.piece(1 - p.tp, dp, slice(0, self.left)), self.rows.at[1, k - 1], p)
            if self.left < self.cols:
                part = self.piece(1 - p.tp, dp, slice(self.left, self.cols))
                arrived(part, self.across.at[k], p)
            got = self.piece(1 - p.tp, dp)
            self.go(got, got, self.from_mate.at[1, k], p.mate())

    def finish(self):
        p = self.p
        for part in range(2):
            tp = p.tp if part == 0 else 1 - p.tp
            for k in range(p.chips):
                dp = p.chip_before(k) * 2 + 1 - p.core
                arrived(self.piece(tp, dp), self.from_mate.at[part, k], p)

    def drain(self):
        for copy in self.copies:
            copy.wait_send()


def twice(x):
    return jnp.concatenate([x, x], axis=1)


def fill_masks(dm, maskp, maskx):
    block = block_index()
    keys = lax.broadcasted_iota(jnp.int32, maskp.shape, 0)
    cols = lax.broadcasted_iota(jnp.int32, maskp.shape, 1) % dm.PB
    maskp[...] = jnp.where(keys <= cols + block * dm.PB, 0.0, NEG)
    keys = lax.broadcasted_iota(jnp.int32, maskx.shape, 0)
    cols = lax.broadcasted_iota(jnp.int32, maskx.shape, 1) % dm.NCH
    seen = (keys // CL == cols // dm.CH) & (
        keys % CL <= cols % dm.CH + half_index() * dm.CH
    )
    maskx[...] = jnp.where(seen, 0.0, NEG)


def heads_columns(a, b):
    lo_a, lo_b = sublane_pick(a.shape, True), sublane_pick(b.shape, True)
    zero_a, zero_b = jnp.zeros_like(a), jnp.zeros_like(b)
    return jnp.concatenate(
        [
            jnp.where(lo_a, a, zero_a),
            jnp.where(lo_a, zero_a, a),
            jnp.where(lo_b, b, zero_b),
            jnp.where(lo_b, zero_b, b),
        ],
        axis=1,
    )


def heads_rows(a, b):
    lo_a, lo_b = lane_pick(a.shape, True), lane_pick(b.shape, True)
    zero_a, zero_b = jnp.zeros_like(a), jnp.zeros_like(b)
    return jnp.concatenate(
        [
            jnp.where(lo_a, a, zero_a),
            jnp.where(lo_a, zero_a, a),
            jnp.where(lo_b, b, zero_b),
            jnp.where(lo_b, zero_b, b),
        ],
        axis=0,
    )


def forward_kernel(
    dm,
    left,
    prompt,
    cont,
    cos_few,
    sin_few,
    wq,
    wm,
    cot_p,
    cot_c,
    q_out,
    att_out,
    lse_out,
    ln_out,
    cos,
    sin,
    nt_hbm,
    own_nt_hbm,
    k_hbm,
    v_hbm,
    w_hbm,
    wm_out,
    own_p_hbm,
    own_c_hbm,
    cot_p_out,
    cot_c_out,
    nt_out,
    own_out,
    k_out,
    v_out,
    maskp,
    maskx,
    sbuf,
    all_rows,
    own_rows,
    xp,
    xc,
    w,
    put_sem,
    trade_send,
    trade_recv,
    x_send,
    x_plane,
    x_mate,
    c_send,
    c_mate,
    own_sem,
    *sems,
):
    G, R, PB, NCH, D, NP, NT = dm.G, dm.R, dm.PB, dm.NCH, dm.D, dm.NP, dm.NT
    NC, CH = dm.NC, dm.CH
    HC = (w.shape[2] - 128) // 3
    TP = w.shape[0]
    p = Peers()
    block = block_index()
    gq = WeightGather(p, wq, w, wq.shape[1] // 256 * 128, *sems[:4])
    gm = WeightGather(p, wm, wm_out, left, *sems[4:])
    size = wq.shape[0]
    mine = pl.ds(pl.multiple_of(p.dp * size, 16), size)

    landing = [xp.at[p.ctx * 2 + p.tp], xc.at[p.tp], cot_p_out, cot_c_out]

    def moved(i):
        src = [prompt, cont, cot_p, cot_c][i]
        return pltpu.make_async_remote_copy(
            src_ref=src,
            dst_ref=landing[i],
            send_sem=trade_send.at[i],
            recv_sem=trade_recv.at[i],
            device_id=p.partner(),
            device_id_type=MESH,
        )

    def kept(i):
        return pltpu.make_async_copy([prompt, cont, cot_p, cot_c][i], landing[i], trade_send.at[i])

    moves = p.core != p.tp

    def trade(i):
        @pl.when(moves)
        def _():
            moved(i).start()

        @pl.when(jnp.logical_not(moves))
        def _():
            kept(i).start()

    def traded(i):
        @pl.when(moves)
        def _():
            moved(i).wait_recv()

        @pl.when(jnp.logical_not(moves))
        def _():
            kept(i).wait()

    local = [
        pltpu.make_async_copy(wq, w.at[p.tp, mine, :], own_sem.at[0]),
        pltpu.make_async_copy(wm, wm_out.at[p.tp, mine, :], own_sem.at[1]),
    ]
    for copy in local:
        copy.start()
    p.greet(trades=True)
    trade(0)
    gq.start()
    traded(0)
    own = xp.at[block]
    sent = []
    for k in range(1, p.ctxs):
        sent.append(send(own, own, x_send.at[k - 1], x_plane.at[k - 1], p.plane(k)))
    sent.append(send(own, own, x_send.at[p.ctxs - 1], x_mate.at[0], p.mate()))
    fill_masks(dm, maskp, maskx)
    second = lax.broadcasted_iota(jnp.int32, (128, 128), 1) % HD >= HD // 2
    for i in range(0, dm.P + CL, 128):
        part = cos_few[:, i : i + 128]
        cos[i : i + 128, :] = jnp.concatenate([part] * 4, axis=0).T
        part = sin_few[:, i : i + 128]
        part = jnp.concatenate([part] * 4, axis=0).T
        sin[i : i + 128, :] = jnp.where(second, part, -part)
    gq.relay_rows()
    gq.relay_across()
    trade(1)
    gm.start()
    gq.relay_last()
    traded(1)
    sent.append(send(xc.at[p.core], xc.at[p.core], c_send, c_mate, p.mate()))
    gq.finish()
    local[0].wait()
    puts = [
        pltpu.make_async_copy(w, w_hbm, put_sem.at[0]),
        pltpu.make_async_copy(xp.at[block], own_p_hbm, put_sem.at[1]),
        pltpu.make_async_copy(xc.at[p.core], own_c_hbm, put_sem.at[2]),
    ]
    for put in puts:
        put.start()
    ln = w[0, :, 3 * HC :].astype(F32).T[:8, :]
    ln_out[...] = ln
    gain, bias = ln[0:1, :], ln[1:2, :]

    def normed(x):
        hat, _ = norm_stats(x.astype(F32))
        return (hat * gain + bias).astype(BF16)

    def turned(x, table):
        rows = x.shape[0]
        return rotate(x, cos[pl.ds(table, rows), :], sin[pl.ds(table, rows), :])

    x = jnp.concatenate([xp[block].reshape(NP, D), xc[p.core].reshape(NT - NP, D)], axis=0)
    n = normed(x)
    own_rows[...] = n
    places = [(g * PB, PB, pl.multiple_of(block * PB, PB)) for g in range(G)]
    places += [
        (NP + i * CH, CH, pl.multiple_of(dm.P + p.core * CH, CH)) for i in range(G * NC)
    ]
    for t in range(TP):
        qq = dot(n, w[t, :, :HC])
        for first, count, table in places:
            for j in range(HC // 128):
                tile = turned(qq[first : first + count, j * 128 : (j + 1) * 128], table).astype(BF16)
                q_out[first : first + count, t * HC + j * 128 : t * HC + (j + 1) * 128] = (
                    tile.astype(F32) * 0.125
                ).astype(BF16)
    own_out[...] = transpose(own_rows[...])

    def keys_values(x, places):
        n = normed(x)
        for first, count, g, row, table in places:
            all_rows[pl.ds(pl.multiple_of(g * R + row, 16), count), :] = n[first : first + count]
        for t in range(TP):
            kk = dot(n, w[t, :, HC : 2 * HC])
            for first, count, g, row, table in places:
                for j in range(HC // 128):
                    tile = turned(kk[first : first + count, j * 128 : (j + 1) * 128], table)
                    k_out[g, pl.ds(row, count), t * HC + j * 128 : t * HC + (j + 1) * 128] = tile.astype(BF16)
            vv = dot(n, w[t, :, 2 * HC : 3 * HC]).astype(BF16)
            for first, count, g, row, table in places:
                v_out[g, pl.ds(row, count), t * HC : (t + 1) * HC] = vv[first : first + count]

    arrived(xc.at[1 - p.core], c_mate, p)
    x = [xc[e, g, c] for g in range(G) for c in range(NC) for e in range(2)]
    keys_values(
        jnp.concatenate(x, axis=0),
        [((g * NC + c) * CL, CL, g, dm.P + c * CL, dm.P) for g in range(G) for c in range(NC)],
    )

    def relay(k):
        b = p.ctx_before(k) * 2 + p.core
        return pltpu.make_async_remote_copy(
            src_ref=xp.at[b],
            dst_ref=xp.at[b],
            send_sem=x_send.at[p.ctxs + k - 1],
            recv_sem=x_mate.at[k],
            device_id=p.mate(),
            device_id_type=MESH,
        )

    def plane(k, carry):
        c = p.ctx_before(k)

        @pl.when(k > 0)
        def _():
            arrived(xp.at[c * 2 + p.core], x_plane.at[k - 1], p)
            relay(k).start()

        arrived(xp.at[c * 2 + 1 - p.core], x_mate.at[k], p)
        x = xp[pl.ds(c * 2, 2)].reshape(2 * NP, D)
        places = []
        for e in range(2):
            row = pl.multiple_of((c * 2 + e) * PB, PB)
            places += [((e * G + g) * PB, PB, g, row, row) for g in range(G)]
        keys_values(x, places)
        return carry

    lax.fori_loop(0, p.ctxs, plane, 0)
    puts += [
        pltpu.make_async_copy(k_out, k_hbm, put_sem.at[3]),
        pltpu.make_async_copy(v_out, v_hbm, put_sem.at[4]),
    ]
    for put in puts[3:]:
        put.start()

    def turn(i, carry):
        rows = pl.ds(pl.multiple_of(i * 256, 256), 256)
        nt_out[:, rows] = transpose(all_rows[rows, :])
        return carry

    lax.fori_loop(0, G * R // 256, turn, 0)
    puts += [
        pltpu.make_async_copy(nt_out, nt_hbm, put_sem.at[5]),
        pltpu.make_async_copy(own_out, own_nt_hbm, put_sem.at[6]),
    ]
    for put in puts[5:]:
        put.start()
    gm.relay_across()
    gm.relay_rows()
    trade(2)
    trade(3)

    TILE = 256
    tiles = dm.P // TILE

    def attend(i, carry):
        g, pair = i // dm.PAIRS, i % dm.PAIRS
        lanes = pl.ds(pl.multiple_of(pair * 128, 128), 128)
        qp = q_out[pl.ds(pl.multiple_of(g * PB, PB), PB), lanes]
        qc = q_out[pl.ds(pl.multiple_of(dm.NP + g * NCH, NCH), NCH), lanes]
        qt = heads_columns(transpose(qp), transpose(qc))
        top = None
        for j in range(tiles):
            s = dot(k_out[g, j * TILE : (j + 1) * TILE, lanes], qt)
            sbuf[j * TILE : (j + 1) * TILE, : 2 * PB] = (
                s[:, : 2 * PB] + twice(maskp[j * TILE : (j + 1) * TILE, :])
            )
            sbuf[j * TILE : (j + 1) * TILE, 2 * PB :] = s[:, 2 * PB :]
            here = jnp.max(sbuf[j * TILE : (j + 1) * TILE, :], axis=0, keepdims=True)
            top = here if top is None else jnp.maximum(top, here)
        sx = dot(k_out[g, dm.P :, lanes], qt[:, 2 * PB :]) + maskx[...]
        topx = jnp.max(sx, axis=0, keepdims=True)
        top = jnp.concatenate([top[:, : 2 * PB], jnp.maximum(top[:, 2 * PB :], topx)], axis=1)
        total, acc = None, None
        for j in range(tiles):
            e = jnp.exp(sbuf[j * TILE : (j + 1) * TILE, :] - top)
            here = jnp.sum(e, axis=0, keepdims=True)
            vt = transpose(v_out[g, j * TILE : (j + 1) * TILE, lanes])
            part = dot(vt, e.astype(BF16))
            total = here if total is None else total + here
            acc = part if acc is None else acc + part
        ex = jnp.exp(sx - top[:, 2 * PB :])
        partx = dot(transpose(v_out[g, dm.P :, lanes]), ex.astype(BF16))
        totalx = jnp.sum(ex, axis=0, keepdims=True)
        total = jnp.concatenate([total[:, : 2 * PB], total[:, 2 * PB :] + totalx], axis=1)
        acc_p = acc[:, : 2 * PB] / total[:, : 2 * PB]
        acc_c = (acc[:, 2 * PB :] + partx) / total[:, 2 * PB :]
        lse_out[i] = top + jnp.log(total)
        outp = jnp.where(sublane_pick((128, PB), True), acc_p[:, :PB], acc_p[:, PB:])
        outc = jnp.where(sublane_pick((128, NCH), True), acc_c[:, :NCH], acc_c[:, NCH:])
        att_out[pl.ds(pl.multiple_of(g * PB, PB), PB), lanes] = outp.T.astype(BF16)
        att_out[pl.ds(pl.multiple_of(dm.NP + g * NCH, NCH), NCH), lanes] = outc.T.astype(BF16)
        return carry

    lax.fori_loop(0, G * dm.PAIRS, attend, 0)
    gm.relay_last()
    gm.finish()
    gq.drain()
    gm.drain()
    for copy in sent:
        copy.wait_send()
    for k in range(1, p.ctxs):
        relay(k).wait_send()
    local[1].wait()
    for i in (2, 3):
        traded(i)

    @pl.when(moves)
    def _():
        for i in range(4):
            moved(i).wait_send()

    for put in puts:
        put.wait()


class Reduce:
    REFS = 13

    def __init__(self, p, cross_first, refs):
        self.p, self.n, self.cross_first = p, len(cross_first), cross_first
        self.mine, self.got, self.row, self.acr, self.zin = refs[:5]
        self.sc, self.rc, self.sy, self.ry, self.sx, self.rx, self.sz, self.rz = refs[5:13]
        mid = p.ctxs // 2
        self.centre = (p.ctx == mid - 1) | (p.ctx == mid)
        self.outer = (p.ctx > 0) & (p.ctx < p.ctxs - 1)
        step = jnp.where(p.ctx < mid, 1, -1)
        self.inner_at = p.ctx + step
        self.outer_at = jnp.clip(p.ctx - step, 0, p.ctxs - 1)

    @staticmethod
    def scratch(cross_first, chips, size, width):
        n = len(cross_first)
        dma = pltpu.SemaphoreType.DMA
        far = max(chips - 1, 1)
        rows = n + sum(1 for c in cross_first if not c)
        parts = sum(chips if c else 1 for c in cross_first)
        return [
            pltpu.VMEM((2, chips * 2 * size, width), BF16),
            pltpu.VMEM((2 * n, chips, size, width), BF16),
            pltpu.VMEM((rows, far, size, width), BF16),
            pltpu.VMEM((parts, size, width), BF16),
            pltpu.VMEM((n, 2, size, width), BF16),
            dma((2 * n, chips)),
            dma((2 * n, chips)),
            dma((2 * n, far)),
            dma((2 * n, far)),
            dma((n,)),
            dma((n,)),
            dma((n, 2)),
            dma((n, 2)),
        ]

    def copy(self, src, dst, send_sem, recv_sem, device):
        return pltpu.make_async_remote_copy(
            src_ref=src,
            dst_ref=dst,
            send_sem=send_sem,
            recv_sem=recv_sem,
            device_id=device,
            device_id_type=MESH,
        )

    def slot(self, whose, j):
        return 0 if whose == "other" else 1

    def crosses(self, i):
        return self.cross_first[i % self.n]

    def travels(self, i):
        return i >= self.n or not self.crosses(i)

    def mine_of(self, y, core):
        size = self.got.shape[2]
        return pl.ds(pl.multiple_of((2 * y + core) * size, 16), size)

    def by_core(self, i, slot, y):
        p = self.p
        return self.copy(
            self.mine.at[slot, self.mine_of(y, 1 - p.core), :],
            self.got.at[i, y],
            self.sc.at[i, y],
            self.rc.at[i, y],
            p.mate(),
        )

    def row_slot(self, i):
        return sum(1 for e in range(i) if self.travels(e))

    def by_row(self, i, k):
        p = self.p
        return self.copy(
            self.got.at[i, p.chip_after(k)],
            self.row.at[self.row_slot(i), k - 1],
            self.sy.at[i, k - 1],
            self.ry.at[i, k - 1],
            p.row(k),
        )

    def by_tp(self, j):
        p = self.p
        slot = self.acr_slot(j)
        if self.crosses(j):
            src, dst = self.got.at[j], self.acr.at[pl.ds(slot, p.chips)]
        else:
            src, dst = self.got.at[j, p.chip], self.acr.at[slot]
        return self.copy(src, dst, self.sx.at[j], self.rx.at[j], p.across())

    def acr_slot(self, j):
        return sum(self.p.chips if c else 1 for c in self.cross_first[:j])

    def inward(self, j):
        slot = jnp.where(self.centre, 1, 0)
        return self.copy(
            self.got.at[self.n + j, self.p.chip],
            self.zin.at[j, slot],
            self.sz.at[j, 0],
            self.rz.at[j, slot],
            self.p.at(ctx=self.inner_at),
        )

    def outward(self, j):
        return self.copy(
            self.got.at[self.n + j, self.p.chip],
            self.zin.at[j, 1],
            self.sz.at[j, 1],
            self.rz.at[j, 1],
            self.p.at(ctx=self.outer_at),
        )

    def add(self, i, y, other):
        self.got[i, y] = (self.got[i, y].astype(F32) + other.astype(F32)).astype(BF16)

    def cores_send(self, i, slot):
        for y in range(self.p.chips):
            self.by_core(i, slot, y).start()

    def cores_sent(self, i, slot):
        for y in range(self.p.chips):
            self.by_core(i, slot, y).wait_send()

    def rows_send(self, i):
        for k in range(1, self.p.chips):
            self.by_row(i, k).start()

    def cores_sum(self, i, slot):
        p = self.p
        for y in range(p.chips):
            self.by_core(i, slot, y).wait_recv()
            self.add(i, y, self.mine[slot, self.mine_of(y, p.core), :])
        if not self.crosses(i):
            self.rows_send(i)
        elif i < self.n:
            self.by_tp(i).start()

    def cross_sum(self, j):
        self.by_tp(j).wait_recv()
        for y in range(self.p.chips):
            self.add(self.n + j, y, self.acr[self.acr_slot(j) + y])
        self.rows_send(self.n + j)

    def rows_sum(self, i):
        p = self.p
        for k in range(1, p.chips):
            self.by_row(i, k).wait_recv()
            self.add(i, p.chip, self.row[self.row_slot(i), k - 1])
        if i < self.n:
            self.by_tp(i).start()
            return
        j = i - self.n
        if not self.crosses(i):
            self.by_tp(j).wait_recv()
            self.add(i, p.chip, self.acr[self.acr_slot(j)])

        @pl.when(jnp.logical_not(self.outer))
        def _():
            self.inward(j).start()

    def ctx_in(self, j):
        @pl.when(self.outer)
        def _():
            pltpu.make_async_copy(self.zin.at[j, 0], self.zin.at[j, 0], self.rz.at[j, 0]).wait()
            self.add(self.n + j, self.p.chip, self.zin[j, 0])
            self.inward(j).start()

    def ctx_mid(self, j):
        @pl.when(self.centre)
        def _():
            self.from_inner(j)
            self.add(self.n + j, self.p.chip, self.zin[j, 1])

            @pl.when(self.outer)
            def _():
                self.outward(j).start()

    def ctx_end(self, j):
        @pl.when(jnp.logical_not(self.centre))
        def _():
            self.from_inner(j)
            self.got[self.n + j, self.p.chip] = self.zin[j, 1]

            @pl.when(self.outer)
            def _():
                self.outward(j).start()

    def from_inner(self, j):
        pltpu.make_async_copy(self.zin.at[j, 1], self.zin.at[j, 1], self.rz.at[j, 1]).wait()
        self.inward(j).wait_send()

    def result(self, j):
        return self.got[self.n + j, self.p.chip].astype(F32)

    def drain(self):
        p = self.p
        for i in range(2 * self.n):
            if self.travels(i):
                for k in range(1, p.chips):
                    self.by_row(i, k).wait_send()
        for j in range(self.n):
            self.by_tp(j).wait_send()

            @pl.when(self.outer)
            def _():
                self.outward(j).wait_send()


class SmallSum:
    def __init__(self, p, sm, near, rows, across, planes, ss, rc, ry, rx, rz):
        self.p, self.sm, self.near, self.rows, self.across, self.planes = p, sm, near, rows, across, planes
        self.ss, self.rc, self.ry, self.rx, self.rz = ss, rc, ry, rx, rz

    def copy(self, index, src, dst, recv_sem, device):
        return pltpu.make_async_remote_copy(
            src_ref=src,
            dst_ref=dst,
            send_sem=self.ss.at[index],
            recv_sem=recv_sem,
            device_id=device,
            device_id_type=MESH,
        )

    def to_mate(self):
        return self.copy(0, self.sm, self.near, self.rc, self.p.mate())

    def to_row(self, k):
        mine = self.rows.at[self.p.chip]
        return self.copy(1 + k, mine, mine, self.ry.at[k - 1], self.p.row(k))

    def to_across(self):
        return self.copy(1, self.across.at[0], self.across.at[1], self.rx, self.p.across())

    def to_plane(self, k):
        mine = self.planes.at[self.p.ctx]
        return self.copy(self.p.chips + k, mine, mine, self.rz.at[k - 1], self.p.plane(k))

    def step(self, which):
        p = self.p
        if which == 0:
            self.to_mate().start()
        elif which == 1:
            self.to_mate().wait_recv()
            self.rows[p.chip] = self.sm[...] + self.near[...]
            for k in range(1, p.chips):
                self.to_row(k).start()
        elif which == 2:
            for k in range(1, p.chips):
                arrived(self.rows.at[p.chip_before(k)], self.ry.at[k - 1], p)
            total = self.rows[0]
            for y in range(1, p.chips):
                total += self.rows[y]
            self.across[0] = total
            self.to_across().start()
        elif which == 3:
            self.to_across().wait_recv()
            self.planes[p.ctx] = self.across[0] + self.across[1]
            for k in range(1, p.ctxs):
                self.to_plane(k).start()

    def result(self):
        p = self.p
        for k in range(1, p.ctxs):
            arrived(self.planes.at[p.ctx_before(k)], self.rz.at[k - 1], p)
        total = self.planes[0]
        for z in range(1, p.ctxs):
            total += self.planes[z]
        self.to_mate().wait_send()
        self.to_across().wait_send()
        for k in range(1, p.chips):
            self.to_row(k).wait_send()
        for k in range(1, p.ctxs):
            self.to_plane(k).wait_send()
        return total


SMALL_AT = {2: 1, 5: 2, 8: 3}
PLAN = {
    ("m", 1): [("a", "cores_sum", "other", 0)],
    ("m", 3): [("a", "cores_sum", "own", 0)],
    ("m", 4): [("a", "cores_sum", "other", 1), ("a", "rows_sum", "other", 0)],
    ("m", 5): [("a", "cores_sum", "own", 1)],
    ("e", 0): [("a", "cores_sum", "other", 2)],
    ("a", 0): [("a", "rows_sum", "own", 0)],
    ("a", 1): [("a", "cores_sum", "own", 2)],
    ("p", 0, 0): [("a", "ctx_in", "own", 0)],
    ("p", 0, 1): [("b", "cores_sum", "own", 0), ("b", "cores_sum", "other", 0)],
    ("p", 0, 3): [("a", "cross_sum", "own", 2), ("a", "rows_sum", "other", 1)],
    ("a", 7): [("a", "ctx_mid", "own", 0)],
    ("a", 8): [("a", "rows_sum", "own", 2), ("hop", 0, 0), ("b", "cores_sum", "other", 1)],
    ("a", 9): [("a", "rows_sum", "own", 1), ("b", "cores_sum", "own", 1), ("b", "cores_sum", "other", 2), ("hop", 0, 1)],
    ("a", 10): [("a", "ctx_in", "own", 2), ("b", "cross_sum", "own", 0)],
    ("a", 11): [("b", "cores_sum", "own", 2), ("hop", 0, 2)],
    ("p", 1, 1): [("b", "cores_sum", "other", 3), ("a", "ctx_in", "own", 1), ("b", "cross_sum", "own", 1)],
    ("p", 1, 3): [("a", "ctx_mid", "own", 2)],
    ("t", 0): [("hop", 1, 0)],
    ("t", 2): [("b", "rows_sum", "other", 3), ("a", "ctx_mid", "own", 1)],
    ("t", 3): [("b", "cross_sum", "own", 2), ("b", "rows_sum", "own", 0), ("b", "cores_sum", "own", 3)],
    ("t", 4): [("b", "rows_sum", "own", 1)],
    ("t", 5): [("hop", 1, 1)],
    ("t", 6): [("b", "ctx_in", "own", 0), ("b", "rows_sum", "own", 3)],
    ("t", 8): [("b", "ctx_in", "own", 1)],
    ("t", 9): [("hop", 1, 2), ("b", "ctx_in", "own", 3), ("b", "rows_sum", "own", 2)],
    ("t", 10): [("b", "ctx_mid", "own", 0)],
    ("t", 11): [("b", "ctx_in", "own", 2)],
    ("t", 14): [("b", "ctx_mid", "own", 1), ("b", "ctx_mid", "own", 3)],
    ("t", 18): [("b", "ctx_mid", "own", 2)],
}


def schedule(ra, rb, on, planes, hop):
    for stage, steps in PLAN.items():
        if stage[0] == "p":
            stage = ("p", stage[1] * planes + stage[2])
        for step in steps:
            if step[0] == "hop":
                on(stage, partial(hop, step[1], step[2]))
                continue
            name, what, whose, j = step
            r = ra if name == "a" else rb
            if what == "cores_sum":
                on(stage, partial(r.cores_sum, j if whose == "other" else r.n + j, r.slot(whose, j)))
            elif what == "rows_sum":
                on(stage, partial(r.rows_sum, j if whose == "other" else r.n + j))
            else:
                on(stage, partial(getattr(r, what), j))


def backward_kernel(
    dm,
    T,
    FC,
    plan_a,
    plan_b,
    mix,
    att,
    own_p,
    own_c,
    cot_p,
    cot_c,
    ln,
    q,
    lse,
    cos,
    sin,
    wm,
    k_hbm,
    v_hbm,
    nt_hbm,
    own_nt_hbm,
    wq_hbm,
    home_arrays_p,
    home_arrays_c,
    early_p,
    early_c,
    home_cot_p,
    home_cot_c,
    out_p,
    out_c,
    gin_p,
    gin_c,
    gq_out,
    go_out,
    gu_out,
    gd_out,
    small_out,
    resid,
    blk,
    gh,
    wo,
    ring,
    gatt,
    nt,
    own_nt,
    maskp,
    maskx,
    kbuf,
    vbuf,
    dk,
    dv,
    dq,
    dxm,
    dxz,
    dxcm,
    blk_away,
    blk_home,
    gin_home,
    put_sem,
    ring_sem,
    wo_sem,
    kv_sem,
    nt_sem,
    wq_sem,
    home_sem,
    b_send,
    b_recv,
    g_send,
    g_recv,
    m_send,
    m_recv,
    z_send,
    z_recv,
    c_send,
    c_recv,
    sm,
    sm_near,
    sm_rows,
    sm_across,
    sm_planes,
    sm_ss,
    sm_rc,
    sm_ry,
    sm_rx,
    sm_rz,
    *refs,
):
    G, R, PB, NCH, D, NX, NP, NT = dm.G, dm.R, dm.PB, dm.NCH, dm.D, dm.NX, dm.NP, dm.NT
    TP, HC = wo.shape[0], wo.shape[2]
    PT = dm.PAIRS // TP
    p = Peers()
    n_a, NB = len(plan_a), len(plan_b)
    ra = Reduce(p, plan_a, refs[: Reduce.REFS])
    rb = Reduce(p, plan_b, refs[Reduce.REFS :])
    block = block_index()
    TILE = 256
    tiles = dm.P // TILE
    chips = p.chips
    S = D // (2 * chips)

    def begin(copies):
        for copy in copies:
            copy.start()

    def ready(copies):
        for copy in copies:
            copy.wait()

    def load_tile(i, slot):
        t = jnp.where(lax.rem(i, 2) == 0, 1 - p.tp, p.tp)
        first = pl.multiple_of(HC + i // 2 * T, 128)
        return [
            pltpu.make_async_copy(
                wm.at[t, :, pl.ds(first, T)], ring.at[slot, :, pl.ds(0, T)], ring_sem.at[0, slot]
            ),
            pltpu.make_async_copy(
                wm.at[t, :, pl.ds(first + FC, T)], ring.at[slot, :, pl.ds(T, T)], ring_sem.at[1, slot]
            ),
        ]

    def pair_at(it):
        turn = it % dm.PAIRS
        return jnp.where(turn % 2 == 0, 1 - p.tp, p.tp) * PT + turn // 2

    def load_kv(it, slot):
        pair, g = pair_at(it), it // dm.PAIRS
        lanes = pl.ds(pl.multiple_of(pair * 128, 128), 128)
        return [
            pltpu.make_async_copy(k_hbm.at[g, :, lanes], kbuf.at[slot], kv_sem.at[0, slot]),
            pltpu.make_async_copy(v_hbm.at[g, :, lanes], vbuf.at[slot], kv_sem.at[1, slot]),
        ]

    wo_load = pltpu.make_async_copy(wm.at[:, :, pl.ds(0, HC)], wo, wo_sem)
    wo_load.start()
    begin(load_tile(0, 0))
    begin(load_kv(0, 0))
    p.greet(trades=True)
    fill_masks(dm, maskp, maskx)
    gain_two, bias_two = ln[2:3, :], ln[3:4, :]

    hn, gd = slice(0, NT), slice(NT, 2 * NT)
    STEP = 128

    def by_rows(step):
        def prompt_part(i, carry):
            rows = pl.ds(pl.multiple_of(i * STEP, STEP), STEP)
            step(own_p[rows, :], cot_p[rows, :], i * STEP)
            return carry

        def cont_part(i, carry):
            rows = pl.ds(pl.multiple_of(i * STEP, STEP), STEP)
            step(own_c[rows, :], cot_c[rows, :], NP + i * STEP)
            return carry

        lax.fori_loop(0, NP // STEP, prompt_part, 0)
        lax.fori_loop(0, (NT - NP) // STEP, cont_part, 0)

    def shifted(first, row):
        return pl.ds(pl.multiple_of(first + row, STEP), STEP)

    wo_load.wait()

    def enter(x, cot, row):
        rows = shifted(0, row)
        r = x.astype(F32)
        for t in range(TP):
            r += dot_nt(att[rows, t * HC : (t + 1) * HC], wo[t])
        resid[rows, :] = r
        blk[rows, :] = r
        h, _ = norm_stats(r)
        n = (h * gain_two + bias_two).astype(BF16)
        dk[rows, :] = n
        nt[:, rows] = transpose(n)
        g = (mix[4] * cot.astype(F32)).astype(BF16)
        dk[shifted(NT, row), :] = g
        nt[:, shifted(NT, row)] = transpose(g)
        gh[rows, :] = jnp.zeros((STEP, D), F32)

    by_rows(enter)

    during = {}

    def on(stage, step):
        during.setdefault(stage, []).append(step)

    def run_when(index, name):
        for (kind, when), steps in during.items():
            if kind == name:

                @pl.when(index == when)
                def _():
                    for step in steps:
                        step()


    sums = SmallSum(p, sm, sm_near, sm_rows, sm_across, sm_planes, sm_ss, sm_rc, sm_ry, sm_rx, sm_rz)
    hops = [(c, b) for c in range(1, p.ctxs - 1) for b in range(c + 1, p.ctxs)]

    def hop(g, part):
        third = pl.cdiv(len(hops), 3)
        for c, b in hops[part * third : (part + 1) * third]:

            @pl.when(p.ctx == c)
            def _():
                at = b - c
                landed(g, at)
                mine = dx_rows(g, b, p.core)[...].astype(F32)
                dxz[g, at] = (dxz[g, at].astype(F32) + mine).astype(BF16)
                rightward(g, dxz.at[g, at], c, b).start()

            far, to = p.ctxs - 1 - c, p.ctxs - 1 - b

            @pl.when(p.ctx == far)
            def _():
                at = p.ctxs - far + to
                landed(g, at)
                mine = dx_rows(g, to, p.core)[...].astype(F32)
                dxz[g, at] = (dxz[g, at].astype(F32) + mine).astype(BF16)
                leftward(g, dxz.at[g, at], far, to).start()

    schedule(ra, rb, on, p.ctxs, hop)

    def run(name):
        for kind, when in sorted(key for key in during if key[0] == name):
            for step in during[kind, when]:
                step()

    def feed(i, carry):
        slot = lax.rem(i, 2)

        @pl.when(i + 1 < 2 * n_a)
        def _():
            begin(load_tile(i + 1, 1 - slot))

        ready(load_tile(i, slot))
        up, dn = ring[slot, :, :T], ring[slot, :, T : 2 * T]
        c0 = 0.7978845608028654
        HALF = NT // 2
        for e in range(2):
            rows = slice(e * HALF, (e + 1) * HALF)
            u = dot(dk[rows, :], up)
            if e == 1:
                run_when(i, "m")
            u2 = u * u
            th = jnp.tanh(c0 * u * (1.0 + 0.044715 * u2))
            half = 0.5 * (1.0 + th)
            act = (u * half).astype(BF16)
            slope = half + 0.5 * u * (1.0 - th * th) * (c0 * (1.0 + 3 * 0.044715 * u2))
            dv[rows, :T] = act
            blk[rows, :] += dot_nt(act, dn)
            gu = (dot(dk[NT + e * HALF : NT + (e + 1) * HALF, :], dn) * slope).astype(BF16)
            dv[NT + e * HALF : NT + (e + 1) * HALF, :T] = gu
            gh[rows, :] += dot_nt(gu, up)

        @pl.when(i >= 2)
        def _():
            ra.cores_sent(slot * n_a + i // 2 - 1, slot)

        for y in range(chips):
            mine = slice(y * 2 * S, (y + 1) * 2 * S)
            ra.mine[slot, mine, :T] = dot(nt[mine, hn], dv[gd, :T]).astype(BF16)
            ra.mine[slot, mine, T:] = dot(nt[mine, gd], dv[hn, :T]).astype(BF16)
        ra.cores_send(slot * n_a + i // 2, slot)
        return carry

    lax.fori_loop(0, 2 * n_a, feed, 0)
    run("e")
    blk_away[:NT, :] = blk[...].astype(BF16)
    away = ra.copy(blk_away.at[pl.ds(0, NT), :], blk_home, b_send, b_recv, p.partner())

    @pl.when(p.core != p.tp)
    def _():
        away.start()

    @pl.when(p.core == p.tp)
    def _():
        blk_home[...] = blk_away[:NT, :]

    sm[...] = jnp.zeros_like(sm)

    def leave(x, cot, row):
        rows = shifted(0, row)
        cot = cot.astype(F32)
        sm[2:3, :] += jnp.sum(cot * blk[rows, :], axis=0, keepdims=True)
        h, scale = norm_stats(resid[rows, :])
        g = gh[rows, :]
        sm[0:1, :] += jnp.sum(g * h, axis=0, keepdims=True)
        sm[1:2, :] += jnp.sum(g, axis=0, keepdims=True)
        gr = mix[4] * cot + norm_back(g, gain_two, h, scale)
        resid[rows, :] = gr
        gb = gr.astype(BF16)
        nt[:, shifted(NT, row)] = transpose(gb)
        for t in range(TP):
            gatt[rows, t * HC : (t + 1) * HC] = dot(gb, wo[t]).astype(BF16)

    by_rows(leave)
    for slot, i in enumerate((0, NB)):
        t = p.tp if slot else 1 - p.tp
        lanes = pl.ds(pl.multiple_of(t * HC, 128), HC)
        for y in range(chips):
            mine = slice(y * 2 * S, (y + 1) * 2 * S)
            rb.mine[slot, mine, :] = dot(nt[mine, gd], att[:, lanes]).astype(BF16)
        rb.cores_send(i, slot)
    nt_load = [
        pltpu.make_async_copy(nt_hbm, nt, nt_sem.at[0]),
        pltpu.make_async_copy(own_nt_hbm, own_nt, nt_sem.at[1]),
    ]
    begin(nt_load)
    wq_load = pltpu.make_async_copy(wq_hbm.at[:, :, pl.ds(0, 3 * HC)], ring.at[:, :, pl.ds(0, 3 * HC)], wq_sem)
    wq_load.start()
    during.setdefault(("a", dm.PAIRS - 1), []).insert(0, partial(ready, nt_load))

    def attend(turn, g):
        it = g * dm.PAIRS + turn
        pair = pair_at(it)
        slot = it % 2

        @pl.when(it + 1 < G * dm.PAIRS)
        def _():
            begin(load_kv(it + 1, 1 - slot))

        lanes = pl.ds(pl.multiple_of(pair * 128, 128), 128)
        rp = pl.ds(pl.multiple_of(g * PB, PB), PB)
        rc = pl.ds(pl.multiple_of(dm.NP + g * NCH, NCH), NCH)
        qp, qc = q[rp, lanes], q[rc, lanes]
        gp, gc = gatt[rp, lanes], gatt[rc, lanes]
        ap, ac = att[rp, lanes].astype(F32), att[rc, lanes].astype(F32)
        qt = heads_columns(transpose(qp), transpose(qc))
        gpt, gct = gp.astype(F32).T, gc.astype(F32).T
        gt = heads_columns(gpt.astype(BF16), gct.astype(BF16))
        qs, gs = heads_rows(qp, qc), heads_rows(gp, gc)
        prodp, prodc = gpt * ap.T, gct * ac.T
        delta = jnp.concatenate(
            [
                jnp.sum(prodp[:HD], axis=0, keepdims=True),
                jnp.sum(prodp[HD:], axis=0, keepdims=True),
                jnp.sum(prodc[:HD], axis=0, keepdims=True),
                jnp.sum(prodc[HD:], axis=0, keepdims=True),
            ],
            axis=1,
        )
        stat = lse[g * dm.PAIRS + pair]
        ready(load_kv(it, slot))

        def grads(s, kt, vt, cols):
            pr = jnp.exp(s - stat[:, cols:])
            dp = dot(vt, gt[:, cols:])
            ds = (pr * (dp - delta[:, cols:])).astype(BF16)
            gv = dot(pr.astype(BF16), gs[cols:])
            gk = dot(ds, qs[cols:])
            gq = dot(transpose(kt), ds)
            return gk, gv, gq

        acc = None
        for j in range(tiles):
            rows = slice(j * TILE, (j + 1) * TILE)
            kt = kbuf[slot, rows, :]
            s = dot(kt, qt)
            s = jnp.concatenate([s[:, : 2 * PB] + twice(maskp[rows, :]), s[:, 2 * PB :]], axis=1)
            gk, gv, gq = grads(s, kt, vbuf[slot, rows, :], 0)
            gk = rotate_back(gk, cos[rows, :], sin[rows, :]).astype(BF16)
            gv = gv.astype(BF16)
            out = pl.ds(pl.multiple_of(g * R + j * TILE, 128), TILE)
            dk[out, lanes] = gk
            dv[out, lanes] = gv
            if j == tiles // 2:
                run_when(it, "a")
            acc = gq if acc is None else acc + gq
        kt = kbuf[slot, dm.P :, :]
        s = dot(kt, qt[:, 2 * PB :]) + maskx[...]
        gk, gv, gq = grads(s, kt, vbuf[slot, dm.P :, :], 2 * PB)
        for c in range(dm.NC):
            rows = slice(dm.P, dm.P + CL)
            out = pl.ds(pl.multiple_of(g * R + dm.P + c * CL, CL), CL)
            part = rotate_back(gk[c * CL : (c + 1) * CL], cos[rows, :], sin[rows, :])
            dk[out, lanes] = part.astype(BF16)
            dv[out, lanes] = gv[c * CL : (c + 1) * CL].astype(BF16)
        accp = acc[:, : 2 * PB] * 0.125
        accc = (acc[:, 2 * PB :] + gq) * 0.125
        outp = jnp.where(sublane_pick((128, PB), True), accp[:, :PB], accp[:, PB:]).T
        outc = jnp.where(sublane_pick((128, NCH), True), accc[:, :NCH], accc[:, NCH:]).T
        tab = pl.ds(pl.multiple_of(block * PB, PB), PB)
        dq[rp, lanes] = rotate_back(outp, cos[tab, :], sin[tab, :]).astype(BF16)
        tab = pl.ds(pl.multiple_of(dm.P + p.core * dm.CH, dm.CH), dm.CH)
        for c in range(dm.NC):
            part = rotate_back(outc[c * dm.CH : (c + 1) * dm.CH], cos[tab, :], sin[tab, :])
            rows = pl.ds(pl.multiple_of(dm.NP + g * NCH + c * dm.CH, dm.CH), dm.CH)
            dq[rows, lanes] = part.astype(BF16)

        @pl.when(g == G - 1)
        def _():
            put = turn % 2
            index = put * NB + 1 + turn // 2
            rb.cores_sent(index - 1, put)
            both = jnp.concatenate([dk[:, lanes], dv[:, lanes]], axis=1)
            for y in range(chips):
                mine = slice(y * 2 * S, (y + 1) * 2 * S)
                rb.mine[put, mine, 128:] = dot(nt[mine, :], both).astype(BF16)
                rb.mine[put, mine, :128] = dot(own_nt[mine, :], dq[:, lanes]).astype(BF16)
            rb.cores_send(index, put)

        return g

    w = ring

    def project(rows):
        total = None
        for t in range(TP):
            part = dot_nt(dk[rows, t * HC : (t + 1) * HC], w[t, :, HC : 2 * HC])
            total = part if total is None else total + part
            total += dot_nt(dv[rows, t * HC : (t + 1) * HC], w[t, :, 2 * HC : 3 * HC])
        return total

    NCONT = NT - NP
    gain_one = ln[0:1, :]
    halves = lambda core, g: pl.ds(pl.multiple_of(core * NCONT + g * NCH, 16), NCH)

    def dx_at(g, c, first, count):
        if g == G - 1:
            return dk.at[pl.ds(pl.multiple_of(g * R + c * 2 * PB + first, PB), count), :]
        fit = D // (2 * PB)
        row = pl.multiple_of(c % fit * 2 * PB + first, PB)
        return ra.mine.at[c // fit, pl.ds(row, count), pl.ds(0, D)]

    def dx_rows(g, c, core):
        return dx_at(g, c, core * PB, PB)

    def to_mate(g, k):
        i = g * p.ctxs + k
        rows = dx_rows(g, p.ctx_after(k), 1 - p.core)
        return ra.copy(rows, dxm.at[i], m_send.at[i], m_recv.at[i], p.mate())

    def rightward(g, src, c, b):
        i = b - c - 1
        return ra.copy(src, dxz.at[g, i], z_send.at[g, b], z_recv.at[g, i], p.at(ctx=c + 1))

    def leftward(g, src, c, b):
        i = p.ctxs - c + 1 + b
        return ra.copy(src, dxz.at[g, i], z_send.at[g, b], z_recv.at[g, i], p.at(ctx=c - 1))

    def landed(g, i):
        pltpu.make_async_copy(dxz.at[g, i], dxz.at[g, i], z_recv.at[g, i]).wait()

    def each_group(g, step):
        for e in range(G):

            @pl.when(g == e)
            def _():
                step(e)

    def cont_copy(g):
        return ra.copy(
            blk_away.at[halves(1 - p.core, g), :],
            dxcm.at[pl.ds(pl.multiple_of(g * NCH, 16), NCH), :],
            c_send.at[g],
            c_recv.at[g],
            p.mate(),
        )

    def norm_sums(x, turned, rows):
        sm[8:9, :] += jnp.sum(x.astype(F32), axis=0, keepdims=True)
        for d in range(0, D, 128):
            gh[:128, d : d + 128] += dot(turned[d : d + 128, rows], x[:, d : d + 128])

    def norm_grads():
        same = lax.broadcasted_iota(jnp.int32, (128, 128), 0) == lax.broadcasted_iota(
            jnp.int32, (128, 128), 1
        )
        for d in range(0, D, 128):
            cols = slice(d, d + 128)
            x = blk[:, cols].astype(BF16)
            sm[8:9, cols] += jnp.sum(x.astype(F32), axis=0, keepdims=True)
            gh[:128, cols] += dot(own_nt[cols, :], x)
            total = jnp.sum(jnp.where(same, gh[:128, cols], 0.0), axis=0, keepdims=True)
            sm[7:8, cols] = (total - ln[1:2, cols] * sm[8:9, cols]) / ln[0:1, cols]

    gh[:128, :] = jnp.zeros((128, D), F32)

    def group(g, carry):
        lax.fori_loop(0, dm.PAIRS, attend, g)

        @pl.when(g == 0)
        def _():
            wq_load.wait()
            ra.cores_sent(n_a - 1, 0)
            ra.cores_sent(2 * n_a - 1, 1)

            @pl.when(p.core != p.tp)
            def _():
                away.wait_send()

        def planes(i, carry):
            @pl.when(i < p.ctxs)
            def _():
                k = lax.rem(i + 1, p.ctxs)
                both = pl.ds(pl.multiple_of(g * R + p.ctx_after(k) * 2 * PB, 2 * PB), 2 * PB)
                total = project(both).astype(BF16)
                norm_sums(total, nt, both)

                def out(e):
                    dx_at(e, p.ctx_after(k), 0, 2 * PB)[...] = total
                    to_mate(e, k).start()

                each_group(g, out)
                run_when(g * p.ctxs + i, "p")

            @pl.when(i > 0)
            def _():
                k = lax.rem(i, p.ctxs)

                def back(e):
                    to_mate(e, k).wait_recv()
                    b = p.ctx_after(k)
                    mine = dx_rows(e, b, p.core)
                    mine[...] = (mine[...].astype(F32) + dxm[e * p.ctxs + k].astype(F32)).astype(BF16)

                    @pl.when((k > 0) & (p.ctx == 0))
                    def _():
                        rightward(e, mine, 0, b).start()

                    @pl.when((k > 0) & (p.ctx == p.ctxs - 1))
                    def _():
                        leftward(e, mine, p.ctxs - 1, b).start()

                each_group(g, back)

            return carry

        lax.fori_loop(0, p.ctxs + 1, planes, 0)
        rows = pl.ds(pl.multiple_of(g * R + dm.P, CL), NX)
        total = project(rows).astype(BF16)
        norm_sums(total, nt, rows)
        for c in range(dm.NC):
            for e in range(2):
                out = pl.ds(pl.multiple_of(e * NCONT + g * NCH + c * dm.CH, dm.CH), dm.CH)
                blk_away[out, :] = total[c * CL + e * dm.CH : c * CL + (e + 1) * dm.CH]
        cont_copy(g).start()
        for first, count in ((g * PB, PB), (NP + g * NCH, NCH)):
            rows = pl.ds(pl.multiple_of(first, 16), count)
            total = dot_nt(dq[rows, :HC], w[0, :, :HC])
            for t in range(1, TP):
                total += dot_nt(dq[rows, t * HC : (t + 1) * HC], w[t, :, :HC])
            blk[rows, :] = total
        return carry

    def enter_back(gn, x, rows):
        gn += blk[rows, :]
        hat, scale = norm_stats(x.astype(F32))
        gatt[rows, :] = (resid[rows, :] + norm_back(gn, gain_one, hat, scale)).astype(BF16)

    def gin_away(part):
        rows = pl.ds(0, NP) if part == 0 else pl.ds(NP, NT - NP)
        return ra.copy(gatt.at[rows, :], gin_home.at[rows, :], g_send.at[part], g_recv.at[part], p.partner())

    def give(part):
        rows = slice(0, NP) if part == 0 else slice(NP, NT)

        @pl.when(p.core != p.tp)
        def _():
            gin_away(part).start()

        @pl.when(p.core == p.tp)
        def _():
            gin_home[rows, :] = gatt[rows, :]

    lax.fori_loop(0, G, group, 0)
    homes = []
    for i, (a, c) in enumerate(
        [(home_arrays_p, home_arrays_c)]
        + [(early_p.at[e], early_c.at[e]) for e in range(3)]
        + [(home_cot_p, home_cot_c)]
    ):
        homes.append(pltpu.make_async_copy(a, dv.at[pl.ds(i * NT, NP), :], home_sem.at[0, i]))
        homes.append(pltpu.make_async_copy(c, dv.at[pl.ds(i * NT + NP, NT - NP), :], home_sem.at[1, i]))
    begin(homes)

    def cont_back(g, carry):
        cont_copy(g).wait_recv()
        here = pl.ds(pl.multiple_of(g * NCH, 16), NCH)
        gn = blk_away[halves(p.core, g), :].astype(F32) + dxcm[here, :].astype(F32)
        enter_back(gn, own_c[here, :], pl.ds(pl.multiple_of(NP + g * NCH, 16), NCH))
        return carry

    lax.fori_loop(0, G, cont_back, 0)
    give(1)

    ready(homes)

    @pl.when(p.core != p.tp)
    def _():
        away.wait_recv()

    def blend(i, carry):
        rows = shifted(0, i * STEP)
        res = mix[4] * blk_home[rows, :].astype(F32)
        c = dv[shifted(4 * NT, i * STEP), :].astype(F32)
        for e in range(4):
            a = dv[shifted(e * NT, i * STEP), :].astype(F32)
            res += mix[e] * a
            sm[3 + e : 4 + e, :] += jnp.sum(c * a, axis=0, keepdims=True)
        blk_home[rows, :] = res.astype(BF16)
        return carry

    lax.fori_loop(0, NT // STEP, blend, 0)
    puts = [
        pltpu.make_async_copy(blk_home.at[pl.ds(0, NP), :], out_p, put_sem.at[0]),
        pltpu.make_async_copy(blk_home.at[pl.ds(NP, NT - NP), :], out_c, put_sem.at[1]),
    ]
    begin(puts)
    norm_grads()
    sums.step(0)
    for when in range(10):
        for step in during.get(("t", when), []):
            step()
        if SMALL_AT.get(when):
            sums.step(SMALL_AT[when])

    for g in range(G):
        here = slice(g * PB, (g + 1) * PB)

        @pl.when(p.ctx > 0)
        def _():
            landed(g, 0)
            blk[here, :] += dxz[g, 0].astype(F32)

        @pl.when(p.ctx < p.ctxs - 1)
        def _():
            landed(g, p.ctxs)
            blk[here, :] += dxz[g, p.ctxs].astype(F32)

        enter_back(dx_rows(g, p.ctx, p.core)[...].astype(F32), own_p[here, :], here)
    give(0)
    for when in range(10, 20):
        for step in during.get(("t", when), []):
            step()
    small_out[...] = sums.result()
    gu_puts = []
    for j in range(n_a):
        ra.ctx_end(j)
        total = ra.result(j)
        gd_out[:, j * T : (j + 1) * T] = total[:, T:]
        if len(gu_puts) > 0:
            gu_puts[-1].wait()
        gh[:S, :T] = total[:, :T]
        gu_puts.append(
            pltpu.make_async_copy(
                gh.at[pl.ds(0, S), pl.ds(0, T)], gu_out.at[:, pl.ds(j * T, T)], put_sem.at[2]
            )
        )
        gu_puts[-1].start()
    gu_puts[-1].wait()
    for j in range(NB):
        rb.ctx_end(j)
        total = rb.result(j)
        if j == 0:
            go_out[...] = total
        else:
            for c in range(3):
                gq_out[c, :, (j - 1) * 128 : j * 128] = total[:, c * 128 : (c + 1) * 128]

    @pl.when(p.core != p.tp)
    def _():
        for part in range(2):
            gin_away(part).wait_recv()
            gin_away(part).wait_send()

    more = [
        pltpu.make_async_copy(gin_home.at[pl.ds(0, NP), :], gin_p, put_sem.at[2]),
        pltpu.make_async_copy(gin_home.at[pl.ds(NP, NT - NP), :], gin_c, put_sem.at[3]),
    ]
    begin(more)
    ready(puts + more)
    rb.cores_sent(NB - 1, 0)
    rb.cores_sent(2 * NB - 1, 1)
    for g in range(G):
        for k in range(p.ctxs):
            to_mate(g, k).wait_send()
        for k in range(1, p.ctxs):
            b = p.ctx_after(k)
            ra.copy(dxz.at[g, 0], dxz.at[g, 0], z_send.at[g, b], z_send.at[g, b], p.mate()).wait_send()
        cont_copy(g).wait_send()
    ra.drain()
    rb.drain()


def deliver_kernel(count, *refs):
    sources, small, targets = refs[:count], refs[count], refs[count + 1 : 2 * count + 1]
    outs = refs[2 * count + 1 : 2 * count + 6]
    kept = refs[2 * count + 6 : 3 * count + 6]
    in_sem, out_sem, parts = refs[3 * count + 6 :]
    loads = [pltpu.make_async_copy(sources[i], kept[i], in_sem.at[i]) for i in range(count)]
    puts = [pltpu.make_async_copy(kept[i], targets[i], out_sem.at[i]) for i in range(count)]
    for load in loads:
        load.start()
    S = parts.shape[2]
    norms = jnp.concatenate([small[7:9, :], small[0:2, :], jnp.zeros((4, small.shape[1]), F32)], axis=0)
    for d in range(parts.shape[0]):
        parts[d] = norms[:, d * S : (d + 1) * S]
    mine = parts[lax.axis_index("dp")]
    for i in range(4):
        outs[i][...] = mine[i : i + 1, :]
    sums = jnp.sum(small[...], axis=1, keepdims=True)
    order = (3, 4, 5, 6, 2)
    lanes = lax.broadcasted_iota(jnp.int32, (1, 5), 1)
    mix = jnp.zeros((1, 5), F32)
    for i, row in enumerate(order):
        mix = jnp.where(lanes == i, sums[row : row + 1, :], mix)
    outs[4][...] = mix
    for i in range(count):
        loads[i].wait()
        puts[i].start()
    for put in puts:
        put.wait()


def params(**more):
    return pltpu.CompilerParams(vmem_limit_bytes=VMEM_LIMIT, **more)


def per_device(
    prompt_in,
    cont_in,
    prompt_embed,
    cont_embed,
    prompt_earlier,
    cont_earlier,
    ln1_gain,
    ln1_bias,
    ln2_gain,
    ln2_bias,
    w_qkv,
    w_out,
    w_up,
    w_down,
    mix_weights,
    prompt_cot,
    cont_cot,
):
    G, PB, D = prompt_in.shape
    NC, CH = cont_in.shape[1], cont_in.shape[2]
    TP = lax.axis_size("tp")
    PROMPT = PB * TP * lax.axis_size("ctx")
    HC, FC = w_qkv.shape[2], w_up.shape[1]
    S = w_qkv.shape[0]
    dm = Dims(G, PROMPT, PB, NC, CH, D, HC * TP // HD)
    R, NT, NP = dm.R, dm.NT, dm.NP

    sds = jax.ShapeDtypeStruct
    chips, ctxs = lax.axis_size("dp") // 2, lax.axis_size("ctx")
    norms = jnp.concatenate([ln1_gain, ln1_bias, ln2_gain, ln2_bias]).reshape(4, S)
    norms = jnp.pad(norms, ((0, 124), (0, 0))).T
    wq_shard = jnp.concatenate([w_qkv.reshape(S, 3 * HC), norms], axis=1)
    wm_shard = jnp.concatenate([w_out.T, w_up, w_down.T], axis=1)

    positions = jnp.arange(PROMPT + CL, dtype=jnp.int32).astype(F32)
    freq = 10000.0 ** (-(jnp.arange(HD // 2, dtype=jnp.int32).astype(F32) / (HD // 2)))
    angles = freq[:, None] * positions[None, :]
    cos_few, sin_few = jnp.cos(angles), jnp.sin(angles)

    any_ = pl.BlockSpec(memory_space=pl.ANY)
    vmem = pl.BlockSpec(memory_space=pltpu.VMEM)
    dma = pltpu.SemaphoreType.DMA
    left = (HC + 2 * FC) // 128 * 2 // 3 * 128
    q, att, lse, ln, cos, sin, nt, own_nt, k, v, wq, wm, own_p, own_c, cot_p, cot_c = pl.pallas_call(
        partial(forward_kernel, dm, left),
        out_shape=(
            sds((NT, D), BF16),
            sds((NT, D), BF16),
            sds((G * dm.PAIRS, 1, dm.COLS), F32),
            sds((8, D), F32),
            sds((PROMPT + CL, 128), F32),
            sds((PROMPT + CL, 128), F32),
            sds((D, G * R), BF16),
            sds((D, NT), BF16),
            sds((G, R, D), BF16),
            sds((G, R, D), BF16),
            sds((TP, D, 3 * HC + 128), BF16),
            sds((TP, D, HC + 2 * FC), BF16),
            sds(prompt_in.shape, BF16),
            sds(cont_in.shape, BF16),
            sds(prompt_in.shape, BF16),
            sds(cont_in.shape, BF16),
        ),
        in_specs=[vmem] * 5 + [any_] * 3,
        out_specs=(vmem,) * 6 + (any_,) * 10,
        scratch_shapes=[
            pltpu.VMEM((D, G * R), BF16),
            pltpu.VMEM((D, NT), BF16),
            pltpu.VMEM((G, R, D), BF16),
            pltpu.VMEM((G, R, D), BF16),
            pltpu.VMEM((PROMPT, PB), F32),
            pltpu.VMEM((dm.NX, 2 * dm.NCH), F32),
            pltpu.VMEM((PROMPT, dm.COLS), F32),
            pltpu.VMEM((G * R, D), BF16),
            pltpu.VMEM((NT, D), BF16),
            pltpu.VMEM((2 * ctxs, G, PB, D), BF16),
            pltpu.VMEM((2, G, NC, CH, D), BF16),
            pltpu.VMEM((TP, D, 3 * HC + 128), BF16),
            dma((7,)),
            dma((4,)),
            dma((4,)),
            dma((2 * ctxs - 1,)),
            dma((ctxs - 1,)),
            dma((ctxs,)),
            dma,
            dma,
            dma((2,)),
        ]
        + WeightGather.semaphores(chips)
        + WeightGather.semaphores(chips),
        compiler_params=params(collective_id=0, has_side_effects=True),
        name="forward",
    )(prompt_in, cont_in, cos_few, sin_few, wq_shard, wm_shard, prompt_cot, cont_cot)
    T = 512 if FC % 512 == 0 else 256
    plan_a, plan_b = [False, False, True], [True, True, True, False]
    far = max(chips - 1, 1)
    rows = lambda x: x.reshape(-1, D)
    out_p, out_c, gin_p, gin_c, gq, go, gu, gd, small = pl.pallas_call(
        partial(backward_kernel, dm, T, FC, plan_a, plan_b),
        out_shape=(
            sds((NP, D), BF16),
            sds((NT - NP, D), BF16),
            sds((NP, D), BF16),
            sds((NT - NP, D), BF16),
            sds((3, S, HC), F32),
            sds((S, HC), F32),
            sds((S, FC), F32),
            sds((S, FC), F32),
            sds((16, D), F32),
        ),
        in_specs=[pl.BlockSpec(memory_space=pltpu.SMEM)] + [vmem] * 10 + [any_] * 12,
        out_specs=(any_,) * 4 + (vmem, vmem, any_, vmem, vmem),
        scratch_shapes=[
            pltpu.VMEM((NT, D), F32),
            pltpu.VMEM((NT, D), F32),
            pltpu.VMEM((NT, D), F32),
            pltpu.VMEM((TP, D, HC), BF16),
            pltpu.VMEM((2, D, max(2 * T, 3 * HC)), BF16),
            pltpu.VMEM((NT, D), BF16),
            pltpu.VMEM((D, G * R), BF16),
            pltpu.VMEM((D, NT), BF16),
            pltpu.VMEM((PROMPT, PB), F32),
            pltpu.VMEM((dm.NX, 2 * dm.NCH), F32),
            pltpu.VMEM((2, R, 128), BF16),
            pltpu.VMEM((2, R, 128), BF16),
            pltpu.VMEM((G * R, D), BF16),
            pltpu.VMEM((G * R, D), BF16),
            pltpu.VMEM((NT, D), BF16),
            pltpu.VMEM((G * ctxs, PB, D), BF16),
            pltpu.VMEM((G, ctxs + 1, PB, D), BF16),
            pltpu.VMEM((NT - NP, D), BF16),
            pltpu.VMEM((max(NT, 2 * (NT - NP)), D), BF16),
            pltpu.VMEM((NT, D), BF16),
            pltpu.VMEM((NT, D), BF16),
            dma((4,)),
            dma((2, 2)),
            dma,
            dma((2, 2)),
            dma((2,)),
            dma,
            dma((2, 5)),
            dma,
            dma,
            dma((2,)),
            dma((2,)),
            dma((G * ctxs,)),
            dma((G * ctxs,)),
            dma((G, ctxs)),
            dma((G, ctxs + 1)),
            dma((G,)),
            dma((G,)),
            pltpu.VMEM((16, D), F32),
            pltpu.VMEM((16, D), F32),
            pltpu.VMEM((chips, 16, D), F32),
            pltpu.VMEM((2, 16, D), F32),
            pltpu.VMEM((ctxs, 16, D), F32),
            dma((1 + chips + ctxs,)),
            dma,
            dma((far,)),
            dma,
            dma((ctxs - 1,)),
        ]
        + Reduce.scratch(plan_a, chips, S, 2 * T)
        + Reduce.scratch(plan_b, chips, S, HC),
        compiler_params=params(collective_id=1, has_side_effects=True),
        name="backward",
    )(
        mix_weights,
        att,
        rows(own_p),
        rows(own_c),
        rows(cot_p),
        rows(cot_c),
        ln,
        q,
        lse,
        cos,
        sin,
        wm,
        k,
        v,
        nt,
        own_nt,
        wq,
        rows(prompt_embed),
        rows(cont_embed),
        prompt_earlier.reshape(3, NP, D),
        cont_earlier.reshape(3, NT - NP, D),
        rows(prompt_cot),
        rows(cont_cot),
    )
    results = (out_p, out_c, gin_p, gin_c, gq, go, gu, gd)
    shapes = tuple(sds(x.shape, x.dtype) for x in results)
    out = pl.pallas_call(
        partial(deliver_kernel, len(results)),
        out_shape=shapes + (sds((1, S), F32),) * 4 + (sds((1, 5), F32),),
        in_specs=[any_] * len(results) + [vmem],
        out_specs=(any_,) * len(results) + (vmem,) * 5,
        scratch_shapes=[pltpu.VMEM(x.shape, x.dtype) for x in results]
        + [dma((len(results),)), dma((len(results),)), pltpu.VMEM((2 * chips, 8, S), F32)],
        compiler_params=params(),
        name="deliver",
    )(*results, small)
    out_p, out_c, gin_p, gin_c, gq, go, gu, gd = out[:8]
    gains = [x.reshape(S) for x in out[8:12]]
    return (
        out_p.reshape(prompt_in.shape),
        out_c.reshape(cont_in.shape),
        gin_p.reshape(prompt_in.shape),
        gin_c.reshape(cont_in.shape),
        *gains,
        jnp.transpose(gq, (1, 0, 2)),
        go.T,
        gu,
        gd.T,
        out[12].reshape(5),
    )


def solution(mesh):
    tokens = P("dp", ("ctx", "tp"), None)
    conts = P("dp", "ctx", "tp", None)
    weights = (P("dp", None, "tp"), P("tp", "dp"), P("dp", "tp"), P("tp", "dp"))
    in_specs = (
        tokens,
        conts,
        tokens,
        conts,
        P(None, "dp", ("ctx", "tp"), None),
        P(None, "dp", "ctx", "tp", None),
        P("dp"),
        P("dp"),
        P("dp"),
        P("dp"),
        *weights,
        P(),
        tokens,
        conts,
    )
    out_specs = (
        tokens,
        conts,
        tokens,
        conts,
        P("dp"),
        P("dp"),
        P("dp"),
        P("dp"),
        *weights,
        P(),
    )
    return jax.shard_map(
        per_device, mesh=mesh, in_specs=in_specs, out_specs=out_specs, check_vma=False
    )
```
